32 devices in a mesh: rep: 4 (over y, x), grp: 8 (over z, core).
Axes of the slice: x: 2, y: 2, z: 4, core: 2. Of those that a mesh axis runs over, the one named last changes fastest.
Arguments:
- block_in: bfloat16 [2, 4, 1024, 1024], P(None, 'rep', 'grp'), may hold values from -6 to 6
- cotangent: bfloat16 [2, 4, 1024, 1024], P(None, 'rep', 'grp'), may hold values from -6 to 6
- w_qkv: bfloat16 [2, 1024, 3072], P(None, 'grp'), may hold values from -0.1875 to 0.1875
- w_out: bfloat16 [2, 1024, 1024], P(None, 'grp'), may hold values from -0.1875 to 0.1875
- w_up: bfloat16 [2, 1024, 4096], P(None, 'grp'), may hold values from -0.1875 to 0.1875
- w_down: bfloat16 [2, 4096, 1024], P(None, 'grp'), may hold values from -0.09375 to 0.09375
- norm_gains: bfloat16 [2, 1024, 4], P(None, 'grp'), may hold values from 0.25 to 1.75
Outputs:
- block_out: bfloat16 [2, 4, 1024, 1024], P(None, 'rep', 'grp')
- block_in_grad: float32 [2, 4, 1024, 1024], P(None, 'rep', 'grp')
- w_qkv_grad: float32 [2, 1024, 3072], P(None, 'grp')
- w_out_grad: float32 [2, 1024, 1024], P(None, 'grp')
- w_up_grad: float32 [2, 1024, 4096], P(None, 'grp')
- w_down_grad: float32 [2, 4096, 1024], P(None, 'grp')
- norm_gains_grad: float32 [2, 1024, 4], P(None, 'grp')
The draws below stay inside these ranges and needn't reach their ends.
All inputs are finite; a program needn't handle non-finite values.
Results may differ from the reference program's by a relative error of at most 0.023.
Values may be sent and summed in bfloat16 or wider, within the bound.
A program may use at most 384 MiB of HBM per device.

```python
import jax
import jax.numpy as jnp
from jax import lax

D = 1024
FF = 4096
HEADS = 16
HDIM = 64
LAYERS = 2
MICRO = 2
SEQS = 4
LENGTH = 1024


def steps_of(key, extent, split, least, high):
    loudness = 1.0
    for position, shards_of in split:
        heights = jax.random.uniform(jax.random.fold_in(jax.random.fold_in(key, 6), position), (shards_of,), jnp.float32, least / len(split), high / len(split))
        loudness = loudness * jnp.repeat(jnp.exp(heights), extent[position] // shards_of).reshape((-1,) + (1,) * (len(extent) - 1 - position))
    return loudness


def normal_values(rng, extent, deviation, reach, shards=(), held_as=jnp.bfloat16):
    values = jax.random.normal(rng, extent, jnp.float32) * deviation
    if len(shards) > 0:
        values = steps_of(rng, extent, shards, -0.22, 0.18) * values
    return jnp.clip(values, min=-reach, max=reach).astype(held_as)


def setup_inputs(seed: int = 0) -> dict:
    arg_keys = jax.random.split(jax.random.key(seed), 8)
    block_in = normal_values(arg_keys[0], (MICRO, SEQS, LENGTH, D), 1.0, 6.0, ((1, 4), (2, 8)))
    cotangent = normal_values(arg_keys[1], (MICRO, SEQS, LENGTH, D), 1.0, 6.0, ((1, 4), (2, 8)))
    w_qkv = normal_values(arg_keys[2], (LAYERS, D, 3 * D), D ** -0.5, 0.1875, ((1, 8),))
    w_out = normal_values(arg_keys[3], (LAYERS, D, D), D ** -0.5, 0.1875, ((1, 8),))
    w_up = normal_values(arg_keys[4], (LAYERS, D, FF), D ** -0.5, 0.1875, ((1, 8),))
    w_down = normal_values(arg_keys[5], (LAYERS, FF, D), FF ** -0.5, 0.09375, ((1, 8),))
    norm_gains = jnp.clip(1.0 + 0.15 * jax.random.normal(arg_keys[6], (LAYERS, D, 4), jnp.float32), 0.25, 1.75).astype(jnp.bfloat16)
    return dict(block_in=block_in, cotangent=cotangent, w_qkv=w_qkv, w_out=w_out, w_up=w_up, w_down=w_down, norm_gains=norm_gains)


EPS = 1e-06
HIGH = lax.Precision.HIGHEST

@jax.custom_vjp
def low(v):
    return lax.optimization_barrier(v.astype(jnp.bfloat16)).astype(jnp.float32)

@jax.custom_vjp
def low_back(v):
    return v

def low_keep(v):
    return (low(v), None)

def low_pass(kept, grad):
    return (grad,)

def back_keep(v):
    return (v, None)

def back_low(kept, grad):
    return (low(grad),)
low.defvjp(low_keep, low_pass)
low_back.defvjp(back_keep, back_low)

def norm_apply(values, gains):
    return values * lax.rsqrt(lax.optimization_barrier(jnp.mean(values * values, axis=-1, keepdims=True)) + EPS) * gains

def product(left, right):
    return jnp.dot(left, right, precision=HIGH)

def attention(query, keys, values):
    length = query.shape[0]
    width = min(512, length)
    count = length // width
    scale = HDIM ** (-0.5)

    def one_block(inputs):
        query_rows, row_start = inputs
        scores = jnp.einsum('qhd,khd->hqk', query_rows, keys, precision=HIGH) * scale
        scores = low_back(scores)
        query_pos = row_start + jnp.arange(width, dtype=jnp.int32)
        key_pos = jnp.arange(length, dtype=jnp.int32)
        allowed = key_pos[None, :] <= query_pos[:, None]
        scores = jnp.where(allowed[None], scores, -1e+30)
        probs = low(jax.nn.softmax(scores, axis=-1))
        return jnp.einsum('hqk,khd->qhd', probs, values, precision=HIGH)
    query_blocks = query.reshape(count, width, HEADS, HDIM)
    starts = jnp.arange(count, dtype=jnp.int32) * width
    mixed = lax.map(jax.checkpoint(one_block), (query_blocks, starts))
    return mixed.reshape(length, HEADS * HDIM)

def layer(hidden, w_qkv_one, w_out_one, w_up_one, w_down_one, gains):
    length = hidden.shape[0]
    normed = low(norm_apply(hidden, gains[:, 0]))
    qkv = low(low_back(product(normed, w_qkv_one)))
    query = qkv[:, :D].reshape(length, HEADS, HDIM)
    keys = qkv[:, D:2 * D].reshape(length, HEADS, HDIM)
    values = qkv[:, 2 * D:].reshape(length, HEADS, HDIM)
    mixed = low(low_back(attention(query, keys, values)))
    attn_out = low_back(product(mixed, w_out_one))
    resid = hidden + norm_apply(attn_out, gains[:, 1])
    mlp_in = low(norm_apply(resid, gains[:, 2]))
    up_out = low_back(product(mlp_in, w_up_one))
    active = low(jax.nn.gelu(up_out))
    down_out = low_back(product(active, w_down_one))
    return resid + norm_apply(down_out, gains[:, 3])

def stack_run(params, hidden):
    for layer_idx in range(LAYERS):
        hidden = layer(hidden, *[member[layer_idx] for member in params])
    return hidden

def reference(block_in, cotangent, w_qkv, w_out, w_up, w_down, norm_gains):
    params = tuple((member.astype(jnp.float32) for member in (w_qkv, w_out, w_up, w_down, norm_gains)))
    inputs = block_in.astype(jnp.float32).reshape(MICRO * SEQS, LENGTH, D)
    cotangents = cotangent.astype(jnp.float32).reshape(MICRO * SEQS, LENGTH, D)
    zeros = tuple((jnp.zeros_like(member) for member in params))

    def seq_step(totals, pair):
        hidden, grad_out = pair
        result, puller = jax.vjp(stack_run, params, hidden)
        param_grads, hidden_grad = puller(grad_out)
        totals = tuple((left + right for left, right in zip(totals, param_grads)))
        return (totals, (result.astype(jnp.bfloat16), hidden_grad))
    totals, (results, hidden_grads) = lax.scan(seq_step, zeros, (inputs, cotangents))
    return (results.reshape(MICRO, SEQS, LENGTH, D), hidden_grads.reshape(MICRO, SEQS, LENGTH, D), totals[0], totals[1], totals[2], totals[3], totals[4])
```

```python
import functools

import jax
import jax.numpy as jnp
from jax import lax
from jax.experimental import pallas as pl
from jax.experimental.pallas import tpu as pltpu
from jax.sharding import PartitionSpec as P

HEADS = 16
HDIM = 64
EPS = 1e-06
NEGATIVE = -1e30
BF = jnp.bfloat16
F32 = jnp.float32


def flip(axis, bit, value):
    size = lax.axis_size(axis)
    return lax.ppermute(value, axis, [(i, i ^ bit) for i in range(size)])


core = functools.partial(flip, "grp", 1)
near = functools.partial(flip, "grp", 2)
far = functools.partial(flip, "grp", 4)
along_x = functools.partial(flip, "rep", 1)
along_y = functools.partial(flip, "rep", 2)


def pick(stacked, index):
    return lax.dynamic_index_in_dim(stacked, index, 0, keepdims=False)


def dot(left, right):
    return jnp.dot(left, right, preferred_element_type=F32)


def dot_tn(left, right):
    return lax.dot_general(left, right, (((0,), (0,)), ((), ())), preferred_element_type=F32)


def dot_nt(left, right):
    return lax.dot_general(left, right, (((1,), (1,)), ((), ())), preferred_element_type=F32)


def norm(values, gain):
    return values * lax.rsqrt(jnp.mean(values * values, axis=-1, keepdims=True) + EPS) * gain


def norm_back(values, gain, grad):
    rstd = lax.rsqrt(jnp.mean(values * values, axis=-1, keepdims=True) + EPS)
    hat = values * rstd
    scaled = grad * gain
    back = rstd * (scaled - hat * jnp.mean(scaled * hat, axis=-1, keepdims=True))
    return back, jnp.sum(grad * hat, axis=0)


def head_mask(width, head):
    lanes = lax.broadcasted_iota(jnp.int32, (1, width), 1)
    return (lanes // HDIM) == head


def attend_kernel(block, qkv_ref, mixed_ref, lse_ref):
    length, width = mixed_ref.shape
    heads = width // HDIM
    row = lax.broadcasted_iota(jnp.int32, (block, block), 0)
    col = lax.broadcasted_iota(jnp.int32, (block, block), 1)
    below = col <= row
    zero = jnp.zeros((), BF)
    lane = lax.broadcasted_iota(jnp.int32, (1, 128), 1)
    for start in range(0, length, block):
        stop = start + block
        query = qkv_ref[start:stop, :width] * jnp.asarray(HDIM**-0.5, BF)
        total = jnp.zeros((block, width), F32)
        stats = jnp.zeros((block, 128), F32)
        for head in range(heads):
            mask = head_mask(width, head)
            keys = jnp.where(mask, qkv_ref[:stop, width : 2 * width], zero)
            vals = jnp.where(mask, qkv_ref[:stop, 2 * width :], zero)
            scores = dot_nt(query, keys)
            last = jnp.where(below, scores[:, start:], NEGATIVE)
            scores = jnp.concatenate([scores[:, :start], last], axis=1) if start else last
            top = jnp.max(scores, axis=1, keepdims=True)
            terms = jnp.exp(scores - top)
            sums = jnp.sum(terms, axis=1, keepdims=True)
            total = total + dot(terms.astype(BF), vals) * (1.0 / sums)
            stats = jnp.where(lane == head, top + jnp.log(sums), stats)
        mixed_ref[start:stop, :] = total.astype(BF)
        lse_ref[start:stop, :] = stats


def attend(qkv):
    length, width = qkv.shape[0], qkv.shape[1] // 3
    heads = width // HDIM
    return pl.pallas_call(
        functools.partial(attend_kernel, 256),
        out_shape=(
            jax.ShapeDtypeStruct((length, width), BF),
            jax.ShapeDtypeStruct((length, 128), F32),
        ),
        compiler_params=pltpu.CompilerParams(vmem_limit_bytes=40 << 20),
        cost_estimate=pl.CostEstimate(
            flops=8 * heads * length * length * HDIM,
            bytes_accessed=length * width * 8 + length * 512,
            transcendentals=heads * length * length // 2,
        ),
    )(qkv)


def attend_back_kernel(block, qkv_ref, lse_ref, grad_ref, out_ref, dk_ref, dv_ref):
    length, width = grad_ref.shape
    heads = width // HDIM
    row = lax.broadcasted_iota(jnp.int32, (block, block), 0)
    col = lax.broadcasted_iota(jnp.int32, (block, block), 1)
    below = col <= row
    zero = jnp.zeros((), BF)
    scale = HDIM**-0.5
    dk_ref[...] = jnp.zeros_like(dk_ref)
    dv_ref[...] = jnp.zeros_like(dv_ref)
    for start in range(0, length, block):
        stop = start + block
        query = qkv_ref[start:stop, :width] * jnp.asarray(scale, BF)
        grad = grad_ref[start:stop, :]
        dq = jnp.zeros((block, width), F32)
        for head in range(heads):
            mask = head_mask(width, head)
            keys = jnp.where(mask, qkv_ref[:stop, width : 2 * width], zero)
            vals = jnp.where(mask, qkv_ref[:stop, 2 * width :], zero)
            scores = dot_nt(query, keys)
            last = jnp.where(below, scores[:, start:], NEGATIVE)
            scores = jnp.concatenate([scores[:, :start], last], axis=1) if start else last
            probs = jnp.exp(scores - lse_ref[start:stop, head : head + 1])
            prob_grad = dot_nt(grad, vals)
            delta = jnp.sum(probs * prob_grad, axis=1, keepdims=True)
            score_grad = (probs * (prob_grad - delta)).astype(BF)
            dq = dq + dot(score_grad, keys)
            dk_ref[:stop, :] += dot_tn(score_grad, jnp.where(mask, query, zero))
            dv_ref[:stop, :] += dot_tn(probs.astype(BF), jnp.where(mask, grad, zero))
        out_ref[start:stop, :width] = (dq * scale).astype(BF)
    out_ref[:, width : 2 * width] = dk_ref[...].astype(BF)
    out_ref[:, 2 * width :] = dv_ref[...].astype(BF)


def attend_back(qkv, lse, grad):
    length, width = grad.shape
    heads = width // HDIM
    return pl.pallas_call(
        functools.partial(attend_back_kernel, 256),
        out_shape=jax.ShapeDtypeStruct((length, 3 * width), BF),
        scratch_shapes=[pltpu.VMEM((length, width), F32)] * 2,
        compiler_params=pltpu.CompilerParams(vmem_limit_bytes=40 << 20),
        cost_estimate=pl.CostEstimate(
            flops=20 * heads * length * length * HDIM,
            bytes_accessed=length * width * 14 + length * 512,
            transcendentals=heads * length * length // 2,
        ),
    )(qkv, lse, grad)


def gather4(mine, place):
    other = core(mine)
    across = near(mine)
    corner = core(across)
    halves, rows, width = mine.shape
    whole = jnp.zeros((halves, 4, rows, width), mine.dtype)
    for value, where in ((mine, place), (other, place ^ 1), (across, place ^ 2), (corner, place ^ 3)):
        whole = lax.dynamic_update_slice(whole, value[:, None], (0, where, 0, 0))
    return whole.reshape(halves * 4 * rows, width)


def scatter4(part, place):
    total, width = part.shape
    part = part.reshape(2, 4, total // 8, width)

    def term(where):
        return lax.dynamic_slice(part, (0, where, 0, 0), (2, 1, total // 8, width))[:, 0]

    across = core(term(place ^ 3).astype(BF)).astype(F32) + term(place ^ 2)
    across = near(across.astype(BF))
    mine = core(term(place ^ 1).astype(BF)).astype(F32) + term(place)
    return (mine + across.astype(F32)).reshape(total // 4, width)


def spread_rep(mine, rep):
    return lax.all_gather(mine, "rep", axis=0, tiled=False)


def columns_in(weight, groups, unit, rep, place):
    rows, total = weight.shape
    quarter = pick(weight.reshape(4, rows // 4, total), rep)
    whole = lax.all_gather(quarter, "grp", axis=0, tiled=False)
    whole = whole.reshape(8, rows // 4, groups, 4, unit)
    mine = lax.dynamic_index_in_dim(whole, place, 3, keepdims=False)
    mine = mine.reshape(8, rows // 4, groups * unit)
    return lax.all_gather(mine, "rep", axis=1, tiled=True).reshape(8 * rows, groups * unit)


def columns_out(grad, groups, unit, rep, place, upper):
    total, width = grad.shape
    rows = total // 32
    low = grad.reshape(8, 4, rows, width)
    mine = lax.psum_scatter(low, "rep", scatter_dimension=1, tiled=False)
    mine = mine.reshape(2, 4, rows, width)
    other = far(pick(mine, 1 - upper))
    mine = (pick(mine, upper).astype(F32) + other.astype(F32)).astype(BF)
    side = place // 2
    mine = mine.reshape(2, 2, rows, width)
    other = near(pick(mine, 1 - side))
    mine = pick(mine, side)
    mine = jnp.where(side == 0, jnp.stack([mine, other]), jnp.stack([other, mine]))
    which = place % 2
    keep = lax.dynamic_index_in_dim(mine, which, 1, keepdims=False)
    give = lax.dynamic_index_in_dim(mine, 1 - which, 1, keepdims=False)
    other = core(give)
    both = jnp.where(which == 0, jnp.stack([keep, other], 1), jnp.stack([other, keep], 1))
    both = both.reshape(4, rows, groups, unit).transpose(1, 2, 0, 3).reshape(rows, groups * 4 * unit)
    return lax.all_gather(both, "rep", axis=0, tiled=True).astype(F32)


def rows_in(weight, upper):
    other = far(weight)
    return jnp.where(
        upper == 0, jnp.concatenate([weight, other]), jnp.concatenate([other, weight])
    )


def rows_out(grad, rep, upper):
    total, width = grad.shape
    rows = total // 8
    low = grad.reshape(2, 4, rows, width)
    mine = lax.psum_scatter(low, "rep", scatter_dimension=1, tiled=False)
    other = far(pick(mine, 1 - upper))
    mine = (pick(mine, upper).astype(F32) + other.astype(F32)).astype(BF)
    return lax.all_gather(mine, "rep", axis=0, tiled=True).astype(F32)


def body_pairs(block_in, cotangent, w_qkv, w_out, w_up, w_down, norm_gains):
    layers, rows, width = w_out.shape
    tokens = block_in.shape[2]
    hidden_unit = w_down.shape[1]
    rep = lax.axis_index("rep")
    grp = lax.axis_index("grp")
    place, upper = grp % 4, grp // 4

    gains = lax.all_gather(norm_gains, "grp", axis=1, tiled=True).astype(F32)
    gains = jnp.transpose(gains, (0, 2, 1))

    def bring(two):
        mine = pick(two[:, 0], upper)
        other = far(pick(two[:, 0], 1 - upper))
        return jnp.where(upper == 0, jnp.stack([mine, other]), jnp.stack([other, mine])).astype(F32)

    def send_back(mine):
        keep = pick(mine, upper)
        other = far(pick(mine, 1 - upper))
        return jnp.where(upper == 0, jnp.stack([keep, other]), jnp.stack([other, keep]))

    hidden = bring(block_in).reshape(2 * tokens, width)
    weights = []
    for layer in range(layers):
        weights.append(
            (
                columns_in(w_qkv[layer], 6, rows, rep, place),
                rows_in(w_out[layer], upper),
                columns_in(w_up[layer], 2, hidden_unit, rep, place),
                rows_in(w_down[layer], upper),
            )
        )

    def gather(values):
        return gather4(values.reshape(2, tokens, width), place)

    saved = []
    for layer in range(layers):
        qkv_w, out_w, up_w, down_w = weights[layer]
        gain = gains[layer]
        normed = gather(norm(hidden, gain[0]).astype(BF))
        qkv = dot(normed, qkv_w).astype(BF)
        mixed, lse = attend(qkv)
        attn_out = scatter4(dot(mixed, out_w), place)
        resid = hidden + norm(attn_out, gain[1])
        mlp_in = gather(norm(resid, gain[2]).astype(BF))
        up_out = dot(mlp_in, up_w)
        active = jax.nn.gelu(up_out).astype(BF)
        down_out = scatter4(dot(active, down_w), place)
        saved.append((hidden, normed, qkv, mixed, lse, attn_out, resid, mlp_in, up_out, active, down_out))
        hidden = resid + norm(down_out, gain[3])
    block_out = send_back(hidden.astype(BF).reshape(2, tokens, width))[:, None]

    grad = bring(cotangent).reshape(2 * tokens, width)
    results = [None] * layers
    gain_grads = [None] * layers
    for layer in reversed(range(layers)):
        qkv_w, out_w, up_w, down_w = weights[layer]
        gain = gains[layer]
        hidden, normed, qkv, mixed, lse, attn_out, resid, mlp_in, up_out, active, down_out = saved[layer]
        down_grad, four = norm_back(down_out, gain[3], grad)
        down_low = gather(down_grad.astype(BF))
        down_w_grad = dot_tn(active, down_low).astype(BF)
        active_grad = dot_nt(down_low, down_w)
        unused, puller = jax.vjp(jax.nn.gelu, up_out)
        up_low = puller(active_grad)[0].astype(BF)
        up_w_grad = dot_tn(mlp_in, up_low).astype(BF)
        mlp_grad = scatter4(dot_nt(up_low, up_w), place)
        part, three = norm_back(resid, gain[2], mlp_grad)
        resid_grad = grad + part
        attn_grad, two = norm_back(attn_out, gain[1], resid_grad)
        attn_low = gather(attn_grad.astype(BF))
        out_w_grad = dot_tn(mixed, attn_low).astype(BF)
        mixed_grad = dot_nt(attn_low, out_w).astype(BF)
        qkv_grad = attend_back(qkv, lse, mixed_grad)
        qkv_w_grad = dot_tn(normed, qkv_grad).astype(BF)
        normed_grad = scatter4(dot_nt(qkv_grad, qkv_w), place)
        part, one = norm_back(hidden, gain[0], normed_grad)
        grad = resid_grad + part
        gain_grads[layer] = jnp.stack([one, two, three, four], axis=1)
        results[layer] = (
            columns_out(qkv_w_grad, 6, rows, rep, place, upper),
            rows_out(out_w_grad, rep, upper),
            columns_out(up_w_grad, 2, hidden_unit, rep, place, upper),
            rows_out(down_w_grad, rep, upper),
        )
    block_in_grad = send_back(grad.astype(BF).reshape(2, tokens, width)).astype(F32)[:, None]
    gain_all = lax.psum(jnp.stack(gain_grads), ("rep", "grp"))
    gain_mine = lax.dynamic_slice_in_dim(gain_all, grp * rows, rows, 1)
    stacked = [jnp.stack([results[layer][k] for layer in range(layers)]) for k in range(4)]
    return (block_out, block_in_grad, *stacked, gain_mine)


def norm_apply(values, gains):
    return values * lax.rsqrt(jnp.mean(values * values, axis=-1, keepdims=True) + EPS) * gains


def inner_rows(left, right):
    return lax.dot_general(
        left, right, (((0,), (0,)), ((), ())), preferred_element_type=jnp.float32
    )


def times_trans(left, right):
    return lax.dot_general(
        left, right, (((1,), (1,)), ((), ())), preferred_element_type=jnp.float32
    )


def split_blocks(whole):
    length = whole.shape[0]
    width = min(512, length)
    count = length // width
    return (whole.reshape(count, width, HEADS, HDIM), width, count)


def block_at(blocks, index):
    return lax.dynamic_index_in_dim(blocks, index, 0, keepdims=False)


def key_scores(query, key_block, key_start, query_pos):
    scale = HDIM ** (-0.5)
    scores = (
        jnp.einsum("qhd,khd->hqk", query, key_block, preferred_element_type=jnp.float32) * scale
    )
    key_pos = key_start + jnp.arange(key_block.shape[0], dtype=jnp.int32)
    allowed = key_pos[None, :] <= query_pos[:, None]
    return (scores, allowed[None])


def attend_split(query, keys_all, values_all, query_pos):
    key_blocks, width, count = split_blocks(keys_all)
    value_blocks = split_blocks(values_all)[0]
    row_count = query.shape[0]
    upper = query_pos[row_count - 1] // width + 1

    def total_step(index, carry):
        running, total = carry
        scores, allowed = key_scores(query, block_at(key_blocks, index), index * width, query_pos)
        newest = jnp.maximum(running, jnp.max(jnp.where(allowed, scores, NEGATIVE), axis=-1))
        terms = jnp.where(allowed, jnp.exp(scores - newest[..., None]), 0.0)
        total = total * jnp.exp(running - newest) + jnp.sum(terms, axis=-1)
        return (newest, total)

    start_run = jnp.full((HEADS, row_count), NEGATIVE, jnp.float32)
    start_total = jnp.zeros((HEADS, row_count), jnp.float32)
    running, total = lax.fori_loop(0, upper, total_step, (start_run, start_total))
    log_total = running + jnp.log(total)

    def mix_step(index, accum):
        scores, allowed = key_scores(query, block_at(key_blocks, index), index * width, query_pos)
        probs = jnp.where(allowed, jnp.exp(scores - log_total[..., None]), 0.0)
        return accum + jnp.einsum(
            "hqk,khd->qhd",
            probs.astype(jnp.bfloat16),
            block_at(value_blocks, index),
            preferred_element_type=jnp.float32,
        )

    start_mix = jnp.zeros((row_count, HEADS, HDIM), jnp.float32)
    mixed = lax.fori_loop(0, upper, mix_step, start_mix)
    return (mixed.reshape(row_count, HEADS * HDIM), log_total)


def attend_back_split(query, keys_all, values_all, log_total, out_grad, delta, query_pos):
    key_blocks, width, count = split_blocks(keys_all)
    value_blocks = split_blocks(values_all)[0]
    row_count = query.shape[0]
    upper = query_pos[row_count - 1] // width + 1
    scale = HDIM ** (-0.5)

    def back_step(index, carry):
        query_acc, pieces = carry
        key_block = block_at(key_blocks, index)
        value_block = block_at(value_blocks, index)
        scores, allowed = key_scores(query, key_block, index * width, query_pos)
        probs = jnp.where(allowed, jnp.exp(scores - log_total[..., None]), 0.0)
        prob_grad = jnp.einsum(
            "qhd,khd->hqk", out_grad, value_block, preferred_element_type=jnp.float32
        )
        score_grad = (probs * (prob_grad - delta[..., None])).astype(jnp.bfloat16)
        query_acc = (
            query_acc
            + jnp.einsum("hqk,khd->qhd", score_grad, key_block, preferred_element_type=jnp.float32)
            * scale
        )
        key_grad = (
            jnp.einsum("hqk,qhd->khd", score_grad, query, preferred_element_type=jnp.float32)
            * scale
        )
        value_grad = jnp.einsum(
            "hqk,qhd->khd", probs.astype(jnp.bfloat16), out_grad, preferred_element_type=jnp.float32
        )
        joined = jnp.concatenate(
            [key_grad.reshape(width, HEADS * HDIM), value_grad.reshape(width, HEADS * HDIM)], axis=1
        )
        pieces = lax.dynamic_update_index_in_dim(pieces, joined, index, 0)
        return (query_acc, pieces)

    start_acc = jnp.zeros((row_count, HEADS, HDIM), jnp.float32)
    start_pieces = jnp.zeros((count, width, 2 * HEADS * HDIM), jnp.float32)
    query_grad, pieces = lax.fori_loop(0, upper, back_step, (start_acc, start_pieces))
    return (query_grad.reshape(row_count, HEADS * HDIM), pieces.reshape(-1, pieces.shape[-1]))


def layer_forward(hidden_in, weights, query_pos):
    w_qkv_full, w_out_full, w_up_full, w_down_full, gain_full = weights
    gains_f = gain_full.astype(jnp.float32)
    row_count = hidden_in.shape[0]
    width = w_out_full.shape[1]
    normed = norm_apply(hidden_in, gains_f[:, 0]).astype(jnp.bfloat16)
    qkv_low = jnp.dot(normed, w_qkv_full, preferred_element_type=jnp.float32).astype(jnp.bfloat16)
    query = qkv_low[:, :width]
    keys_all, values_all = (
        lax.all_gather(qkv_low[:, width : 2 * width], "grp", axis=0, tiled=True),
        lax.all_gather(qkv_low[:, 2 * width :], "grp", axis=0, tiled=True),
    )
    mixed, log_total = attend_split(
        query.reshape(row_count, HEADS, HDIM),
        keys_all.reshape(-1, HEADS, HDIM),
        values_all.reshape(-1, HEADS, HDIM),
        query_pos,
    )
    mixed_low = mixed.astype(jnp.bfloat16)
    attn_out = jnp.dot(mixed_low, w_out_full, preferred_element_type=jnp.float32)
    resid = hidden_in + norm_apply(attn_out, gains_f[:, 1])
    mlp_in = norm_apply(resid, gains_f[:, 2]).astype(jnp.bfloat16)
    up_out = jnp.dot(mlp_in, w_up_full, preferred_element_type=jnp.float32)
    active = jax.nn.gelu(up_out).astype(jnp.bfloat16)
    down_out = jnp.dot(active, w_down_full, preferred_element_type=jnp.float32)
    result = resid + norm_apply(down_out, gains_f[:, 3])
    kept = (
        hidden_in,
        normed,
        qkv_low,
        mixed,
        mixed_low,
        log_total,
        attn_out,
        resid,
        mlp_in,
        up_out,
        active,
        down_out,
    )
    return (result, kept)


def layer_backward(grad_out, weights, kept, query_pos):
    w_qkv_full, w_out_full, w_up_full, w_down_full, gain_full = weights
    (
        hidden_in,
        normed,
        qkv_low,
        mixed,
        mixed_low,
        log_total,
        attn_out,
        resid,
        mlp_in,
        up_out,
        active,
        down_out,
    ) = kept
    gains_f = gain_full.astype(jnp.float32)
    row_count = hidden_in.shape[0]
    width = w_out_full.shape[1]
    unused, puller = jax.vjp(norm_apply, down_out, gains_f[:, 3])
    down_grad, gain_four = puller(grad_out)
    down_low = down_grad.astype(jnp.bfloat16)
    w_down_grad = inner_rows(active, down_low)
    active_grad = times_trans(down_low, w_down_full)
    unused, puller = jax.vjp(jax.nn.gelu, up_out)
    up_low = puller(active_grad)[0].astype(jnp.bfloat16)
    w_up_grad = inner_rows(mlp_in, up_low)
    mlp_grad = times_trans(up_low, w_up_full)
    unused, puller = jax.vjp(norm_apply, resid, gains_f[:, 2])
    resid_part, gain_three = puller(mlp_grad)
    resid_grad = grad_out + resid_part
    unused, puller = jax.vjp(norm_apply, attn_out, gains_f[:, 1])
    attn_grad, gain_two = puller(resid_grad)
    attn_low = attn_grad.astype(jnp.bfloat16)
    w_out_grad = inner_rows(mixed_low, attn_low)
    mixed_grad = times_trans(attn_low, w_out_full).astype(jnp.bfloat16)
    keys_all, values_all = (
        lax.all_gather(qkv_low[:, width : 2 * width], "grp", axis=0, tiled=True),
        lax.all_gather(qkv_low[:, 2 * width :], "grp", axis=0, tiled=True),
    )
    delta = jnp.sum(
        (mixed_grad.astype(jnp.float32) * mixed).reshape(row_count, HEADS, HDIM), axis=-1
    ).T
    query_low = qkv_low[:, :width]
    query_grad, key_value_terms = attend_back_split(
        query_low.reshape(row_count, HEADS, HDIM),
        keys_all.reshape(-1, HEADS, HDIM),
        values_all.reshape(-1, HEADS, HDIM),
        log_total,
        mixed_grad.reshape(row_count, HEADS, HDIM),
        delta,
        query_pos,
    )
    key_value_grad = lax.psum_scatter(
        key_value_terms.astype(jnp.bfloat16), "grp", scatter_dimension=0, tiled=True
    ).astype(jnp.float32)
    qkv_grad = jnp.concatenate([query_grad, key_value_grad], axis=1).astype(jnp.bfloat16)
    w_qkv_grad = inner_rows(normed, qkv_grad)
    normed_grad = times_trans(qkv_grad, w_qkv_full)
    unused, puller = jax.vjp(norm_apply, hidden_in, gains_f[:, 0])
    input_part, gain_one = puller(normed_grad)
    gain_grad = jnp.stack([gain_one, gain_two, gain_three, gain_four], axis=1)
    return (resid_grad + input_part, (w_qkv_grad, w_out_grad, w_up_grad, w_down_grad, gain_grad))


def body_general(block_in, cotangent, w_qkv, w_out, w_up, w_down, norm_gains):
    layer_count = w_qkv.shape[0]
    micro_count = block_in.shape[0]
    row_count = block_in.shape[2]
    query_pos = lax.axis_index("grp") * row_count + jnp.arange(row_count, dtype=jnp.int32)
    totals = [None] * layer_count
    outputs = []
    input_grads = []
    for micro_idx in range(micro_count):
        hidden = block_in[micro_idx, 0].astype(jnp.float32)
        saved = []
        for layer_idx in range(layer_count):
            hidden, kept = layer_forward(
                hidden,
                (
                    lax.all_gather(w_qkv[layer_idx], "grp", axis=0, tiled=True),
                    lax.all_gather(w_out[layer_idx], "grp", axis=0, tiled=True),
                    lax.all_gather(w_up[layer_idx], "grp", axis=0, tiled=True),
                    lax.all_gather(w_down[layer_idx], "grp", axis=0, tiled=True),
                    lax.all_gather(norm_gains[layer_idx], "grp", axis=0, tiled=True),
                ),
                query_pos,
            )
            saved.append(kept)
        outputs.append(hidden.astype(jnp.bfloat16))
        grad_flow = cotangent[micro_idx, 0].astype(jnp.float32)
        for layer_idx in reversed(range(layer_count)):
            grad_flow, parts = layer_backward(
                grad_flow,
                (
                    lax.all_gather(w_qkv[layer_idx], "grp", axis=0, tiled=True),
                    lax.all_gather(w_out[layer_idx], "grp", axis=0, tiled=True),
                    lax.all_gather(w_up[layer_idx], "grp", axis=0, tiled=True),
                    lax.all_gather(w_down[layer_idx], "grp", axis=0, tiled=True),
                    lax.all_gather(norm_gains[layer_idx], "grp", axis=0, tiled=True),
                ),
                saved[layer_idx],
                query_pos,
            )
            if totals[layer_idx] is None:
                totals[layer_idx] = parts
            else:
                totals[layer_idx] = tuple(
                    (left + right for left, right in zip(totals[layer_idx], parts))
                )
        input_grads.append(grad_flow)
    reduced = []
    for layer_idx in range(layer_count):
        accum = totals[layer_idx]
        shards = (
            lax.psum_scatter(
                accum[0].astype(jnp.bfloat16), "grp", scatter_dimension=0, tiled=True
            ).astype(jnp.float32),
            lax.psum_scatter(
                accum[1].astype(jnp.bfloat16), "grp", scatter_dimension=0, tiled=True
            ).astype(jnp.float32),
            lax.psum_scatter(
                accum[2].astype(jnp.bfloat16), "grp", scatter_dimension=0, tiled=True
            ).astype(jnp.float32),
            lax.psum_scatter(
                accum[3].astype(jnp.bfloat16), "grp", scatter_dimension=0, tiled=True
            ).astype(jnp.float32),
            lax.psum_scatter(
                accum[4].astype(jnp.bfloat16), "grp", scatter_dimension=0, tiled=True
            ).astype(jnp.float32),
        )
        reduced.append(
            (
                lax.psum(shards[0].astype(jnp.bfloat16), "rep").astype(jnp.float32),
                lax.psum(shards[1].astype(jnp.bfloat16), "rep").astype(jnp.float32),
                lax.psum(shards[2].astype(jnp.bfloat16), "rep").astype(jnp.float32),
                lax.psum(shards[3].astype(jnp.bfloat16), "rep").astype(jnp.float32),
                lax.psum(shards[4].astype(jnp.bfloat16), "rep").astype(jnp.float32),
            )
        )
    block_out = jnp.stack(outputs)[:, None]
    block_in_grad = jnp.stack(input_grads)[:, None]
    stacked = [
        jnp.stack([reduced[layer_idx][member] for layer_idx in range(layer_count)])
        for member in range(5)
    ]
    return (block_out, block_in_grad, stacked[0], stacked[1], stacked[2], stacked[3], stacked[4])


def solution(mesh):
    rep_size, grp_size = mesh.shape["rep"], mesh.shape["grp"]

    def body(block_in, cotangent, w_qkv, w_out, w_up, w_down, norm_gains):
        fits = (rep_size, grp_size, block_in.shape[0]) == (4, 8, 2)
        chosen = body_pairs if fits else body_general
        return chosen(block_in, cotangent, w_qkv, w_out, w_up, w_down, norm_gains)

    tokens = P(None, "rep", "grp", None)
    rows = P(None, "grp", None)
    return jax.shard_map(
        body,
        mesh=mesh,
        in_specs=(tokens, tokens, rows, rows, rows, rows, rows),
        out_specs=(tokens, tokens, rows, rows, rows, rows, rows),
        check_vma=False,
    )
```

```python
import functools
import types

import jax
import jax.numpy as jnp
from jax import lax
from jax.experimental import pallas as pl
from jax.experimental.pallas import tpu as pltpu
from jax.sharding import PartitionSpec as P

HEADS = 16
HDIM = 64
EPS = 1e-06
NEGATIVE = -1e30
BF = jnp.bfloat16
F32 = jnp.float32


def flip(axis, bit, value):
    size = lax.axis_size(axis)
    return lax.ppermute(value, axis, [(i, i ^ bit) for i in range(size)])


core = functools.partial(flip, "grp", 1)
near = functools.partial(flip, "grp", 2)
far = functools.partial(flip, "grp", 4)
along_x = functools.partial(flip, "rep", 1)
along_y = functools.partial(flip, "rep", 2)


def pick(stacked, index):
    return lax.dynamic_index_in_dim(stacked, index, 0, keepdims=False)


def dot(left, right):
    return jnp.dot(left, right, preferred_element_type=F32)


def dot_tn(left, right):
    return lax.dot_general(left, right, (((0,), (0,)), ((), ())), preferred_element_type=F32)


def dot_nt(left, right):
    return lax.dot_general(left, right, (((1,), (1,)), ((), ())), preferred_element_type=F32)


def norm(values, gain):
    return values * lax.rsqrt(jnp.mean(values * values, axis=-1, keepdims=True) + EPS) * gain


def norm_back(values, gain, grad):
    rstd = lax.rsqrt(jnp.mean(values * values, axis=-1, keepdims=True) + EPS)
    hat = values * rstd
    scaled = grad * gain
    back = rstd * (scaled - hat * jnp.mean(scaled * hat, axis=-1, keepdims=True))
    return back, jnp.sum(grad * hat, axis=0)


def head_mask(width, head):
    lanes = lax.broadcasted_iota(jnp.int32, (1, width), 1)
    return (lanes // HDIM) == head


def attend_kernel(block, qkv_ref, mixed_ref, lse_ref):
    length, width = mixed_ref.shape
    heads = width // HDIM
    row = lax.broadcasted_iota(jnp.int32, (block, block), 0)
    col = lax.broadcasted_iota(jnp.int32, (block, block), 1)
    below = col <= row
    zero = jnp.zeros((), BF)
    lane = lax.broadcasted_iota(jnp.int32, (1, 128), 1)
    for start in range(0, length, block):
        stop = start + block
        query = qkv_ref[start:stop, :width] * jnp.asarray(HDIM**-0.5, BF)
        total = jnp.zeros((block, width), F32)
        stats = jnp.zeros((block, 128), F32)
        for head in range(heads):
            mask = head_mask(width, head)
            keys = jnp.where(mask, qkv_ref[:stop, width : 2 * width], zero)
            vals = jnp.where(mask, qkv_ref[:stop, 2 * width :], zero)
            scores = dot_nt(query, keys)
            last = jnp.where(below, scores[:, start:], NEGATIVE)
            scores = jnp.concatenate([scores[:, :start], last], axis=1) if start else last
            top = jnp.max(scores, axis=1, keepdims=True)
            terms = jnp.exp(scores - top)
            sums = jnp.sum(terms, axis=1, keepdims=True)
            total = total + dot(terms.astype(BF), vals) * (1.0 / sums)
            stats = jnp.where(lane == head, top + jnp.log(sums), stats)
        mixed_ref[start:stop, :] = total.astype(BF)
        lse_ref[start:stop, :] = stats


def attend(qkv):
    length, width = qkv.shape[0], qkv.shape[1] // 3
    heads = width // HDIM
    return pl.pallas_call(
        functools.partial(attend_kernel, 256),
        out_shape=(
            jax.ShapeDtypeStruct((length, width), BF),
            jax.ShapeDtypeStruct((length, 128), F32),
        ),
        compiler_params=pltpu.CompilerParams(vmem_limit_bytes=40 << 20),
        cost_estimate=pl.CostEstimate(
            flops=8 * heads * length * length * HDIM,
            bytes_accessed=length * width * 8 + length * 512,
            transcendentals=heads * length * length // 2,
        ),
    )(qkv)


def attend_back_kernel(block, qkv_ref, lse_ref, grad_ref, out_ref, dk_ref, dv_ref):
    length, width = grad_ref.shape
    heads = width // HDIM
    row = lax.broadcasted_iota(jnp.int32, (block, block), 0)
    col = lax.broadcasted_iota(jnp.int32, (block, block), 1)
    below = col <= row
    zero = jnp.zeros((), BF)
    scale = HDIM**-0.5
    dk_ref[...] = jnp.zeros_like(dk_ref)
    dv_ref[...] = jnp.zeros_like(dv_ref)
    for start in range(0, length, block):
        stop = start + block
        query = qkv_ref[start:stop, :width] * jnp.asarray(scale, BF)
        grad = grad_ref[start:stop, :]
        dq = jnp.zeros((block, width), F32)
        for head in range(heads):
            mask = head_mask(width, head)
            keys = jnp.where(mask, qkv_ref[:stop, width : 2 * width], zero)
            vals = jnp.where(mask, qkv_ref[:stop, 2 * width :], zero)
            scores = dot_nt(query, keys)
            last = jnp.where(below, scores[:, start:], NEGATIVE)
            scores = jnp.concatenate([scores[:, :start], last], axis=1) if start else last
            probs = jnp.exp(scores - lse_ref[start:stop, head : head + 1])
            prob_grad = dot_nt(grad, vals)
            delta = jnp.sum(probs * prob_grad, axis=1, keepdims=True)
            score_grad = (probs * (prob_grad - delta)).astype(BF)
            dq = dq + dot(score_grad, keys)
            dk_ref[:stop, :] += dot_tn(score_grad, jnp.where(mask, query, zero))
            dv_ref[:stop, :] += dot_tn(probs.astype(BF), jnp.where(mask, grad, zero))
        out_ref[start:stop, :width] = (dq * scale).astype(BF)
    out_ref[:, width : 2 * width] = dk_ref[...].astype(BF)
    out_ref[:, 2 * width :] = dv_ref[...].astype(BF)


def attend_back(qkv, lse, grad):
    length, width = grad.shape
    heads = width // HDIM
    return pl.pallas_call(
        functools.partial(attend_back_kernel, 256),
        out_shape=jax.ShapeDtypeStruct((length, 3 * width), BF),
        scratch_shapes=[pltpu.VMEM((length, width), F32)] * 2,
        compiler_params=pltpu.CompilerParams(vmem_limit_bytes=40 << 20),
        cost_estimate=pl.CostEstimate(
            flops=20 * heads * length * length * HDIM,
            bytes_accessed=length * width * 14 + length * 512,
            transcendentals=heads * length * length // 2,
        ),
    )(qkv, lse, grad)


MESH_ID = pl.DeviceIdType.MESH
TOK = 128


class Place:
    def __init__(self):
        rep, grp = lax.axis_index("rep"), lax.axis_index("grp")
        self.rep, self.grp = rep, grp
        self.x, self.y = lax.rem(rep, 2), lax.div(rep, 2)
        self.t, self.upper = lax.rem(grp, 4), lax.div(grp, 4)
        self.c, self.side = lax.rem(grp, 2), lax.div(self.t, 2)
        base = self.upper * 4
        self.core = (rep, base + self.side * 2 + 1 - self.c)
        self.near = (rep, base + (1 - self.side) * 2 + self.c)
        self.far = (rep, (1 - self.upper) * 4 + self.t)
        self.along_x = (self.y * 2 + 1 - self.x, grp)
        self.along_y = ((1 - self.y) * 2 + self.x, grp)
        self.near_t = (1 - self.side) * 2 + self.c


class Copies:
    def __init__(self, send, recv, here):
        self.sems, self.here = (send, recv), here
        self.sent, self.local_count, self.stores = [], 0, []

    def remote(self, source, target, device):
        at = len(self.sent)
        copy = pltpu.make_async_remote_copy(
            src_ref=source,
            dst_ref=target,
            send_sem=self.sems[0].at[at],
            recv_sem=self.sems[1].at[at],
            device_id=device,
            device_id_type=MESH_ID,
        )
        copy.start()
        self.sent.append(copy)
        return copy

    def local(self, source, target):
        copy = pltpu.make_async_copy(source, target, self.here.at[self.local_count])
        self.local_count += 1
        copy.start()
        return copy

    def store(self, source, target):
        self.stores.append(self.local(source, target))

    def finish(self):
        for copy in self.sent:
            copy.wait_send()
        for copy in self.stores:
            copy.wait()


def meet(devices):
    barrier = pltpu.get_barrier_semaphore()
    for device in devices:
        pl.semaphore_signal(barrier, inc=1, device_id=device, device_id_type=MESH_ID)
    pl.semaphore_wait(barrier, len(devices))


def loop(count, step):
    def run(index, carry):
        step(index)
        return carry

    lax.fori_loop(0, count, run, 0)


def tile_of(index, size):
    return pl.ds(pl.multiple_of(index * size, size), size)


def times(left, right_ref, tile, sink):
    def step(index):
        at = tile_of(index, tile)
        sink(at, dot(left(), right_ref[:, at]))

    loop(right_ref.shape[1] // tile, step)


def times_rows(left, right_ref, tile, sink):
    def step(index):
        at = tile_of(index, tile)
        sink(at, dot_nt(left(), right_ref[at, :]))

    loop(right_ref.shape[0] // tile, step)


def gram(left_ref, right_ref, tile, out_ref):
    def step(index):
        at = tile_of(index, tile)
        out_ref[at, :] = dot_tn(left_ref[:, at], right_ref[...]).astype(BF)

    loop(left_ref.shape[1] // tile, step)


class Gather:
    def __init__(self, copies, place, buf):
        self.copies, self.place, self.buf = copies, place, buf
        self.flight = {}

    def rows(self, stream, where):
        start = (stream * 4 + where) * TOK
        return pl.ds(pl.multiple_of(start, TOK), TOK)

    def pair(self, stream, side):
        start = (stream * 4 + side * 2) * TOK
        return pl.ds(pl.multiple_of(start, TOK), 2 * TOK)

    def start(self, stream, block):
        at = self.rows(stream, self.place.t)
        self.buf[at, :] = block
        mine = self.buf.at[at, :]
        across = self.copies.remote(mine, mine, self.place.near)
        beside = self.copies.remote(mine, mine, self.place.core)
        self.flight[stream] = [across, beside]

    def wait_chip(self, stream):
        self.flight[stream][1].wait_recv()

    def forward(self, stream):
        self.flight[stream][0].wait_recv()
        got = self.buf.at[self.rows(stream, self.place.near_t), :]
        self.flight[stream].append(self.copies.remote(got, got, self.place.core))

    def wait_rest(self, stream):
        self.flight[stream][2].wait_recv()


class Scatter:
    def __init__(self, copies, place, ns, name):
        self.copies, self.place = copies, place
        self.away, self.own, self.give, self.take, self.send, self.got = (
            getattr(ns, name + part) for part in ("away", "own", "give", "take", "send", "got")
        )
        self.flight = {}

    def push(self, stream, product):
        place, copies = self.place, self.copies
        mine = pl.ds(pl.multiple_of(place.c * TOK, TOK), TOK)
        other = pl.ds(pl.multiple_of((1 - place.c) * TOK, TOK), TOK)

        def to_away(at, value):
            self.away[:, at] = value

        def to_own(at, value):
            self.own[stream, :, at] = value

        product(1 - place.side, to_away)
        self.give[stream, 0] = self.away[other, :].astype(BF)
        first = copies.remote(self.give.at[stream, 0], self.take.at[stream, 0], place.core)
        product(place.side, to_own)
        first.wait_recv()
        self.send[stream] = (self.away[mine, :] + self.take[stream, 0].astype(F32)).astype(BF)
        across = copies.remote(self.send.at[stream], self.got.at[stream], place.near)
        self.give[stream, 1] = self.own[stream, other, :].astype(BF)
        second = copies.remote(self.give.at[stream, 1], self.take.at[stream, 1], place.core)
        self.flight[stream] = (second, across)

    def result(self, stream):
        second, across = self.flight[stream]
        mine = pl.ds(pl.multiple_of(self.place.c * TOK, TOK), TOK)
        second.wait_recv()
        total = self.own[stream, mine, :] + self.take[stream, 1].astype(F32)
        across.wait_recv()
        return total + self.got[stream].astype(F32)


def scatter_scratch(name, width):
    return {
        name + "away": pltpu.VMEM((2 * TOK, width), F32),
        name + "own": pltpu.VMEM((2, 2 * TOK, width), F32),
        name + "give": pltpu.VMEM((2, 2, TOK, width), BF),
        name + "take": pltpu.VMEM((2, 2, TOK, width), BF),
        name + "send": pltpu.VMEM((2, TOK, width), BF),
        name + "got": pltpu.VMEM((2, TOK, width), BF),
    }


def gelu_both(x):
    cubic = x * x * 0.044715
    bent = jnp.tanh(0.7978845608028654 * (x + cubic * x))
    half = 0.5 * (1.0 + bent)
    slope = half + 0.5 * x * (1.0 - bent * bent) * (0.7978845608028654 * (1.0 + 3.0 * cubic))
    return x * half, slope


def norm_back_in(values, gain, grad):
    rstd = lax.rsqrt(jnp.mean(values * values, axis=-1, keepdims=True) + EPS)
    hat = values * rstd
    scaled = grad * gain
    back = rstd * (scaled - hat * jnp.mean(scaled * hat, axis=-1, keepdims=True))
    return back, jnp.sum(grad * hat, axis=0, keepdims=True)


def launch(name, body, inputs, outputs, scratch, slot, remotes, locals_, vmem, flops):
    names = list(inputs) + list(outputs) + list(scratch)

    def kernel(*refs):
        ns = types.SimpleNamespace(**dict(zip(names, refs)))
        ns.copies = Copies(*refs[len(names) :])
        body(ns)
        ns.copies.finish()

    moved = sum(v.size * v.dtype.itemsize for v in [*inputs.values(), *outputs.values()])
    results = pl.pallas_call(
        kernel,
        name=name,
        out_shape=list(outputs.values()),
        in_specs=[pl.BlockSpec(memory_space=pl.ANY)] * len(inputs),
        out_specs=[pl.BlockSpec(memory_space=pl.ANY)] * len(outputs),
        scratch_shapes=[
            *scratch.values(),
            pltpu.SemaphoreType.DMA((remotes,)),
            pltpu.SemaphoreType.DMA((remotes,)),
            pltpu.SemaphoreType.DMA((locals_,)),
        ],
        compiler_params=pltpu.CompilerParams(
            collective_id=slot, has_side_effects=True, vmem_limit_bytes=vmem << 20
        ),
        cost_estimate=pl.CostEstimate(flops=flops, bytes_accessed=moved, transcendentals=0),
    )(*inputs.values())
    return dict(zip(outputs, results))


def next_qkv(ns, place, blocks):
    gather = Gather(ns.copies, place, ns.normed_v)
    for stream in range(2):
        gather.start(stream, blocks[stream]())
    ns.load_wq.wait()
    for stream in range(2):

        def project(side):
            at = gather.pair(stream, side)

            def sink(cols, value):
                ns.qkv_v[at, cols] = value.astype(BF)

            times(lambda: ns.normed_v[at, :], ns.wq_v, 384, sink)

        gather.wait_chip(stream)
        project(place.side)
        gather.forward(stream)
        gather.wait_rest(stream)
        project(1 - place.side)
        here = pl.ds(stream * 4 * TOK, 4 * TOK)
        ns.copies.store(ns.normed_v.at[here, :], ns.normed.at[here, :])
        ns.copies.store(ns.qkv_v.at[here, :], ns.qkv.at[here, :])


def fwd_mid(ns, place, gain):
    copies = ns.copies
    attn = Scatter(copies, place, ns, "attn_")
    down = Scatter(copies, place, ns, "down_")
    gather = Gather(copies, place, ns.mlp_v)
    ns.load_wo.wait()
    ns.load_mixed.wait()
    for stream in range(2):

        def product(side, sink):
            at = gather.pair(stream, side)
            times(lambda: ns.mixed_v[at, :], ns.wo_v, 512, sink)

        attn.push(stream, product)
    ns.load_hidden.wait()
    for stream in range(2):
        value = attn.result(stream)
        ns.attn_out_v[stream] = value
        resid = ns.hidden_v[stream] + norm(value, gain(1))
        ns.resid_v[stream] = resid
        gather.start(stream, norm(resid, gain(2)).astype(BF))
    ns.load_wu.wait()
    ns.load_wd.wait()
    for stream in range(2):

        def expand(side):
            at = gather.pair(stream, side)

            def sink(cols, value):
                active, slope = gelu_both(value)
                ns.active_v[at, cols] = active.astype(BF)
                ns.slope_v[at, cols] = slope.astype(BF)

            times(lambda: ns.mlp_v[at, :], ns.wu_v, 256, sink)

        gather.wait_chip(stream)
        expand(place.side)
        gather.forward(stream)
        gather.wait_rest(stream)
        expand(1 - place.side)

        def product(side, sink):
            at = gather.pair(stream, side)
            times(lambda: ns.active_v[at, :], ns.wd_v, 512, sink)

        down.push(stream, product)
    return down


def bwd_mid(ns, place, gain, grads):
    copies = ns.copies
    up = Scatter(copies, place, ns, "up_")
    first = Gather(copies, place, ns.down_grad_v)
    second = Gather(copies, place, ns.attn_grad_v)
    for stream in range(2):
        grad = grads[stream]()
        ns.grad_v[stream] = grad
        back, four = norm_back_in(ns.down_out_v[stream], gain(3), grad)
        ns.dg_v[3:4, :] += four
        first.start(stream, back.astype(BF))
    for stream in range(2):

        def shrink(side):
            at = first.pair(stream, side)

            def sink(cols, value):
                slope = ns.slope_v[at, cols].astype(F32)
                ns.up_grad_v[at, cols] = (value * slope).astype(BF)

            times_rows(lambda: ns.down_grad_v[at, :], ns.wd_v, 512, sink)

        first.wait_chip(stream)
        shrink(place.side)
        first.forward(stream)
        first.wait_rest(stream)
        shrink(1 - place.side)

        def product(side, sink):
            at = first.pair(stream, side)
            times_rows(lambda: ns.up_grad_v[at, :], ns.wu_v, 512, sink)

        up.push(stream, product)
    gram(ns.active_v, ns.down_grad_v, 256, ns.gd_v)
    copies.store(ns.gd_v, ns.gd)
    for stream in range(2):
        back, three = norm_back_in(ns.resid_v[stream], gain(2), up.result(stream))
        grad = ns.grad_v[stream] + back
        ns.grad_v[stream] = grad
        ns.dg_v[2:3, :] += three
        back, two = norm_back_in(ns.attn_out_v[stream], gain(1), grad)
        ns.dg_v[1:2, :] += two
        second.start(stream, back.astype(BF))
    copies.store(ns.grad_v, ns.resid_grad)
    gram(ns.mlp_v, ns.up_grad_v, 256, ns.gu_v)
    copies.store(ns.gu_v, ns.gu)
    for stream in range(2):

        def project(side):
            at = second.pair(stream, side)
            ns.mixed_grad_v[at, :] = dot_nt(ns.attn_grad_v[at, :], ns.wo_v[...]).astype(BF)

        second.wait_chip(stream)
        project(place.side)
        second.forward(stream)
        second.wait_rest(stream)
        project(1 - place.side)
        here = pl.ds(stream * 4 * TOK, 4 * TOK)
        copies.store(ns.mixed_grad_v.at[here, :], ns.mixed_grad.at[here, :])
    ns.go_v[...] = dot_tn(ns.mixed_v[...], ns.attn_grad_v[...]).astype(BF)
    copies.store(ns.go_v, ns.go)


def bwd_head(ns, place, gain):
    copies = ns.copies
    qkv = Scatter(copies, place, ns, "qkv_")
    walk = Gather(copies, place, None)
    ns.load_wq.wait()
    ns.load_qkv_grad.wait()
    for stream in range(2):

        def product(side, sink):
            at = walk.pair(stream, side)
            times_rows(lambda: ns.qkv_grad_v[at, :], ns.wq_v, 512, sink)

        qkv.push(stream, product)
    ns.load_normed.wait()
    gram(ns.normed_v, ns.qkv_grad_v, 256, ns.gq_v)
    copies.store(ns.gq_v, ns.gq)
    ns.load_hidden.wait()
    ns.load_grad_in.wait()

    def result(stream):
        back, one = norm_back_in(ns.hidden_v[stream], gain(0), qkv.result(stream))
        ns.dg_head_v[...] += one
        return ns.grad_in_v[stream] + back

    return [functools.partial(result, stream) for stream in range(2)]


def struct(shape, dtype):
    return jax.ShapeDtypeStruct(shape, dtype)


def load(ns, *names):
    for name in names:
        setattr(ns, "load_" + name, ns.copies.local(getattr(ns, name), getattr(ns, name + "_v")))


def start_kernel(hidden, wq, gains):
    width, part = wq.shape
    length = 8 * TOK
    inputs = dict(hidden=hidden, wq=wq, gains=gains)
    outputs = dict(normed=struct((length, width), BF), qkv=struct((length, part), BF))
    scratch = dict(
        hidden_v=pltpu.VMEM((2, TOK, width), F32),
        wq_v=pltpu.VMEM(wq.shape, BF),
        gains_v=pltpu.VMEM(gains.shape, F32),
        normed_v=pltpu.VMEM((length, width), BF),
        qkv_v=pltpu.VMEM((length, part), BF),
    )

    def body(ns):
        place = Place()
        load(ns, "hidden", "gains", "wq")
        meet([place.core, place.near])
        ns.load_hidden.wait()
        ns.load_gains.wait()
        blocks = [
            functools.partial(
                lambda s: norm(ns.hidden_v[s], ns.gains_v[0:1, :]).astype(BF), stream
            )
            for stream in range(2)
        ]
        next_qkv(ns, place, blocks)

    return launch("start", body, inputs, outputs, scratch, 0, 8, 8, 60, 2 * length * width * part)


def forward_kernel(layer, mixed, hidden, gains, weights, wq):
    wo, wu, wd = weights
    width, units = wu.shape
    part = wq.shape[1]
    length = 8 * TOK
    inputs = dict(mixed=mixed, hidden=hidden, gains=gains, wo=wo, wu=wu, wd=wd, wq=wq)
    blocks = struct((2, TOK, width), F32)
    wide = struct((length, width), BF)
    outputs = dict(
        attn_out=blocks,
        resid=blocks,
        mlp=wide,
        active=struct((length, units), BF),
        slope=struct((length, units), BF),
        down_out=blocks,
        hidden_out=blocks,
        normed=wide,
        qkv=struct((length, part), BF),
    )
    scratch = {
        name + "_v": pltpu.VMEM(value.shape, value.dtype)
        for name, value in {**inputs, **outputs}.items()
    }
    scratch |= scatter_scratch("attn_", width) | scatter_scratch("down_", width)

    def body(ns):
        place = Place()
        load(ns, "mixed", "wo", "gains", "hidden", "wu", "wd", "wq")
        meet([place.core, place.near])
        ns.load_gains.wait()

        def gain(index, level=layer):
            return ns.gains_v[level * 4 + index : level * 4 + index + 1, :]

        down = fwd_mid(ns, place, gain)
        for name in ("attn_out", "resid", "mlp", "active", "slope"):
            ns.copies.store(getattr(ns, name + "_v"), getattr(ns, name))

        def block(stream):
            value = down.result(stream)
            ns.down_out_v[stream] = value
            hidden_out = ns.resid_v[stream] + norm(value, gain(3))
            ns.hidden_out_v[stream] = hidden_out
            return norm(hidden_out, gain(0, layer + 1)).astype(BF)

        next_qkv(ns, place, [functools.partial(block, stream) for stream in range(2)])
        for name in ("down_out", "hidden_out"):
            ns.copies.store(getattr(ns, name + "_v"), getattr(ns, name))

    flops = 2 * length * width * (wo.shape[0] + 2 * units + part)
    return launch("forward", body, inputs, outputs, scratch, 1, 32, 32, 60, flops)


def turn_kernel(layer, mixed, hidden, gains, weights, cotangent):
    wo, wu, wd = weights
    width, units = wu.shape
    length = 8 * TOK
    inputs = dict(mixed=mixed, hidden=hidden, gains=gains, wo=wo, wu=wu, wd=wd, cot=cotangent)
    blocks = struct((2, TOK, width), F32)
    outputs = dict(
        out=struct((2, TOK, width), BF),
        resid_grad=blocks,
        mixed_grad=struct(mixed.shape, BF),
        gd=struct(wd.shape, BF),
        gu=struct(wu.shape, BF),
        go=struct(wo.shape, BF),
        dg=struct((8, width), F32),
    )
    kept = dict(
        attn_out=blocks,
        resid=blocks,
        grad=blocks,
        mlp=struct((length, width), BF),
        active=struct((length, units), BF),
        slope=struct((length, units), BF),
        up_grad=struct((length, units), BF),
        down_out=blocks,
        down_grad=struct((length, width), BF),
        attn_grad=struct((length, width), BF),
    )
    scratch = {
        name + "_v": pltpu.VMEM(value.shape, value.dtype)
        for name, value in {**inputs, **outputs, **kept}.items()
        if name != "resid_grad"
    }
    for name in ("attn_", "down_", "up_"):
        scratch |= scatter_scratch(name, width)

    def body(ns):
        place = Place()
        load(ns, "mixed", "wo", "gains", "hidden", "wu", "wd", "cot")
        meet([place.core, place.near])
        ns.load_gains.wait()
        ns.dg_v[...] = jnp.zeros_like(ns.dg_v)

        def gain(index):
            return ns.gains_v[layer * 4 + index : layer * 4 + index + 1, :]

        down = fwd_mid(ns, place, gain)
        ns.load_cot.wait()

        def grad(stream):
            value = down.result(stream)
            ns.down_out_v[stream] = value
            return ns.cot_v[stream].astype(F32)

        bwd_mid(ns, place, gain, [functools.partial(grad, stream) for stream in range(2)])
        for stream in range(2):
            out = ns.resid_v[stream] + norm(ns.down_out_v[stream], gain(3))
            ns.out_v[stream] = out.astype(BF)
        ns.copies.store(ns.out_v, ns.out)
        ns.copies.store(ns.dg_v, ns.dg)

    flops = 6 * length * width * (wo.shape[0] + 2 * units)
    return launch("turn", body, inputs, outputs, scratch, 2, 48, 32, 62, flops)


def backward_kernel(layer, qkv_grad, wq, normed, hidden, grad_in, gains, saved, weights):
    wo, wu, wd = weights
    width, units = wu.shape
    length = 8 * TOK
    inputs = dict(
        qkv_grad=qkv_grad, wq=wq, normed=normed, hidden=hidden, grad_in=grad_in, gains=gains,
        wo=wo, wu=wu, wd=wd, **saved,
    )
    blocks = struct((2, TOK, width), F32)
    outputs = dict(
        resid_grad=blocks,
        mixed_grad=struct((length, wo.shape[0]), BF),
        gq=struct(wq.shape, BF),
        gd=struct(wd.shape, BF),
        gu=struct(wu.shape, BF),
        go=struct(wo.shape, BF),
        dg=struct((8, width), F32),
        dg_head=struct((1, width), F32),
    )
    kept = dict(
        grad=blocks,
        up_grad=struct((length, units), BF),
        down_grad=struct((length, width), BF),
        attn_grad=struct((length, width), BF),
    )
    scratch = {
        name + "_v": pltpu.VMEM(value.shape, value.dtype)
        for name, value in {**inputs, **outputs, **kept}.items()
        if name != "resid_grad"
    }
    for name in ("qkv_", "up_"):
        scratch |= scatter_scratch(name, width)

    def body(ns):
        place = Place()
        load(ns, "qkv_grad", "wq", "gains", "normed", "hidden", "grad_in")
        load(ns, "wd", "slope", "wu", "active", *(n for n in saved if n not in ("slope", "active")), "wo")
        meet([place.core, place.near])
        ns.load_gains.wait()
        ns.dg_v[...] = jnp.zeros_like(ns.dg_v)
        ns.dg_head_v[...] = jnp.zeros_like(ns.dg_head_v)

        def gain(index, level=layer):
            return ns.gains_v[level * 4 + index : level * 4 + index + 1, :]

        grads = bwd_head(ns, place, lambda index: gain(index, layer + 1))
        for name in ("wd", "wu", "wo", *saved):
            getattr(ns, "load_" + name).wait()
        bwd_mid(ns, place, gain, grads)
        ns.copies.store(ns.dg_v, ns.dg)
        ns.copies.store(ns.dg_head_v, ns.dg_head)

    flops = 6 * length * width * (wo.shape[0] + 2 * units) + 4 * length * width * wq.shape[1]
    return launch("backward", body, inputs, outputs, scratch, 3, 48, 48, 62, flops)


def last_kernel(qkv_grad, wq, normed, hidden, grad_in, gains):
    width = wq.shape[0]
    inputs = dict(
        qkv_grad=qkv_grad, wq=wq, normed=normed, hidden=hidden, grad_in=grad_in, gains=gains
    )
    outputs = dict(
        out=struct((2, TOK, width), BF), gq=struct(wq.shape, BF), dg_head=struct((1, width), F32)
    )
    scratch = {
        name + "_v": pltpu.VMEM(value.shape, value.dtype)
        for name, value in {**inputs, **outputs}.items()
    }
    scratch |= scatter_scratch("qkv_", width)

    def body(ns):
        place = Place()
        load(ns, "qkv_grad", "wq", "gains", "normed", "hidden", "grad_in")
        meet([place.core, place.near])
        ns.load_gains.wait()
        ns.dg_head_v[...] = jnp.zeros_like(ns.dg_head_v)
        grads = bwd_head(ns, place, lambda index: ns.gains_v[index : index + 1, :])
        for stream in range(2):
            ns.out_v[stream] = grads[stream]().astype(BF)
        ns.copies.store(ns.out_v, ns.out)
        ns.copies.store(ns.dg_head_v, ns.dg_head)

    flops = 4 * 8 * TOK * width * wq.shape[1]
    return launch("last", body, inputs, outputs, scratch, 4, 16, 16, 60, flops)


def spread_rep(mine, rep):
    return lax.all_gather(mine, "rep", axis=0, tiled=False)


def columns_in(weight, groups, unit, rep, place):
    rows, total = weight.shape
    quarter = pick(weight.reshape(4, rows // 4, total), rep)
    whole = lax.all_gather(quarter, "grp", axis=0, tiled=False)
    whole = whole.reshape(8, rows // 4, groups, 4, unit)
    mine = lax.dynamic_index_in_dim(whole, place, 3, keepdims=False)
    mine = mine.reshape(8, rows // 4, groups * unit)
    return lax.all_gather(mine, "rep", axis=1, tiled=True).reshape(8 * rows, groups * unit)


def columns_out(grad, groups, unit, rep, place, upper):
    total, width = grad.shape
    rows = total // 32
    low = grad.reshape(8, 4, rows, width)
    mine = lax.psum_scatter(low, "rep", scatter_dimension=1, tiled=False)
    mine = mine.reshape(2, 4, rows, width)
    other = far(pick(mine, 1 - upper))
    mine = (pick(mine, upper).astype(F32) + other.astype(F32)).astype(BF)
    side = place // 2
    mine = mine.reshape(2, 2, rows, width)
    other = near(pick(mine, 1 - side))
    mine = pick(mine, side)
    mine = jnp.where(side == 0, jnp.stack([mine, other]), jnp.stack([other, mine]))
    which = place % 2
    keep = lax.dynamic_index_in_dim(mine, which, 1, keepdims=False)
    give = lax.dynamic_index_in_dim(mine, 1 - which, 1, keepdims=False)
    other = core(give)
    both = jnp.where(which == 0, jnp.stack([keep, other], 1), jnp.stack([other, keep], 1))
    both = both.reshape(4, rows, groups, unit).transpose(1, 2, 0, 3).reshape(rows, groups * 4 * unit)
    return lax.all_gather(both, "rep", axis=0, tiled=True).astype(F32)


def rows_in(weight, upper):
    other = far(weight)
    return jnp.where(
        upper == 0, jnp.concatenate([weight, other]), jnp.concatenate([other, weight])
    )


def rows_out(grad, rep, upper):
    total, width = grad.shape
    rows = total // 8
    low = grad.reshape(2, 4, rows, width)
    mine = lax.psum_scatter(low, "rep", scatter_dimension=1, tiled=False)
    other = far(pick(mine, 1 - upper))
    mine = (pick(mine, upper).astype(F32) + other.astype(F32)).astype(BF)
    return lax.all_gather(mine, "rep", axis=0, tiled=True).astype(F32)


def body_pairs(block_in, cotangent, w_qkv, w_out, w_up, w_down, norm_gains):
    layers, rows, width = w_out.shape
    tokens = block_in.shape[2]
    hidden_unit = w_down.shape[1]
    rep = lax.axis_index("rep")
    grp = lax.axis_index("grp")
    place, upper = grp % 4, grp // 4

    gains = lax.all_gather(norm_gains, "grp", axis=1, tiled=True).astype(F32)
    gains = jnp.transpose(gains, (0, 2, 1)).reshape(layers * 4, width)

    def bring(two):
        mine = pick(two[:, 0], upper)
        other = far(pick(two[:, 0], 1 - upper))
        return jnp.where(upper == 0, jnp.stack([mine, other]), jnp.stack([other, mine]))

    def send_back(mine):
        keep = pick(mine, upper)
        other = far(pick(mine, 1 - upper))
        return jnp.where(upper == 0, jnp.stack([keep, other]), jnp.stack([other, keep]))

    first = bring(block_in).astype(F32)
    weights = []
    for layer in range(layers):
        weights.append(
            (
                columns_in(w_qkv[layer], 6, rows, rep, place),
                rows_in(w_out[layer], upper),
                columns_in(w_up[layer], 2, hidden_unit, rep, place),
                rows_in(w_down[layer], upper),
            )
        )
    begun = start_kernel(first, weights[0][0], gains)
    mixed_0, lse_0 = attend(begun["qkv"])
    lower = forward_kernel(0, mixed_0, first, gains, weights[0][1:], weights[1][0])
    mixed_1, lse_1 = attend(lower["qkv"])
    upper_out = turn_kernel(
        1, mixed_1, lower["hidden_out"], gains, weights[1][1:], bring(cotangent)
    )
    block_out = send_back(upper_out["out"])[:, None]
    qkv_grad_1 = attend_back(lower["qkv"], lse_1, upper_out["mixed_grad"])
    saved = {
        name: lower[name] for name in ("down_out", "slope", "active", "resid", "attn_out", "mlp")
    }
    lower_out = backward_kernel(
        0, qkv_grad_1, weights[1][0], lower["normed"], lower["hidden_out"], upper_out["resid_grad"],
        gains, dict(saved, mixed=mixed_0), weights[0][1:],
    )
    qkv_grad_0 = attend_back(begun["qkv"], lse_0, lower_out["mixed_grad"])
    last = last_kernel(
        qkv_grad_0, weights[0][0], begun["normed"], first, lower_out["resid_grad"], gains
    )
    block_in_grad = send_back(last["out"]).astype(F32)[:, None]

    gain_grad = jnp.concatenate(
        [last["dg_head"], lower_out["dg"][1:4], lower_out["dg_head"], upper_out["dg"][1:4]]
    )
    gain_all = lax.psum(gain_grad, ("rep", "grp"))
    gain_mine = lax.dynamic_slice_in_dim(gain_all, grp * rows, rows, 1)
    gain_mine = jnp.transpose(gain_mine.reshape(layers, 4, rows), (0, 2, 1))
    results = []
    for gq, out in ((last["gq"], lower_out), (lower_out["gq"], upper_out)):
        results.append(
            (
                columns_out(gq, 6, rows, rep, place, upper),
                rows_out(out["go"], rep, upper),
                columns_out(out["gu"], 2, hidden_unit, rep, place, upper),
                rows_out(out["gd"], rep, upper),
            )
        )
    stacked = [jnp.stack([results[layer][k] for layer in range(layers)]) for k in range(4)]
    return (block_out, block_in_grad, *stacked, gain_mine)


def norm_apply(values, gains):
    return values * lax.rsqrt(jnp.mean(values * values, axis=-1, keepdims=True) + EPS) * gains


def inner_rows(left, right):
    return lax.dot_general(
        left, right, (((0,), (0,)), ((), ())), preferred_element_type=jnp.float32
    )


def times_trans(left, right):
    return lax.dot_general(
        left, right, (((1,), (1,)), ((), ())), preferred_element_type=jnp.float32
    )


def split_blocks(whole):
    length = whole.shape[0]
    width = min(512, length)
    count = length // width
    return (whole.reshape(count, width, HEADS, HDIM), width, count)


def block_at(blocks, index):
    return lax.dynamic_index_in_dim(blocks, index, 0, keepdims=False)


def key_scores(query, key_block, key_start, query_pos):
    scale = HDIM ** (-0.5)
    scores = (
        jnp.einsum("qhd,khd->hqk", query, key_block, preferred_element_type=jnp.float32) * scale
    )
    key_pos = key_start + jnp.arange(key_block.shape[0], dtype=jnp.int32)
    allowed = key_pos[None, :] <= query_pos[:, None]
    return (scores, allowed[None])


def attend_split(query, keys_all, values_all, query_pos):
    key_blocks, width, count = split_blocks(keys_all)
    value_blocks = split_blocks(values_all)[0]
    row_count = query.shape[0]
    upper = query_pos[row_count - 1] // width + 1

    def total_step(index, carry):
        running, total = carry
        scores, allowed = key_scores(query, block_at(key_blocks, index), index * width, query_pos)
        newest = jnp.maximum(running, jnp.max(jnp.where(allowed, scores, NEGATIVE), axis=-1))
        terms = jnp.where(allowed, jnp.exp(scores - newest[..., None]), 0.0)
        total = total * jnp.exp(running - newest) + jnp.sum(terms, axis=-1)
        return (newest, total)

    start_run = jnp.full((HEADS, row_count), NEGATIVE, jnp.float32)
    start_total = jnp.zeros((HEADS, row_count), jnp.float32)
    running, total = lax.fori_loop(0, upper, total_step, (start_run, start_total))
    log_total = running + jnp.log(total)

    def mix_step(index, accum):
        scores, allowed = key_scores(query, block_at(key_blocks, index), index * width, query_pos)
        probs = jnp.where(allowed, jnp.exp(scores - log_total[..., None]), 0.0)
        return accum + jnp.einsum(
            "hqk,khd->qhd",
            probs.astype(jnp.bfloat16),
            block_at(value_blocks, index),
            preferred_element_type=jnp.float32,
        )

    start_mix = jnp.zeros((row_count, HEADS, HDIM), jnp.float32)
    mixed = lax.fori_loop(0, upper, mix_step, start_mix)
    return (mixed.reshape(row_count, HEADS * HDIM), log_total)


def attend_back_split(query, keys_all, values_all, log_total, out_grad, delta, query_pos):
    key_blocks, width, count = split_blocks(keys_all)
    value_blocks = split_blocks(values_all)[0]
    row_count = query.shape[0]
    upper = query_pos[row_count - 1] // width + 1
    scale = HDIM ** (-0.5)

    def back_step(index, carry):
        query_acc, pieces = carry
        key_block = block_at(key_blocks, index)
        value_block = block_at(value_blocks, index)
        scores, allowed = key_scores(query, key_block, index * width, query_pos)
        probs = jnp.where(allowed, jnp.exp(scores - log_total[..., None]), 0.0)
        prob_grad = jnp.einsum(
            "qhd,khd->hqk", out_grad, value_block, preferred_element_type=jnp.float32
        )
        score_grad = (probs * (prob_grad - delta[..., None])).astype(jnp.bfloat16)
        query_acc = (
            query_acc
            + jnp.einsum("hqk,khd->qhd", score_grad, key_block, preferred_element_type=jnp.float32)
            * scale
        )
        key_grad = (
            jnp.einsum("hqk,qhd->khd", score_grad, query, preferred_element_type=jnp.float32)
            * scale
        )
        value_grad = jnp.einsum(
            "hqk,qhd->khd", probs.astype(jnp.bfloat16), out_grad, preferred_element_type=jnp.float32
        )
        joined = jnp.concatenate(
            [key_grad.reshape(width, HEADS * HDIM), value_grad.reshape(width, HEADS * HDIM)], axis=1
        )
        pieces = lax.dynamic_update_index_in_dim(pieces, joined, index, 0)
        return (query_acc, pieces)

    start_acc = jnp.zeros((row_count, HEADS, HDIM), jnp.float32)
    start_pieces = jnp.zeros((count, width, 2 * HEADS * HDIM), jnp.float32)
    query_grad, pieces = lax.fori_loop(0, upper, back_step, (start_acc, start_pieces))
    return (query_grad.reshape(row_count, HEADS * HDIM), pieces.reshape(-1, pieces.shape[-1]))


def layer_forward(hidden_in, weights, query_pos):
    w_qkv_full, w_out_full, w_up_full, w_down_full, gain_full = weights
    gains_f = gain_full.astype(jnp.float32)
    row_count = hidden_in.shape[0]
    width = w_out_full.shape[1]
    normed = norm_apply(hidden_in, gains_f[:, 0]).astype(jnp.bfloat16)
    qkv_low = jnp.dot(normed, w_qkv_full, preferred_element_type=jnp.float32).astype(jnp.bfloat16)
    query = qkv_low[:, :width]
    keys_all, values_all = (
        lax.all_gather(qkv_low[:, width : 2 * width], "grp", axis=0, tiled=True),
        lax.all_gather(qkv_low[:, 2 * width :], "grp", axis=0, tiled=True),
    )
    mixed, log_total = attend_split(
        query.reshape(row_count, HEADS, HDIM),
        keys_all.reshape(-1, HEADS, HDIM),
        values_all.reshape(-1, HEADS, HDIM),
        query_pos,
    )
    mixed_low = mixed.astype(jnp.bfloat16)
    attn_out = jnp.dot(mixed_low, w_out_full, preferred_element_type=jnp.float32)
    resid = hidden_in + norm_apply(attn_out, gains_f[:, 1])
    mlp_in = norm_apply(resid, gains_f[:, 2]).astype(jnp.bfloat16)
    up_out = jnp.dot(mlp_in, w_up_full, preferred_element_type=jnp.float32)
    active = jax.nn.gelu(up_out).astype(jnp.bfloat16)
    down_out = jnp.dot(active, w_down_full, preferred_element_type=jnp.float32)
    result = resid + norm_apply(down_out, gains_f[:, 3])
    kept = (
        hidden_in,
        normed,
        qkv_low,
        mixed,
        mixed_low,
        log_total,
        attn_out,
        resid,
        mlp_in,
        up_out,
        active,
        down_out,
    )
    return (result, kept)


def layer_backward(grad_out, weights, kept, query_pos):
    w_qkv_full, w_out_full, w_up_full, w_down_full, gain_full = weights
    (
        hidden_in,
        normed,
        qkv_low,
        mixed,
        mixed_low,
        log_total,
        attn_out,
        resid,
        mlp_in,
        up_out,
        active,
        down_out,
    ) = kept
    gains_f = gain_full.astype(jnp.float32)
    row_count = hidden_in.shape[0]
    width = w_out_full.shape[1]
    unused, puller = jax.vjp(norm_apply, down_out, gains_f[:, 3])
    down_grad, gain_four = puller(grad_out)
    down_low = down_grad.astype(jnp.bfloat16)
    w_down_grad = inner_rows(active, down_low)
    active_grad = times_trans(down_low, w_down_full)
    unused, puller = jax.vjp(jax.nn.gelu, up_out)
    up_low = puller(active_grad)[0].astype(jnp.bfloat16)
    w_up_grad = inner_rows(mlp_in, up_low)
    mlp_grad = times_trans(up_low, w_up_full)
    unused, puller = jax.vjp(norm_apply, resid, gains_f[:, 2])
    resid_part, gain_three = puller(mlp_grad)
    resid_grad = grad_out + resid_part
    unused, puller = jax.vjp(norm_apply, attn_out, gains_f[:, 1])
    attn_grad, gain_two = puller(resid_grad)
    attn_low = attn_grad.astype(jnp.bfloat16)
    w_out_grad = inner_rows(mixed_low, attn_low)
    mixed_grad = times_trans(attn_low, w_out_full).astype(jnp.bfloat16)
    keys_all, values_all = (
        lax.all_gather(qkv_low[:, width : 2 * width], "grp", axis=0, tiled=True),
        lax.all_gather(qkv_low[:, 2 * width :], "grp", axis=0, tiled=True),
    )
    delta = jnp.sum(
        (mixed_grad.astype(jnp.float32) * mixed).reshape(row_count, HEADS, HDIM), axis=-1
    ).T
    query_low = qkv_low[:, :width]
    query_grad, key_value_terms = attend_back_split(
        query_low.reshape(row_count, HEADS, HDIM),
        keys_all.reshape(-1, HEADS, HDIM),
        values_all.reshape(-1, HEADS, HDIM),
        log_total,
        mixed_grad.reshape(row_count, HEADS, HDIM),
        delta,
        query_pos,
    )
    key_value_grad = lax.psum_scatter(
        key_value_terms.astype(jnp.bfloat16), "grp", scatter_dimension=0, tiled=True
    ).astype(jnp.float32)
    qkv_grad = jnp.concatenate([query_grad, key_value_grad], axis=1).astype(jnp.bfloat16)
    w_qkv_grad = inner_rows(normed, qkv_grad)
    normed_grad = times_trans(qkv_grad, w_qkv_full)
    unused, puller = jax.vjp(norm_apply, hidden_in, gains_f[:, 0])
    input_part, gain_one = puller(normed_grad)
    gain_grad = jnp.stack([gain_one, gain_two, gain_three, gain_four], axis=1)
    return (resid_grad + input_part, (w_qkv_grad, w_out_grad, w_up_grad, w_down_grad, gain_grad))


def body_general(block_in, cotangent, w_qkv, w_out, w_up, w_down, norm_gains):
    layer_count = w_qkv.shape[0]
    micro_count = block_in.shape[0]
    row_count = block_in.shape[2]
    query_pos = lax.axis_index("grp") * row_count + jnp.arange(row_count, dtype=jnp.int32)
    totals = [None] * layer_count
    outputs = []
    input_grads = []
    for micro_idx in range(micro_count):
        hidden = block_in[micro_idx, 0].astype(jnp.float32)
        saved = []
        for layer_idx in range(layer_count):
            hidden, kept = layer_forward(
                hidden,
                (
                    lax.all_gather(w_qkv[layer_idx], "grp", axis=0, tiled=True),
                    lax.all_gather(w_out[layer_idx], "grp", axis=0, tiled=True),
                    lax.all_gather(w_up[layer_idx], "grp", axis=0, tiled=True),
                    lax.all_gather(w_down[layer_idx], "grp", axis=0, tiled=True),
                    lax.all_gather(norm_gains[layer_idx], "grp", axis=0, tiled=True),
                ),
                query_pos,
            )
            saved.append(kept)
        outputs.append(hidden.astype(jnp.bfloat16))
        grad_flow = cotangent[micro_idx, 0].astype(jnp.float32)
        for layer_idx in reversed(range(layer_count)):
            grad_flow, parts = layer_backward(
                grad_flow,
                (
                    lax.all_gather(w_qkv[layer_idx], "grp", axis=0, tiled=True),
                    lax.all_gather(w_out[layer_idx], "grp", axis=0, tiled=True),
                    lax.all_gather(w_up[layer_idx], "grp", axis=0, tiled=True),
                    lax.all_gather(w_down[layer_idx], "grp", axis=0, tiled=True),
                    lax.all_gather(norm_gains[layer_idx], "grp", axis=0, tiled=True),
                ),
                saved[layer_idx],
                query_pos,
            )
            if totals[layer_idx] is None:
                totals[layer_idx] = parts
            else:
                totals[layer_idx] = tuple(
                    (left + right for left, right in zip(totals[layer_idx], parts))
                )
        input_grads.append(grad_flow)
    reduced = []
    for layer_idx in range(layer_count):
        accum = totals[layer_idx]
        shards = (
            lax.psum_scatter(
                accum[0].astype(jnp.bfloat16), "grp", scatter_dimension=0, tiled=True
            ).astype(jnp.float32),
            lax.psum_scatter(
                accum[1].astype(jnp.bfloat16), "grp", scatter_dimension=0, tiled=True
            ).astype(jnp.float32),
            lax.psum_scatter(
                accum[2].astype(jnp.bfloat16), "grp", scatter_dimension=0, tiled=True
            ).astype(jnp.float32),
            lax.psum_scatter(
                accum[3].astype(jnp.bfloat16), "grp", scatter_dimension=0, tiled=True
            ).astype(jnp.float32),
            lax.psum_scatter(
                accum[4].astype(jnp.bfloat16), "grp", scatter_dimension=0, tiled=True
            ).astype(jnp.float32),
        )
        reduced.append(
            (
                lax.psum(shards[0].astype(jnp.bfloat16), "rep").astype(jnp.float32),
                lax.psum(shards[1].astype(jnp.bfloat16), "rep").astype(jnp.float32),
                lax.psum(shards[2].astype(jnp.bfloat16), "rep").astype(jnp.float32),
                lax.psum(shards[3].astype(jnp.bfloat16), "rep").astype(jnp.float32),
                lax.psum(shards[4].astype(jnp.bfloat16), "rep").astype(jnp.float32),
            )
        )
    block_out = jnp.stack(outputs)[:, None]
    block_in_grad = jnp.stack(input_grads)[:, None]
    stacked = [
        jnp.stack([reduced[layer_idx][member] for layer_idx in range(layer_count)])
        for member in range(5)
    ]
    return (block_out, block_in_grad, stacked[0], stacked[1], stacked[2], stacked[3], stacked[4])


def solution(mesh):
    rep_size, grp_size = mesh.shape["rep"], mesh.shape["grp"]

    def body(block_in, cotangent, w_qkv, w_out, w_up, w_down, norm_gains):
        sizes = (rep_size, grp_size, block_in.shape[0], w_qkv.shape[0], block_in.shape[2])
        fits = sizes == (4, 8, 2, 2, TOK)
        chosen = body_pairs if fits else body_general
        return chosen(block_in, cotangent, w_qkv, w_out, w_up, w_down, norm_gains)

    tokens = P(None, "rep", "grp", None)
    rows = P(None, "grp", None)
    return jax.shard_map(
        body,
        mesh=mesh,
        in_specs=(tokens, tokens, rows, rows, rows, rows, rows),
        out_specs=(tokens, tokens, rows, rows, rows, rows, rows),
        check_vma=False,
    )
```

```python
import functools
import types

import jax
import jax.numpy as jnp
from jax import lax
from jax.experimental import pallas as pl
from jax.experimental.pallas import tpu as pltpu
from jax.sharding import PartitionSpec as P

HEADS = 16
HDIM = 64
EPS = 1e-06
NEGATIVE = -1e30
BF = jnp.bfloat16
REP, GRP = "rep", "grp"
F32 = jnp.float32


def dot(left, right):
    return jnp.dot(left, right, preferred_element_type=F32)


def dot_tn(left, right):
    return lax.dot_general(left, right, (((0,), (0,)), ((), ())), preferred_element_type=F32)


def dot_nt(left, right):
    return lax.dot_general(left, right, (((1,), (1,)), ((), ())), preferred_element_type=F32)


def norm(values, gain):
    return values * lax.rsqrt(jnp.mean(values * values, axis=-1, keepdims=True) + EPS) * gain


def head_mask(width, head):
    lanes = lax.broadcasted_iota(jnp.int32, (1, width), 1)
    return (lanes // HDIM) == head


def attend_kernel(block, qkv_ref, mixed_ref, lse_ref, tick):
    length, width = mixed_ref.shape
    heads = width // HDIM
    row = lax.broadcasted_iota(jnp.int32, (block, block), 0)
    col = lax.broadcasted_iota(jnp.int32, (block, block), 1)
    below = col <= row
    zero = jnp.zeros((), BF)
    lane = lax.broadcasted_iota(jnp.int32, (1, 128), 1)
    for start in range(0, length, block):
        stop = start + block
        query = qkv_ref[start:stop, :width] * jnp.asarray(HDIM**-0.5, BF)
        total = jnp.zeros((block, width), F32)
        stats = jnp.zeros((block, 128), F32)
        for head in range(heads):
            mask = head_mask(width, head)
            keys = jnp.where(mask, qkv_ref[:stop, width : 2 * width], zero)
            vals = jnp.where(mask, qkv_ref[:stop, 2 * width :], zero)
            scores = dot_nt(query, keys)
            last = jnp.where(below, scores[:, start:], NEGATIVE)
            scores = jnp.concatenate([scores[:, :start], last], axis=1) if start else last
            top = jnp.max(scores, axis=1, keepdims=True)
            terms = jnp.exp(scores - top)
            sums = jnp.sum(terms, axis=1, keepdims=True)
            total = total + dot(terms.astype(BF), vals) * (1.0 / sums)
            stats = jnp.where(lane == head, top + jnp.log(sums), stats)
        mixed_ref[start:stop, :] = total.astype(BF)
        lse_ref[start:stop, :] = stats
        tick()


def attend_back_kernel(block, qkv_ref, lse_ref, grad_ref, out_ref, dk_ref, dv_ref, tick):
    length, width = grad_ref.shape
    heads = width // HDIM
    row = lax.broadcasted_iota(jnp.int32, (block, block), 0)
    col = lax.broadcasted_iota(jnp.int32, (block, block), 1)
    below = col <= row
    zero = jnp.zeros((), BF)
    scale = HDIM**-0.5
    dk_ref[...] = jnp.zeros_like(dk_ref)
    dv_ref[...] = jnp.zeros_like(dv_ref)
    for start in range(0, length, block):
        stop = start + block
        query = qkv_ref[start:stop, :width] * jnp.asarray(scale, BF)
        grad = grad_ref[start:stop, :]
        dq = jnp.zeros((block, width), F32)
        for head in range(heads):
            mask = head_mask(width, head)
            keys = jnp.where(mask, qkv_ref[:stop, width : 2 * width], zero)
            vals = jnp.where(mask, qkv_ref[:stop, 2 * width :], zero)
            scores = dot_nt(query, keys)
            last = jnp.where(below, scores[:, start:], NEGATIVE)
            scores = jnp.concatenate([scores[:, :start], last], axis=1) if start else last
            probs = jnp.exp(scores - lse_ref[start:stop, head : head + 1])
            prob_grad = dot_nt(grad, vals)
            delta = jnp.sum(probs * prob_grad, axis=1, keepdims=True)
            score_grad = (probs * (prob_grad - delta)).astype(BF)
            dq = dq + dot(score_grad, keys)
            dk_ref[:stop, :] += dot_tn(score_grad, jnp.where(mask, query, zero))
            dv_ref[:stop, :] += dot_tn(probs.astype(BF), jnp.where(mask, grad, zero))
        out_ref[start:stop, :width] = (dq * scale).astype(BF)
        tick()
    out_ref[:, width : 2 * width] = dk_ref[...].astype(BF)
    out_ref[:, 2 * width :] = dv_ref[...].astype(BF)


MESH_ID = pl.DeviceIdType.MESH
HELD, ONE, TWO, SUM, LINE, FULL = "_v", "one", "two", "sum", "line", "full"
PASSED = ("give", "take", "send", "got")
ATTN, DOWN, UP, QKV = "attn", "down", "up", "qkv"
D0, U0, Q0, O0 = "d0", "u0", "q0", "o0"
D1, U1, Q1, O1 = "d1", "u1", "q1", "o1"
TOK = 128


class Place:
    def __init__(self):
        rep, grp = lax.axis_index(REP), lax.axis_index(GRP)
        self.rep, self.grp = rep, grp
        self.x, self.y = lax.rem(rep, 2), lax.div(rep, 2)
        self.t, self.upper = lax.rem(grp, 4), lax.div(grp, 4)
        self.c, self.side = lax.rem(grp, 2), lax.div(self.t, 2)
        base = self.upper * 4
        self.core = (rep, base + self.side * 2 + 1 - self.c)
        self.near = (rep, base + (1 - self.side) * 2 + self.c)
        self.far = (rep, (1 - self.upper) * 4 + self.t)
        self.along_x = (self.y * 2 + 1 - self.x, grp)
        self.along_y = ((1 - self.y) * 2 + self.x, grp)
        self.near_t = (1 - self.side) * 2 + self.c

    def line(self, offset):
        c = 1 - self.c if offset & 1 else self.c
        side = 1 - self.side if offset & 2 else self.side
        upper = 1 - self.upper if offset & 4 else self.upper
        return (self.rep, upper * 4 + side * 2 + c), upper, side * 2 + c


class Copies:
    def __init__(self, send, recv, here):
        self.sems, self.here = (send, recv), here
        self.sent, self.local_count, self.stores = [], 0, []

    def remote(self, source, target, device):
        at = len(self.sent)
        assert at < self.sems[0].shape[0]
        copy = pltpu.make_async_remote_copy(
            src_ref=source,
            dst_ref=target,
            send_sem=self.sems[0].at[at],
            recv_sem=self.sems[1].at[at],
            device_id=device,
            device_id_type=MESH_ID,
        )
        copy.start()
        self.sent.append(copy)
        return copy

    def local(self, source, target):
        assert self.local_count < self.here.shape[0]
        copy = pltpu.make_async_copy(source, target, self.here.at[self.local_count])
        self.local_count += 1
        copy.start()
        return copy

    def store(self, source, target):
        self.stores.append(self.local(source, target))

    def finish(self):
        for copy in self.sent:
            copy.wait_send()
        for copy in self.stores:
            copy.wait()


def meet(devices):
    barrier = pltpu.get_barrier_semaphore()
    for device in devices:
        pl.semaphore_signal(barrier, inc=1, device_id=device, device_id_type=MESH_ID)
    pl.semaphore_wait(barrier, len(devices))


class Plan:
    def __init__(self, *entries):
        self.entries = list(entries)

    def tick(self):
        if self.entries:
            for action in self.entries.pop(0):
                action()

    def drain(self):
        while self.entries:
            self.tick()


def stages(task):
    return lambda: next(task, None)


def spread(copies, place, part, last=True):
    x, y, every = place.x, place.y, slice(None)
    one = copies.remote(part(0, y, x), part(0, y, x), place.along_x)
    two = copies.remote(part(1, y, x), part(1, y, x), place.along_y)
    yield
    one.wait_recv()
    three = copies.remote(part(0, y, every), part(0, y, every), place.along_y)
    two.wait_recv()
    four = copies.remote(part(1, every, x), part(1, every, x), place.along_x)
    yield
    three.wait_recv()
    four.wait_recv()
    if last:
        yield


def deal(copies, place, source, target):
    moved = []
    own = copies.local(source.at[place.t], target)
    for offset in range(1, 8):
        if offset == 4:
            yield
        device, upper, t = place.line(offset)
        moved.append(copies.remote(source.at[t], target, device))
    yield
    own.wait()
    for copy in moved:
        copy.wait_recv()
    yield


def add_low(one, two):
    return (one.astype(F32) + two.astype(F32)).astype(BF)


def reduce_rep(copies, place, grad, ns, name):
    x, y = place.x, place.y
    count = grad.shape[1]

    def step_one():
        one = getattr(ns, name + ONE)
        first = copies.remote(grad.at[0, :, :, 1 - x], one.at[0], place.along_x)
        second = copies.remote(grad.at[1, :, 1 - y], one.at[1], place.along_y)
        yield
        first.wait_recv()
        second.wait_recv()
        for i in range(count):
            for j in range(2):
                grad[0, i, j, x] = add_low(grad[0, i, j, x], one[0, i, j])
                grad[1, i, y, j] = add_low(grad[1, i, y, j], one[1, i, j])
        yield

    def step_two():
        two, total = getattr(ns, name + TWO), getattr(ns, name + SUM)
        first = copies.remote(grad.at[0, :, 1 - y, x], two.at[0], place.along_y)
        second = copies.remote(grad.at[1, :, y, 1 - x], two.at[1], place.along_x)
        own = [copies.local(grad.at[half, :, y, x], total.at[half]) for half in range(2)]
        yield
        first.wait_recv()
        second.wait_recv()
        for half in range(2):
            own[half].wait()
            for i in range(count):
                total[half, i] = add_low(total[half, i], two[half, i])
        yield

    return step_one(), step_two()


def line_columns(copies, place, ns, name):
    total, line, full = (getattr(ns, name + part) for part in (SUM, LINE, FULL))
    moved = []
    for offset in range(1, 8):
        device, upper, t = place.line(offset)
        here = line.at[place.upper, place.t]
        moved.append(copies.remote(total.at[upper, t], here, device))
    line[place.upper, place.t] = total[place.upper, place.t]
    yield
    for copy in moved:
        copy.wait_recv()
    for t in range(4):
        full[place.y, place.x, t] = add_low(line[0, t], line[1, t])
    yield


def line_rows(copies, place, ns, name):
    total, line, full = (getattr(ns, name + part) for part in (SUM, LINE, FULL))
    moved = copies.remote(total.at[1 - place.upper, 0], line, place.far)
    yield
    moved.wait_recv()
    rows = line.shape[0] // 2
    for half in range(2):
        at = pl.ds(half * rows, rows)
        full[place.y, place.x, half] = add_low(total[place.upper, 0, at, :], line[at, :])
    yield


def whole_columns(copies, place, ns, name, target, groups):
    full = getattr(ns, name + FULL)
    yield from spread(copies, place, lambda half, a, b: full.at[a, b, pl.ds(2 * half, 2)], False)
    unit = full.shape[4] // groups
    for t in range(4):
        for k in range(groups):
            source = full.at[:, :, t, :, k * unit : (k + 1) * unit]
            start = (k * 4 + t) * unit
            copies.store(source, target.at[:, :, :, start : start + unit])
    yield


def whole_rows(copies, place, ns, name, target):
    full = getattr(ns, name + FULL)
    yield from spread(copies, place, lambda half, a, b: full.at[a, b, half], False)
    copies.store(full, target)
    yield


def reduce_scratch(name, count, rows, width, steps=3):
    total = {}
    if steps & 1:
        total[name + ONE] = pltpu.VMEM((2, count, 2, rows, width), BF)
    if steps & 2:
        total[name + TWO] = pltpu.VMEM((2, count, rows, width), BF)
        total[name + SUM] = pltpu.VMEM((2, count, rows, width), BF)
    return total


def finish_scratch(name, count, rows, width):
    if count == 1:
        line, full = (rows, width), (2, 2, 2, rows // 2, width)
    else:
        line, full = (2, count, rows, width), (2, 2, count, rows, width)
    return {name + LINE: pltpu.VMEM(line, BF), name + FULL: pltpu.VMEM(full, BF)}


def by_device(shape, count):
    rows, width = shape
    return struct((2, count, 2, 2, rows // (8 * count), width), BF)


def loop(count, step):
    def run(index, carry):
        step(index)
        return carry

    lax.fori_loop(0, count, run, 0)


def tile_of(index, size):
    return pl.ds(pl.multiple_of(index * size, size), size)


def matrix(value):
    return value.reshape(-1, value.shape[-1])


def times(left, right_ref, tile, sink):
    every = (slice(None),) * (len(right_ref.shape) - 1)

    def step(index):
        at = tile_of(index, tile)
        sink(at, dot(left(), matrix(right_ref[(*every, at)])))

    loop(right_ref.shape[-1] // tile, step)


def times_rows(left, right_ref, tile, sink):
    flat = len(right_ref.shape) == 2

    def step(index):
        if flat:
            at = tile_of(index, tile)
            sink(at, dot_nt(left(), right_ref[at, :]))
        else:
            block = matrix(right_ref[index])
            sink(tile_of(index, block.shape[0]), dot_nt(left(), block))

    loop(right_ref.shape[0] // (tile if flat else 1), step)


def gram(left_ref, right_ref, out_ref):
    count, tile = out_ref.shape[1], 256
    total = left_ref.shape[1]
    if total == tile:
        value = dot_tn(left_ref[...], right_ref[...]).astype(BF)
        out_ref[...] = value.reshape(out_ref.shape)
        return

    def step(index):
        value = dot_tn(left_ref[:, tile_of(index, tile)], right_ref[...]).astype(BF)
        half, part = lax.div(index, 2), lax.rem(index, 2)
        if count == 1:
            out_ref[half, 0, part] = value.reshape(out_ref.shape[3:])
        else:
            out_ref[half, pl.ds(part * 2, 2)] = value.reshape(2, *out_ref.shape[2:])

    loop(total // tile, step)


class Gather:
    def __init__(self, copies, place, buf):
        self.copies, self.place, self.buf = copies, place, buf
        self.flight = {}

    def rows(self, stream, where):
        start = (stream * 4 + where) * TOK
        return pl.ds(pl.multiple_of(start, TOK), TOK)

    def pair(self, stream, side):
        start = (stream * 4 + side * 2) * TOK
        return pl.ds(pl.multiple_of(start, TOK), 2 * TOK)

    def start(self, stream, block):
        at = self.rows(stream, self.place.t)
        self.buf[at, :] = block
        mine = self.buf.at[at, :]
        across = self.copies.remote(mine, mine, self.place.near)
        beside = self.copies.remote(mine, mine, self.place.core)
        self.flight[stream] = [across, beside]

    def wait_chip(self, stream):
        self.flight[stream][1].wait_recv()

    def forward(self, stream):
        self.flight[stream][0].wait_recv()
        got = self.buf.at[self.rows(stream, self.place.near_t), :]
        self.flight[stream].append(self.copies.remote(got, got, self.place.core))

    def wait_rest(self, stream):
        self.flight[stream][2].wait_recv()


class Scatter:
    def __init__(self, copies, place, ns, name):
        self.copies, self.place = copies, place
        self.away, self.own = ns.terms_away, ns.terms_own
        self.give, self.take, self.send, self.got = (
            getattr(ns, name + part) for part in PASSED
        )
        self.flight = {}

    def push(self, stream, product):
        place, copies = self.place, self.copies
        mine = pl.ds(pl.multiple_of(place.c * TOK, TOK), TOK)
        other = pl.ds(pl.multiple_of((1 - place.c) * TOK, TOK), TOK)

        def to_away(at, value):
            self.away[:, at] = value

        def to_own(at, value):
            self.own[stream, :, at] = value

        product(1 - place.side, to_away)
        self.give[stream, 0] = self.away[other, :].astype(BF)
        first = copies.remote(self.give.at[stream, 0], self.take.at[stream, 0], place.core)
        product(place.side, to_own)
        first.wait_recv()
        self.send[stream] = (self.away[mine, :] + self.take[stream, 0].astype(F32)).astype(BF)
        across = copies.remote(self.send.at[stream], self.got.at[stream], place.near)
        self.give[stream, 1] = self.own[stream, other, :].astype(BF)
        second = copies.remote(self.give.at[stream, 1], self.take.at[stream, 1], place.core)
        self.flight[stream] = (second, across)

    def result(self, stream):
        second, across = self.flight[stream]
        mine = pl.ds(pl.multiple_of(self.place.c * TOK, TOK), TOK)
        second.wait_recv()
        total = self.own[stream, mine, :] + self.take[stream, 1].astype(F32)
        across.wait_recv()
        return total + self.got[stream].astype(F32)


def scatter_scratch(name, width):
    give, take, send, got = (name + part for part in PASSED)
    return {
        "terms_away": pltpu.VMEM((2 * TOK, width), F32),
        "terms_own": pltpu.VMEM((2, 2 * TOK, width), F32),
        give: pltpu.VMEM((2, 2, TOK, width), BF),
        take: pltpu.VMEM((2, 2, TOK, width), BF),
        send: pltpu.VMEM((2, TOK, width), BF),
        got: pltpu.VMEM((2, TOK, width), BF),
    }


def gelu_both(x):
    cubic = x * x * 0.044715
    bent = jnp.tanh(0.7978845608028654 * (x + cubic * x))
    half = 0.5 * (1.0 + bent)
    slope = half + 0.5 * x * (1.0 - bent * bent) * (0.7978845608028654 * (1.0 + 3.0 * cubic))
    return x * half, slope


def norm_back_in(values, gain, grad):
    rstd = lax.rsqrt(jnp.mean(values * values, axis=-1, keepdims=True) + EPS)
    hat = values * rstd
    scaled = grad * gain
    back = rstd * (scaled - hat * jnp.mean(scaled * hat, axis=-1, keepdims=True))
    return back, jnp.sum(grad * hat, axis=0, keepdims=True)


def next_qkv(ns, place, blocks, tick, wait_weights, early=False):
    gather = Gather(ns.copies, place, ns.normed_v)
    for stream in range(2):
        gather.start(stream, blocks[stream]())
        tick()
    if early:
        for stream in range(2):
            gather.forward(stream)
            tick()
    wait_weights()
    wq = ns.wq_v
    for stream in range(2):

        def project(side):
            at = gather.pair(stream, side)

            def sink(cols, value):
                ns.qkv_v[at, cols] = value.astype(BF)

            times(lambda: ns.normed_v[at, :], wq, 384, sink)

        gather.wait_chip(stream)
        project(place.side)
        if not early:
            gather.forward(stream)
        gather.wait_rest(stream)
        project(1 - place.side)
        tick()
        here = pl.ds(stream * 4 * TOK, 4 * TOK)
        ns.copies.store(ns.normed_v.at[here, :], ns.normed.at[here, :])
        ns.copies.store(ns.qkv_v.at[here, :], ns.qkv.at[here, :])


def fwd_mid(ns, place, gain, tick, wait_out, wait_up, wait_down):
    copies = ns.copies
    attn = Scatter(copies, place, ns, ATTN)
    down = Scatter(copies, place, ns, DOWN)
    gather = Gather(copies, place, ns.mlp_v)
    wo, wu, wd = ns.wo_v, ns.wu_v, ns.wd_v
    wait_out()
    for stream in range(2):

        def product(side, sink):
            at = gather.pair(stream, side)
            times(lambda: ns.mixed_v[at, :], wo, 512, sink)

        attn.push(stream, product)
        tick()
    ns.load.hidden.wait()
    for stream in range(2):
        value = attn.result(stream)
        ns.attn_out_v[stream] = value
        resid = ns.hidden_v[stream].astype(F32) + norm(value, gain(1))
        ns.resid_v[stream] = resid
        gather.start(stream, norm(resid, gain(2)).astype(BF))
        tick()
    wait_up()
    for stream in range(2):

        def expand(side):
            at = gather.pair(stream, side)

            def sink(cols, value):
                active, slope = gelu_both(value)
                ns.active_v[at, cols] = active.astype(BF)
                ns.slope_v[at, cols] = slope.astype(BF)

            times(lambda: ns.mlp_v[at, :], wu, 256, sink)

        gather.wait_chip(stream)
        expand(place.side)
        gather.forward(stream)
        gather.wait_rest(stream)
        expand(1 - place.side)
        if stream == 0:
            wait_down()

        def product(side, sink):
            at = gather.pair(stream, side)
            times(lambda: ns.active_v[at, :], wd, 512, sink)

        down.push(stream, product)
        tick()
    return down


def bwd_mid(ns, place, layer, grads, tick, on_down, on_up):
    copies, gain, base = ns.copies, rows_of(ns, layer), layer * 4
    up = Scatter(copies, place, ns, UP)
    first = Gather(copies, place, ns.down_grad_v)
    second = Gather(copies, place, ns.attn_grad_v)
    wo, wu, wd = ns.wo_v, ns.wu_v, ns.wd_v
    for stream in range(2):
        grad = grads[stream]()
        ns.grad_v[stream] = grad
        back, four = norm_back_in(ns.down_out_v[stream], gain(3), grad)
        ns.dg_v[base + 3 : base + 4, :] += four
        first.start(stream, back.astype(BF))
        tick()
    for stream in range(2):

        def shrink(side):
            at = first.pair(stream, side)

            def sink(cols, value):
                slope = ns.slope_v[at, cols].astype(F32)
                ns.up_grad_v[at, cols] = (value * slope).astype(BF)

            times_rows(lambda: ns.down_grad_v[at, :], wd, 512, sink)

        first.wait_chip(stream)
        shrink(place.side)
        first.forward(stream)
        first.wait_rest(stream)
        shrink(1 - place.side)

        def product(side, sink):
            at = first.pair(stream, side)
            times_rows(lambda: ns.up_grad_v[at, :], wu, 512, sink)

        up.push(stream, product)
        tick()
    for stream in range(2):
        back, three = norm_back_in(ns.resid_v[stream], gain(2), up.result(stream))
        grad = ns.grad_v[stream] + back
        ns.grad_v[stream] = grad
        ns.dg_v[base + 2 : base + 3, :] += three
        back, two = norm_back_in(ns.attn_out_v[stream], gain(1), grad)
        ns.dg_v[base + 1 : base + 2, :] += two
        second.start(stream, back.astype(BF))
        tick()
        if stream == 0:
            gram(ns.active_v, ns.down_grad_v, ns.gd_v)
            on_down()
        else:
            gram(ns.mlp_v, ns.up_grad_v, ns.gu_v)
            on_up()
            tick()
    copies.store(ns.grad_v, ns.resid_grad)
    for stream in range(2):

        def project(side):
            at = second.pair(stream, side)
            ns.mixed_grad_v[at, :] = dot_nt(ns.attn_grad_v[at, :], matrix(wo[...])).astype(BF)

        second.wait_chip(stream)
        project(place.side)
        second.forward(stream)
        second.wait_rest(stream)
        project(1 - place.side)
        tick()
        here = pl.ds(stream * 4 * TOK, 4 * TOK)
        copies.store(ns.mixed_grad_v.at[here, :], ns.mixed_grad.at[here, :])
    gram(ns.mixed_v, ns.attn_grad_v, ns.go_v)


def bwd_head(ns, place, layer, tick, on_qkv, weight_first):
    copies, gain = ns.copies, rows_of(ns, layer)
    qkv = Scatter(copies, place, ns, QKV)
    walk = Gather(copies, place, None)

    def weight():
        ns.load.normed.wait()
        gram(ns.normed_v, ns.qkv_grad_v, ns.gq_v)
        on_qkv()
        tick()

    if weight_first:
        weight()
    ns.load.wq.wait()
    for stream in range(2):

        def product(side, sink):
            at = walk.pair(stream, side)
            times_rows(lambda: ns.qkv_grad_v[at, :], ns.wq_v, 512, sink)

        qkv.push(stream, product)
        tick()
    if not weight_first:
        weight()
    ns.load.hidden.wait()
    ns.load.grad.wait()

    def result(stream):
        back, one = norm_back_in(ns.hidden_v[stream].astype(F32), gain(0), qkv.result(stream))
        ns.dg_v[layer * 4 : layer * 4 + 1, :] += one
        return ns.grad_v[stream] + back

    return [functools.partial(result, stream) for stream in range(2)]


def kernel_of(body, inputs, outputs, scratch, slot, remotes, locals_, vmem, flops):
    names = [*inputs, *outputs, *scratch]

    def kernel(*refs):
        ns = types.SimpleNamespace(**dict(zip(names, refs)))
        ns.copies = Copies(*refs[len(names) :])
        ns.load = types.SimpleNamespace()
        for name in inputs:
            if name + HELD in scratch:
                copy = ns.copies.local(getattr(ns, name), getattr(ns, name + HELD))
                setattr(ns.load, name, copy)
        body(ns)
        ns.copies.finish()

    moved = sum(v.size * v.dtype.itemsize for v in [*inputs.values(), *outputs.values()])
    return kernel, dict(
        name=body.__name__,
        out_shape=list(outputs.values()),
        in_specs=[pl.BlockSpec(memory_space=pl.ANY)] * len(inputs),
        out_specs=[pl.BlockSpec(memory_space=pl.ANY)] * len(outputs),
        scratch_shapes=[
            *scratch.values(),
            pltpu.SemaphoreType.DMA((remotes,)),
            pltpu.SemaphoreType.DMA((remotes,)),
            pltpu.SemaphoreType.DMA((locals_,)),
        ],
        compiler_params=pltpu.CompilerParams(
            collective_id=slot, has_side_effects=True, vmem_limit_bytes=vmem << 20
        ),
        cost_estimate=pl.CostEstimate(flops=flops, bytes_accessed=moved, transcendentals=0),
    )


def named(outputs, results):
    return types.SimpleNamespace(**dict(zip(outputs, results)))


def held(*groups):
    merged = {name: value for group in groups for name, value in group.items()}
    return {name + HELD: pltpu.VMEM(value.shape, value.dtype) for name, value in merged.items()}


def struct(shape, dtype):
    return jax.ShapeDtypeStruct(shape, dtype)


def rows_of(ns, layer):
    return lambda index, level=layer: ns.gains_v[level * 4 + index : level * 4 + index + 1, :]


def quarter_of(ns, place, weight, layer, target):
    rows = weight.shape[1] // 4
    at = pl.ds(pl.multiple_of(place.rep * rows, rows), rows)
    return ns.copies.local(weight.at[layer, at, :], target)


def arrange(quarter, dealt, groups):
    unit = quarter.shape[1] // (groups * 4)
    for t in range(4):
        for k in range(groups):
            start = (k * 4 + t) * unit
            dealt[t, :, k * unit : (k + 1) * unit] = quarter[:, start : start + unit]


def by_rows(ref, place):
    return lambda half, a, b: ref.at[1 - place.upper, a, b, half]


def by_columns(ref):
    return lambda half, a, b: ref.at[half, :, a, b]


def start_kernel(block, gain_part, w_qkv, w_up, w_out):
    width, part = block.shape[2], w_qkv.shape[2] // 4
    units = w_up.shape[2] // 4
    length, rows = 8 * TOK, width // 32
    inputs = dict(block=block, gain_part=gain_part, w_qkv=w_qkv, w_up=w_up, w_out=w_out)
    gains = struct((gain_part.shape[0], width), F32)
    hidden = struct(block.shape, BF)
    normed = struct((length, width), BF)
    qkv = struct((length, part), BF)
    wq = struct((2, 4, 2, 2, rows, part), BF)
    outputs = dict(
        hidden=hidden,
        gains=gains,
        normed=normed,
        qkv=qkv,
        wq=wq,
        part_u=struct((2, 4, rows, units), BF),
        part_o=struct(w_out.shape[3:], BF),
    )
    kept = dict(
        hidden=hidden,
        gains=gains,
        normed=normed,
        qkv=qkv,
        wq=wq,
        quarter_q=struct((rows, 4 * part), BF),
        quarter_u=struct((rows, 4 * units), BF),
        deal_q=struct((4, rows, part), BF),
        deal_u=struct((4, rows, units), BF),
    )
    scratch = held(kept)

    def start(ns):
        place, copies = Place(), ns.copies
        upper, y, x = place.upper, place.y, place.x
        columns = pl.ds(pl.multiple_of(place.grp * TOK, TOK), TOK)
        line = [place.line(offset)[0] for offset in range(1, 8)]
        quarter_q = quarter_of(ns, place, ns.w_qkv, 0, ns.quarter_q_v)
        quarter_u = quarter_of(ns, place, ns.w_up, 0, ns.quarter_u_v)
        kept = copies.local(ns.block.at[upper], ns.hidden_v.at[upper])
        gain_own = copies.local(ns.gain_part, ns.gains_v.at[:, columns])
        quarter_q.wait()
        arrange(ns.quarter_q_v, ns.deal_q_v, 6)
        meet([*line, place.along_x, place.along_y])
        gain_rest = [copies.remote(ns.gain_part, ns.gains_v.at[:, columns], at) for at in line]
        wq_dealt = deal(copies, place, ns.deal_q_v, ns.wq_v.at[upper, place.t, y, x])
        next(wq_dealt)
        next(wq_dealt)
        brought = copies.remote(ns.block.at[1 - upper], ns.hidden_v.at[upper], place.far)
        wq_spread = spread(copies, place, by_columns(ns.wq_v))
        up_dealt = deal(copies, place, ns.deal_u_v, ns.part_u.at[upper, place.t])
        rest = []

        def others():
            next(up_dealt)
            rest.append(copies.remote(ns.w_out.at[0, y, x], ns.part_o, place.far))

        def wait_weights():
            next(wq_spread)
            copies.store(ns.wq_v, ns.wq)

        quarter_u.wait()
        arrange(ns.quarter_u_v, ns.deal_u_v, 2)
        next(up_dealt)
        next(wq_dealt)
        next(wq_spread)
        kept.wait()
        gain_own.wait()
        for copy in gain_rest:
            copy.wait_recv()
        next(wq_spread)
        brought.wait_recv()
        copies.store(ns.hidden_v, ns.hidden)
        copies.store(ns.gains_v, ns.gains)
        blocks = [
            functools.partial(
                lambda s: norm(ns.hidden_v[s].astype(F32), ns.gains_v[0:1, :]).astype(BF), stream
            )
            for stream in range(2)
        ]
        plan = Plan([], [others])
        next_qkv(ns, place, blocks, plan.tick, wait_weights, early=True)
        plan.drain()
        next(up_dealt)
        rest[0].wait_recv()

    flops = 2 * length * width * part
    kernel, options = kernel_of(start, inputs, outputs, scratch, 0, 48, 64, 60, flops)
    results = pl.pallas_call(kernel, **options)(*inputs.values())
    return named(outputs, results)


def forward_kernel(begun, w_qkv, w_up, w_down, w_out):
    hidden, gains = begun.hidden, begun.gains
    length, part = begun.qkv.shape
    width, mixed_width = hidden.shape[2], part // 3
    units, rows = w_up.shape[2] // 4, width // 32
    inputs = dict(
        qkv_in=begun.qkv, hidden=hidden, gains=gains, w_qkv=w_qkv, w_up=w_up, w_down=w_down,
        w_out=w_out, part_u=begun.part_u, part_o=begun.part_o,
    )
    blocks = struct((2, TOK, width), F32)
    wide = struct((length, width), BF)
    next_u, next_o = struct((2, 4, rows, units), BF), struct((2, *w_out.shape[1:]), BF)
    outputs = dict(
        mixed=struct((length, mixed_width), BF),
        lse=struct((length, 128), F32),
        attn_out=blocks,
        resid=blocks,
        mlp=wide,
        active=struct((length, units), BF),
        slope=struct((length, units), BF),
        down_out=blocks,
        hidden_out=blocks,
        normed=wide,
        qkv=struct((length, part), BF),
        wu=struct((2, 4, 2, 2, rows, units), BF),
        wd=struct((2, *w_down.shape[1:]), BF),
        wo=next_o,
        wq=struct((2, 4, 2, 2, rows, part), BF),
    )
    kept = dict(
        qkv_in=begun.qkv,
        hidden=hidden,
        gains=gains,
        quarter_q=struct((rows, 4 * part), BF),
        quarter_u=struct((rows, 4 * units), BF),
        deal_q=struct((4, rows, part), BF),
        deal_u=struct((4, rows, units), BF),
    )
    scratch = held(outputs, kept)
    outputs = dict(outputs, next_u=next_u, next_o=next_o)
    scratch |= scatter_scratch(ATTN, width) | scatter_scratch(DOWN, width)

    def forward(ns):
        place, copies = Place(), ns.copies
        upper, t, y, x = place.upper, place.t, place.y, place.x
        part_o = copies.local(ns.part_o, ns.wo_v.at[1 - upper, y, x])
        part_u = copies.local(ns.part_u, ns.wu_v.at[:, :, y, x])
        quarter_q = quarter_of(ns, place, ns.w_qkv, 1, ns.quarter_q_v)
        whole_o = copies.local(ns.w_out.at[0], ns.wo_v.at[upper])
        whole_d = copies.local(ns.w_down.at[0], ns.wd_v.at[upper])
        quarter_u = quarter_of(ns, place, ns.w_up, 1, ns.quarter_u_v)
        line = [place.line(offset)[0] for offset in range(1, 8)]
        meet([*line, place.along_x, place.along_y])
        down_in = copies.remote(ns.w_down.at[0, y, x], ns.wd_v.at[upper, y, x], place.far)
        part_o.wait()
        part_u.wait()
        out_spread = spread(copies, place, by_rows(ns.wo_v, place))
        up_spread = spread(copies, place, by_columns(ns.wu_v))
        down_spread = spread(copies, place, by_rows(ns.wd_v, place))
        next(out_spread)
        quarter_q.wait()
        arrange(ns.quarter_q_v, ns.deal_q_v, 6)
        q_deal = deal(copies, place, ns.deal_q_v, ns.wq_v.at[upper, t, y, x])
        next(q_deal)
        next(q_deal)
        q_spread = spread(copies, place, by_columns(ns.wq_v))
        u_deal = deal(copies, place, ns.deal_u_v, ns.next_u.at[upper, t])
        o_spread = spread(copies, place, by_rows(ns.next_o, place))
        rest = []

        def out_part():
            rest.append(copies.remote(ns.w_out.at[1, y, x], ns.next_o.at[upper, y, x], place.far))

        def deal_up():
            quarter_u.wait()
            arrange(ns.quarter_u_v, ns.deal_u_v, 2)
            next(u_deal)
            next(u_deal)

        def down_arrived():
            down_in.wait_recv()
            next(down_spread)

        def out_arrived():
            rest[0].wait_recv()
            next(o_spread)

        plan = Plan(
            [stages(out_spread), stages(up_spread)],
            [],
            [],
            [],
            [stages(up_spread)],
            [deal_up],
            [down_arrived],
            [stages(down_spread), out_part],
            [stages(q_deal), stages(q_spread)],
            [stages(q_spread)],
            [out_arrived],
            [],
            [stages(o_spread)],
            [stages(o_spread)],
        )
        ns.load.qkv_in.wait()
        attend_kernel(256, ns.qkv_in_v, ns.mixed_v, ns.lse_v, plan.tick)
        copies.store(ns.mixed_v, ns.mixed)
        copies.store(ns.lse_v, ns.lse)
        ns.load.gains.wait()
        gain = rows_of(ns, 0)

        def wait_out():
            next(out_spread)
            whole_o.wait()
            copies.store(ns.wo_v, ns.wo)

        def wait_down():
            next(down_spread)
            whole_d.wait()
            copies.store(ns.wu_v, ns.wu)
            copies.store(ns.wd_v, ns.wd)

        def wait_next():
            next(q_spread)
            copies.store(ns.wq_v, ns.wq)

        down = fwd_mid(ns, place, gain, plan.tick, wait_out, lambda: next(up_spread), wait_down)
        copies.store(ns.attn_out_v, ns.attn_out)
        copies.store(ns.resid_v, ns.resid)
        copies.store(ns.mlp_v, ns.mlp)
        copies.store(ns.active_v, ns.active)
        copies.store(ns.slope_v, ns.slope)

        def block(stream):
            value = down.result(stream)
            ns.down_out_v[stream] = value
            hidden_out = ns.resid_v[stream] + norm(value, gain(3))
            ns.hidden_out_v[stream] = hidden_out
            return norm(hidden_out, gain(0, 1)).astype(BF)

        blocks = [functools.partial(block, stream) for stream in range(2)]
        next_qkv(ns, place, blocks, plan.tick, wait_next)
        copies.store(ns.down_out_v, ns.down_out)
        copies.store(ns.hidden_out_v, ns.hidden_out)
        plan.drain()
        next(u_deal)

    flops = 2 * length * width * (mixed_width + 2 * units + part)
    kernel, options = kernel_of(forward, inputs, outputs, scratch, 1, 80, 64, 62, flops)
    results = pl.pallas_call(kernel, **options)(*inputs.values())
    return named(outputs, results)


def turn_kernel(lower, gains, w_down, w_out, cotangent):
    hidden = lower.hidden_out
    width = hidden.shape[2]
    length, part = lower.qkv.shape
    mixed_width = part // 3
    inputs = dict(
        qkv_in=lower.qkv, gains=gains, hidden=hidden, cot=cotangent,
        part_u=lower.next_u, part_o=lower.next_o, w_down=w_down, w_out=w_out,
    )
    rows, units = lower.next_u.shape[2:]
    blocks = struct((2, TOK, width), F32)
    outputs = dict(
        out=struct((2, TOK, width), BF),
        lse=struct((length, 128), F32),
        mixed_grad=struct((length, mixed_width), BF),
        gd=by_device((units, width), 1),
        gu=by_device((width, units), 4),
        go=by_device((mixed_width, width), 1),
        dg=struct((8, width), F32),
    )
    kept = dict(
        qkv_in=lower.qkv,
        hidden=hidden,
        gains=gains,
        cot=cotangent,
        wd=struct((2, *w_down.shape[1:]), BF),
        wo=lower.next_o,
        wu=struct((2, 4, 2, 2, rows, units), BF),
        mixed=struct((length, mixed_width), BF),
        attn_out=blocks,
        resid=blocks,
        grad=blocks,
        mlp=struct((length, width), BF),
        active=struct((length, units), BF),
        slope=struct((length, units), BF),
        up_grad=struct((length, units), BF),
        down_out=blocks,
        down_grad=struct((length, width), BF),
        attn_grad=struct((length, width), BF),
    )
    scratch = held(outputs, kept)
    outputs |= dict(resid_grad=blocks)
    for name in (ATTN, DOWN, UP):
        scratch |= scatter_scratch(name, width)
    scratch |= reduce_scratch(D1, 1, units // 8, width, 1) | reduce_scratch(U1, 4, rows, units, 1)

    def turn(ns):
        place, copies = Place(), ns.copies
        upper, y, x = place.upper, place.y, place.x
        part_u = copies.local(ns.part_u, ns.wu_v.at[:, :, y, x])
        part_o = copies.local(ns.part_o.at[1 - upper], ns.wo_v.at[1 - upper])
        whole_o = copies.local(ns.w_out.at[1], ns.wo_v.at[upper])
        whole_d = copies.local(ns.w_down.at[1], ns.wd_v.at[upper])
        meet([place.core, place.near, place.far, place.along_x, place.along_y])
        down_in = copies.remote(ns.w_down.at[1, y, x], ns.wd_v.at[upper, y, x], place.far)
        part_u.wait()
        up_spread = spread(copies, place, by_columns(ns.wu_v))
        down_spread = spread(copies, place, by_rows(ns.wd_v, place))
        next(up_spread)
        ns.load.qkv_in.wait()
        far_in = []

        def bring():
            ns.load.cot.wait()
            far_in.append(copies.remote(ns.cot.at[1 - upper], ns.cot_far_v, place.far))

        def down_arrived():
            down_in.wait_recv()
            next(down_spread)

        plan = Plan(
            [],
            [],
            [],
            [],
            [stages(up_spread)],
            [],
            [down_arrived],
            [stages(down_spread), bring],
        )
        attend_kernel(256, ns.qkv_in_v, ns.mixed_v, ns.lse_v, plan.tick)
        copies.store(ns.lse_v, ns.lse)
        ns.load.gains.wait()
        ns.dg_v[...] = jnp.zeros_like(ns.dg_v)
        gain = rows_of(ns, 1)

        def wait_out():
            part_o.wait()
            whole_o.wait()

        def wait_down():
            next(down_spread)
            whole_d.wait()

        down = fwd_mid(
            ns, place, gain, plan.tick, wait_out, lambda: next(up_spread), wait_down
        )
        far_in[0].wait_recv()

        def grad(stream):
            value = down.result(stream)
            ns.down_out_v[stream] = value
            own = jnp.where(upper == stream, ns.cot_v[stream], ns.cot_far_v[...])
            return own.astype(F32)

        def finish():
            for stream in range(2):
                out = ns.resid_v[stream] + norm(ns.down_out_v[stream], gain(3))
                ns.out_v[stream] = out.astype(BF)
            copies.store(ns.out_v.at[upper], ns.out.at[upper])
            far_in.append(copies.remote(ns.out_v.at[1 - upper], ns.out.at[upper], place.far))

        d_first, unused = reduce_rep(copies, place, ns.gd_v, ns, D1)
        u_first, unused = reduce_rep(copies, place, ns.gu_v, ns, U1)
        plan = Plan(
            [],
            [finish],
            [],
            [],
            [],
        )
        grads = [functools.partial(grad, stream) for stream in range(2)]
        bwd_mid(ns, place, 1, grads, plan.tick, stages(d_first), stages(u_first))
        copies.store(ns.go_v, ns.go)
        copies.store(ns.dg_v, ns.dg)
        next(d_first)
        copies.store(ns.gd_v, ns.gd)
        next(u_first)
        copies.store(ns.gu_v, ns.gu)
        far_in[1].wait_recv()

    scratch["cot_far_v"] = pltpu.VMEM((TOK, width), BF)
    flops = 6 * length * width * (mixed_width + 2 * units)
    kernel, options = kernel_of(turn, inputs, outputs, scratch, 2, 64, 64, 63, flops)
    results = pl.pallas_call(kernel, **options)(*inputs.values())
    return named(outputs, results)


def backward_kernel(begun, lower, turned):
    wo, wu, wd, wq = (matrix(value) for value in (lower.wo, lower.wu, lower.wd, lower.wq))
    width, units = wu.shape
    length, part = lower.qkv.shape
    mixed_width = wo.shape[0]
    inputs = dict(
        d1=turned.gd, u1=turned.gu, o1=turned.go, qkv_in=lower.qkv, lse=turned.lse,
        mixed_grad=turned.mixed_grad, dg=turned.dg, gains=begun.gains, wq=wq, normed=lower.normed,
        hidden=lower.hidden_out, grad=turned.resid_grad, down_out=lower.down_out, wd=wd,
        slope=lower.slope, wu=wu, active=lower.active, mlp=lower.mlp, resid=lower.resid,
        attn_out=lower.attn_out, wo=wo, mixed=lower.mixed,
    )
    blocks = struct((2, TOK, width), F32)
    kept = dict(
        gq=by_device(wq.shape, 4),
        gd=by_device(wd.shape, 1),
        gu=by_device(wu.shape, 4),
        go=by_device(wo.shape, 1),
        qkv_grad=struct(lower.qkv.shape, BF),
        dk=struct((length, mixed_width), F32),
        dv=struct((length, mixed_width), F32),
        down_grad=struct((length, width), BF),
        attn_grad=struct((length, width), BF),
    )
    outputs = dict(
        resid_grad=blocks,
        mixed_out=struct((length, mixed_width), BF),
        gd=kept["gd"],
        gu=kept["gu"],
        go=kept["go"],
        dg_out=turned.dg,
        full_d=struct((2, 2, 2, units // 16, width), BF),
        full_u=struct((2, 2, width // 32, 4 * units), BF),
        full_q=struct((2, 2, width // 32, 4 * part), BF),
        full_o=struct((2, 2, 2, mixed_width // 16, width), BF),
    )
    loaded = dict(inputs)
    del loaded["d1"], loaded["u1"]
    scratch = held(loaded, kept)
    for name in (QKV, UP):
        scratch |= scatter_scratch(name, width)
    rows = width // 32
    for name, count, high, wide, steps in (
        (D1, 1, units // 8, width, 2),
        (U1, 4, rows, units, 2),
        (Q1, 4, rows, part, 3),
        (O1, 1, mixed_width // 8, width, 3),
    ):
        scratch |= finish_scratch(name, count, high, wide)
        scratch |= reduce_scratch(name, count, high, wide, steps)
    scratch |= reduce_scratch(D0, 1, units // 8, width, 1)

    def backward(ns):
        place, copies = Place(), ns.copies
        ns.up_grad_v = ns.normed_v
        line = [place.line(offset)[0] for offset in range(1, 8)]
        meet([*line, place.along_x, place.along_y])
        unused, d1_second = reduce_rep(copies, place, ns.d1, ns, D1)
        unused, u1_second = reduce_rep(copies, place, ns.u1, ns, U1)
        o1_first, o1_second = reduce_rep(copies, place, ns.o1_v, ns, O1)
        q1_first, q1_second = reduce_rep(copies, place, ns.gq_v, ns, Q1)
        d0_first, unused = reduce_rep(copies, place, ns.gd_v, ns, D0)
        d1_line = line_rows(copies, place, ns, D1)
        u1_line = line_columns(copies, place, ns, U1)
        o1_line = line_rows(copies, place, ns, O1)
        q1_line = line_columns(copies, place, ns, Q1)
        d1_whole = whole_rows(copies, place, ns, D1, ns.full_d)
        u1_whole = whole_columns(copies, place, ns, U1, ns.full_u, 2)
        q1_whole = whole_columns(copies, place, ns, Q1, ns.full_q, 6)
        o1_whole = whole_rows(copies, place, ns, O1, ns.full_o)
        next(d1_second)
        next(u1_second)
        ns.load.o1.wait()
        next(o1_first)
        ns.load.qkv_in.wait()
        ns.load.lse.wait()
        ns.load.mixed_grad.wait()
        ns.load.dg.wait()
        plan = Plan(
            [],
            [],
            [stages(d1_second), stages(d1_line)],
            [],
            [stages(u1_second), stages(u1_line)],
            [stages(o1_first), stages(o1_second)],
            [],
            [stages(d1_line), stages(d1_whole), stages(o1_second), stages(o1_line)],
            [stages(q1_first), stages(q1_second), stages(d1_whole), stages(u1_line)]
            + [stages(u1_whole)],
            [stages(q1_second), stages(q1_line)],
            [stages(d1_whole)],
            [stages(u1_whole)],
            [stages(q1_line), stages(q1_whole), stages(o1_line), stages(o1_whole)],
            [],
            [stages(u1_whole)],
            [stages(d0_first), stages(q1_whole), stages(o1_whole)],
        )
        attend_back_kernel(
            256, ns.qkv_in_v, ns.lse_v, ns.mixed_grad_v, ns.qkv_grad_v, ns.dk_v, ns.dv_v, plan.tick
        )
        ns.load.gains.wait()
        grads = bwd_head(ns, place, 1, plan.tick, stages(q1_first), False)
        for copy in (ns.load.down_out, ns.load.wd, ns.load.slope, ns.load.wu, ns.load.active):
            copy.wait()
        for copy in (ns.load.mlp, ns.load.resid, ns.load.attn_out, ns.load.wo, ns.load.mixed):
            copy.wait()
        ns.mixed_grad = ns.mixed_out
        store_up = functools.partial(copies.store, ns.gu_v, ns.gu)
        bwd_mid(ns, place, 0, grads, plan.tick, stages(d0_first), store_up)
        plan.drain()
        copies.store(ns.go_v, ns.go)
        copies.store(ns.gd_v, ns.gd)
        copies.store(ns.dg_v, ns.dg_out)
        next(q1_whole)
        next(o1_whole)

    flops = 6 * length * width * (mixed_width + 2 * units) + 4 * length * width * part
    kernel, options = kernel_of(backward, inputs, outputs, scratch, 3, 128, 128, 63, flops)
    results = pl.pallas_call(kernel, **options)(*inputs.values())
    return named(outputs, results)


def last_kernel(begun, lower, back):
    wq = matrix(begun.wq)
    width, part = wq.shape
    length, mixed_width = back.mixed_out.shape
    units, rows = back.gu.shape[-1], width // 32
    inputs = dict(
        u0=back.gu, d0=back.gd, o0=back.go, qkv_in=begun.qkv, lse=lower.lse,
        mixed_grad=back.mixed_out, dg=back.dg_out, gains=begun.gains, normed=begun.normed, wq=wq,
        hidden=begun.hidden, grad=back.resid_grad,
    )
    outputs = dict(
        out=struct((2, TOK, width), BF),
        gain_grad=struct((8, TOK), F32),
        full_d=struct(back.full_d.shape, BF),
        full_u=struct(back.full_u.shape, BF),
        full_q=struct(back.full_q.shape, BF),
        full_o=struct(back.full_o.shape, BF),
    )
    kept = dict(
        out=outputs["out"],
        gq=by_device(wq.shape, 4),
        qkv_grad=struct(begun.qkv.shape, BF),
        dk=struct((length, mixed_width), F32),
        dv=struct((length, mixed_width), F32),
        dg_line=struct((8, 8, TOK), F32),
        dg_pass=struct((5, 8, TOK), F32),
    )
    loaded = dict(inputs)
    del loaded["d0"]
    scratch = held(loaded, kept)
    scratch |= scatter_scratch(QKV, width)
    for name, count, high, wide, steps in (
        (D0, 1, units // 8, width, 2),
        (U0, 4, rows, units, 3),
        (Q0, 4, rows, part, 3),
        (O0, 1, mixed_width // 8, width, 3),
    ):
        scratch |= reduce_scratch(name, count, high, wide, steps)
        scratch |= finish_scratch(name, count, high, wide)

    def last(ns):
        place, copies = Place(), ns.copies
        line = [place.line(offset)[0] for offset in range(1, 8)]
        meet([*line, place.along_x, place.along_y])
        unused, d0_second = reduce_rep(copies, place, ns.d0, ns, D0)
        u0_first, u0_second = reduce_rep(copies, place, ns.u0_v, ns, U0)
        o0_first, o0_second = reduce_rep(copies, place, ns.o0_v, ns, O0)
        q0_first, q0_second = reduce_rep(copies, place, ns.gq_v, ns, Q0)
        d0_line = line_rows(copies, place, ns, D0)
        o0_line = line_rows(copies, place, ns, O0)
        u0_line = line_columns(copies, place, ns, U0)
        q0_line = line_columns(copies, place, ns, Q0)
        d0_whole = whole_rows(copies, place, ns, D0, ns.full_d)
        o0_whole = whole_rows(copies, place, ns, O0, ns.full_o)
        u0_whole = whole_columns(copies, place, ns, U0, ns.full_u, 2)
        q0_whole = whole_columns(copies, place, ns, Q0, ns.full_q, 6)
        ns.load.u0.wait()
        next(u0_first)
        next(d0_second)
        ns.load.qkv_in.wait()
        ns.load.lse.wait()
        ns.load.mixed_grad.wait()
        ns.load.dg.wait()
        ns.load.o0.wait()
        plan = Plan(
            [],
            [],
            [],
            [],
            [],
            [],
            [stages(d0_second), stages(d0_line), stages(u0_first)],
        )
        attend_back_kernel(
            256, ns.qkv_in_v, ns.lse_v, ns.mixed_grad_v, ns.qkv_grad_v, ns.dk_v, ns.dv_v, plan.tick
        )
        ns.load.gains.wait()
        grads = bwd_head(ns, place, 0, plan.tick, stages(q0_first), True)
        upper = place.upper
        ns.out_v[0] = grads[0]().astype(BF)
        for task in (q0_first, q0_second, u0_second, o0_first):
            next(task)
        ns.out_v[1] = grads[1]().astype(BF)
        copies.store(ns.out_v.at[upper], ns.out.at[upper])
        gain_grad = gain_sum(ns, copies, place)
        for task in (gain_grad, q0_second, q0_line):
            next(task)
        moved = copies.remote(ns.out_v.at[1 - upper], ns.out.at[upper], place.far)
        for task in (
            d0_line, d0_whole, u0_second, u0_line, o0_first, o0_second, q0_line, q0_whole,
            d0_whole, o0_second, o0_line, gain_grad, q0_whole, u0_line, u0_whole, o0_line,
            o0_whole, gain_grad, d0_whole, q0_whole, u0_whole, o0_whole, gain_grad, u0_whole,
            o0_whole,
        ):
            next(task)
        moved.wait_recv()

    flops = 4 * length * width * part
    kernel, options = kernel_of(last, inputs, outputs, scratch, 4, 128, 128, 60, flops)
    results = pl.pallas_call(kernel, **options)(*inputs.values())
    return named(outputs, results)


def gain_sum(ns, copies, place):
    def columns(grp):
        return pl.ds(pl.multiple_of(grp * TOK, TOK), TOK)

    moved = []
    for offset in range(1, 8):
        device, upper, t = place.line(offset)
        source = ns.dg_v.at[:, columns(upper * 4 + t)]
        moved.append(copies.remote(source, ns.dg_line_v.at[place.grp], device))
    ns.dg_line_v[place.grp] = ns.dg_v[:, columns(place.grp)]
    yield
    for copy in moved:
        copy.wait_recv()
    ns.dg_pass_v[0] = jnp.sum(ns.dg_line_v[...], axis=0)
    moved = copies.remote(ns.dg_pass_v.at[0], ns.dg_pass_v.at[1], place.along_x)
    yield
    moved.wait_recv()
    ns.dg_pass_v[2] = ns.dg_pass_v[0] + ns.dg_pass_v[1]
    moved = copies.remote(ns.dg_pass_v.at[2], ns.dg_pass_v.at[3], place.along_y)
    yield
    moved.wait_recv()
    ns.dg_pass_v[4] = ns.dg_pass_v[2] + ns.dg_pass_v[3]
    copies.store(ns.dg_pass_v.at[4], ns.gain_grad)
    yield


def body_pairs(block_in, cotangent, w_qkv, w_out, w_up, w_down, norm_gains):
    layers, rows, width = w_out.shape
    hidden_unit = w_down.shape[1]
    gain_part = jnp.transpose(norm_gains.astype(F32), (0, 2, 1)).reshape(layers * 4, rows)
    down_parts = w_down.reshape(layers, 2, 2, 2, hidden_unit // 8, width)
    out_parts = w_out.reshape(layers, 2, 2, 2, rows // 8, width)

    begun = start_kernel(block_in[:, 0], gain_part, w_qkv, w_up, out_parts)
    lower = forward_kernel(begun, w_qkv, w_up, down_parts, out_parts)
    turned = turn_kernel(lower, begun.gains, down_parts, out_parts, cotangent[:, 0])
    back = backward_kernel(begun, lower, turned)
    last = last_kernel(begun, lower, back)

    def whole(zero, one, like):
        return jnp.stack([zero, one]).reshape(like.shape).astype(F32)

    return (
        turned.out[:, None],
        last.out.astype(F32)[:, None],
        whole(last.full_q, back.full_q, w_qkv),
        whole(last.full_o, back.full_o, w_out),
        whole(last.full_u, back.full_u, w_up),
        whole(last.full_d, back.full_d, w_down),
        jnp.transpose(last.gain_grad.reshape(layers, 4, rows), (0, 2, 1)),
    )


def norm_apply(values, gains):
    return values * lax.rsqrt(jnp.mean(values * values, axis=-1, keepdims=True) + EPS) * gains


def inner_rows(left, right):
    return lax.dot_general(
        left, right, (((0,), (0,)), ((), ())), preferred_element_type=jnp.float32
    )


def times_trans(left, right):
    return lax.dot_general(
        left, right, (((1,), (1,)), ((), ())), preferred_element_type=jnp.float32
    )


def split_blocks(whole):
    length = whole.shape[0]
    width = min(512, length)
    count = length // width
    return (whole.reshape(count, width, HEADS, HDIM), width, count)


def block_at(blocks, index):
    return lax.dynamic_index_in_dim(blocks, index, 0, keepdims=False)


def key_scores(query, key_block, key_start, query_pos):
    scale = HDIM ** (-0.5)
    scores = (
        jnp.einsum("qhd,khd->hqk", query, key_block, preferred_element_type=jnp.float32) * scale
    )
    key_pos = key_start + jnp.arange(key_block.shape[0], dtype=jnp.int32)
    allowed = key_pos[None, :] <= query_pos[:, None]
    return (scores, allowed[None])


def attend_split(query, keys_all, values_all, query_pos):
    key_blocks, width, count = split_blocks(keys_all)
    value_blocks = split_blocks(values_all)[0]
    row_count = query.shape[0]
    upper = query_pos[row_count - 1] // width + 1

    def total_step(index, carry):
        running, total = carry
        scores, allowed = key_scores(query, block_at(key_blocks, index), index * width, query_pos)
        newest = jnp.maximum(running, jnp.max(jnp.where(allowed, scores, NEGATIVE), axis=-1))
        terms = jnp.where(allowed, jnp.exp(scores - newest[..., None]), 0.0)
        total = total * jnp.exp(running - newest) + jnp.sum(terms, axis=-1)
        return (newest, total)

    start_run = jnp.full((HEADS, row_count), NEGATIVE, jnp.float32)
    start_total = jnp.zeros((HEADS, row_count), jnp.float32)
    running, total = lax.fori_loop(0, upper, total_step, (start_run, start_total))
    log_total = running + jnp.log(total)

    def mix_step(index, accum):
        scores, allowed = key_scores(query, block_at(key_blocks, index), index * width, query_pos)
        probs = jnp.where(allowed, jnp.exp(scores - log_total[..., None]), 0.0)
        return accum + jnp.einsum(
            "hqk,khd->qhd",
            probs.astype(jnp.bfloat16),
            block_at(value_blocks, index),
            preferred_element_type=jnp.float32,
        )

    start_mix = jnp.zeros((row_count, HEADS, HDIM), jnp.float32)
    mixed = lax.fori_loop(0, upper, mix_step, start_mix)
    return (mixed.reshape(row_count, HEADS * HDIM), log_total)


def attend_back_split(query, keys_all, values_all, log_total, out_grad, delta, query_pos):
    key_blocks, width, count = split_blocks(keys_all)
    value_blocks = split_blocks(values_all)[0]
    row_count = query.shape[0]
    upper = query_pos[row_count - 1] // width + 1
    scale = HDIM ** (-0.5)

    def back_step(index, carry):
        query_acc, pieces = carry
        key_block = block_at(key_blocks, index)
        value_block = block_at(value_blocks, index)
        scores, allowed = key_scores(query, key_block, index * width, query_pos)
        probs = jnp.where(allowed, jnp.exp(scores - log_total[..., None]), 0.0)
        prob_grad = jnp.einsum(
            "qhd,khd->hqk", out_grad, value_block, preferred_element_type=jnp.float32
        )
        score_grad = (probs * (prob_grad - delta[..., None])).astype(jnp.bfloat16)
        query_acc = (
            query_acc
            + jnp.einsum("hqk,khd->qhd", score_grad, key_block, preferred_element_type=jnp.float32)
            * scale
        )
        key_grad = (
            jnp.einsum("hqk,qhd->khd", score_grad, query, preferred_element_type=jnp.float32)
            * scale
        )
        value_grad = jnp.einsum(
            "hqk,qhd->khd", probs.astype(jnp.bfloat16), out_grad, preferred_element_type=jnp.float32
        )
        joined = jnp.concatenate(
            [key_grad.reshape(width, HEADS * HDIM), value_grad.reshape(width, HEADS * HDIM)], axis=1
        )
        pieces = lax.dynamic_update_index_in_dim(pieces, joined, index, 0)
        return (query_acc, pieces)

    start_acc = jnp.zeros((row_count, HEADS, HDIM), jnp.float32)
    start_pieces = jnp.zeros((count, width, 2 * HEADS * HDIM), jnp.float32)
    query_grad, pieces = lax.fori_loop(0, upper, back_step, (start_acc, start_pieces))
    return (query_grad.reshape(row_count, HEADS * HDIM), pieces.reshape(-1, pieces.shape[-1]))


def layer_forward(hidden_in, weights, query_pos):
    w_qkv_full, w_out_full, w_up_full, w_down_full, gain_full = weights
    gains_f = gain_full.astype(jnp.float32)
    row_count = hidden_in.shape[0]
    width = w_out_full.shape[1]
    normed = norm_apply(hidden_in, gains_f[:, 0]).astype(jnp.bfloat16)
    qkv_low = jnp.dot(normed, w_qkv_full, preferred_element_type=jnp.float32).astype(jnp.bfloat16)
    query = qkv_low[:, :width]
    keys_all, values_all = (
        lax.all_gather(qkv_low[:, width : 2 * width], "grp", axis=0, tiled=True),
        lax.all_gather(qkv_low[:, 2 * width :], "grp", axis=0, tiled=True),
    )
    mixed, log_total = attend_split(
        query.reshape(row_count, HEADS, HDIM),
        keys_all.reshape(-1, HEADS, HDIM),
        values_all.reshape(-1, HEADS, HDIM),
        query_pos,
    )
    mixed_low = mixed.astype(jnp.bfloat16)
    attn_out = jnp.dot(mixed_low, w_out_full, preferred_element_type=jnp.float32)
    resid = hidden_in + norm_apply(attn_out, gains_f[:, 1])
    mlp_in = norm_apply(resid, gains_f[:, 2]).astype(jnp.bfloat16)
    up_out = jnp.dot(mlp_in, w_up_full, preferred_element_type=jnp.float32)
    active = jax.nn.gelu(up_out).astype(jnp.bfloat16)
    down_out = jnp.dot(active, w_down_full, preferred_element_type=jnp.float32)
    result = resid + norm_apply(down_out, gains_f[:, 3])
    kept = (
        hidden_in,
        normed,
        qkv_low,
        mixed,
        mixed_low,
        log_total,
        attn_out,
        resid,
        mlp_in,
        up_out,
        active,
        down_out,
    )
    return (result, kept)


def layer_backward(grad_out, weights, kept, query_pos):
    w_qkv_full, w_out_full, w_up_full, w_down_full, gain_full = weights
    (
        hidden_in,
        normed,
        qkv_low,
        mixed,
        mixed_low,
        log_total,
        attn_out,
        resid,
        mlp_in,
        up_out,
        active,
        down_out,
    ) = kept
    gains_f = gain_full.astype(jnp.float32)
    row_count = hidden_in.shape[0]
    width = w_out_full.shape[1]
    unused, puller = jax.vjp(norm_apply, down_out, gains_f[:, 3])
    down_grad, gain_four = puller(grad_out)
    down_low = down_grad.astype(jnp.bfloat16)
    w_down_grad = inner_rows(active, down_low)
    active_grad = times_trans(down_low, w_down_full)
    unused, puller = jax.vjp(jax.nn.gelu, up_out)
    up_low = puller(active_grad)[0].astype(jnp.bfloat16)
    w_up_grad = inner_rows(mlp_in, up_low)
    mlp_grad = times_trans(up_low, w_up_full)
    unused, puller = jax.vjp(norm_apply, resid, gains_f[:, 2])
    resid_part, gain_three = puller(mlp_grad)
    resid_grad = grad_out + resid_part
    unused, puller = jax.vjp(norm_apply, attn_out, gains_f[:, 1])
    attn_grad, gain_two = puller(resid_grad)
    attn_low = attn_grad.astype(jnp.bfloat16)
    w_out_grad = inner_rows(mixed_low, attn_low)
    mixed_grad = times_trans(attn_low, w_out_full).astype(jnp.bfloat16)
    keys_all, values_all = (
        lax.all_gather(qkv_low[:, width : 2 * width], "grp", axis=0, tiled=True),
        lax.all_gather(qkv_low[:, 2 * width :], "grp", axis=0, tiled=True),
    )
    delta = jnp.sum(
        (mixed_grad.astype(jnp.float32) * mixed).reshape(row_count, HEADS, HDIM), axis=-1
    ).T
    query_low = qkv_low[:, :width]
    query_grad, key_value_terms = attend_back_split(
        query_low.reshape(row_count, HEADS, HDIM),
        keys_all.reshape(-1, HEADS, HDIM),
        values_all.reshape(-1, HEADS, HDIM),
        log_total,
        mixed_grad.reshape(row_count, HEADS, HDIM),
        delta,
        query_pos,
    )
    key_value_grad = lax.psum_scatter(
        key_value_terms.astype(jnp.bfloat16), "grp", scatter_dimension=0, tiled=True
    ).astype(jnp.float32)
    qkv_grad = jnp.concatenate([query_grad, key_value_grad], axis=1).astype(jnp.bfloat16)
    w_qkv_grad = inner_rows(normed, qkv_grad)
    normed_grad = times_trans(qkv_grad, w_qkv_full)
    unused, puller = jax.vjp(norm_apply, hidden_in, gains_f[:, 0])
    input_part, gain_one = puller(normed_grad)
    gain_grad = jnp.stack([gain_one, gain_two, gain_three, gain_four], axis=1)
    return (resid_grad + input_part, (w_qkv_grad, w_out_grad, w_up_grad, w_down_grad, gain_grad))


def body_general(block_in, cotangent, w_qkv, w_out, w_up, w_down, norm_gains):
    layer_count = w_qkv.shape[0]
    micro_count = block_in.shape[0]
    row_count = block_in.shape[2]
    query_pos = lax.axis_index("grp") * row_count + jnp.arange(row_count, dtype=jnp.int32)
    totals = [None] * layer_count
    outputs = []
    input_grads = []
    for micro_idx in range(micro_count):
        hidden = block_in[micro_idx, 0].astype(jnp.float32)
        saved = []
        for layer_idx in range(layer_count):
            hidden, kept = layer_forward(
                hidden,
                (
                    lax.all_gather(w_qkv[layer_idx], "grp", axis=0, tiled=True),
                    lax.all_gather(w_out[layer_idx], "grp", axis=0, tiled=True),
                    lax.all_gather(w_up[layer_idx], "grp", axis=0, tiled=True),
                    lax.all_gather(w_down[layer_idx], "grp", axis=0, tiled=True),
                    lax.all_gather(norm_gains[layer_idx], "grp", axis=0, tiled=True),
                ),
                query_pos,
            )
            saved.append(kept)
        outputs.append(hidden.astype(jnp.bfloat16))
        grad_flow = cotangent[micro_idx, 0].astype(jnp.float32)
        for layer_idx in reversed(range(layer_count)):
            grad_flow, parts = layer_backward(
                grad_flow,
                (
                    lax.all_gather(w_qkv[layer_idx], "grp", axis=0, tiled=True),
                    lax.all_gather(w_out[layer_idx], "grp", axis=0, tiled=True),
                    lax.all_gather(w_up[layer_idx], "grp", axis=0, tiled=True),
                    lax.all_gather(w_down[layer_idx], "grp", axis=0, tiled=True),
                    lax.all_gather(norm_gains[layer_idx], "grp", axis=0, tiled=True),
                ),
                saved[layer_idx],
                query_pos,
            )
            if totals[layer_idx] is None:
                totals[layer_idx] = parts
            else:
                totals[layer_idx] = tuple(
                    (left + right for left, right in zip(totals[layer_idx], parts))
                )
        input_grads.append(grad_flow)
    reduced = []
    for layer_idx in range(layer_count):
        accum = totals[layer_idx]
        shards = (
            lax.psum_scatter(
                accum[0].astype(jnp.bfloat16), "grp", scatter_dimension=0, tiled=True
            ).astype(jnp.float32),
            lax.psum_scatter(
                accum[1].astype(jnp.bfloat16), "grp", scatter_dimension=0, tiled=True
            ).astype(jnp.float32),
            lax.psum_scatter(
                accum[2].astype(jnp.bfloat16), "grp", scatter_dimension=0, tiled=True
            ).astype(jnp.float32),
            lax.psum_scatter(
                accum[3].astype(jnp.bfloat16), "grp", scatter_dimension=0, tiled=True
            ).astype(jnp.float32),
            lax.psum_scatter(
                accum[4].astype(jnp.bfloat16), "grp", scatter_dimension=0, tiled=True
            ).astype(jnp.float32),
        )
        reduced.append(
            (
                lax.psum(shards[0].astype(jnp.bfloat16), "rep").astype(jnp.float32),
                lax.psum(shards[1].astype(jnp.bfloat16), "rep").astype(jnp.float32),
                lax.psum(shards[2].astype(jnp.bfloat16), "rep").astype(jnp.float32),
                lax.psum(shards[3].astype(jnp.bfloat16), "rep").astype(jnp.float32),
                lax.psum(shards[4].astype(jnp.bfloat16), "rep").astype(jnp.float32),
            )
        )
    block_out = jnp.stack(outputs)[:, None]
    block_in_grad = jnp.stack(input_grads)[:, None]
    stacked = [
        jnp.stack([reduced[layer_idx][member] for layer_idx in range(layer_count)])
        for member in range(5)
    ]
    return (block_out, block_in_grad, stacked[0], stacked[1], stacked[2], stacked[3], stacked[4])


def solution(mesh):
    rep_size, grp_size = mesh.shape["rep"], mesh.shape["grp"]

    def body(block_in, cotangent, w_qkv, w_out, w_up, w_down, norm_gains):
        sizes = (rep_size, grp_size, block_in.shape[0], w_qkv.shape[0], block_in.shape[2])
        fits = sizes == (4, 8, 2, 2, TOK)
        chosen = body_pairs if fits else body_general
        return chosen(block_in, cotangent, w_qkv, w_out, w_up, w_down, norm_gains)

    tokens = P(None, "rep", "grp", None)
    rows = P(None, "grp", None)
    return jax.shard_map(
        body,
        mesh=mesh,
        in_specs=(tokens, tokens, rows, rows, rows, rows, rows),
        out_specs=(tokens, tokens, rows, rows, rows, rows, rows),
        check_vma=False,
    )
```

```python
import functools
import types

import jax
import jax.numpy as jnp
from jax import lax
from jax.experimental import pallas as pl
from jax.experimental.pallas import tpu as pltpu
from jax.sharding import PartitionSpec as P

HEADS = 16
HDIM = 64
EPS = 1e-06
NEGATIVE = -1e30
BF = jnp.bfloat16
REP, GRP = "rep", "grp"
F32 = jnp.float32


def dot(left, right):
    return jnp.dot(left, right, preferred_element_type=F32)


def dot_tn(left, right):
    return lax.dot_general(left, right, (((0,), (0,)), ((), ())), preferred_element_type=F32)


def dot_nt(left, right):
    return lax.dot_general(left, right, (((1,), (1,)), ((), ())), preferred_element_type=F32)


def norm(values, gain):
    return values * lax.rsqrt(jnp.mean(values * values, axis=-1, keepdims=True) + EPS) * gain


def head_mask(width, head):
    lanes = lax.broadcasted_iota(jnp.int32, (1, width), 1)
    return (lanes // HDIM) == head


def causal_scores(query, keys, below, start):
    scores = dot_nt(query, keys)
    last = jnp.where(below, scores[:, start:], NEGATIVE)
    return jnp.concatenate([scores[:, :start], last], axis=1) if start else last


def each_head(heads, one_head, tick):
    half = heads // 2 if tick else heads
    for first in range(0, heads, half):
        loop(half, lambda index: one_head(index + first))
        if tick and first == 0:
            tick()


def attend(ns, stream, block=256):
    length, width = ns.mixed_v.shape
    qkv_ref, lse_ref, sum_ref = ns.qkv_in_v, ns.lse_v, ns.terms_own.at[stream]
    row = lax.broadcasted_iota(jnp.int32, (block, block), 0)
    col = lax.broadcasted_iota(jnp.int32, (block, block), 1)
    below = col <= row
    zero = jnp.zeros((), BF)
    lane = lax.broadcasted_iota(jnp.int32, (1, 128), 1)
    base, high = stream * length // 2, (stream + 1) * length // 2
    sum_ref[...] = jnp.zeros_like(sum_ref)
    lse_ref[base:high, :] = jnp.zeros((length // 2, 128), F32)

    def one_head(head):
        mask = head_mask(width, head)
        for start in range(base, high, block):
            stop = start + block
            query = qkv_ref[start:stop, :width] * jnp.asarray(HDIM**-0.5, BF)
            query = jnp.where(mask, query, zero)
            scores = causal_scores(query, qkv_ref[:stop, width : 2 * width], below, start)
            top = jnp.max(scores, axis=1, keepdims=True)
            terms = jnp.exp(scores - top)
            sums = jnp.sum(terms, axis=1, keepdims=True)
            mixed = dot(terms.astype(BF), qkv_ref[:stop, 2 * width :]) * (1.0 / sums)
            sum_ref[:, start - base : stop - base] += jnp.where(mask, mixed, 0.0)
            stats = lse_ref[start:stop, :]
            lse_ref[start:stop, :] = jnp.where(lane == head, top + jnp.log(sums), stats)

    each_head(width // HDIM, one_head, None)
    for start in range(base, high, block):
        ns.mixed_v[start : start + block, :] = sum_ref[:, start - base : start - base + width].astype(BF)


def attend_back(ns, stream, tick, block=256):
    length, width = ns.mixed_grad_v.shape
    qkv_ref, grad_ref, sum_ref = ns.qkv_in_v, ns.mixed_grad_v, ns.terms_own.at[stream]
    row = lax.broadcasted_iota(jnp.int32, (block, block), 0)
    col = lax.broadcasted_iota(jnp.int32, (block, block), 1)
    below = col <= row
    zero = jnp.zeros((), BF)
    scale = HDIM**-0.5
    lane = lax.broadcasted_iota(jnp.int32, (1, 128), 1)
    base, high = stream * length // 2, (stream + 1) * length // 2
    sum_ref[...] = jnp.zeros_like(sum_ref)

    def one_head(head):
        mask = head_mask(width, head)
        for start in range(base, high, block):
            stop = start + block
            query = qkv_ref[start:stop, :width] * jnp.asarray(scale, BF)
            query = jnp.where(mask, query, zero)
            grad = jnp.where(mask, grad_ref[start:stop, :], zero)
            keys, vals = qkv_ref[:stop, width : 2 * width], qkv_ref[:stop, 2 * width :]
            scores = causal_scores(query, keys, below, start)
            lse = jnp.where(lane == head, ns.lse_v[start:stop, :], 0.0)
            probs = jnp.exp(scores - jnp.sum(lse, axis=1, keepdims=True))
            prob_grad = dot_nt(grad, vals)
            delta = jnp.sum(probs * prob_grad, axis=1, keepdims=True)
            score_grad = (probs * (prob_grad - delta)).astype(BF)
            query_grad = jnp.where(mask, dot(score_grad, keys), 0.0)
            sum_ref[:, start - base : stop - base] += query_grad
            ns.dk_v[:stop, :] += dot_tn(score_grad, query)
            ns.dv_v[:stop, :] += dot_tn(probs.astype(BF), grad)

    each_head(width // HDIM, one_head, tick)
    for start in range(base, high, block):
        value = sum_ref[:, start - base : start - base + width] * scale
        ns.qkv_grad_v[start : start + block, :width] = value.astype(BF)
    ns.qkv_grad_v[base:high, width : 2 * width] = ns.dk_v[base:high, :].astype(BF)
    ns.qkv_grad_v[base:high, 2 * width :] = ns.dv_v[base:high, :].astype(BF)


MESH_ID = pl.DeviceIdType.MESH
HELD, ONE, TWO, SUM, LINE, FULL = "_v", "one", "two", "sum", "line", "full"
PASSED = ("give", "take", "send", "got")
ATTN, DOWN, UP, QKV = "attn", "down", "up", "qkv"
D0, U0, Q0, O0 = "d0", "u0", "q0", "o0"
D1, U1, Q1, O1 = "d1", "u1", "q1", "o1"
TOK = 128


class Place:
    def __init__(self):
        rep, grp = lax.axis_index(REP), lax.axis_index(GRP)
        self.rep, self.grp = rep, grp
        self.x, self.y = lax.rem(rep, 2), lax.div(rep, 2)
        self.t, self.upper = lax.rem(grp, 4), lax.div(grp, 4)
        self.c, self.side = lax.rem(grp, 2), lax.div(self.t, 2)
        base = self.upper * 4
        self.core = (rep, base + self.side * 2 + 1 - self.c)
        self.near = (rep, base + (1 - self.side) * 2 + self.c)
        self.far = (rep, (1 - self.upper) * 4 + self.t)
        self.along_x = (self.y * 2 + 1 - self.x, grp)
        self.along_y = ((1 - self.y) * 2 + self.x, grp)
        self.near_t = (1 - self.side) * 2 + self.c

    def line(self, offset):
        c = 1 - self.c if offset & 1 else self.c
        side = 1 - self.side if offset & 2 else self.side
        upper = 1 - self.upper if offset & 4 else self.upper
        return (self.rep, upper * 4 + side * 2 + c), upper, side * 2 + c


class Copies:
    def __init__(self, send, recv, here):
        self.sems, self.here = (send, recv), here
        self.sent, self.local_count, self.stores = [], 0, []

    def remote(self, source, target, device):
        at = len(self.sent)
        assert at < self.sems[0].shape[0]
        copy = pltpu.make_async_remote_copy(
            src_ref=source,
            dst_ref=target,
            send_sem=self.sems[0].at[at],
            recv_sem=self.sems[1].at[at],
            device_id=device,
            device_id_type=MESH_ID,
        )
        copy.start()
        self.sent.append(copy)
        return copy

    def local(self, source, target):
        assert self.local_count < self.here.shape[0]
        copy = pltpu.make_async_copy(source, target, self.here.at[self.local_count])
        self.local_count += 1
        copy.start()
        return copy

    def store(self, source, target):
        self.stores.append(self.local(source, target))

    def finish(self):
        for copy in self.sent:
            copy.wait_send()
        for copy in self.stores:
            copy.wait()


def meet(devices):
    barrier = pltpu.get_barrier_semaphore()
    for device in devices:
        pl.semaphore_signal(barrier, inc=1, device_id=device, device_id_type=MESH_ID)
    pl.semaphore_wait(barrier, len(devices))


class Plan:
    def __init__(self, *entries):
        self.entries = list(entries)

    def tick(self):
        if self.entries:
            for action in self.entries.pop(0):
                action()

    def drain(self):
        while self.entries:
            self.tick()


def stages(task):
    return lambda: next(task, None)


def spread(copies, place, part, last=True):
    x, y, every = place.x, place.y, slice(None)
    one = copies.remote(part(0, y, x), part(0, y, x), place.along_x)
    two = copies.remote(part(1, y, x), part(1, y, x), place.along_y)
    yield
    one.wait_recv()
    three = copies.remote(part(0, y, every), part(0, y, every), place.along_y)
    two.wait_recv()
    four = copies.remote(part(1, every, x), part(1, every, x), place.along_x)
    yield
    three.wait_recv()
    four.wait_recv()
    if last:
        yield


def deal(copies, place, source, target):
    moved = []
    own = copies.local(source.at[place.t], target)
    for offset in range(1, 8):
        if offset == 4:
            yield
        device, upper, t = place.line(offset)
        moved.append(copies.remote(source.at[t], target, device))
    yield
    own.wait()
    for copy in moved:
        copy.wait_recv()
    yield


def add_low(one, two):
    return (one.astype(F32) + two.astype(F32)).astype(BF)


def reduce_rep(copies, place, grad, ns, name):
    x, y = place.x, place.y
    count = grad.shape[1]

    def step_one():
        one = getattr(ns, name + ONE)
        first = copies.remote(grad.at[0, :, :, 1 - x], one.at[0], place.along_x)
        second = copies.remote(grad.at[1, :, 1 - y], one.at[1], place.along_y)
        yield
        first.wait_recv()
        second.wait_recv()
        for i in range(count):
            for j in range(2):
                grad[0, i, j, x] = add_low(grad[0, i, j, x], one[0, i, j])
                grad[1, i, y, j] = add_low(grad[1, i, y, j], one[1, i, j])
        yield

    def step_two():
        two, total = getattr(ns, name + TWO), getattr(ns, name + SUM)
        first = copies.remote(grad.at[0, :, 1 - y, x], two.at[0], place.along_y)
        second = copies.remote(grad.at[1, :, y, 1 - x], two.at[1], place.along_x)
        own = [copies.local(grad.at[half, :, y, x], total.at[half]) for half in range(2)]
        yield
        first.wait_recv()
        second.wait_recv()
        for half in range(2):
            own[half].wait()
            for i in range(count):
                total[half, i] = add_low(total[half, i], two[half, i])
        yield

    return step_one(), step_two()


def line_columns(copies, place, ns, name):
    total, line, full = (getattr(ns, name + part) for part in (SUM, LINE, FULL))
    moved = []
    for offset in range(1, 8):
        device, upper, t = place.line(offset)
        here = line.at[place.upper, place.t]
        moved.append(copies.remote(total.at[upper, t], here, device))
    line[place.upper, place.t] = total[place.upper, place.t]
    yield
    for copy in moved:
        copy.wait_recv()
    for t in range(4):
        full[place.y, place.x, t] = add_low(line[0, t], line[1, t])
    yield


def line_rows(copies, place, ns, name):
    total, line, full = (getattr(ns, name + part) for part in (SUM, LINE, FULL))
    moved = copies.remote(total.at[1 - place.upper, 0], line, place.far)
    yield
    moved.wait_recv()
    rows = line.shape[0] // 2
    for half in range(2):
        at = pl.ds(half * rows, rows)
        full[place.y, place.x, half] = add_low(total[place.upper, 0, at, :], line[at, :])
    yield


def whole_columns(copies, place, ns, name, target, groups):
    full = getattr(ns, name + FULL)
    yield from spread(copies, place, lambda half, a, b: full.at[a, b, pl.ds(2 * half, 2)], False)
    unit = full.shape[4] // groups
    for t in range(4):
        for k in range(groups):
            source = full.at[:, :, t, :, k * unit : (k + 1) * unit]
            start = (k * 4 + t) * unit
            copies.store(source, target.at[:, :, :, start : start + unit])
    yield


def whole_rows(copies, place, ns, name, target):
    full = getattr(ns, name + FULL)
    yield from spread(copies, place, lambda half, a, b: full.at[a, b, half], False)
    copies.store(full, target)
    yield


def reduce_scratch(name, count, rows, width, steps=3):
    total = {}
    if steps & 1:
        total[name + ONE] = pltpu.VMEM((2, count, 2, rows, width), BF)
    if steps & 2:
        total[name + TWO] = pltpu.VMEM((2, count, rows, width), BF)
        total[name + SUM] = pltpu.VMEM((2, count, rows, width), BF)
    return total


def finish_scratch(name, count, rows, width):
    if count == 1:
        line, full = (rows, width), (2, 2, 2, rows // 2, width)
    else:
        line, full = (2, count, rows, width), (2, 2, count, rows, width)
    return {name + LINE: pltpu.VMEM(line, BF), name + FULL: pltpu.VMEM(full, BF)}


def by_device(shape, count):
    rows, width = shape
    return struct((2, count, 2, 2, rows // (8 * count), width), BF)


def loop(count, step):
    def run(index, carry):
        step(index)
        return carry

    lax.fori_loop(0, count, run, 0)


def tile_of(index, size):
    return pl.ds(pl.multiple_of(index * size, size), size)


def matrix(value):
    return value.reshape(-1, value.shape[-1])


def times(left, right_ref, tile, sink):
    every = (slice(None),) * (len(right_ref.shape) - 1)

    def step(index):
        at = tile_of(index, tile)
        sink(at, dot(left(), matrix(right_ref[(*every, at)])))

    loop(right_ref.shape[-1] // tile, step)


def times_rows(left, right_ref, tile, sink):
    flat = len(right_ref.shape) == 2

    def step(index):
        if flat:
            at = tile_of(index, tile)
            sink(at, dot_nt(left(), right_ref[at, :]))
        else:
            block = matrix(right_ref[index])
            sink(tile_of(index, block.shape[0]), dot_nt(left(), block))

    loop(right_ref.shape[0] // (tile if flat else 1), step)


def gram(left_ref, right_ref, out_ref):
    count, tile = out_ref.shape[1], 256
    total = left_ref.shape[1]
    if total == tile:
        value = dot_tn(left_ref[...], right_ref[...]).astype(BF)
        out_ref[...] = value.reshape(out_ref.shape)
        return

    def step(index):
        value = dot_tn(left_ref[:, tile_of(index, tile)], right_ref[...]).astype(BF)
        half, part = lax.div(index, 2), lax.rem(index, 2)
        if count == 1:
            out_ref[half, 0, part] = value.reshape(out_ref.shape[3:])
        else:
            out_ref[half, pl.ds(part * 2, 2)] = value.reshape(2, *out_ref.shape[2:])

    loop(total // tile, step)


class Gather:
    def __init__(self, copies, place, buf, order=(0, 1)):
        self.copies, self.place, self.buf, self.order = copies, place, buf, order
        self.flight = {}

    def rows(self, stream, where):
        start = (self.order[stream] * 4 + where) * TOK
        return pl.ds(pl.multiple_of(start, TOK), TOK)

    def pair(self, stream, side):
        start = (self.order[stream] * 4 + side * 2) * TOK
        return pl.ds(pl.multiple_of(start, TOK), 2 * TOK)

    def start(self, stream, block):
        at = self.rows(stream, self.place.t)
        self.buf[at, :] = block
        mine = self.buf.at[at, :]
        across = self.copies.remote(mine, mine, self.place.near)
        beside = self.copies.remote(mine, mine, self.place.core)
        self.flight[stream] = [across, beside]

    def wait_chip(self, stream):
        self.flight[stream][1].wait_recv()

    def forward(self, stream):
        self.flight[stream][0].wait_recv()
        got = self.buf.at[self.rows(stream, self.place.near_t), :]
        self.flight[stream].append(self.copies.remote(got, got, self.place.core))

    def wait_rest(self, stream):
        self.flight[stream][2].wait_recv()


class Scatter:
    def __init__(self, copies, place, ns, name):
        self.copies, self.place = copies, place
        self.away, self.own = ns.terms_away, ns.terms_own
        self.give, self.take, self.send, self.got = (
            getattr(ns, name + part) for part in PASSED
        )
        self.flight = {}

    def push(self, stream, product):
        place, copies = self.place, self.copies
        mine = pl.ds(pl.multiple_of(place.c * TOK, TOK), TOK)
        other = pl.ds(pl.multiple_of((1 - place.c) * TOK, TOK), TOK)

        def to_away(at, value):
            self.away[:, at] = value

        def to_own(at, value):
            self.own[stream, :, at] = value

        product(1 - place.side, to_away)
        self.give[stream, 0] = self.away[other, :].astype(BF)
        first = copies.remote(self.give.at[stream, 0], self.take.at[stream, 0], place.core)
        product(place.side, to_own)
        first.wait_recv()
        self.send[stream] = (self.away[mine, :] + self.take[stream, 0].astype(F32)).astype(BF)
        across = copies.remote(self.send.at[stream], self.got.at[stream], place.near)
        self.give[stream, 1] = self.own[stream, other, :].astype(BF)
        second = copies.remote(self.give.at[stream, 1], self.take.at[stream, 1], place.core)
        self.flight[stream] = (second, across)

    def result(self, stream):
        second, across = self.flight[stream]
        mine = pl.ds(pl.multiple_of(self.place.c * TOK, TOK), TOK)
        second.wait_recv()
        total = self.own[stream, mine, :] + self.take[stream, 1].astype(F32)
        across.wait_recv()
        return total + self.got[stream].astype(F32)


def scatter_scratch(name, width):
    give, take, send, got = (name + part for part in PASSED)
    return {
        "terms_away": pltpu.VMEM((2 * TOK, width), F32),
        "terms_own": pltpu.VMEM((2, 2 * TOK, width), F32),
        give: pltpu.VMEM((2, 2, TOK, width), BF),
        take: pltpu.VMEM((2, 2, TOK, width), BF),
        send: pltpu.VMEM((2, TOK, width), BF),
        got: pltpu.VMEM((2, TOK, width), BF),
    }


def gelu_both(x):
    cubic = x * x * 0.044715
    bent = jnp.tanh(0.7978845608028654 * (x + cubic * x))
    half = 0.5 * (1.0 + bent)
    slope = half + 0.5 * x * (1.0 - bent * bent) * (0.7978845608028654 * (1.0 + 3.0 * cubic))
    return x * half, slope


def norm_back_in(values, gain, grad):
    rstd = lax.rsqrt(jnp.mean(values * values, axis=-1, keepdims=True) + EPS)
    hat = values * rstd
    scaled = grad * gain
    back = rstd * (scaled - hat * jnp.mean(scaled * hat, axis=-1, keepdims=True))
    return back, jnp.sum(grad * hat, axis=0, keepdims=True)


def next_qkv(ns, place, blocks, tick, wait_weights, order=(0, 1), late=None):
    gather = Gather(ns.copies, place, ns.normed_v, order)
    for stream in range(2):
        if late and stream == 1:
            late()
        gather.start(stream, blocks[stream]())
        tick()
    if late:
        for stream in range(2):
            gather.forward(stream)
            tick()
    wait_weights()
    for stream in range(2):

        def project(side):
            at = gather.pair(stream, side)

            def sink(cols, value):
                ns.qkv_v[at, cols] = value.astype(BF)

            times(lambda: ns.normed_v[at, :], ns.wq_v, 384, sink)

        gather.wait_chip(stream)
        project(place.side)
        if not late:
            gather.forward(stream)
        gather.wait_rest(stream)
        project(1 - place.side)
        tick()
        here = pl.ds(pl.multiple_of(order[stream] * 4 * TOK, 4 * TOK), 4 * TOK)
        ns.copies.store(ns.normed_v.at[here, :], ns.normed.at[here, :])
        ns.copies.store(ns.qkv_v.at[here, :], ns.qkv.at[here, :])


def fwd_mid(ns, place, gain, tick, wait_out, wait_up, wait_down):
    copies = ns.copies
    attn = Scatter(copies, place, ns, ATTN)
    down = Scatter(copies, place, ns, DOWN)
    gather = Gather(copies, place, ns.mlp_v)
    wo, wu, wd = ns.wo_v, ns.wu_v, ns.wd_v
    for stream in range(2):

        def product(side, sink):
            at = gather.pair(stream, side)
            times(lambda: ns.mixed_v[at, :], wo, 512, sink)

        attend(ns, stream)
        tick()
        if stream == 0:
            wait_out()
        attn.push(stream, product)
        tick()
    ns.load.hidden.wait()
    for stream in range(2):
        value = attn.result(stream)
        ns.attn_out_v[stream] = value
        resid = ns.hidden_v[stream].astype(F32) + norm(value, gain(1))
        ns.resid_v[stream] = resid
        gather.start(stream, norm(resid, gain(2)).astype(BF))
        tick()
    wait_up()
    for stream in range(2):

        def expand(side):
            at = gather.pair(stream, side)

            def sink(cols, value):
                active, slope = gelu_both(value)
                ns.active_v[at, cols] = active.astype(BF)
                ns.slope_v[at, cols] = slope.astype(BF)

            times(lambda: ns.mlp_v[at, :], wu, 256, sink)

        gather.wait_chip(stream)
        expand(place.side)
        gather.forward(stream)
        gather.wait_rest(stream)
        expand(1 - place.side)
        if stream == 0:
            wait_down()

        def product(side, sink):
            at = gather.pair(stream, side)
            times(lambda: ns.active_v[at, :], wd, 512, sink)

        down.push(stream, product)
        tick()
    return down


def bwd_mid(ns, place, layer, grads, tick, on_down, on_up, order=(0, 1)):
    copies, gain, base = ns.copies, rows_of(ns, layer), layer * 4
    up = Scatter(copies, place, ns, UP)
    first = Gather(copies, place, ns.down_grad_v)
    second = Gather(copies, place, ns.attn_grad_v)
    wo, wu, wd = ns.wo_v, ns.wu_v, ns.wd_v
    for stream in order:
        grad = grads[stream]()
        ns.grad_v[stream] = grad
        back, four = norm_back_in(ns.down_out_v[stream], gain(3), grad)
        ns.dg_v[base + 3 : base + 4, :] += four
        first.start(stream, back.astype(BF))
        tick()
    for stream in order:

        def shrink(side):
            at = first.pair(stream, side)

            def sink(cols, value):
                slope = ns.slope_v[at, cols].astype(F32)
                ns.up_grad_v[at, cols] = (value * slope).astype(BF)

            times_rows(lambda: ns.down_grad_v[at, :], wd, 512, sink)

        first.wait_chip(stream)
        shrink(place.side)
        first.forward(stream)
        first.wait_rest(stream)
        shrink(1 - place.side)

        def product(side, sink):
            at = first.pair(stream, side)
            times_rows(lambda: ns.up_grad_v[at, :], wu, 512, sink)

        up.push(stream, product)
        tick()
    for stream in order:
        back, three = norm_back_in(ns.resid_v[stream], gain(2), up.result(stream))
        grad = ns.grad_v[stream] + back
        ns.grad_v[stream] = grad
        ns.dg_v[base + 2 : base + 3, :] += three
        back, two = norm_back_in(ns.attn_out_v[stream], gain(1), grad)
        ns.dg_v[base + 1 : base + 2, :] += two
        second.start(stream, back.astype(BF))
        tick()
        if stream == order[0]:
            gram(ns.active_v, ns.down_grad_v, ns.gd_v)
            on_down()
        else:
            gram(ns.mlp_v, ns.up_grad_v, ns.gu_v)
            on_up()
            tick()
    copies.store(ns.grad_v, ns.resid_grad)
    for stream in order:

        def project(side):
            at = second.pair(stream, side)
            ns.mixed_grad_v[at, :] = dot_nt(ns.attn_grad_v[at, :], matrix(wo[...])).astype(BF)

        second.wait_chip(stream)
        project(place.side)
        second.forward(stream)
        second.wait_rest(stream)
        project(1 - place.side)
        tick()
        here = pl.ds(stream * 4 * TOK, 4 * TOK)
        copies.store(ns.mixed_grad_v.at[here, :], ns.mixed_grad.at[here, :])
    gram(ns.mixed_v, ns.attn_grad_v, ns.go_v)


def bwd_head(ns, place, layer, tick, on_qkv, weight_first):
    copies, gain = ns.copies, rows_of(ns, layer)
    qkv = Scatter(copies, place, ns, QKV)
    walk = Gather(copies, place, None)

    def weight():
        ns.load.normed.wait()
        gram(ns.normed_v, ns.qkv_grad_v, ns.gq_v)
        on_qkv()
        tick()

    ns.dk_v[...] = jnp.zeros_like(ns.dk_v)
    ns.dv_v[...] = jnp.zeros_like(ns.dv_v)
    for stream in (1, 0):

        def product(side, sink):
            at = walk.pair(stream, side)
            times_rows(lambda: ns.qkv_grad_v[at, :], ns.wq_v, 512, sink)

        attend_back(ns, stream, tick if stream == 1 else None)
        tick()
        if stream == 1:
            ns.load.wq.wait()
        elif weight_first:
            weight()
        qkv.push(stream, product)
        tick()
    if not weight_first:
        weight()
    ns.load.hidden.wait()
    ns.load.grad.wait()

    def result(stream):
        back, one = norm_back_in(ns.hidden_v[stream].astype(F32), gain(0), qkv.result(stream))
        ns.dg_v[layer * 4 : layer * 4 + 1, :] += one
        return ns.grad_v[stream] + back

    return [functools.partial(result, stream) for stream in range(2)]


def kernel_of(body, inputs, outputs, scratch, slot, remotes, locals_, vmem, flops):
    names = [*inputs, *outputs, *scratch]

    def kernel(*refs):
        ns = types.SimpleNamespace(**dict(zip(names, refs)))
        ns.copies = Copies(*refs[len(names) :])
        ns.load = types.SimpleNamespace()
        for name in inputs:
            if name + HELD in scratch:
                copy = ns.copies.local(getattr(ns, name), getattr(ns, name + HELD))
                setattr(ns.load, name, copy)
        body(ns)
        ns.copies.finish()

    moved = sum(v.size * v.dtype.itemsize for v in [*inputs.values(), *outputs.values()])
    return kernel, dict(
        name=body.__name__,
        out_shape=list(outputs.values()),
        in_specs=[pl.BlockSpec(memory_space=pl.ANY)] * len(inputs),
        out_specs=[pl.BlockSpec(memory_space=pl.ANY)] * len(outputs),
        scratch_shapes=[
            *scratch.values(),
            pltpu.SemaphoreType.DMA((remotes,)),
            pltpu.SemaphoreType.DMA((remotes,)),
            pltpu.SemaphoreType.DMA((locals_,)),
        ],
        compiler_params=pltpu.CompilerParams(
            collective_id=slot, has_side_effects=True, vmem_limit_bytes=vmem << 20
        ),
        cost_estimate=pl.CostEstimate(flops=flops, bytes_accessed=moved, transcendentals=0),
    )


def named(outputs, results):
    return types.SimpleNamespace(**dict(zip(outputs, results)))


def held(*groups):
    merged = {name: value for group in groups for name, value in group.items()}
    return {name + HELD: pltpu.VMEM(value.shape, value.dtype) for name, value in merged.items()}


def struct(shape, dtype):
    return jax.ShapeDtypeStruct(shape, dtype)


def rows_of(ns, layer):
    return lambda index, level=layer: ns.gains_v[level * 4 + index : level * 4 + index + 1, :]


def quarter_of(ns, place, weight, layer, target):
    rows = weight.shape[1] // 4
    at = pl.ds(pl.multiple_of(place.rep * rows, rows), rows)
    return ns.copies.local(weight.at[layer, at, :], target)


def arrange(quarter, dealt, groups):
    unit = quarter.shape[1] // (groups * 4)
    for t in range(4):
        for k in range(groups):
            start = (k * 4 + t) * unit
            dealt[t, :, k * unit : (k + 1) * unit] = quarter[:, start : start + unit]


def by_rows(ref, place):
    return lambda half, a, b: ref.at[1 - place.upper, a, b, half]


def by_columns(ref):
    return lambda half, a, b: ref.at[half, :, a, b]


def start_kernel(block, gain_part, w_qkv, w_up, w_out):
    width, part = block.shape[2], w_qkv.shape[2] // 4
    units = w_up.shape[2] // 4
    length, rows = 8 * TOK, width // 32
    inputs = dict(block=block, gain_part=gain_part, w_qkv=w_qkv, w_up=w_up, w_out=w_out)
    gains = struct((gain_part.shape[0], width), F32)
    hidden = struct(block.shape, BF)
    normed = struct((length, width), BF)
    qkv = struct((length, part), BF)
    wq = struct((2, 4, 2, 2, rows, part), BF)
    outputs = dict(
        hidden=hidden,
        gains=gains,
        normed=normed,
        qkv=qkv,
        wq=wq,
        part_u=struct((2, 4, rows, units), BF),
        half_o=struct(w_out.shape[1:], BF),
    )
    kept = dict(
        half_o=struct(w_out.shape[1:], BF),
        hidden=hidden,
        gains=gains,
        normed=normed,
        qkv=qkv,
        wq=wq,
        quarter_q=struct((rows, 4 * part), BF),
        quarter_u=struct((rows, 4 * units), BF),
        deal_q=struct((4, rows, part), BF),
        deal_u=struct((4, rows, units), BF),
    )
    scratch = held(kept)

    def start(ns):
        place, copies = Place(), ns.copies
        upper, y, x = place.upper, place.y, place.x
        columns = pl.ds(pl.multiple_of(place.grp * TOK, TOK), TOK)
        line = [place.line(offset)[0] for offset in range(1, 8)]
        quarter_q = quarter_of(ns, place, ns.w_qkv, 0, ns.quarter_q_v)
        quarter_u = quarter_of(ns, place, ns.w_up, 0, ns.quarter_u_v)
        kept = copies.local(ns.block.at[upper], ns.hidden_v.at[upper])
        gain_own = copies.local(ns.gain_part, ns.gains_v.at[:, columns])
        quarter_q.wait()
        arrange(ns.quarter_q_v, ns.deal_q_v, 6)
        meet([*line, place.along_x, place.along_y])
        gain_rest = [copies.remote(ns.gain_part, ns.gains_v.at[:, columns], at) for at in line]
        wq_dealt = deal(copies, place, ns.deal_q_v, ns.wq_v.at[upper, place.t, y, x])
        next(wq_dealt)
        next(wq_dealt)
        brought = copies.remote(ns.block.at[1 - upper], ns.hidden_v.at[upper], place.far)
        out_in = copies.remote(ns.w_out.at[0, y, x], ns.half_o_v.at[y, x], place.far)
        wq_spread = spread(copies, place, by_columns(ns.wq_v))
        out_spread = spread(copies, place, lambda half, a, b: ns.half_o_v.at[a, b, half])
        up_dealt = deal(copies, place, ns.deal_u_v, ns.part_u.at[upper, place.t])
        quarter_u.wait()
        arrange(ns.quarter_u_v, ns.deal_u_v, 2)
        next(up_dealt)
        kept.wait()
        gain_own.wait()
        for copy in gain_rest:
            copy.wait_recv()

        def late():
            next(wq_spread)
            brought.wait_recv()
            copies.store(ns.hidden_v, ns.hidden)

        def out_arrived():
            out_in.wait_recv()
            next(out_spread)

        def wait_weights():
            next(wq_spread)
            copies.store(ns.wq_v, ns.wq)

        copies.store(ns.gains_v, ns.gains)
        order = (upper, 1 - upper)
        blocks = [
            functools.partial(
                lambda s: norm(ns.hidden_v[s].astype(F32), ns.gains_v[0:1, :]).astype(BF), stream
            )
            for stream in order
        ]
        plan = Plan(
            [stages(wq_dealt), stages(wq_spread)],
            [stages(up_dealt)],
            [out_arrived],
            [stages(out_spread)],
        )
        next_qkv(ns, place, blocks, plan.tick, wait_weights, order, late)
        next(out_spread)
        copies.store(ns.half_o_v, ns.half_o)
        next(up_dealt)

    flops = 2 * length * width * part
    kernel, options = kernel_of(start, inputs, outputs, scratch, 0, 48, 64, 60, flops)
    results = pl.pallas_call(kernel, **options)(*inputs.values())
    return named(outputs, results)


def forward_kernel(begun, w_qkv, w_up, w_down, w_out):
    hidden, gains = begun.hidden, begun.gains
    length, part = begun.qkv.shape
    width, mixed_width = hidden.shape[2], part // 3
    units, rows = w_up.shape[2] // 4, width // 32
    inputs = dict(
        qkv_in=begun.qkv, hidden=hidden, gains=gains, w_qkv=w_qkv, w_up=w_up, w_down=w_down,
        w_out=w_out, part_u=begun.part_u, half_o=begun.half_o,
    )
    blocks = struct((2, TOK, width), F32)
    wide = struct((length, width), BF)
    next_u, next_o = struct((2, 4, rows, units), BF), struct((2, *w_out.shape[1:]), BF)
    outputs = dict(
        mixed=struct((length, mixed_width), BF),
        lse=struct((length, 128), F32),
        attn_out=blocks,
        resid=blocks,
        mlp=wide,
        active=struct((length, units), BF),
        slope=struct((length, units), BF),
        down_out=blocks,
        hidden_out=blocks,
        normed=wide,
        qkv=struct((length, part), BF),
        wu=struct((2, 4, 2, 2, rows, units), BF),
        wd=struct((2, *w_down.shape[1:]), BF),
        wo=next_o,
        wq=struct((2, 4, 2, 2, rows, part), BF),
    )
    kept = dict(
        qkv_in=begun.qkv,
        hidden=hidden,
        gains=gains,
        quarter_q=struct((rows, 4 * part), BF),
        quarter_u=struct((rows, 4 * units), BF),
        deal_q=struct((4, rows, part), BF),
        deal_u=struct((4, rows, units), BF),
    )
    scratch = held(outputs, kept)
    outputs = dict(outputs, next_u=next_u, next_o=next_o)
    scratch |= scatter_scratch(ATTN, width) | scatter_scratch(DOWN, width)

    def forward(ns):
        place, copies = Place(), ns.copies
        upper, t, y, x = place.upper, place.t, place.y, place.x
        half_o = copies.local(ns.half_o, ns.wo_v.at[1 - upper])
        part_u = copies.local(ns.part_u, ns.wu_v.at[:, :, y, x])
        quarter_q = quarter_of(ns, place, ns.w_qkv, 1, ns.quarter_q_v)
        whole_o = copies.local(ns.w_out.at[0], ns.wo_v.at[upper])
        whole_d = copies.local(ns.w_down.at[0], ns.wd_v.at[upper])
        quarter_u = quarter_of(ns, place, ns.w_up, 1, ns.quarter_u_v)
        line = [place.line(offset)[0] for offset in range(1, 8)]
        meet([*line, place.along_x, place.along_y])
        down_in = copies.remote(ns.w_down.at[0, y, x], ns.wd_v.at[upper, y, x], place.far)
        part_u.wait()
        up_spread = spread(copies, place, by_columns(ns.wu_v))
        down_spread = spread(copies, place, by_rows(ns.wd_v, place))
        next(up_spread)
        quarter_q.wait()
        arrange(ns.quarter_q_v, ns.deal_q_v, 6)
        q_deal = deal(copies, place, ns.deal_q_v, ns.wq_v.at[upper, t, y, x])
        next(q_deal)
        next(q_deal)
        q_spread = spread(copies, place, by_columns(ns.wq_v))
        u_deal = deal(copies, place, ns.deal_u_v, ns.next_u.at[upper, t])
        o_spread = spread(copies, place, by_rows(ns.next_o, place))
        rest = []

        def out_part():
            rest.append(copies.remote(ns.w_out.at[1, y, x], ns.next_o.at[upper, y, x], place.far))

        def deal_up():
            quarter_u.wait()
            arrange(ns.quarter_u_v, ns.deal_u_v, 2)
            next(u_deal)
            next(u_deal)

        def down_arrived():
            down_in.wait_recv()
            next(down_spread)

        def out_arrived():
            rest[0].wait_recv()
            next(o_spread)

        plan = Plan(
            [],
            [],
            [stages(up_spread)],
            [deal_up],
            [down_arrived],
            [stages(down_spread), out_part],
            [stages(q_deal), stages(q_spread)],
            [stages(q_spread)],
            [out_arrived],
            [],
            [stages(o_spread)],
            [stages(o_spread)],
        )
        ns.load.qkv_in.wait()
        ns.load.gains.wait()
        gain = rows_of(ns, 0)

        def wait_out():
            half_o.wait()
            whole_o.wait()
            copies.store(ns.wo_v, ns.wo)

        def wait_down():
            next(down_spread)
            whole_d.wait()
            copies.store(ns.wu_v, ns.wu)
            copies.store(ns.wd_v, ns.wd)

        def wait_next():
            next(q_spread)
            copies.store(ns.wq_v, ns.wq)

        down = fwd_mid(ns, place, gain, plan.tick, wait_out, lambda: next(up_spread), wait_down)
        copies.store(ns.mixed_v, ns.mixed)
        copies.store(ns.lse_v, ns.lse)
        copies.store(ns.attn_out_v, ns.attn_out)
        copies.store(ns.resid_v, ns.resid)
        copies.store(ns.mlp_v, ns.mlp)
        copies.store(ns.active_v, ns.active)
        copies.store(ns.slope_v, ns.slope)

        def block(stream):
            value = down.result(stream)
            ns.down_out_v[stream] = value
            hidden_out = ns.resid_v[stream] + norm(value, gain(3))
            ns.hidden_out_v[stream] = hidden_out
            return norm(hidden_out, gain(0, 1)).astype(BF)

        blocks = [functools.partial(block, stream) for stream in range(2)]
        next_qkv(ns, place, blocks, plan.tick, wait_next)
        copies.store(ns.down_out_v, ns.down_out)
        copies.store(ns.hidden_out_v, ns.hidden_out)
        plan.drain()
        next(u_deal)

    flops = 2 * length * width * (mixed_width + 2 * units + part)
    kernel, options = kernel_of(forward, inputs, outputs, scratch, 1, 80, 64, 62, flops)
    results = pl.pallas_call(kernel, **options)(*inputs.values())
    return named(outputs, results)


def turn_kernel(lower, gains, w_down, w_out, cotangent):
    hidden = lower.hidden_out
    width = hidden.shape[2]
    length, part = lower.qkv.shape
    mixed_width = part // 3
    inputs = dict(
        qkv_in=lower.qkv, gains=gains, hidden=hidden, cot=cotangent,
        part_u=lower.next_u, part_o=lower.next_o, w_down=w_down, w_out=w_out,
    )
    rows, units = lower.next_u.shape[2:]
    blocks = struct((2, TOK, width), F32)
    outputs = dict(
        out=struct((2, TOK, width), BF),
        lse=struct((length, 128), F32),
        mixed_grad=struct((length, mixed_width), BF),
        gd=by_device((units, width), 1),
        gu=by_device((width, units), 4),
        go=by_device((mixed_width, width), 1),
        dg=struct((8, width), F32),
    )
    kept = dict(
        qkv_in=lower.qkv,
        hidden=hidden,
        gains=gains,
        cot=cotangent,
        wd=struct((2, *w_down.shape[1:]), BF),
        wo=lower.next_o,
        wu=struct((2, 4, 2, 2, rows, units), BF),
        mixed=struct((length, mixed_width), BF),
        attn_out=blocks,
        resid=blocks,
        grad=blocks,
        mlp=struct((length, width), BF),
        active=struct((length, units), BF),
        slope=struct((length, units), BF),
        up_grad=struct((length, units), BF),
        down_out=blocks,
        down_grad=struct((length, width), BF),
        attn_grad=struct((length, width), BF),
    )
    scratch = held(outputs, kept)
    outputs |= dict(resid_grad=blocks)
    for name in (ATTN, DOWN, UP):
        scratch |= scatter_scratch(name, width)
    scratch |= reduce_scratch(D1, 1, units // 8, width, 1) | reduce_scratch(U1, 4, rows, units, 1)

    def turn(ns):
        place, copies = Place(), ns.copies
        upper, y, x = place.upper, place.y, place.x
        part_u = copies.local(ns.part_u, ns.wu_v.at[:, :, y, x])
        part_o = copies.local(ns.part_o.at[1 - upper], ns.wo_v.at[1 - upper])
        whole_o = copies.local(ns.w_out.at[1], ns.wo_v.at[upper])
        whole_d = copies.local(ns.w_down.at[1], ns.wd_v.at[upper])
        meet([place.core, place.near, place.far, place.along_x, place.along_y])
        down_in = copies.remote(ns.w_down.at[1, y, x], ns.wd_v.at[upper, y, x], place.far)
        part_u.wait()
        up_spread = spread(copies, place, by_columns(ns.wu_v))
        down_spread = spread(copies, place, by_rows(ns.wd_v, place))
        next(up_spread)
        ns.load.qkv_in.wait()
        far_in = []

        def bring():
            ns.load.cot.wait()
            far_in.append(copies.remote(ns.cot.at[1 - upper], ns.cot_far_v, place.far))

        def down_arrived():
            down_in.wait_recv()
            next(down_spread)

        plan = Plan(
            [],
            [],
            [stages(up_spread)],
            [],
            [down_arrived],
            [stages(down_spread), bring],
        )
        ns.load.gains.wait()
        ns.dg_v[...] = jnp.zeros_like(ns.dg_v)
        gain = rows_of(ns, 1)

        def wait_out():
            part_o.wait()
            whole_o.wait()

        def wait_down():
            next(down_spread)
            whole_d.wait()

        down = fwd_mid(
            ns, place, gain, plan.tick, wait_out, lambda: next(up_spread), wait_down
        )
        copies.store(ns.lse_v, ns.lse)
        far_in[0].wait_recv()

        def grad(stream):
            value = down.result(stream)
            ns.down_out_v[stream] = value
            own = jnp.where(upper == stream, ns.cot_v[stream], ns.cot_far_v[...])
            return own.astype(F32)

        def finish():
            for stream in range(2):
                out = ns.resid_v[stream] + norm(ns.down_out_v[stream], gain(3))
                ns.out_v[stream] = out.astype(BF)
            copies.store(ns.out_v.at[upper], ns.out.at[upper])
            far_in.append(copies.remote(ns.out_v.at[1 - upper], ns.out.at[upper], place.far))

        d_first, unused = reduce_rep(copies, place, ns.gd_v, ns, D1)
        u_first, unused = reduce_rep(copies, place, ns.gu_v, ns, U1)
        plan = Plan(
            [],
            [finish],
            [],
            [],
            [],
        )
        grads = [functools.partial(grad, stream) for stream in range(2)]
        bwd_mid(ns, place, 1, grads, plan.tick, stages(d_first), stages(u_first))
        copies.store(ns.go_v, ns.go)
        copies.store(ns.dg_v, ns.dg)
        next(d_first)
        copies.store(ns.gd_v, ns.gd)
        next(u_first)
        copies.store(ns.gu_v, ns.gu)
        far_in[1].wait_recv()

    scratch["cot_far_v"] = pltpu.VMEM((TOK, width), BF)
    flops = 6 * length * width * (mixed_width + 2 * units)
    kernel, options = kernel_of(turn, inputs, outputs, scratch, 2, 64, 64, 63, flops)
    results = pl.pallas_call(kernel, **options)(*inputs.values())
    return named(outputs, results)


def backward_kernel(begun, lower, turned):
    wo, wu, wd, wq = (matrix(value) for value in (lower.wo, lower.wu, lower.wd, lower.wq))
    width, units = wu.shape
    length, part = lower.qkv.shape
    mixed_width = wo.shape[0]
    inputs = dict(
        d1=turned.gd, u1=turned.gu, o1=turned.go, qkv_in=lower.qkv, lse=turned.lse,
        mixed_grad=turned.mixed_grad, dg=turned.dg, gains=begun.gains, wq=wq, normed=lower.normed,
        hidden=lower.hidden_out, grad=turned.resid_grad, down_out=lower.down_out, wd=wd,
        slope=lower.slope, wu=wu, active=lower.active, mlp=lower.mlp, resid=lower.resid,
        attn_out=lower.attn_out, wo=wo, mixed=lower.mixed,
    )
    blocks = struct((2, TOK, width), F32)
    kept = dict(
        gq=by_device(wq.shape, 4),
        gd=by_device(wd.shape, 1),
        gu=by_device(wu.shape, 4),
        go=by_device(wo.shape, 1),
        qkv_grad=struct(lower.qkv.shape, BF),
        dk=struct((length, mixed_width), F32),
        dv=struct((length, mixed_width), F32),
        down_grad=struct((length, width), BF),
        attn_grad=struct((length, width), BF),
    )
    outputs = dict(
        resid_grad=blocks,
        mixed_out=struct((length, mixed_width), BF),
        gd=kept["gd"],
        gu=kept["gu"],
        go=kept["go"],
        dg_out=turned.dg,
        full_d=struct((2, 2, 2, units // 16, width), BF),
        full_u=struct((2, 2, width // 32, 4 * units), BF),
        full_q=struct((2, 2, width // 32, 4 * part), BF),
        full_o=struct((2, 2, 2, mixed_width // 16, width), BF),
    )
    loaded = dict(inputs)
    del loaded["d1"], loaded["u1"]
    scratch = held(loaded, kept)
    for name in (QKV, UP):
        scratch |= scatter_scratch(name, width)
    rows = width // 32
    for name, count, high, wide, steps in (
        (D1, 1, units // 8, width, 2),
        (U1, 4, rows, units, 2),
        (Q1, 4, rows, part, 3),
        (O1, 1, mixed_width // 8, width, 3),
    ):
        scratch |= finish_scratch(name, count, high, wide)
        scratch |= reduce_scratch(name, count, high, wide, steps)
    scratch |= reduce_scratch(D0, 1, units // 8, width, 1)

    def backward(ns):
        place, copies = Place(), ns.copies
        ns.up_grad_v = ns.normed_v
        line = [place.line(offset)[0] for offset in range(1, 8)]
        meet([*line, place.along_x, place.along_y])
        unused, d1_second = reduce_rep(copies, place, ns.d1, ns, D1)
        unused, u1_second = reduce_rep(copies, place, ns.u1, ns, U1)
        o1_first, o1_second = reduce_rep(copies, place, ns.o1_v, ns, O1)
        q1_first, q1_second = reduce_rep(copies, place, ns.gq_v, ns, Q1)
        d0_first, unused = reduce_rep(copies, place, ns.gd_v, ns, D0)
        d1_line = line_rows(copies, place, ns, D1)
        u1_line = line_columns(copies, place, ns, U1)
        o1_line = line_rows(copies, place, ns, O1)
        q1_line = line_columns(copies, place, ns, Q1)
        d1_whole = whole_rows(copies, place, ns, D1, ns.full_d)
        u1_whole = whole_columns(copies, place, ns, U1, ns.full_u, 2)
        q1_whole = whole_columns(copies, place, ns, Q1, ns.full_q, 6)
        o1_whole = whole_rows(copies, place, ns, O1, ns.full_o)
        next(u1_second)
        next(d1_second)
        ns.load.o1.wait()
        next(o1_first)
        ns.load.qkv_in.wait()
        ns.load.lse.wait()
        ns.load.mixed_grad.wait()
        ns.load.dg.wait()
        plan = Plan(
            [stages(u1_second), stages(u1_line)],
            [],
            [stages(d1_second)],
            [stages(o1_first), stages(o1_second)],
            [],
            [],
            [stages(d1_line), stages(o1_second), stages(o1_line), stages(u1_line)]
            + [stages(u1_whole)],
            [stages(q1_first), stages(q1_second), stages(u1_whole)],
            [stages(q1_second), stages(q1_line), stages(d1_line), stages(d1_whole)],
            [stages(u1_whole), stages(d1_whole)],
            [],
            [stages(q1_line), stages(q1_whole), stages(o1_line), stages(o1_whole)],
            [stages(d1_whole)],
            [],
            [stages(d0_first), stages(q1_whole), stages(o1_whole)],
        )
        ns.load.gains.wait()
        grads = bwd_head(ns, place, 1, plan.tick, stages(q1_first), False)
        for copy in (ns.load.down_out, ns.load.wd, ns.load.slope, ns.load.wu, ns.load.active):
            copy.wait()
        for copy in (ns.load.mlp, ns.load.resid, ns.load.attn_out, ns.load.wo, ns.load.mixed):
            copy.wait()
        ns.mixed_grad = ns.mixed_out
        store_up = functools.partial(copies.store, ns.gu_v, ns.gu)
        bwd_mid(ns, place, 0, grads, plan.tick, stages(d0_first), store_up, (1, 0))
        plan.drain()
        copies.store(ns.go_v, ns.go)
        copies.store(ns.gd_v, ns.gd)
        copies.store(ns.dg_v, ns.dg_out)
        next(q1_whole)
        next(o1_whole)

    flops = 6 * length * width * (mixed_width + 2 * units) + 4 * length * width * part
    kernel, options = kernel_of(backward, inputs, outputs, scratch, 3, 128, 128, 63, flops)
    results = pl.pallas_call(kernel, **options)(*inputs.values())
    return named(outputs, results)


def last_kernel(begun, lower, back):
    wq = matrix(begun.wq)
    width, part = wq.shape
    length, mixed_width = back.mixed_out.shape
    units, rows = back.gu.shape[-1], width // 32
    inputs = dict(
        u0=back.gu, d0=back.gd, o0=back.go, qkv_in=begun.qkv, lse=lower.lse,
        mixed_grad=back.mixed_out, dg=back.dg_out, gains=begun.gains, normed=begun.normed, wq=wq,
        hidden=begun.hidden, grad=back.resid_grad,
    )
    outputs = dict(
        out=struct((2, TOK, width), BF),
        gain_grad=struct((8, TOK), F32),
        full_d=struct(back.full_d.shape, BF),
        full_u=struct(back.full_u.shape, BF),
        full_q=struct(back.full_q.shape, BF),
        full_o=struct(back.full_o.shape, BF),
    )
    kept = dict(
        out=outputs["out"],
        gq=by_device(wq.shape, 4),
        qkv_grad=struct(begun.qkv.shape, BF),
        dk=struct((length, mixed_width), F32),
        dv=struct((length, mixed_width), F32),
        dg_line=struct((8, 8, TOK), F32),
        dg_pass=struct((5, 8, TOK), F32),
    )
    loaded = dict(inputs)
    del loaded["d0"]
    scratch = held(loaded, kept)
    scratch |= scatter_scratch(QKV, width)
    for name, count, high, wide, steps in (
        (D0, 1, units // 8, width, 2),
        (U0, 4, rows, units, 3),
        (Q0, 4, rows, part, 3),
        (O0, 1, mixed_width // 8, width, 3),
    ):
        scratch |= reduce_scratch(name, count, high, wide, steps)
        scratch |= finish_scratch(name, count, high, wide)

    def last(ns):
        place, copies = Place(), ns.copies
        line = [place.line(offset)[0] for offset in range(1, 8)]
        meet([*line, place.along_x, place.along_y])
        unused, d0_second = reduce_rep(copies, place, ns.d0, ns, D0)
        u0_first, u0_second = reduce_rep(copies, place, ns.u0_v, ns, U0)
        o0_first, o0_second = reduce_rep(copies, place, ns.o0_v, ns, O0)
        q0_first, q0_second = reduce_rep(copies, place, ns.gq_v, ns, Q0)
        d0_line = line_rows(copies, place, ns, D0)
        o0_line = line_rows(copies, place, ns, O0)
        u0_line = line_columns(copies, place, ns, U0)
        q0_line = line_columns(copies, place, ns, Q0)
        d0_whole = whole_rows(copies, place, ns, D0, ns.full_d)
        o0_whole = whole_rows(copies, place, ns, O0, ns.full_o)
        u0_whole = whole_columns(copies, place, ns, U0, ns.full_u, 2)
        q0_whole = whole_columns(copies, place, ns, Q0, ns.full_q, 6)
        next(d0_second)
        ns.load.u0.wait()
        next(u0_first)
        ns.load.qkv_in.wait()
        ns.load.lse.wait()
        ns.load.mixed_grad.wait()
        ns.load.dg.wait()
        ns.load.o0.wait()
        plan = Plan(
            [stages(d0_second), stages(d0_line)],
            [],
            [],
            [],
            [],
            [stages(d0_line), stages(d0_whole), stages(u0_first), stages(u0_second)],
        )
        ns.load.gains.wait()
        grads = bwd_head(ns, place, 0, plan.tick, stages(q0_first), True)
        upper = place.upper
        ns.out_v[1] = grads[1]().astype(BF)
        for task in (q0_first, q0_second, o0_first):
            next(task)
        ns.out_v[0] = grads[0]().astype(BF)
        copies.store(ns.out_v.at[upper], ns.out.at[upper])
        gain_grad = gain_sum(ns, copies, place)
        next(gain_grad)
        moved = copies.remote(ns.out_v.at[1 - upper], ns.out.at[upper], place.far)
        for task in (
            d0_whole, u0_second, u0_line, q0_second, q0_line, o0_first, o0_second, gain_grad,
            u0_line, u0_whole, o0_second, o0_line, d0_whole, u0_whole, q0_line, q0_whole,
            o0_line, o0_whole, gain_grad, q0_whole, o0_whole, gain_grad, u0_whole, q0_whole,
            o0_whole,
        ):
            next(task)
        moved.wait_recv()

    flops = 4 * length * width * part
    kernel, options = kernel_of(last, inputs, outputs, scratch, 4, 128, 128, 60, flops)
    results = pl.pallas_call(kernel, **options)(*inputs.values())
    return named(outputs, results)


def gain_sum(ns, copies, place):
    def columns(grp):
        return pl.ds(pl.multiple_of(grp * TOK, TOK), TOK)

    moved = []
    for offset in range(1, 8):
        device, upper, t = place.line(offset)
        source = ns.dg_v.at[:, columns(upper * 4 + t)]
        moved.append(copies.remote(source, ns.dg_line_v.at[place.grp], device))
    ns.dg_line_v[place.grp] = ns.dg_v[:, columns(place.grp)]
    yield
    for copy in moved:
        copy.wait_recv()
    ns.dg_pass_v[0] = jnp.sum(ns.dg_line_v[...], axis=0)
    moved = copies.remote(ns.dg_pass_v.at[0], ns.dg_pass_v.at[1], place.along_x)
    yield
    moved.wait_recv()
    ns.dg_pass_v[2] = ns.dg_pass_v[0] + ns.dg_pass_v[1]
    moved = copies.remote(ns.dg_pass_v.at[2], ns.dg_pass_v.at[3], place.along_y)
    yield
    moved.wait_recv()
    ns.dg_pass_v[4] = ns.dg_pass_v[2] + ns.dg_pass_v[3]
    copies.store(ns.dg_pass_v.at[4], ns.gain_grad)
    yield


def body_pairs(block_in, cotangent, w_qkv, w_out, w_up, w_down, norm_gains):
    layers, rows, width = w_out.shape
    hidden_unit = w_down.shape[1]
    gain_part = jnp.transpose(norm_gains.astype(F32), (0, 2, 1)).reshape(layers * 4, rows)
    down_parts = w_down.reshape(layers, 2, 2, 2, hidden_unit // 8, width)
    out_parts = w_out.reshape(layers, 2, 2, 2, rows // 8, width)

    begun = start_kernel(block_in[:, 0], gain_part, w_qkv, w_up, out_parts)
    lower = forward_kernel(begun, w_qkv, w_up, down_parts, out_parts)
    turned = turn_kernel(lower, begun.gains, down_parts, out_parts, cotangent[:, 0])
    back = backward_kernel(begun, lower, turned)
    last = last_kernel(begun, lower, back)

    def whole(zero, one, like):
        return jnp.stack([zero, one]).reshape(like.shape).astype(F32)

    return (
        turned.out[:, None],
        last.out.astype(F32)[:, None],
        whole(last.full_q, back.full_q, w_qkv),
        whole(last.full_o, back.full_o, w_out),
        whole(last.full_u, back.full_u, w_up),
        whole(last.full_d, back.full_d, w_down),
        jnp.transpose(last.gain_grad.reshape(layers, 4, rows), (0, 2, 1)),
    )


def norm_apply(values, gains):
    return values * lax.rsqrt(jnp.mean(values * values, axis=-1, keepdims=True) + EPS) * gains


def inner_rows(left, right):
    return lax.dot_general(
        left, right, (((0,), (0,)), ((), ())), preferred_element_type=jnp.float32
    )


def times_trans(left, right):
    return lax.dot_general(
        left, right, (((1,), (1,)), ((), ())), preferred_element_type=jnp.float32
    )


def split_blocks(whole):
    length = whole.shape[0]
    width = min(512, length)
    count = length // width
    return (whole.reshape(count, width, HEADS, HDIM), width, count)


def block_at(blocks, index):
    return lax.dynamic_index_in_dim(blocks, index, 0, keepdims=False)


def key_scores(query, key_block, key_start, query_pos):
    scale = HDIM ** (-0.5)
    scores = (
        jnp.einsum("qhd,khd->hqk", query, key_block, preferred_element_type=jnp.float32) * scale
    )
    key_pos = key_start + jnp.arange(key_block.shape[0], dtype=jnp.int32)
    allowed = key_pos[None, :] <= query_pos[:, None]
    return (scores, allowed[None])


def attend_split(query, keys_all, values_all, query_pos):
    key_blocks, width, count = split_blocks(keys_all)
    value_blocks = split_blocks(values_all)[0]
    row_count = query.shape[0]
    upper = query_pos[row_count - 1] // width + 1

    def total_step(index, carry):
        running, total = carry
        scores, allowed = key_scores(query, block_at(key_blocks, index), index * width, query_pos)
        newest = jnp.maximum(running, jnp.max(jnp.where(allowed, scores, NEGATIVE), axis=-1))
        terms = jnp.where(allowed, jnp.exp(scores - newest[..., None]), 0.0)
        total = total * jnp.exp(running - newest) + jnp.sum(terms, axis=-1)
        return (newest, total)

    start_run = jnp.full((HEADS, row_count), NEGATIVE, jnp.float32)
    start_total = jnp.zeros((HEADS, row_count), jnp.float32)
    running, total = lax.fori_loop(0, upper, total_step, (start_run, start_total))
    log_total = running + jnp.log(total)

    def mix_step(index, accum):
        scores, allowed = key_scores(query, block_at(key_blocks, index), index * width, query_pos)
        probs = jnp.where(allowed, jnp.exp(scores - log_total[..., None]), 0.0)
        return accum + jnp.einsum(
            "hqk,khd->qhd",
            probs.astype(jnp.bfloat16),
            block_at(value_blocks, index),
            preferred_element_type=jnp.float32,
        )

    start_mix = jnp.zeros((row_count, HEADS, HDIM), jnp.float32)
    mixed = lax.fori_loop(0, upper, mix_step, start_mix)
    return (mixed.reshape(row_count, HEADS * HDIM), log_total)


def attend_back_split(query, keys_all, values_all, log_total, out_grad, delta, query_pos):
    key_blocks, width, count = split_blocks(keys_all)
    value_blocks = split_blocks(values_all)[0]
    row_count = query.shape[0]
    upper = query_pos[row_count - 1] // width + 1
    scale = HDIM ** (-0.5)

    def back_step(index, carry):
        query_acc, pieces = carry
        key_block = block_at(key_blocks, index)
        value_block = block_at(value_blocks, index)
        scores, allowed = key_scores(query, key_block, index * width, query_pos)
        probs = jnp.where(allowed, jnp.exp(scores - log_total[..., None]), 0.0)
        prob_grad = jnp.einsum(
            "qhd,khd->hqk", out_grad, value_block, preferred_element_type=jnp.float32
        )
        score_grad = (probs * (prob_grad - delta[..., None])).astype(jnp.bfloat16)
        query_acc = (
            query_acc
            + jnp.einsum("hqk,khd->qhd", score_grad, key_block, preferred_element_type=jnp.float32)
            * scale
        )
        key_grad = (
            jnp.einsum("hqk,qhd->khd", score_grad, query, preferred_element_type=jnp.float32)
            * scale
        )
        value_grad = jnp.einsum(
            "hqk,qhd->khd", probs.astype(jnp.bfloat16), out_grad, preferred_element_type=jnp.float32
        )
        joined = jnp.concatenate(
            [key_grad.reshape(width, HEADS * HDIM), value_grad.reshape(width, HEADS * HDIM)], axis=1
        )
        pieces = lax.dynamic_update_index_in_dim(pieces, joined, index, 0)
        return (query_acc, pieces)

    start_acc = jnp.zeros((row_count, HEADS, HDIM), jnp.float32)
    start_pieces = jnp.zeros((count, width, 2 * HEADS * HDIM), jnp.float32)
    query_grad, pieces = lax.fori_loop(0, upper, back_step, (start_acc, start_pieces))
    return (query_grad.reshape(row_count, HEADS * HDIM), pieces.reshape(-1, pieces.shape[-1]))


def layer_forward(hidden_in, weights, query_pos):
    w_qkv_full, w_out_full, w_up_full, w_down_full, gain_full = weights
    gains_f = gain_full.astype(jnp.float32)
    row_count = hidden_in.shape[0]
    width = w_out_full.shape[1]
    normed = norm_apply(hidden_in, gains_f[:, 0]).astype(jnp.bfloat16)
    qkv_low = jnp.dot(normed, w_qkv_full, preferred_element_type=jnp.float32).astype(jnp.bfloat16)
    query = qkv_low[:, :width]
    keys_all, values_all = (
        lax.all_gather(qkv_low[:, width : 2 * width], "grp", axis=0, tiled=True),
        lax.all_gather(qkv_low[:, 2 * width :], "grp", axis=0, tiled=True),
    )
    mixed, log_total = attend_split(
        query.reshape(row_count, HEADS, HDIM),
        keys_all.reshape(-1, HEADS, HDIM),
        values_all.reshape(-1, HEADS, HDIM),
        query_pos,
    )
    mixed_low = mixed.astype(jnp.bfloat16)
    attn_out = jnp.dot(mixed_low, w_out_full, preferred_element_type=jnp.float32)
    resid = hidden_in + norm_apply(attn_out, gains_f[:, 1])
    mlp_in = norm_apply(resid, gains_f[:, 2]).astype(jnp.bfloat16)
    up_out = jnp.dot(mlp_in, w_up_full, preferred_element_type=jnp.float32)
    active = jax.nn.gelu(up_out).astype(jnp.bfloat16)
    down_out = jnp.dot(active, w_down_full, preferred_element_type=jnp.float32)
    result = resid + norm_apply(down_out, gains_f[:, 3])
    kept = (
        hidden_in,
        normed,
        qkv_low,
        mixed,
        mixed_low,
        log_total,
        attn_out,
        resid,
        mlp_in,
        up_out,
        active,
        down_out,
    )
    return (result, kept)


def layer_backward(grad_out, weights, kept, query_pos):
    w_qkv_full, w_out_full, w_up_full, w_down_full, gain_full = weights
    (
        hidden_in,
        normed,
        qkv_low,
        mixed,
        mixed_low,
        log_total,
        attn_out,
        resid,
        mlp_in,
        up_out,
        active,
        down_out,
    ) = kept
    gains_f = gain_full.astype(jnp.float32)
    row_count = hidden_in.shape[0]
    width = w_out_full.shape[1]
    unused, puller = jax.vjp(norm_apply, down_out, gains_f[:, 3])
    down_grad, gain_four = puller(grad_out)
    down_low = down_grad.astype(jnp.bfloat16)
    w_down_grad = inner_rows(active, down_low)
    active_grad = times_trans(down_low, w_down_full)
    unused, puller = jax.vjp(jax.nn.gelu, up_out)
    up_low = puller(active_grad)[0].astype(jnp.bfloat16)
    w_up_grad = inner_rows(mlp_in, up_low)
    mlp_grad = times_trans(up_low, w_up_full)
    unused, puller = jax.vjp(norm_apply, resid, gains_f[:, 2])
    resid_part, gain_three = puller(mlp_grad)
    resid_grad = grad_out + resid_part
    unused, puller = jax.vjp(norm_apply, attn_out, gains_f[:, 1])
    attn_grad, gain_two = puller(resid_grad)
    attn_low = attn_grad.astype(jnp.bfloat16)
    w_out_grad = inner_rows(mixed_low, attn_low)
    mixed_grad = times_trans(attn_low, w_out_full).astype(jnp.bfloat16)
    keys_all, values_all = (
        lax.all_gather(qkv_low[:, width : 2 * width], "grp", axis=0, tiled=True),
        lax.all_gather(qkv_low[:, 2 * width :], "grp", axis=0, tiled=True),
    )
    delta = jnp.sum(
        (mixed_grad.astype(jnp.float32) * mixed).reshape(row_count, HEADS, HDIM), axis=-1
    ).T
    query_low = qkv_low[:, :width]
    query_grad, key_value_terms = attend_back_split(
        query_low.reshape(row_count, HEADS, HDIM),
        keys_all.reshape(-1, HEADS, HDIM),
        values_all.reshape(-1, HEADS, HDIM),
        log_total,
        mixed_grad.reshape(row_count, HEADS, HDIM),
        delta,
        query_pos,
    )
    key_value_grad = lax.psum_scatter(
        key_value_terms.astype(jnp.bfloat16), "grp", scatter_dimension=0, tiled=True
    ).astype(jnp.float32)
    qkv_grad = jnp.concatenate([query_grad, key_value_grad], axis=1).astype(jnp.bfloat16)
    w_qkv_grad = inner_rows(normed, qkv_grad)
    normed_grad = times_trans(qkv_grad, w_qkv_full)
    unused, puller = jax.vjp(norm_apply, hidden_in, gains_f[:, 0])
    input_part, gain_one = puller(normed_grad)
    gain_grad = jnp.stack([gain_one, gain_two, gain_three, gain_four], axis=1)
    return (resid_grad + input_part, (w_qkv_grad, w_out_grad, w_up_grad, w_down_grad, gain_grad))


def body_general(block_in, cotangent, w_qkv, w_out, w_up, w_down, norm_gains):
    layer_count = w_qkv.shape[0]
    micro_count = block_in.shape[0]
    row_count = block_in.shape[2]
    query_pos = lax.axis_index("grp") * row_count + jnp.arange(row_count, dtype=jnp.int32)
    totals = [None] * layer_count
    outputs = []
    input_grads = []
    for micro_idx in range(micro_count):
        hidden = block_in[micro_idx, 0].astype(jnp.float32)
        saved = []
        for layer_idx in range(layer_count):
            hidden, kept = layer_forward(
                hidden,
                (
                    lax.all_gather(w_qkv[layer_idx], "grp", axis=0, tiled=True),
                    lax.all_gather(w_out[layer_idx], "grp", axis=0, tiled=True),
                    lax.all_gather(w_up[layer_idx], "grp", axis=0, tiled=True),
                    lax.all_gather(w_down[layer_idx], "grp", axis=0, tiled=True),
                    lax.all_gather(norm_gains[layer_idx], "grp", axis=0, tiled=True),
                ),
                query_pos,
            )
            saved.append(kept)
        outputs.append(hidden.astype(jnp.bfloat16))
        grad_flow = cotangent[micro_idx, 0].astype(jnp.float32)
        for layer_idx in reversed(range(layer_count)):
            grad_flow, parts = layer_backward(
                grad_flow,
                (
                    lax.all_gather(w_qkv[layer_idx], "grp", axis=0, tiled=True),
                    lax.all_gather(w_out[layer_idx], "grp", axis=0, tiled=True),
                    lax.all_gather(w_up[layer_idx], "grp", axis=0, tiled=True),
                    lax.all_gather(w_down[layer_idx], "grp", axis=0, tiled=True),
                    lax.all_gather(norm_gains[layer_idx], "grp", axis=0, tiled=True),
                ),
                saved[layer_idx],
                query_pos,
            )
            if totals[layer_idx] is None:
                totals[layer_idx] = parts
            else:
                totals[layer_idx] = tuple(
                    (left + right for left, right in zip(totals[layer_idx], parts))
                )
        input_grads.append(grad_flow)
    reduced = []
    for layer_idx in range(layer_count):
        accum = totals[layer_idx]
        shards = (
            lax.psum_scatter(
                accum[0].astype(jnp.bfloat16), "grp", scatter_dimension=0, tiled=True
            ).astype(jnp.float32),
            lax.psum_scatter(
                accum[1].astype(jnp.bfloat16), "grp", scatter_dimension=0, tiled=True
            ).astype(jnp.float32),
            lax.psum_scatter(
                accum[2].astype(jnp.bfloat16), "grp", scatter_dimension=0, tiled=True
            ).astype(jnp.float32),
            lax.psum_scatter(
                accum[3].astype(jnp.bfloat16), "grp", scatter_dimension=0, tiled=True
            ).astype(jnp.float32),
            lax.psum_scatter(
                accum[4].astype(jnp.bfloat16), "grp", scatter_dimension=0, tiled=True
            ).astype(jnp.float32),
        )
        reduced.append(
            (
                lax.psum(shards[0].astype(jnp.bfloat16), "rep").astype(jnp.float32),
                lax.psum(shards[1].astype(jnp.bfloat16), "rep").astype(jnp.float32),
                lax.psum(shards[2].astype(jnp.bfloat16), "rep").astype(jnp.float32),
                lax.psum(shards[3].astype(jnp.bfloat16), "rep").astype(jnp.float32),
                lax.psum(shards[4].astype(jnp.bfloat16), "rep").astype(jnp.float32),
            )
        )
    block_out = jnp.stack(outputs)[:, None]
    block_in_grad = jnp.stack(input_grads)[:, None]
    stacked = [
        jnp.stack([reduced[layer_idx][member] for layer_idx in range(layer_count)])
        for member in range(5)
    ]
    return (block_out, block_in_grad, stacked[0], stacked[1], stacked[2], stacked[3], stacked[4])


def solution(mesh):
    rep_size, grp_size = mesh.shape["rep"], mesh.shape["grp"]

    def body(block_in, cotangent, w_qkv, w_out, w_up, w_down, norm_gains):
        sizes = (rep_size, grp_size, block_in.shape[0], w_qkv.shape[0], block_in.shape[2])
        fits = sizes == (4, 8, 2, 2, TOK)
        chosen = body_pairs if fits else body_general
        return chosen(block_in, cotangent, w_qkv, w_out, w_up, w_down, norm_gains)

    tokens = P(None, "rep", "grp", None)
    rows = P(None, "grp", None)
    return jax.shard_map(
        body,
        mesh=mesh,
        in_specs=(tokens, tokens, rows, rows, rows, rows, rows),
        out_specs=(tokens, tokens, rows, rows, rows, rows, rows),
        check_vma=False,
    )
```

```python
import functools
import types

import jax
import jax.numpy as jnp
from jax import lax
from jax.experimental import pallas as pl
from jax.experimental.pallas import tpu as pltpu
from jax.sharding import PartitionSpec as P

HEADS = 16
HDIM = 64
EPS = 1e-06
NEGATIVE = -1e30
BF = jnp.bfloat16
REP, GRP = "rep", "grp"
F32 = jnp.float32


def dot(left, right):
    return jnp.dot(left, right, preferred_element_type=F32)


def dot_tn(left, right):
    return lax.dot_general(left, right, (((0,), (0,)), ((), ())), preferred_element_type=F32)


def dot_nt(left, right):
    return lax.dot_general(left, right, (((1,), (1,)), ((), ())), preferred_element_type=F32)


def norm(values, gain):
    return values * lax.rsqrt(jnp.mean(values * values, axis=-1, keepdims=True) + EPS) * gain


def head_mask(width, head):
    lanes = lax.broadcasted_iota(jnp.int32, (1, width), 1)
    return (lanes // HDIM) == head


def causal_scores(query, keys, below, start):
    scores = dot_nt(query, keys)
    last = jnp.where(below, scores[:, start:], NEGATIVE)
    return jnp.concatenate([scores[:, :start], last], axis=1) if start else last


def each_head(heads, one_head, tick):
    half = heads // 2 if tick else heads
    for first in range(0, heads, half):
        loop(half, lambda index: one_head(index + first))
        if tick and first == 0:
            tick()


def attend(ns, stream, block=256):
    length, width = ns.mixed_v.shape
    qkv_ref, lse_ref, sum_ref = ns.qkv_in_v, ns.lse_v, ns.terms_own.at[stream]
    row = lax.broadcasted_iota(jnp.int32, (block, block), 0)
    col = lax.broadcasted_iota(jnp.int32, (block, block), 1)
    below = col <= row
    zero = jnp.zeros((), BF)
    lane = lax.broadcasted_iota(jnp.int32, (1, 128), 1)
    base, high = stream * length // 2, (stream + 1) * length // 2
    sum_ref[...] = jnp.zeros_like(sum_ref)
    lse_ref[base:high, :] = jnp.zeros((length // 2, 128), F32)

    def one_head(head):
        mask = head_mask(width, head)
        for start in range(base, high, block):
            stop = start + block
            query = qkv_ref[start:stop, :width] * jnp.asarray(HDIM**-0.5, BF)
            query = jnp.where(mask, query, zero)
            scores = causal_scores(query, qkv_ref[:stop, width : 2 * width], below, start)
            top = jnp.max(scores, axis=1, keepdims=True)
            terms = jnp.exp(scores - top)
            sums = jnp.sum(terms, axis=1, keepdims=True)
            mixed = dot(terms.astype(BF), qkv_ref[:stop, 2 * width :]) * (1.0 / sums)
            sum_ref[:, start - base : stop - base] += jnp.where(mask, mixed, 0.0)
            stats = lse_ref[start:stop, :]
            lse_ref[start:stop, :] = jnp.where(lane == head, top + jnp.log(sums), stats)

    each_head(width // HDIM, one_head, None)
    for start in range(base, high, block):
        ns.mixed_v[start : start + block, :] = sum_ref[:, start - base : start - base + width].astype(BF)


def attend_back(ns, stream, tick, block=256):
    length, width = ns.mixed_grad_v.shape
    qkv_ref, grad_ref, sum_ref = ns.qkv_in_v, ns.mixed_grad_v, ns.terms_own.at[stream]
    row = lax.broadcasted_iota(jnp.int32, (block, block), 0)
    col = lax.broadcasted_iota(jnp.int32, (block, block), 1)
    below = col <= row
    zero = jnp.zeros((), BF)
    scale = HDIM**-0.5
    lane = lax.broadcasted_iota(jnp.int32, (1, 128), 1)
    base, high = stream * length // 2, (stream + 1) * length // 2
    sum_ref[...] = jnp.zeros_like(sum_ref)

    def one_head(head):
        mask = head_mask(width, head)
        for start in range(base, high, block):
            stop = start + block
            query = qkv_ref[start:stop, :width] * jnp.asarray(scale, BF)
            query = jnp.where(mask, query, zero)
            grad = jnp.where(mask, grad_ref[start:stop, :], zero)
            keys, vals = qkv_ref[:stop, width : 2 * width], qkv_ref[:stop, 2 * width :]
            scores = causal_scores(query, keys, below, start)
            lse = jnp.where(lane == head, ns.lse_v[start:stop, :], 0.0)
            probs = jnp.exp(scores - jnp.sum(lse, axis=1, keepdims=True))
            prob_grad = dot_nt(grad, vals)
            delta = jnp.sum(probs * prob_grad, axis=1, keepdims=True)
            score_grad = (probs * (prob_grad - delta)).astype(BF)
            query_grad = jnp.where(mask, dot(score_grad, keys), 0.0)
            sum_ref[:, start - base : stop - base] += query_grad
            ns.dk_v[:stop, :] += dot_tn(score_grad, query)
            ns.dv_v[:stop, :] += dot_tn(probs.astype(BF), grad)

    each_head(width // HDIM, one_head, tick)
    for start in range(base, high, block):
        value = sum_ref[:, start - base : start - base + width] * scale
        ns.qkv_grad_v[start : start + block, :width] = value.astype(BF)
    ns.qkv_grad_v[base:high, width : 2 * width] = ns.dk_v[base:high, :].astype(BF)
    ns.qkv_grad_v[base:high, 2 * width :] = ns.dv_v[base:high, :].astype(BF)


MESH_ID = pl.DeviceIdType.MESH
HELD, ONE, TWO, SUM, LINE, FULL = "_v", "one", "two", "sum", "line", "full"
PASSED = ("give", "take", "send", "got")
ATTN, DOWN, UP, QKV = "attn", "down", "up", "qkv"
D0, U0, Q0, O0 = "d0", "u0", "q0", "o0"
D1, U1, Q1, O1 = "d1", "u1", "q1", "o1"
TOK = 128


class Place:
    def __init__(self):
        rep, grp = lax.axis_index(REP), lax.axis_index(GRP)
        self.rep, self.grp = rep, grp
        self.x, self.y = lax.rem(rep, 2), lax.div(rep, 2)
        self.t, self.upper = lax.rem(grp, 4), lax.div(grp, 4)
        self.c, self.side = lax.rem(grp, 2), lax.div(self.t, 2)
        base = self.upper * 4
        self.core = (rep, base + self.side * 2 + 1 - self.c)
        self.near = (rep, base + (1 - self.side) * 2 + self.c)
        self.far = (rep, (1 - self.upper) * 4 + self.t)
        self.along_x = (self.y * 2 + 1 - self.x, grp)
        self.along_y = ((1 - self.y) * 2 + self.x, grp)
        self.near_t = (1 - self.side) * 2 + self.c

    def line(self, offset):
        c = 1 - self.c if offset & 1 else self.c
        side = 1 - self.side if offset & 2 else self.side
        upper = 1 - self.upper if offset & 4 else self.upper
        return (self.rep, upper * 4 + side * 2 + c), upper, side * 2 + c


class Copies:
    def __init__(self, send, recv, here):
        self.sems, self.here = (send, recv), here
        self.sent, self.local_count, self.stores, self.done = [], 0, [], set()

    def remote(self, source, target, device):
        at = len(self.sent)
        assert at < self.sems[0].shape[0]
        copy = pltpu.make_async_remote_copy(
            src_ref=source,
            dst_ref=target,
            send_sem=self.sems[0].at[at],
            recv_sem=self.sems[1].at[at],
            device_id=device,
            device_id_type=MESH_ID,
        )
        copy.start()
        self.sent.append(copy)
        return copy

    def local(self, source, target):
        assert self.local_count < self.here.shape[0]
        copy = pltpu.make_async_copy(source, target, self.here.at[self.local_count])
        self.local_count += 1
        copy.start()
        return copy

    def store(self, source, target):
        self.stores.append(self.local(source, target))

    def both(self, *copies):
        for copy in copies:
            copy.wait_recv()
            copy.wait_send()
            self.done.add(id(copy))

    def finish(self):
        for copy in self.sent:
            if id(copy) not in self.done:
                copy.wait_send()
        for copy in self.stores:
            copy.wait()


def meet(devices):
    barrier = pltpu.get_barrier_semaphore()
    for device in devices:
        pl.semaphore_signal(barrier, inc=1, device_id=device, device_id_type=MESH_ID)
    pl.semaphore_wait(barrier, len(devices))


class Plan:
    def __init__(self, *entries):
        self.entries = list(entries)

    def tick(self):
        if self.entries:
            for action in self.entries.pop(0):
                action()

    def drain(self):
        while self.entries:
            self.tick()


def stages(task):
    return lambda: next(task, None)


def spread(copies, place, part, last=True):
    x, y, every = place.x, place.y, slice(None)
    one = copies.remote(part(0, y, x), part(0, y, x), place.along_x)
    two = copies.remote(part(1, y, x), part(1, y, x), place.along_y)
    yield
    one.wait_recv()
    three = copies.remote(part(0, y, every), part(0, y, every), place.along_y)
    two.wait_recv()
    four = copies.remote(part(1, every, x), part(1, every, x), place.along_x)
    yield
    three.wait_recv()
    four.wait_recv()
    if last:
        yield


def deal(copies, place, source, target):
    moved = []
    own = copies.local(source.at[place.t], target)
    for offset in range(1, 8):
        if offset == 4:
            yield
        device, upper, t = place.line(offset)
        moved.append(copies.remote(source.at[t], target, device))
    yield
    own.wait()
    for copy in moved:
        copy.wait_recv()
    yield


def add_low(one, two):
    return (one.astype(F32) + two.astype(F32)).astype(BF)


def reduce_rep(copies, place, grad, ns, name):
    x, y = place.x, place.y
    count = grad.shape[1]

    def step_one():
        one = getattr(ns, name + ONE)
        first = copies.remote(grad.at[0, :, :, 1 - x], one.at[0], place.along_x)
        second = copies.remote(grad.at[1, :, 1 - y], one.at[1], place.along_y)
        yield
        copies.both(first, second)
        for i in range(count):
            for j in range(2):
                grad[0, i, j, x] = add_low(grad[0, i, j, x], one[0, i, j])
                grad[1, i, y, j] = add_low(grad[1, i, y, j], one[1, i, j])
        yield

    def step_two():
        two, total = getattr(ns, name + TWO), getattr(ns, name + SUM)
        first = copies.remote(grad.at[0, :, 1 - y, x], two.at[0], place.along_y)
        second = copies.remote(grad.at[1, :, y, 1 - x], two.at[1], place.along_x)
        own = [copies.local(grad.at[half, :, y, x], total.at[half]) for half in range(2)]
        yield
        copies.both(first, second)
        for half in range(2):
            own[half].wait()
            for i in range(count):
                total[half, i] = add_low(total[half, i], two[half, i])
        yield

    return step_one(), step_two()


def line_columns(copies, place, ns, name):
    total, line, full = (getattr(ns, name + part) for part in (SUM, LINE, FULL))
    moved = []
    for offset in range(1, 8):
        device, upper, t = place.line(offset)
        here = line.at[place.upper, place.t]
        moved.append(copies.remote(total.at[upper, t], here, device))
    line[place.upper, place.t] = total[place.upper, place.t]
    yield
    for copy in moved:
        copy.wait_recv()
    for t in range(4):
        full[place.y, place.x, t] = add_low(line[0, t], line[1, t])
    yield


def line_rows(copies, place, ns, name):
    total, line, full = (getattr(ns, name + part) for part in (SUM, LINE, FULL))
    moved = copies.remote(total.at[1 - place.upper, 0], line, place.far)
    yield
    moved.wait_recv()
    rows = line.shape[0] // 2
    for half in range(2):
        at = pl.ds(half * rows, rows)
        full[place.y, place.x, half] = add_low(total[place.upper, 0, at, :], line[at, :])
    yield


def whole_columns(copies, place, ns, name, target, groups):
    full = getattr(ns, name + FULL)
    yield from spread(copies, place, lambda half, a, b: full.at[a, b, pl.ds(2 * half, 2)], False)
    unit = full.shape[4] // groups
    for t in range(4):
        for k in range(groups):
            source = full.at[:, :, t, :, k * unit : (k + 1) * unit]
            start = (k * 4 + t) * unit
            copies.store(source, target.at[:, :, :, start : start + unit])
    yield


def whole_rows(copies, place, ns, name, target):
    full = getattr(ns, name + FULL)
    yield from spread(copies, place, lambda half, a, b: full.at[a, b, half], False)
    copies.store(full, target)
    yield


def reduce_scratch(name, count, rows, width, steps=3):
    total = {}
    if steps & 1:
        total[name + ONE] = pltpu.VMEM((2, count, 2, rows, width), BF)
    if steps & 2:
        total[name + TWO] = pltpu.VMEM((2, count, rows, width), BF)
        total[name + SUM] = pltpu.VMEM((2, count, rows, width), BF)
    return total


def finish_scratch(name, count, rows, width):
    if count == 1:
        line, full = (rows, width), (2, 2, 2, rows // 2, width)
    else:
        line, full = (2, count, rows, width), (2, 2, count, rows, width)
    return {name + LINE: pltpu.VMEM(line, BF), name + FULL: pltpu.VMEM(full, BF)}


def by_device(shape, count):
    rows, width = shape
    return struct((2, count, 2, 2, rows // (8 * count), width), BF)


def loop(count, step):
    def run(index, carry):
        step(index)
        return carry

    lax.fori_loop(0, count, run, 0)


def tile_of(index, size):
    return pl.ds(pl.multiple_of(index * size, size), size)


def matrix(value):
    return value.reshape(-1, value.shape[-1])


def times(left, right_ref, tile, sink):
    every = (slice(None),) * (len(right_ref.shape) - 1)

    def step(index):
        at = tile_of(index, tile)
        sink(at, dot(left(), matrix(right_ref[(*every, at)])))

    loop(right_ref.shape[-1] // tile, step)


def times_rows(left, right_ref, tile, sink):
    flat = len(right_ref.shape) == 2

    def step(index):
        if flat:
            at = tile_of(index, tile)
            sink(at, dot_nt(left(), right_ref[at, :]))
        else:
            block = matrix(right_ref[index])
            sink(tile_of(index, block.shape[0]), dot_nt(left(), block))

    loop(right_ref.shape[0] // (tile if flat else 1), step)


def gram(left_ref, right_ref, out_ref):
    count, tile = out_ref.shape[1], 256
    total = left_ref.shape[1]
    if total == tile:
        value = dot_tn(left_ref[...], right_ref[...]).astype(BF)
        out_ref[...] = value.reshape(out_ref.shape)
        return

    def step(index):
        value = dot_tn(left_ref[:, tile_of(index, tile)], right_ref[...]).astype(BF)
        half, part = lax.div(index, 2), lax.rem(index, 2)
        if count == 1:
            out_ref[half, 0, part] = value.reshape(out_ref.shape[3:])
        else:
            out_ref[half, pl.ds(part * 2, 2)] = value.reshape(2, *out_ref.shape[2:])

    loop(total // tile, step)


class Gather:
    def __init__(self, copies, place, buf, order=(0, 1)):
        self.copies, self.place, self.buf, self.order = copies, place, buf, order
        self.flight = {}

    def rows(self, stream, where):
        start = (self.order[stream] * 4 + where) * TOK
        return pl.ds(pl.multiple_of(start, TOK), TOK)

    def pair(self, stream, side):
        start = (self.order[stream] * 4 + side * 2) * TOK
        return pl.ds(pl.multiple_of(start, TOK), 2 * TOK)

    def start(self, stream, block):
        at = self.rows(stream, self.place.t)
        self.buf[at, :] = block
        mine = self.buf.at[at, :]
        across = self.copies.remote(mine, mine, self.place.near)
        beside = self.copies.remote(mine, mine, self.place.core)
        self.flight[stream] = [across, beside]

    def wait_chip(self, stream):
        self.flight[stream][1].wait_recv()

    def forward(self, stream):
        self.flight[stream][0].wait_recv()
        got = self.buf.at[self.rows(stream, self.place.near_t), :]
        self.flight[stream].append(self.copies.remote(got, got, self.place.core))

    def wait_rest(self, stream):
        self.flight[stream][2].wait_recv()


class Scatter:
    def __init__(self, copies, place, ns, name):
        self.copies, self.place = copies, place
        self.away, self.own = ns.terms_away, ns.terms_own
        self.give, self.take, self.send, self.got = (
            getattr(ns, name + part) for part in PASSED
        )
        self.flight = {}

    def push(self, stream, product):
        place, copies = self.place, self.copies
        mine = pl.ds(pl.multiple_of(place.c * TOK, TOK), TOK)
        other = pl.ds(pl.multiple_of((1 - place.c) * TOK, TOK), TOK)

        def to_away(at, value):
            self.away[:, at] = value

        def to_own(at, value):
            self.own[stream, :, at] = value

        product(1 - place.side, to_away)
        self.give[stream, 0] = self.away[other, :].astype(BF)
        first = copies.remote(self.give.at[stream, 0], self.take.at[stream, 0], place.core)
        product(place.side, to_own)
        first.wait_recv()
        self.send[stream] = (self.away[mine, :] + self.take[stream, 0].astype(F32)).astype(BF)
        across = copies.remote(self.send.at[stream], self.got.at[stream], place.near)
        self.give[stream, 1] = self.own[stream, other, :].astype(BF)
        second = copies.remote(self.give.at[stream, 1], self.take.at[stream, 1], place.core)
        self.flight[stream] = (second, across)

    def result(self, stream):
        second, across = self.flight[stream]
        mine = pl.ds(pl.multiple_of(self.place.c * TOK, TOK), TOK)
        second.wait_recv()
        total = self.own[stream, mine, :] + self.take[stream, 1].astype(F32)
        across.wait_recv()
        return total + self.got[stream].astype(F32)


def scatter_scratch(name, width):
    give, take, send, got = (name + part for part in PASSED)
    return {
        "terms_away": pltpu.VMEM((2 * TOK, width), F32),
        "terms_own": pltpu.VMEM((2, 2 * TOK, width), F32),
        give: pltpu.VMEM((2, 2, TOK, width), BF),
        take: pltpu.VMEM((2, 2, TOK, width), BF),
        send: pltpu.VMEM((2, TOK, width), BF),
        got: pltpu.VMEM((2, TOK, width), BF),
    }


def gelu_both(x):
    cubic = x * x * 0.044715
    bent = jnp.tanh(0.7978845608028654 * (x + cubic * x))
    half = 0.5 * (1.0 + bent)
    slope = half + 0.5 * x * (1.0 - bent * bent) * (0.7978845608028654 * (1.0 + 3.0 * cubic))
    return x * half, slope


def norm_back_in(values, gain, grad):
    rstd = lax.rsqrt(jnp.mean(values * values, axis=-1, keepdims=True) + EPS)
    hat = values * rstd
    scaled = grad * gain
    back = rstd * (scaled - hat * jnp.mean(scaled * hat, axis=-1, keepdims=True))
    return back, jnp.sum(grad * hat, axis=0, keepdims=True)


def next_qkv(ns, place, blocks, tick, wait_weights, order=(0, 1), late=None):
    gather = Gather(ns.copies, place, ns.normed_v, order)
    for stream in range(2):
        if late and stream == 1:
            late()
        gather.start(stream, blocks[stream]())
        tick()
    if late:
        for stream in range(2):
            gather.forward(stream)
            tick()
    wait_weights()
    for stream in range(2):

        def project(side):
            at = gather.pair(stream, side)

            def sink(cols, value):
                ns.qkv_v[at, cols] = value.astype(BF)

            times(lambda: ns.normed_v[at, :], ns.wq_v, 384, sink)

        gather.wait_chip(stream)
        project(place.side)
        if not late:
            gather.forward(stream)
        gather.wait_rest(stream)
        project(1 - place.side)
        tick()
        here = pl.ds(pl.multiple_of(order[stream] * 4 * TOK, 4 * TOK), 4 * TOK)
        ns.copies.store(ns.normed_v.at[here, :], ns.normed.at[here, :])
        ns.copies.store(ns.qkv_v.at[here, :], ns.qkv.at[here, :])


def fwd_mid(ns, place, gain, tick, wait_out, wait_up, wait_down):
    copies = ns.copies
    attn = Scatter(copies, place, ns, ATTN)
    down = Scatter(copies, place, ns, DOWN)
    gather = Gather(copies, place, ns.mlp_v)
    wo, wu, wd = ns.wo_v, ns.wu_v, ns.wd_v
    for stream in range(2):

        def product(side, sink):
            at = gather.pair(stream, side)
            times(lambda: ns.mixed_v[at, :], wo, 512, sink)

        attend(ns, stream)
        tick()
        if stream == 0:
            wait_out()
        attn.push(stream, product)
        tick()
    ns.load.hidden.wait()
    for stream in range(2):
        value = attn.result(stream)
        ns.attn_out_v[stream] = value
        resid = ns.hidden_v[stream].astype(F32) + norm(value, gain(1))
        ns.resid_v[stream] = resid
        gather.start(stream, norm(resid, gain(2)).astype(BF))
        tick()
    wait_up()
    for stream in range(2):

        def expand(side):
            at = gather.pair(stream, side)

            def sink(cols, value):
                active, slope = gelu_both(value)
                ns.active_v[at, cols] = active.astype(BF)
                ns.slope_v[at, cols] = slope.astype(BF)

            times(lambda: ns.mlp_v[at, :], wu, 256, sink)

        gather.wait_chip(stream)
        expand(place.side)
        gather.forward(stream)
        gather.wait_rest(stream)
        expand(1 - place.side)
        if stream == 0:
            wait_down()

        def product(side, sink):
            at = gather.pair(stream, side)
            times(lambda: ns.active_v[at, :], wd, 512, sink)

        down.push(stream, product)
        tick()
    return down


def bwd_mid(ns, place, layer, grads, tick, on_down, on_up, order=(0, 1)):
    copies, gain, base = ns.copies, rows_of(ns, layer), layer * 4
    up = Scatter(copies, place, ns, UP)
    first = Gather(copies, place, ns.down_grad_v)
    second = Gather(copies, place, ns.attn_grad_v)
    wo, wu, wd = ns.wo_v, ns.wu_v, ns.wd_v
    for stream in order:
        grad = grads[stream]()
        ns.grad_v[stream] = grad
        back, four = norm_back_in(ns.down_out_v[stream], gain(3), grad)
        ns.dg_v[base + 3 : base + 4, :] += four
        first.start(stream, back.astype(BF))
        tick()
    for stream in order:

        def shrink(side):
            at = first.pair(stream, side)

            def sink(cols, value):
                slope = ns.slope_v[at, cols].astype(F32)
                ns.up_grad_v[at, cols] = (value * slope).astype(BF)

            times_rows(lambda: ns.down_grad_v[at, :], wd, 512, sink)

        first.wait_chip(stream)
        shrink(place.side)
        first.forward(stream)
        first.wait_rest(stream)
        shrink(1 - place.side)

        def product(side, sink):
            at = first.pair(stream, side)
            times_rows(lambda: ns.up_grad_v[at, :], wu, 512, sink)

        up.push(stream, product)
        tick()
    for stream in order:
        back, three = norm_back_in(ns.resid_v[stream], gain(2), up.result(stream))
        grad = ns.grad_v[stream] + back
        ns.grad_v[stream] = grad
        ns.dg_v[base + 2 : base + 3, :] += three
        back, two = norm_back_in(ns.attn_out_v[stream], gain(1), grad)
        ns.dg_v[base + 1 : base + 2, :] += two
        second.start(stream, back.astype(BF))
        tick()
        if stream == order[0]:
            gram(ns.active_v, ns.down_grad_v, ns.gd_v)
            on_down()
        else:
            gram(ns.mlp_v, ns.up_grad_v, ns.gu_v)
            on_up()
            tick()
    copies.store(ns.grad_v, ns.resid_grad)
    for stream in order:

        def project(side):
            at = second.pair(stream, side)
            ns.mixed_grad_v[at, :] = dot_nt(ns.attn_grad_v[at, :], matrix(wo[...])).astype(BF)

        second.wait_chip(stream)
        project(place.side)
        second.forward(stream)
        second.wait_rest(stream)
        project(1 - place.side)
        tick()
        here = pl.ds(stream * 4 * TOK, 4 * TOK)
        copies.store(ns.mixed_grad_v.at[here, :], ns.mixed_grad.at[here, :])
    gram(ns.mixed_v, ns.attn_grad_v, ns.go_v)


def bwd_head(ns, place, layer, tick, on_qkv, weight_first):
    copies, gain = ns.copies, rows_of(ns, layer)
    qkv = Scatter(copies, place, ns, QKV)
    walk = Gather(copies, place, None)

    def weight():
        ns.load.normed.wait()
        gram(ns.normed_v, ns.qkv_grad_v, ns.gq_v)
        on_qkv()
        tick()

    ns.dk_v[...] = jnp.zeros_like(ns.dk_v)
    ns.dv_v[...] = jnp.zeros_like(ns.dv_v)
    for stream in (1, 0):

        def product(side, sink):
            at = walk.pair(stream, side)
            times_rows(lambda: ns.qkv_grad_v[at, :], ns.wq_v, 512, sink)

        attend_back(ns, stream, tick if stream == 1 else None)
        tick()
        if stream == 1:
            ns.load.wq.wait()
        elif weight_first:
            weight()
        qkv.push(stream, product)
        tick()
    if not weight_first:
        weight()
    ns.load.hidden.wait()
    ns.load.grad.wait()

    def result(stream):
        back, one = norm_back_in(ns.hidden_v[stream].astype(F32), gain(0), qkv.result(stream))
        ns.dg_v[layer * 4 : layer * 4 + 1, :] += one
        return ns.grad_v[stream] + back

    return [functools.partial(result, stream) for stream in range(2)]


def kernel_of(body, inputs, outputs, scratch, slot, remotes, locals_, vmem, flops):
    names = [*inputs, *outputs, *scratch]

    def kernel(*refs):
        ns = types.SimpleNamespace(**dict(zip(names, refs)))
        ns.copies = Copies(*refs[len(names) :])
        ns.load = types.SimpleNamespace()
        for name in inputs:
            if name + HELD in scratch:
                copy = ns.copies.local(getattr(ns, name), getattr(ns, name + HELD))
                setattr(ns.load, name, copy)
        body(ns)
        ns.copies.finish()

    moved = sum(v.size * v.dtype.itemsize for v in [*inputs.values(), *outputs.values()])
    return kernel, dict(
        name=body.__name__,
        out_shape=list(outputs.values()),
        in_specs=[pl.BlockSpec(memory_space=pl.ANY)] * len(inputs),
        out_specs=[pl.BlockSpec(memory_space=pl.ANY)] * len(outputs),
        scratch_shapes=[
            *scratch.values(),
            pltpu.SemaphoreType.DMA((remotes,)),
            pltpu.SemaphoreType.DMA((remotes,)),
            pltpu.SemaphoreType.DMA((locals_,)),
        ],
        compiler_params=pltpu.CompilerParams(
            collective_id=slot, has_side_effects=True, vmem_limit_bytes=vmem << 20
        ),
        cost_estimate=pl.CostEstimate(flops=flops, bytes_accessed=moved, transcendentals=0),
    )


def named(outputs, results):
    return types.SimpleNamespace(**dict(zip(outputs, results)))


def held(*groups):
    merged = {name: value for group in groups for name, value in group.items()}
    return {name + HELD: pltpu.VMEM(value.shape, value.dtype) for name, value in merged.items()}


def struct(shape, dtype):
    return jax.ShapeDtypeStruct(shape, dtype)


def rows_of(ns, layer):
    return lambda index, level=layer: ns.gains_v[level * 4 + index : level * 4 + index + 1, :]


def quarter_of(ns, place, weight, layer, target):
    rows = weight.shape[1] // 4
    at = pl.ds(pl.multiple_of(place.rep * rows, rows), rows)
    return ns.copies.local(weight.at[layer, at, :], target)


def arrange(quarter, dealt, groups):
    unit = quarter.shape[1] // (groups * 4)
    for t in range(4):
        for k in range(groups):
            start = (k * 4 + t) * unit
            dealt[t, :, k * unit : (k + 1) * unit] = quarter[:, start : start + unit]


def by_rows(ref, place):
    return lambda half, a, b: ref.at[1 - place.upper, a, b, half]


def by_columns(ref):
    return lambda half, a, b: ref.at[half, :, a, b]


def start_kernel(block, gain_part, w_qkv, w_up, w_out):
    width, part = block.shape[2], w_qkv.shape[2] // 4
    units = w_up.shape[2] // 4
    length, rows = 8 * TOK, width // 32
    inputs = dict(block=block, gain_part=gain_part, w_qkv=w_qkv, w_up=w_up, w_out=w_out)
    gains = struct((gain_part.shape[0], width), F32)
    hidden = struct(block.shape, BF)
    normed = struct((length, width), BF)
    qkv = struct((length, part), BF)
    wq = struct((2, 4, 2, 2, rows, part), BF)
    outputs = dict(
        hidden=hidden,
        gains=gains,
        normed=normed,
        qkv=qkv,
        wq=wq,
        part_u=struct((2, 4, rows, units), BF),
        half_o=struct(w_out.shape[1:], BF),
    )
    kept = dict(
        half_o=struct(w_out.shape[1:], BF),
        hidden=hidden,
        gains=gains,
        normed=normed,
        qkv=qkv,
        wq=wq,
        quarter_q=struct((rows, 4 * part), BF),
        quarter_u=struct((rows, 4 * units), BF),
        deal_q=struct((4, rows, part), BF),
        deal_u=struct((4, rows, units), BF),
    )
    scratch = held(kept)

    def start(ns):
        place, copies = Place(), ns.copies
        upper, y, x = place.upper, place.y, place.x
        columns = pl.ds(pl.multiple_of(place.grp * TOK, TOK), TOK)
        line = [place.line(offset)[0] for offset in range(1, 8)]
        quarter_q = quarter_of(ns, place, ns.w_qkv, 0, ns.quarter_q_v)
        quarter_u = quarter_of(ns, place, ns.w_up, 0, ns.quarter_u_v)
        kept = copies.local(ns.block.at[upper], ns.hidden_v.at[upper])
        gain_own = copies.local(ns.gain_part, ns.gains_v.at[:, columns])
        quarter_q.wait()
        arrange(ns.quarter_q_v, ns.deal_q_v, 6)
        meet([*line, place.along_x, place.along_y])
        gain_rest = [copies.remote(ns.gain_part, ns.gains_v.at[:, columns], at) for at in line]
        wq_dealt = deal(copies, place, ns.deal_q_v, ns.wq_v.at[upper, place.t, y, x])
        next(wq_dealt)
        next(wq_dealt)
        brought = copies.remote(ns.block.at[1 - upper], ns.hidden_v.at[upper], place.far)
        out_in = copies.remote(ns.w_out.at[0, y, x], ns.half_o_v.at[y, x], place.far)
        wq_spread = spread(copies, place, by_columns(ns.wq_v))
        out_spread = spread(copies, place, lambda half, a, b: ns.half_o_v.at[a, b, half])
        up_dealt = deal(copies, place, ns.deal_u_v, ns.part_u.at[upper, place.t])
        quarter_u.wait()
        arrange(ns.quarter_u_v, ns.deal_u_v, 2)
        next(up_dealt)
        kept.wait()
        gain_own.wait()
        for copy in gain_rest:
            copy.wait_recv()

        def late():
            next(wq_spread)
            brought.wait_recv()
            copies.store(ns.hidden_v, ns.hidden)

        def out_arrived():
            out_in.wait_recv()
            next(out_spread)

        def wait_weights():
            next(wq_spread)
            copies.store(ns.wq_v, ns.wq)

        copies.store(ns.gains_v, ns.gains)
        order = (upper, 1 - upper)
        blocks = [
            functools.partial(
                lambda s: norm(ns.hidden_v[s].astype(F32), ns.gains_v[0:1, :]).astype(BF), stream
            )
            for stream in order
        ]
        plan = Plan(
            [stages(wq_dealt), stages(wq_spread)],
            [stages(up_dealt)],
            [out_arrived],
            [stages(out_spread)],
        )
        next_qkv(ns, place, blocks, plan.tick, wait_weights, order, late)
        next(out_spread)
        copies.store(ns.half_o_v, ns.half_o)
        next(up_dealt)

    flops = 2 * length * width * part
    kernel, options = kernel_of(start, inputs, outputs, scratch, 0, 48, 64, 60, flops)
    results = pl.pallas_call(kernel, **options)(*inputs.values())
    return named(outputs, results)


def forward_kernel(begun, w_qkv, w_up, w_down, w_out):
    hidden, gains = begun.hidden, begun.gains
    length, part = begun.qkv.shape
    width, mixed_width = hidden.shape[2], part // 3
    units, rows = w_up.shape[2] // 4, width // 32
    inputs = dict(
        qkv_in=begun.qkv, hidden=hidden, gains=gains, w_qkv=w_qkv, w_up=w_up, w_down=w_down,
        w_out=w_out, part_u=begun.part_u, half_o=begun.half_o,
    )
    blocks = struct((2, TOK, width), F32)
    wide = struct((length, width), BF)
    next_u, next_o = struct((2, 4, rows, units), BF), struct((2, *w_out.shape[1:]), BF)
    outputs = dict(
        mixed=struct((length, mixed_width), BF),
        lse=struct((length, 128), F32),
        attn_out=blocks,
        resid=blocks,
        mlp=wide,
        active=struct((length, units), BF),
        slope=struct((length, units), BF),
        down_out=blocks,
        hidden_out=blocks,
        normed=wide,
        qkv=struct((length, part), BF),
        wu=struct((2, 4, 2, 2, rows, units), BF),
        wd=struct((2, *w_down.shape[1:]), BF),
        wo=next_o,
        wq=struct((2, 4, 2, 2, rows, part), BF),
    )
    kept = dict(
        qkv_in=begun.qkv,
        hidden=hidden,
        gains=gains,
        quarter_q=struct((rows, 4 * part), BF),
        quarter_u=struct((rows, 4 * units), BF),
        deal_q=struct((4, rows, part), BF),
        deal_u=struct((4, rows, units), BF),
    )
    scratch = held(outputs, kept)
    outputs = dict(outputs, next_u=next_u, next_o=next_o)
    scratch |= scatter_scratch(ATTN, width) | scatter_scratch(DOWN, width)

    def forward(ns):
        place, copies = Place(), ns.copies
        upper, t, y, x = place.upper, place.t, place.y, place.x
        half_o = copies.local(ns.half_o, ns.wo_v.at[1 - upper])
        part_u = copies.local(ns.part_u, ns.wu_v.at[:, :, y, x])
        quarter_q = quarter_of(ns, place, ns.w_qkv, 1, ns.quarter_q_v)
        whole_o = copies.local(ns.w_out.at[0], ns.wo_v.at[upper])
        whole_d = copies.local(ns.w_down.at[0], ns.wd_v.at[upper])
        quarter_u = quarter_of(ns, place, ns.w_up, 1, ns.quarter_u_v)
        line = [place.line(offset)[0] for offset in range(1, 8)]
        meet([*line, place.along_x, place.along_y])
        down_in = copies.remote(ns.w_down.at[0, y, x], ns.wd_v.at[upper, y, x], place.far)
        part_u.wait()
        up_spread = spread(copies, place, by_columns(ns.wu_v))
        down_spread = spread(copies, place, by_rows(ns.wd_v, place))
        next(up_spread)
        quarter_q.wait()
        arrange(ns.quarter_q_v, ns.deal_q_v, 6)
        q_deal = deal(copies, place, ns.deal_q_v, ns.wq_v.at[upper, t, y, x])
        next(q_deal)
        next(q_deal)
        q_spread = spread(copies, place, by_columns(ns.wq_v))
        u_deal = deal(copies, place, ns.deal_u_v, ns.next_u.at[upper, t])
        o_spread = spread(copies, place, by_rows(ns.next_o, place))
        rest = []

        def out_part():
            rest.append(copies.remote(ns.w_out.at[1, y, x], ns.next_o.at[upper, y, x], place.far))

        def deal_up():
            quarter_u.wait()
            arrange(ns.quarter_u_v, ns.deal_u_v, 2)
            next(u_deal)
            next(u_deal)

        def down_arrived():
            down_in.wait_recv()
            next(down_spread)

        def out_arrived():
            rest[0].wait_recv()
            next(o_spread)

        plan = Plan(
            [],
            [],
            [stages(up_spread)],
            [deal_up],
            [down_arrived],
            [stages(down_spread), out_part],
            [stages(q_deal), stages(q_spread)],
            [stages(q_spread)],
            [out_arrived],
            [],
            [stages(o_spread)],
            [stages(o_spread)],
        )
        ns.load.qkv_in.wait()
        ns.load.gains.wait()
        gain = rows_of(ns, 0)

        def wait_out():
            half_o.wait()
            whole_o.wait()
            copies.store(ns.wo_v, ns.wo)

        def wait_down():
            next(down_spread)
            whole_d.wait()
            copies.store(ns.wu_v, ns.wu)
            copies.store(ns.wd_v, ns.wd)

        def wait_next():
            next(q_spread)
            copies.store(ns.wq_v, ns.wq)

        down = fwd_mid(ns, place, gain, plan.tick, wait_out, lambda: next(up_spread), wait_down)
        copies.store(ns.mixed_v, ns.mixed)
        copies.store(ns.lse_v, ns.lse)
        copies.store(ns.attn_out_v, ns.attn_out)
        copies.store(ns.resid_v, ns.resid)
        copies.store(ns.mlp_v, ns.mlp)
        copies.store(ns.active_v, ns.active)
        copies.store(ns.slope_v, ns.slope)

        def block(stream):
            value = down.result(stream)
            ns.down_out_v[stream] = value
            hidden_out = ns.resid_v[stream] + norm(value, gain(3))
            ns.hidden_out_v[stream] = hidden_out
            return norm(hidden_out, gain(0, 1)).astype(BF)

        blocks = [functools.partial(block, stream) for stream in range(2)]
        next_qkv(ns, place, blocks, plan.tick, wait_next)
        copies.store(ns.down_out_v, ns.down_out)
        copies.store(ns.hidden_out_v, ns.hidden_out)
        plan.drain()
        next(u_deal)

    flops = 2 * length * width * (mixed_width + 2 * units + part)
    kernel, options = kernel_of(forward, inputs, outputs, scratch, 1, 80, 64, 62, flops)
    results = pl.pallas_call(kernel, **options)(*inputs.values())
    return named(outputs, results)


def turn_kernel(lower, gains, w_down, w_out, cotangent):
    hidden = lower.hidden_out
    width = hidden.shape[2]
    length, part = lower.qkv.shape
    mixed_width = part // 3
    inputs = dict(
        qkv_in=lower.qkv, gains=gains, hidden=hidden, cot=cotangent,
        part_u=lower.next_u, part_o=lower.next_o, w_down=w_down, w_out=w_out,
    )
    rows, units = lower.next_u.shape[2:]
    blocks = struct((2, TOK, width), F32)
    outputs = dict(
        out=struct((2, TOK, width), BF),
        lse=struct((length, 128), F32),
        mixed_grad=struct((length, mixed_width), BF),
        gd=by_device((units, width), 1),
        gu=by_device((width, units), 4),
        go=by_device((mixed_width, width), 1),
        dg=struct((8, width), F32),
    )
    kept = dict(
        qkv_in=lower.qkv,
        hidden=hidden,
        gains=gains,
        cot=cotangent,
        wd=struct((2, *w_down.shape[1:]), BF),
        wo=lower.next_o,
        wu=struct((2, 4, 2, 2, rows, units), BF),
        mixed=struct((length, mixed_width), BF),
        attn_out=blocks,
        resid=blocks,
        grad=blocks,
        mlp=struct((length, width), BF),
        active=struct((length, units), BF),
        slope=struct((length, units), BF),
        up_grad=struct((length, units), BF),
        down_out=blocks,
        down_grad=struct((length, width), BF),
        attn_grad=struct((length, width), BF),
    )
    scratch = held(outputs, kept)
    outputs |= dict(resid_grad=blocks)
    for name in (ATTN, DOWN, UP):
        scratch |= scatter_scratch(name, width)
    scratch |= reduce_scratch(D1, 1, units // 8, width, 1)

    def turn(ns):
        place, copies = Place(), ns.copies
        upper, y, x = place.upper, place.y, place.x
        part_u = copies.local(ns.part_u, ns.wu_v.at[:, :, y, x])
        part_o = copies.local(ns.part_o.at[1 - upper], ns.wo_v.at[1 - upper])
        whole_o = copies.local(ns.w_out.at[1], ns.wo_v.at[upper])
        whole_d = copies.local(ns.w_down.at[1], ns.wd_v.at[upper])
        meet([place.core, place.near, place.far, place.along_x, place.along_y])
        down_in = copies.remote(ns.w_down.at[1, y, x], ns.wd_v.at[upper, y, x], place.far)
        part_u.wait()
        up_spread = spread(copies, place, by_columns(ns.wu_v))
        down_spread = spread(copies, place, by_rows(ns.wd_v, place))
        next(up_spread)
        ns.load.qkv_in.wait()
        far_in = []

        def bring():
            ns.load.cot.wait()
            far_in.append(copies.remote(ns.cot.at[1 - upper], ns.cot_far_v, place.far))

        def down_arrived():
            down_in.wait_recv()
            next(down_spread)

        plan = Plan(
            [],
            [],
            [stages(up_spread)],
            [],
            [down_arrived],
            [stages(down_spread), bring],
        )
        ns.load.gains.wait()
        ns.dg_v[...] = jnp.zeros_like(ns.dg_v)
        gain = rows_of(ns, 1)

        def wait_out():
            part_o.wait()
            whole_o.wait()

        def wait_down():
            next(down_spread)
            whole_d.wait()

        down = fwd_mid(
            ns, place, gain, plan.tick, wait_out, lambda: next(up_spread), wait_down
        )
        copies.store(ns.lse_v, ns.lse)
        far_in[0].wait_recv()

        def grad(stream):
            value = down.result(stream)
            ns.down_out_v[stream] = value
            own = jnp.where(upper == stream, ns.cot_v[stream], ns.cot_far_v[...])
            return own.astype(F32)

        def finish():
            for stream in range(2):
                out = ns.resid_v[stream] + norm(ns.down_out_v[stream], gain(3))
                ns.out_v[stream] = out.astype(BF)
            copies.store(ns.out_v, ns.out)

        d_first, unused = reduce_rep(copies, place, ns.gd_v, ns, D1)
        plan = Plan(
            [],
            [finish],
            [],
            [],
            [],
        )
        grads = [functools.partial(grad, stream) for stream in range(2)]
        store_up = functools.partial(copies.store, ns.gu_v, ns.gu)
        bwd_mid(ns, place, 1, grads, plan.tick, stages(d_first), store_up)
        copies.store(ns.go_v, ns.go)
        copies.store(ns.dg_v, ns.dg)
        next(d_first)
        copies.store(ns.gd_v, ns.gd)

    scratch["cot_far_v"] = pltpu.VMEM((TOK, width), BF)
    flops = 6 * length * width * (mixed_width + 2 * units)
    kernel, options = kernel_of(turn, inputs, outputs, scratch, 2, 64, 64, 63, flops)
    results = pl.pallas_call(kernel, **options)(*inputs.values())
    return named(outputs, results)


def backward_kernel(begun, lower, turned):
    wo, wu, wd, wq = (matrix(value) for value in (lower.wo, lower.wu, lower.wd, lower.wq))
    width, units = wu.shape
    length, part = lower.qkv.shape
    mixed_width = wo.shape[0]
    inputs = dict(
        gu=turned.gu, d1=turned.gd, o1=turned.go, qkv_in=lower.qkv, lse=turned.lse,
        mixed_grad=turned.mixed_grad, dg=turned.dg, gains=begun.gains, wq=wq, normed=lower.normed,
        hidden=lower.hidden_out, grad=turned.resid_grad, down_out=lower.down_out, wd=wd,
        slope=lower.slope, wu=wu, active=lower.active, mlp=lower.mlp, resid=lower.resid,
        attn_out=lower.attn_out, wo=wo, mixed=lower.mixed,
    )
    blocks = struct((2, TOK, width), F32)
    kept = dict(
        gq=by_device(wq.shape, 4),
        gd=by_device(wd.shape, 1),
        gu=by_device(wu.shape, 4),
        go=by_device(wo.shape, 1),
        qkv_grad=struct(lower.qkv.shape, BF),
        dk=struct((length, mixed_width), F32),
        dv=struct((length, mixed_width), F32),
        down_grad=struct((length, width), BF),
        attn_grad=struct((length, width), BF),
    )
    outputs = dict(
        resid_grad=blocks,
        mixed_out=struct((length, mixed_width), BF),
        gd=kept["gd"],
        up_out=kept["gu"],
        go=kept["go"],
        dg_out=turned.dg,
        full_d=struct((2, 2, 2, units // 16, width), BF),
        full_u=struct((2, 2, width // 32, 4 * units), BF),
        full_q=struct((2, 2, width // 32, 4 * part), BF),
        full_o=struct((2, 2, 2, mixed_width // 16, width), BF),
    )
    loaded = dict(inputs)
    del loaded["d1"]
    scratch = held(loaded, kept)
    for name in (QKV, UP):
        scratch |= scatter_scratch(name, width)
    rows = width // 32
    for name, count, high, wide, steps in (
        (D1, 1, units // 8, width, 2),
        (U1, 4, rows, units, 3),
        (Q1, 4, rows, part, 3),
        (O1, 1, mixed_width // 8, width, 3),
    ):
        scratch |= finish_scratch(name, count, high, wide)
        scratch |= reduce_scratch(name, count, high, wide, steps)
    scratch |= reduce_scratch(D0, 1, units // 8, width, 1)

    def backward(ns):
        place, copies = Place(), ns.copies
        ns.up_grad_v = ns.normed_v
        line = [place.line(offset)[0] for offset in range(1, 8)]
        meet([*line, place.along_x, place.along_y])
        unused, d1_second = reduce_rep(copies, place, ns.d1, ns, D1)
        u1_first, u1_second = reduce_rep(copies, place, ns.gu_v, ns, U1)
        o1_first, o1_second = reduce_rep(copies, place, ns.o1_v, ns, O1)
        q1_first, q1_second = reduce_rep(copies, place, ns.gq_v, ns, Q1)
        d0_first, unused = reduce_rep(copies, place, ns.gd_v, ns, D0)
        d1_line = line_rows(copies, place, ns, D1)
        u1_line = line_columns(copies, place, ns, U1)
        o1_line = line_rows(copies, place, ns, O1)
        q1_line = line_columns(copies, place, ns, Q1)
        d1_whole = whole_rows(copies, place, ns, D1, ns.full_d)
        u1_whole = whole_columns(copies, place, ns, U1, ns.full_u, 2)
        q1_whole = whole_columns(copies, place, ns, Q1, ns.full_q, 6)
        o1_whole = whole_rows(copies, place, ns, O1, ns.full_o)
        next(d1_second)
        ns.load.gu.wait()
        next(u1_first)
        ns.load.o1.wait()
        ns.load.qkv_in.wait()
        ns.load.lse.wait()
        ns.load.mixed_grad.wait()
        ns.load.dg.wait()
        plan = Plan(
            [stages(d1_second), stages(d1_line)],
            [],
            [],
            [stages(u1_first), stages(u1_second), stages(o1_first)],
            [],
            [],
            [stages(u1_second), stages(u1_line), stages(d1_line), stages(d1_whole)],
            [stages(o1_first), stages(o1_second), stages(q1_first), stages(q1_second)],
            [stages(d1_whole), stages(u1_line), stages(u1_whole)]
            + [stages(q1_second), stages(q1_line)],
            [stages(o1_second), stages(o1_line)],
            [stages(d1_whole), stages(u1_whole), stages(q1_line), stages(q1_whole)],
            [],
            [stages(o1_line), stages(o1_whole), stages(q1_whole)],
            [stages(u1_whole)],
            [stages(d0_first), stages(o1_whole)],
        )
        ns.load.gains.wait()
        grads = bwd_head(ns, place, 1, plan.tick, stages(q1_first), False)
        for copy in (ns.load.down_out, ns.load.wd, ns.load.slope, ns.load.wu, ns.load.active):
            copy.wait()
        for copy in (ns.load.mlp, ns.load.resid, ns.load.attn_out, ns.load.wo, ns.load.mixed):
            copy.wait()
        ns.mixed_grad = ns.mixed_out
        store_up = functools.partial(copies.store, ns.gu_v, ns.up_out)
        bwd_mid(ns, place, 0, grads, plan.tick, stages(d0_first), store_up, (1, 0))
        plan.drain()
        copies.store(ns.go_v, ns.go)
        copies.store(ns.gd_v, ns.gd)
        copies.store(ns.dg_v, ns.dg_out)
        next(q1_whole)
        next(o1_whole)

    flops = 6 * length * width * (mixed_width + 2 * units) + 4 * length * width * part
    kernel, options = kernel_of(backward, inputs, outputs, scratch, 3, 128, 128, 63, flops)
    results = pl.pallas_call(kernel, **options)(*inputs.values())
    return named(outputs, results)


def last_kernel(begun, lower, turned, back):
    wq = matrix(begun.wq)
    width, part = wq.shape
    length, mixed_width = back.mixed_out.shape
    units, rows = back.up_out.shape[-1], width // 32
    inputs = dict(
        u0=back.up_out, d0=back.gd, o0=back.go, qkv_in=begun.qkv, lse=lower.lse,
        mixed_grad=back.mixed_out, dg=back.dg_out, gains=begun.gains, normed=begun.normed, wq=wq,
        hidden=begun.hidden, grad=back.resid_grad, second=turned.out,
    )
    outputs = dict(
        out=struct((2, TOK, width), BF),
        block_out=struct((2, TOK, width), BF),
        gain_grad=struct((8, TOK), F32),
        full_d=struct(back.full_d.shape, BF),
        full_u=struct(back.full_u.shape, BF),
        full_q=struct(back.full_q.shape, BF),
        full_o=struct(back.full_o.shape, BF),
    )
    kept = dict(
        out=outputs["out"],
        gq=by_device(wq.shape, 4),
        qkv_grad=struct(begun.qkv.shape, BF),
        dk=struct((length, mixed_width), F32),
        dv=struct((length, mixed_width), F32),
        dg_line=struct((8, 8, TOK), F32),
        dg_pass=struct((5, 8, TOK), F32),
    )
    loaded = dict(inputs)
    del loaded["d0"]
    scratch = held(loaded, kept)
    scratch |= scatter_scratch(QKV, width)
    for name, count, high, wide, steps in (
        (D0, 1, units // 8, width, 2),
        (U0, 4, rows, units, 3),
        (Q0, 4, rows, part, 3),
        (O0, 1, mixed_width // 8, width, 3),
    ):
        scratch |= reduce_scratch(name, count, high, wide, steps)
        scratch |= finish_scratch(name, count, high, wide)

    def last(ns):
        place, copies = Place(), ns.copies
        line = [place.line(offset)[0] for offset in range(1, 8)]
        meet([*line, place.along_x, place.along_y])
        unused, d0_second = reduce_rep(copies, place, ns.d0, ns, D0)
        u0_first, u0_second = reduce_rep(copies, place, ns.u0_v, ns, U0)
        o0_first, o0_second = reduce_rep(copies, place, ns.o0_v, ns, O0)
        q0_first, q0_second = reduce_rep(copies, place, ns.gq_v, ns, Q0)
        d0_line = line_rows(copies, place, ns, D0)
        o0_line = line_rows(copies, place, ns, O0)
        u0_line = line_columns(copies, place, ns, U0)
        q0_line = line_columns(copies, place, ns, Q0)
        d0_whole = whole_rows(copies, place, ns, D0, ns.full_d)
        o0_whole = whole_rows(copies, place, ns, O0, ns.full_o)
        u0_whole = whole_columns(copies, place, ns, U0, ns.full_u, 2)
        q0_whole = whole_columns(copies, place, ns, Q0, ns.full_q, 6)
        upper = place.upper
        second = copies.remote(ns.second.at[1 - upper], ns.block_out.at[upper], place.far)
        next(d0_second)
        ns.load.u0.wait()
        next(u0_first)
        ns.load.qkv_in.wait()
        ns.load.lse.wait()
        ns.load.mixed_grad.wait()
        ns.load.dg.wait()
        ns.load.o0.wait()
        plan = Plan(
            [stages(d0_second), stages(d0_line)],
            [],
            [],
            [stages(u0_first), stages(u0_second)],
            [stages(d0_line), stages(d0_whole)],
            [],
        )
        ns.load.gains.wait()
        grads = bwd_head(ns, place, 0, plan.tick, stages(q0_first), True)
        ns.load.second.wait()
        copies.store(ns.second_v.at[upper], ns.block_out.at[upper])
        ns.out_v[1] = grads[1]().astype(BF)
        for task in (u0_second, u0_line, q0_first, q0_second, o0_first, d0_whole):
            next(task)
        ns.out_v[0] = grads[0]().astype(BF)
        copies.store(ns.out_v.at[upper], ns.out.at[upper])
        gain_grad = gain_sum(ns, copies, place)
        for task in (
            gain_grad, q0_second, q0_line, o0_first, o0_second, u0_line, u0_whole, d0_whole,
            gain_grad, o0_second, o0_line,
        ):
            next(task)
        moved = copies.remote(ns.out_v.at[1 - upper], ns.out.at[upper], place.far)
        for task in (
            u0_whole, q0_line, q0_whole, o0_line, o0_whole, gain_grad, u0_whole, q0_whole,
            o0_whole, gain_grad, q0_whole, o0_whole,
        ):
            next(task)
        moved.wait_recv()
        second.wait_recv()

    flops = 4 * length * width * part
    kernel, options = kernel_of(last, inputs, outputs, scratch, 4, 128, 128, 60, flops)
    results = pl.pallas_call(kernel, **options)(*inputs.values())
    return named(outputs, results)


def gain_sum(ns, copies, place):
    def columns(grp):
        return pl.ds(pl.multiple_of(grp * TOK, TOK), TOK)

    moved = []
    for offset in range(1, 8):
        device, upper, t = place.line(offset)
        source = ns.dg_v.at[:, columns(upper * 4 + t)]
        moved.append(copies.remote(source, ns.dg_line_v.at[place.grp], device))
    ns.dg_line_v[place.grp] = ns.dg_v[:, columns(place.grp)]
    yield
    for copy in moved:
        copy.wait_recv()
    ns.dg_pass_v[0] = jnp.sum(ns.dg_line_v[...], axis=0)
    moved = copies.remote(ns.dg_pass_v.at[0], ns.dg_pass_v.at[1], place.along_x)
    yield
    moved.wait_recv()
    ns.dg_pass_v[2] = ns.dg_pass_v[0] + ns.dg_pass_v[1]
    moved = copies.remote(ns.dg_pass_v.at[2], ns.dg_pass_v.at[3], place.along_y)
    yield
    moved.wait_recv()
    ns.dg_pass_v[4] = ns.dg_pass_v[2] + ns.dg_pass_v[3]
    copies.store(ns.dg_pass_v.at[4], ns.gain_grad)
    yield


def body_pairs(block_in, cotangent, w_qkv, w_out, w_up, w_down, norm_gains):
    layers, rows, width = w_out.shape
    hidden_unit = w_down.shape[1]
    gain_part = jnp.transpose(norm_gains.astype(F32), (0, 2, 1)).reshape(layers * 4, rows)
    down_parts = w_down.reshape(layers, 2, 2, 2, hidden_unit // 8, width)
    out_parts = w_out.reshape(layers, 2, 2, 2, rows // 8, width)

    begun = start_kernel(block_in[:, 0], gain_part, w_qkv, w_up, out_parts)
    lower = forward_kernel(begun, w_qkv, w_up, down_parts, out_parts)
    turned = turn_kernel(lower, begun.gains, down_parts, out_parts, cotangent[:, 0])
    back = backward_kernel(begun, lower, turned)
    last = last_kernel(begun, lower, turned, back)

    def whole(zero, one, like):
        return jnp.stack([zero, one]).reshape(like.shape).astype(F32)

    return (
        last.block_out[:, None],
        last.out.astype(F32)[:, None],
        whole(last.full_q, back.full_q, w_qkv),
        whole(last.full_o, back.full_o, w_out),
        whole(last.full_u, back.full_u, w_up),
        whole(last.full_d, back.full_d, w_down),
        jnp.transpose(last.gain_grad.reshape(layers, 4, rows), (0, 2, 1)),
    )


def norm_apply(values, gains):
    return values * lax.rsqrt(jnp.mean(values * values, axis=-1, keepdims=True) + EPS) * gains


def inner_rows(left, right):
    return lax.dot_general(
        left, right, (((0,), (0,)), ((), ())), preferred_element_type=jnp.float32
    )


def times_trans(left, right):
    return lax.dot_general(
        left, right, (((1,), (1,)), ((), ())), preferred_element_type=jnp.float32
    )


def split_blocks(whole):
    length = whole.shape[0]
    width = min(512, length)
    count = length // width
    return (whole.reshape(count, width, HEADS, HDIM), width, count)


def block_at(blocks, index):
    return lax.dynamic_index_in_dim(blocks, index, 0, keepdims=False)


def key_scores(query, key_block, key_start, query_pos):
    scale = HDIM ** (-0.5)
    scores = (
        jnp.einsum("qhd,khd->hqk", query, key_block, preferred_element_type=jnp.float32) * scale
    )
    key_pos = key_start + jnp.arange(key_block.shape[0], dtype=jnp.int32)
    allowed = key_pos[None, :] <= query_pos[:, None]
    return (scores, allowed[None])


def attend_split(query, keys_all, values_all, query_pos):
    key_blocks, width, count = split_blocks(keys_all)
    value_blocks = split_blocks(values_all)[0]
    row_count = query.shape[0]
    upper = query_pos[row_count - 1] // width + 1

    def total_step(index, carry):
        running, total = carry
        scores, allowed = key_scores(query, block_at(key_blocks, index), index * width, query_pos)
        newest = jnp.maximum(running, jnp.max(jnp.where(allowed, scores, NEGATIVE), axis=-1))
        terms = jnp.where(allowed, jnp.exp(scores - newest[..., None]), 0.0)
        total = total * jnp.exp(running - newest) + jnp.sum(terms, axis=-1)
        return (newest, total)

    start_run = jnp.full((HEADS, row_count), NEGATIVE, jnp.float32)
    start_total = jnp.zeros((HEADS, row_count), jnp.float32)
    running, total = lax.fori_loop(0, upper, total_step, (start_run, start_total))
    log_total = running + jnp.log(total)

    def mix_step(index, accum):
        scores, allowed = key_scores(query, block_at(key_blocks, index), index * width, query_pos)
        probs = jnp.where(allowed, jnp.exp(scores - log_total[..., None]), 0.0)
        return accum + jnp.einsum(
            "hqk,khd->qhd",
            probs.astype(jnp.bfloat16),
            block_at(value_blocks, index),
            preferred_element_type=jnp.float32,
        )

    start_mix = jnp.zeros((row_count, HEADS, HDIM), jnp.float32)
    mixed = lax.fori_loop(0, upper, mix_step, start_mix)
    return (mixed.reshape(row_count, HEADS * HDIM), log_total)


def attend_back_split(query, keys_all, values_all, log_total, out_grad, delta, query_pos):
    key_blocks, width, count = split_blocks(keys_all)
    value_blocks = split_blocks(values_all)[0]
    row_count = query.shape[0]
    upper = query_pos[row_count - 1] // width + 1
    scale = HDIM ** (-0.5)

    def back_step(index, carry):
        query_acc, pieces = carry
        key_block = block_at(key_blocks, index)
        value_block = block_at(value_blocks, index)
        scores, allowed = key_scores(query, key_block, index * width, query_pos)
        probs = jnp.where(allowed, jnp.exp(scores - log_total[..., None]), 0.0)
        prob_grad = jnp.einsum(
            "qhd,khd->hqk", out_grad, value_block, preferred_element_type=jnp.float32
        )
        score_grad = (probs * (prob_grad - delta[..., None])).astype(jnp.bfloat16)
        query_acc = (
            query_acc
            + jnp.einsum("hqk,khd->qhd", score_grad, key_block, preferred_element_type=jnp.float32)
            * scale
        )
        key_grad = (
            jnp.einsum("hqk,qhd->khd", score_grad, query, preferred_element_type=jnp.float32)
            * scale
        )
        value_grad = jnp.einsum(
            "hqk,qhd->khd", probs.astype(jnp.bfloat16), out_grad, preferred_element_type=jnp.float32
        )
        joined = jnp.concatenate(
            [key_grad.reshape(width, HEADS * HDIM), value_grad.reshape(width, HEADS * HDIM)], axis=1
        )
        pieces = lax.dynamic_update_index_in_dim(pieces, joined, index, 0)
        return (query_acc, pieces)

    start_acc = jnp.zeros((row_count, HEADS, HDIM), jnp.float32)
    start_pieces = jnp.zeros((count, width, 2 * HEADS * HDIM), jnp.float32)
    query_grad, pieces = lax.fori_loop(0, upper, back_step, (start_acc, start_pieces))
    return (query_grad.reshape(row_count, HEADS * HDIM), pieces.reshape(-1, pieces.shape[-1]))


def layer_forward(hidden_in, weights, query_pos):
    w_qkv_full, w_out_full, w_up_full, w_down_full, gain_full = weights
    gains_f = gain_full.astype(jnp.float32)
    row_count = hidden_in.shape[0]
    width = w_out_full.shape[1]
    normed = norm_apply(hidden_in, gains_f[:, 0]).astype(jnp.bfloat16)
    qkv_low = jnp.dot(normed, w_qkv_full, preferred_element_type=jnp.float32).astype(jnp.bfloat16)
    query = qkv_low[:, :width]
    keys_all, values_all = (
        lax.all_gather(qkv_low[:, width : 2 * width], "grp", axis=0, tiled=True),
        lax.all_gather(qkv_low[:, 2 * width :], "grp", axis=0, tiled=True),
    )
    mixed, log_total = attend_split(
        query.reshape(row_count, HEADS, HDIM),
        keys_all.reshape(-1, HEADS, HDIM),
        values_all.reshape(-1, HEADS, HDIM),
        query_pos,
    )
    mixed_low = mixed.astype(jnp.bfloat16)
    attn_out = jnp.dot(mixed_low, w_out_full, preferred_element_type=jnp.float32)
    resid = hidden_in + norm_apply(attn_out, gains_f[:, 1])
    mlp_in = norm_apply(resid, gains_f[:, 2]).astype(jnp.bfloat16)
    up_out = jnp.dot(mlp_in, w_up_full, preferred_element_type=jnp.float32)
    active = jax.nn.gelu(up_out).astype(jnp.bfloat16)
    down_out = jnp.dot(active, w_down_full, preferred_element_type=jnp.float32)
    result = resid + norm_apply(down_out, gains_f[:, 3])
    kept = (
        hidden_in,
        normed,
        qkv_low,
        mixed,
        mixed_low,
        log_total,
        attn_out,
        resid,
        mlp_in,
        up_out,
        active,
        down_out,
    )
    return (result, kept)


def layer_backward(grad_out, weights, kept, query_pos):
    w_qkv_full, w_out_full, w_up_full, w_down_full, gain_full = weights
    (
        hidden_in,
        normed,
        qkv_low,
        mixed,
        mixed_low,
        log_total,
        attn_out,
        resid,
        mlp_in,
        up_out,
        active,
        down_out,
    ) = kept
    gains_f = gain_full.astype(jnp.float32)
    row_count = hidden_in.shape[0]
    width = w_out_full.shape[1]
    unused, puller = jax.vjp(norm_apply, down_out, gains_f[:, 3])
    down_grad, gain_four = puller(grad_out)
    down_low = down_grad.astype(jnp.bfloat16)
    w_down_grad = inner_rows(active, down_low)
    active_grad = times_trans(down_low, w_down_full)
    unused, puller = jax.vjp(jax.nn.gelu, up_out)
    up_low = puller(active_grad)[0].astype(jnp.bfloat16)
    w_up_grad = inner_rows(mlp_in, up_low)
    mlp_grad = times_trans(up_low, w_up_full)
    unused, puller = jax.vjp(norm_apply, resid, gains_f[:, 2])
    resid_part, gain_three = puller(mlp_grad)
    resid_grad = grad_out + resid_part
    unused, puller = jax.vjp(norm_apply, attn_out, gains_f[:, 1])
    attn_grad, gain_two = puller(resid_grad)
    attn_low = attn_grad.astype(jnp.bfloat16)
    w_out_grad = inner_rows(mixed_low, attn_low)
    mixed_grad = times_trans(attn_low, w_out_full).astype(jnp.bfloat16)
    keys_all, values_all = (
        lax.all_gather(qkv_low[:, width : 2 * width], "grp", axis=0, tiled=True),
        lax.all_gather(qkv_low[:, 2 * width :], "grp", axis=0, tiled=True),
    )
    delta = jnp.sum(
        (mixed_grad.astype(jnp.float32) * mixed).reshape(row_count, HEADS, HDIM), axis=-1
    ).T
    query_low = qkv_low[:, :width]
    query_grad, key_value_terms = attend_back_split(
        query_low.reshape(row_count, HEADS, HDIM),
        keys_all.reshape(-1, HEADS, HDIM),
        values_all.reshape(-1, HEADS, HDIM),
        log_total,
        mixed_grad.reshape(row_count, HEADS, HDIM),
        delta,
        query_pos,
    )
    key_value_grad = lax.psum_scatter(
        key_value_terms.astype(jnp.bfloat16), "grp", scatter_dimension=0, tiled=True
    ).astype(jnp.float32)
    qkv_grad = jnp.concatenate([query_grad, key_value_grad], axis=1).astype(jnp.bfloat16)
    w_qkv_grad = inner_rows(normed, qkv_grad)
    normed_grad = times_trans(qkv_grad, w_qkv_full)
    unused, puller = jax.vjp(norm_apply, hidden_in, gains_f[:, 0])
    input_part, gain_one = puller(normed_grad)
    gain_grad = jnp.stack([gain_one, gain_two, gain_three, gain_four], axis=1)
    return (resid_grad + input_part, (w_qkv_grad, w_out_grad, w_up_grad, w_down_grad, gain_grad))


def body_general(block_in, cotangent, w_qkv, w_out, w_up, w_down, norm_gains):
    layer_count = w_qkv.shape[0]
    micro_count = block_in.shape[0]
    row_count = block_in.shape[2]
    query_pos = lax.axis_index("grp") * row_count + jnp.arange(row_count, dtype=jnp.int32)
    totals = [None] * layer_count
    outputs = []
    input_grads = []
    for micro_idx in range(micro_count):
        hidden = block_in[micro_idx, 0].astype(jnp.float32)
        saved = []
        for layer_idx in range(layer_count):
            hidden, kept = layer_forward(
                hidden,
                (
                    lax.all_gather(w_qkv[layer_idx], "grp", axis=0, tiled=True),
                    lax.all_gather(w_out[layer_idx], "grp", axis=0, tiled=True),
                    lax.all_gather(w_up[layer_idx], "grp", axis=0, tiled=True),
                    lax.all_gather(w_down[layer_idx], "grp", axis=0, tiled=True),
                    lax.all_gather(norm_gains[layer_idx], "grp", axis=0, tiled=True),
                ),
                query_pos,
            )
            saved.append(kept)
        outputs.append(hidden.astype(jnp.bfloat16))
        grad_flow = cotangent[micro_idx, 0].astype(jnp.float32)
        for layer_idx in reversed(range(layer_count)):
            grad_flow, parts = layer_backward(
                grad_flow,
                (
                    lax.all_gather(w_qkv[layer_idx], "grp", axis=0, tiled=True),
                    lax.all_gather(w_out[layer_idx], "grp", axis=0, tiled=True),
                    lax.all_gather(w_up[layer_idx], "grp", axis=0, tiled=True),
                    lax.all_gather(w_down[layer_idx], "grp", axis=0, tiled=True),
                    lax.all_gather(norm_gains[layer_idx], "grp", axis=0, tiled=True),
                ),
                saved[layer_idx],
                query_pos,
            )
            if totals[layer_idx] is None:
                totals[layer_idx] = parts
            else:
                totals[layer_idx] = tuple(
                    (left + right for left, right in zip(totals[layer_idx], parts))
                )
        input_grads.append(grad_flow)
    reduced = []
    for layer_idx in range(layer_count):
        accum = totals[layer_idx]
        shards = (
            lax.psum_scatter(
                accum[0].astype(jnp.bfloat16), "grp", scatter_dimension=0, tiled=True
            ).astype(jnp.float32),
            lax.psum_scatter(
                accum[1].astype(jnp.bfloat16), "grp", scatter_dimension=0, tiled=True
            ).astype(jnp.float32),
            lax.psum_scatter(
                accum[2].astype(jnp.bfloat16), "grp", scatter_dimension=0, tiled=True
            ).astype(jnp.float32),
            lax.psum_scatter(
                accum[3].astype(jnp.bfloat16), "grp", scatter_dimension=0, tiled=True
            ).astype(jnp.float32),
            lax.psum_scatter(
                accum[4].astype(jnp.bfloat16), "grp", scatter_dimension=0, tiled=True
            ).astype(jnp.float32),
        )
        reduced.append(
            (
                lax.psum(shards[0].astype(jnp.bfloat16), "rep").astype(jnp.float32),
                lax.psum(shards[1].astype(jnp.bfloat16), "rep").astype(jnp.float32),
                lax.psum(shards[2].astype(jnp.bfloat16), "rep").astype(jnp.float32),
                lax.psum(shards[3].astype(jnp.bfloat16), "rep").astype(jnp.float32),
                lax.psum(shards[4].astype(jnp.bfloat16), "rep").astype(jnp.float32),
            )
        )
    block_out = jnp.stack(outputs)[:, None]
    block_in_grad = jnp.stack(input_grads)[:, None]
    stacked = [
        jnp.stack([reduced[layer_idx][member] for layer_idx in range(layer_count)])
        for member in range(5)
    ]
    return (block_out, block_in_grad, stacked[0], stacked[1], stacked[2], stacked[3], stacked[4])


def solution(mesh):
    rep_size, grp_size = mesh.shape["rep"], mesh.shape["grp"]

    def body(block_in, cotangent, w_qkv, w_out, w_up, w_down, norm_gains):
        sizes = (rep_size, grp_size, block_in.shape[0], w_qkv.shape[0], block_in.shape[2])
        fits = sizes == (4, 8, 2, 2, TOK)
        chosen = body_pairs if fits else body_general
        return chosen(block_in, cotangent, w_qkv, w_out, w_up, w_down, norm_gains)

    tokens = P(None, "rep", "grp", None)
    rows = P(None, "grp", None)
    return jax.shard_map(
        body,
        mesh=mesh,
        in_specs=(tokens, tokens, rows, rows, rows, rows, rows),
        out_specs=(tokens, tokens, rows, rows, rows, rows, rows),
        check_vma=False,
    )
```

```python
import functools
import types

import jax
import jax.numpy as jnp
from jax import lax
from jax.experimental import pallas as pl
from jax.experimental.pallas import tpu as pltpu
from jax.sharding import PartitionSpec as P

HEADS = 16
HDIM = 64
EPS = 1e-06
NEGATIVE = -1e30
BF = jnp.bfloat16
REP, GRP = "rep", "grp"
F32 = jnp.float32


def dot(left, right):
    return jnp.dot(left, right, preferred_element_type=F32)


def dot_tn(left, right):
    return lax.dot_general(left, right, (((0,), (0,)), ((), ())), preferred_element_type=F32)


def dot_nt(left, right):
    return lax.dot_general(left, right, (((1,), (1,)), ((), ())), preferred_element_type=F32)


def norm(values, gain):
    return values * lax.rsqrt(jnp.mean(values * values, axis=-1, keepdims=True) + EPS) * gain


def head_mask(width, head):
    lanes = lax.broadcasted_iota(jnp.int32, (1, width), 1)
    return (lanes // HDIM) == head


def causal_scores(query, keys, below, start):
    scores = dot_nt(query, keys)
    last = jnp.where(below, scores[:, start:], NEGATIVE)
    return jnp.concatenate([scores[:, :start], last], axis=1) if start else last


def attend(ns, stream, block=256):
    length, width = ns.mixed_v.shape
    qkv_ref, lse_ref, sum_ref = ns.qkv_in_v, ns.lse_v, ns.terms_own.at[stream]
    row = lax.broadcasted_iota(jnp.int32, (block, block), 0)
    col = lax.broadcasted_iota(jnp.int32, (block, block), 1)
    below = col <= row
    zero = jnp.zeros((), BF)
    lane = lax.broadcasted_iota(jnp.int32, (1, 128), 1)
    base, high = stream * length // 2, (stream + 1) * length // 2
    sum_ref[...] = jnp.zeros_like(sum_ref)
    lse_ref[base:high, :] = jnp.zeros((length // 2, 128), F32)

    def one_head(head):
        mask = head_mask(width, head)
        for start in range(base, high, block):
            stop = start + block
            query = qkv_ref[start:stop, :width] * jnp.asarray(HDIM**-0.5, BF)
            query = jnp.where(mask, query, zero)
            scores = causal_scores(query, qkv_ref[:stop, width : 2 * width], below, start)
            top = jnp.max(scores, axis=1, keepdims=True)
            terms = jnp.exp(scores - top)
            sums = jnp.sum(terms, axis=1, keepdims=True)
            mixed = dot(terms.astype(BF), qkv_ref[:stop, 2 * width :]) * (1.0 / sums)
            sum_ref[:, start - base : stop - base] += jnp.where(mask, mixed, 0.0)
            stats = lse_ref[start:stop, :]
            lse_ref[start:stop, :] = jnp.where(lane == head, top + jnp.log(sums), stats)

    loop(width // HDIM, one_head)
    for start in range(base, high, block):
        ns.mixed_v[start : start + block, :] = sum_ref[:, start - base : start - base + width].astype(BF)


def attend_back(ns, stream, block=256):
    length, width = ns.mixed_grad_v.shape
    qkv_ref, grad_ref, sum_ref = ns.qkv_in_v, ns.mixed_grad_v, ns.terms_own.at[stream]
    row = lax.broadcasted_iota(jnp.int32, (block, block), 0)
    col = lax.broadcasted_iota(jnp.int32, (block, block), 1)
    below = col <= row
    zero = jnp.zeros((), BF)
    scale = HDIM**-0.5
    lane = lax.broadcasted_iota(jnp.int32, (1, 128), 1)
    base, high = stream * length // 2, (stream + 1) * length // 2
    sum_ref[...] = jnp.zeros_like(sum_ref)

    def one_head(head):
        mask = head_mask(width, head)
        for start in range(base, high, block):
            stop = start + block
            query = qkv_ref[start:stop, :width] * jnp.asarray(scale, BF)
            query = jnp.where(mask, query, zero)
            grad = jnp.where(mask, grad_ref[start:stop, :], zero)
            keys, vals = qkv_ref[:stop, width : 2 * width], qkv_ref[:stop, 2 * width :]
            scores = causal_scores(query, keys, below, start)
            lse = jnp.where(lane == head, ns.lse_v[start:stop, :], 0.0)
            probs = jnp.exp(scores - jnp.sum(lse, axis=1, keepdims=True))
            prob_grad = dot_nt(grad, vals)
            delta = jnp.sum(probs * prob_grad, axis=1, keepdims=True)
            score_grad = (probs * (prob_grad - delta)).astype(BF)
            query_grad = jnp.where(mask, dot(score_grad, keys), 0.0)
            sum_ref[:, start - base : stop - base] += query_grad
            ns.dk_v[:stop, :] += dot_tn(score_grad, query)
            ns.dv_v[:stop, :] += dot_tn(probs.astype(BF), grad)

    loop(width // HDIM, one_head)
    for start in range(base, high, block):
        value = sum_ref[:, start - base : start - base + width] * scale
        ns.qkv_grad_v[start : start + block, :width] = value.astype(BF)
    ns.qkv_grad_v[base:high, width : 2 * width] = ns.dk_v[base:high, :].astype(BF)
    ns.qkv_grad_v[base:high, 2 * width :] = ns.dv_v[base:high, :].astype(BF)


MESH_ID = pl.DeviceIdType.MESH
HELD, ONE, TWO, SUM, LINE, FULL = "_v", "one", "two", "sum", "line", "full"
PASSED = ("give", "take", "send", "got")
ATTN, DOWN, UP, QKV = "attn", "down", "up", "qkv"
D0, U0, Q0, O0 = "d0", "u0", "q0", "o0"
D1, U1, Q1, O1 = "d1", "u1", "q1", "o1"
TOK = 128


class Place:
    def __init__(self):
        rep, grp = lax.axis_index(REP), lax.axis_index(GRP)
        self.rep, self.grp = rep, grp
        self.x, self.y = lax.rem(rep, 2), lax.div(rep, 2)
        self.t, self.upper = lax.rem(grp, 4), lax.div(grp, 4)
        self.c, self.side = lax.rem(grp, 2), lax.div(self.t, 2)
        base = self.upper * 4
        self.core = (rep, base + self.side * 2 + 1 - self.c)
        self.near = (rep, base + (1 - self.side) * 2 + self.c)
        self.far = (rep, (1 - self.upper) * 4 + self.t)
        self.along_x = (self.y * 2 + 1 - self.x, grp)
        self.along_y = ((1 - self.y) * 2 + self.x, grp)
        self.near_t = (1 - self.side) * 2 + self.c

    def line(self, offset):
        c = 1 - self.c if offset & 1 else self.c
        side = 1 - self.side if offset & 2 else self.side
        upper = 1 - self.upper if offset & 4 else self.upper
        return (self.rep, upper * 4 + side * 2 + c), upper, side * 2 + c


class Copies:
    def __init__(self, send, recv, here):
        self.sems, self.here = (send, recv), here
        self.sent, self.local_count, self.stores, self.done = [], 0, [], set()

    def remote(self, source, target, device):
        at = len(self.sent)
        assert at < self.sems[0].shape[0]
        copy = pltpu.make_async_remote_copy(
            src_ref=source,
            dst_ref=target,
            send_sem=self.sems[0].at[at],
            recv_sem=self.sems[1].at[at],
            device_id=device,
            device_id_type=MESH_ID,
        )
        copy.start()
        self.sent.append(copy)
        return copy

    def local(self, source, target):
        assert self.local_count < self.here.shape[0]
        copy = pltpu.make_async_copy(source, target, self.here.at[self.local_count])
        self.local_count += 1
        copy.start()
        return copy

    def store(self, source, target):
        self.stores.append(self.local(source, target))

    def both(self, *copies):
        for copy in copies:
            copy.wait_recv()
            copy.wait_send()
            self.done.add(id(copy))

    def finish(self):
        for copy in self.sent:
            if id(copy) not in self.done:
                copy.wait_send()
        for copy in self.stores:
            copy.wait()


def announce(devices):
    barrier = pltpu.get_barrier_semaphore()
    for device in devices:
        pl.semaphore_signal(barrier, inc=1, device_id=device, device_id_type=MESH_ID)


def meet(devices):
    pl.semaphore_wait(pltpu.get_barrier_semaphore(), len(devices))


def with_line(place):
    line = [place.line(offset)[0] for offset in range(1, 8)]
    return [*line, place.along_x, place.along_y]


def with_few(place):
    return [place.core, place.near, place.far, place.along_x, place.along_y]


class Plan:
    def __init__(self, *entries):
        self.entries = list(entries)

    def tick(self):
        if self.entries:
            for action in self.entries.pop(0):
                action()

    def drain(self):
        while self.entries:
            self.tick()


def stages(task):
    return lambda: next(task, None)


def spread(copies, place, part, last=True):
    x, y, every = place.x, place.y, slice(None)
    one = copies.remote(part(0, y, x), part(0, y, x), place.along_x)
    two = copies.remote(part(1, y, x), part(1, y, x), place.along_y)
    yield
    one.wait_recv()
    three = copies.remote(part(0, y, every), part(0, y, every), place.along_y)
    two.wait_recv()
    four = copies.remote(part(1, every, x), part(1, every, x), place.along_x)
    yield
    three.wait_recv()
    four.wait_recv()
    if last:
        yield


def deal(copies, place, source, target):
    moved = []
    own = copies.local(source.at[place.t], target)
    for offset in range(1, 8):
        if offset == 4:
            yield
        device, upper, t = place.line(offset)
        moved.append(copies.remote(source.at[t], target, device))
    yield
    own.wait()
    for copy in moved:
        copy.wait_recv()
    yield


def add_low(one, two):
    return (one.astype(F32) + two.astype(F32)).astype(BF)


def reduce_rep(copies, place, grad, ns, name):
    x, y = place.x, place.y
    count = grad.shape[1]

    def step_one():
        one = getattr(ns, name + ONE)
        first = copies.remote(grad.at[0, :, :, 1 - x], one.at[0], place.along_x)
        second = copies.remote(grad.at[1, :, 1 - y], one.at[1], place.along_y)
        yield
        copies.both(first, second)
        for i in range(count):
            for j in range(2):
                grad[0, i, j, x] = add_low(grad[0, i, j, x], one[0, i, j])
                grad[1, i, y, j] = add_low(grad[1, i, y, j], one[1, i, j])
        yield

    def step_two():
        two, total = getattr(ns, name + TWO), getattr(ns, name + SUM)
        first = copies.remote(grad.at[0, :, 1 - y, x], two.at[0], place.along_y)
        second = copies.remote(grad.at[1, :, y, 1 - x], two.at[1], place.along_x)
        own = [copies.local(grad.at[half, :, y, x], total.at[half]) for half in range(2)]
        yield
        copies.both(first, second)
        for half in range(2):
            own[half].wait()
            for i in range(count):
                total[half, i] = add_low(total[half, i], two[half, i])
        yield

    return step_one(), step_two()


def line_columns(copies, place, ns, name):
    total, line, full = (getattr(ns, name + part) for part in (SUM, LINE, FULL))
    moved = []
    for offset in range(1, 8):
        device, upper, t = place.line(offset)
        here = line.at[place.upper, place.t]
        moved.append(copies.remote(total.at[upper, t], here, device))
    line[place.upper, place.t] = total[place.upper, place.t]
    yield
    for copy in moved:
        copy.wait_recv()
    for t in range(4):
        full[place.y, place.x, t] = add_low(line[0, t], line[1, t])
    yield


def line_rows(copies, place, ns, name):
    total, line, full = (getattr(ns, name + part) for part in (SUM, LINE, FULL))
    moved = copies.remote(total.at[1 - place.upper, 0], line, place.far)
    yield
    moved.wait_recv()
    rows = line.shape[0] // 2
    for half in range(2):
        at = pl.ds(half * rows, rows)
        full[place.y, place.x, half] = add_low(total[place.upper, 0, at, :], line[at, :])
    yield


def whole_columns(copies, place, ns, name, target, groups):
    full = getattr(ns, name + FULL)
    yield from spread(copies, place, lambda half, a, b: full.at[a, b, pl.ds(2 * half, 2)], False)
    unit = full.shape[4] // groups
    for t in range(4):
        for k in range(groups):
            source = full.at[:, :, t, :, k * unit : (k + 1) * unit]
            start = (k * 4 + t) * unit
            copies.store(source, target.at[:, :, :, start : start + unit])
    yield


def whole_rows(copies, place, ns, name, target):
    full = getattr(ns, name + FULL)
    yield from spread(copies, place, lambda half, a, b: full.at[a, b, half], False)
    copies.store(full, target)
    yield


def reduce_scratch(name, count, rows, width, steps=3):
    total = {}
    if steps & 1:
        total[name + ONE] = pltpu.VMEM((2, count, 2, rows, width), BF)
    if steps & 2:
        total[name + TWO] = pltpu.VMEM((2, count, rows, width), BF)
        total[name + SUM] = pltpu.VMEM((2, count, rows, width), BF)
    return total


def finish_scratch(name, count, rows, width):
    if count == 1:
        line, full = (rows, width), (2, 2, 2, rows // 2, width)
    else:
        line, full = (2, count, rows, width), (2, 2, count, rows, width)
    return {name + LINE: pltpu.VMEM(line, BF), name + FULL: pltpu.VMEM(full, BF)}


def by_device(shape, count):
    rows, width = shape
    return struct((2, count, 2, 2, rows // (8 * count), width), BF)


def loop(count, step):
    def run(index, carry):
        step(index)
        return carry

    lax.fori_loop(0, count, run, 0)


def tile_of(index, size):
    return pl.ds(pl.multiple_of(index * size, size), size)


def matrix(value):
    return value.reshape(-1, value.shape[-1])


def times(left, right_ref, tile, sink):
    every = (slice(None),) * (len(right_ref.shape) - 1)

    def step(index):
        at = tile_of(index, tile)
        sink(at, dot(left(), matrix(right_ref[(*every, at)])))

    loop(right_ref.shape[-1] // tile, step)


def times_rows(left, right_ref, tile, sink):
    flat = len(right_ref.shape) == 2

    def step(index):
        if flat:
            at = tile_of(index, tile)
            sink(at, dot_nt(left(), right_ref[at, :]))
        else:
            block = matrix(right_ref[index])
            sink(tile_of(index, block.shape[0]), dot_nt(left(), block))

    loop(right_ref.shape[0] // (tile if flat else 1), step)


def gram(left_ref, right_ref, out_ref):
    count, tile = out_ref.shape[1], 256
    total = left_ref.shape[1]
    if total == tile:
        value = dot_tn(left_ref[...], right_ref[...]).astype(BF)
        out_ref[...] = value.reshape(out_ref.shape)
        return

    def step(index):
        value = dot_tn(left_ref[:, tile_of(index, tile)], right_ref[...]).astype(BF)
        half, part = lax.div(index, 2), lax.rem(index, 2)
        if count == 1:
            out_ref[half, 0, part] = value.reshape(out_ref.shape[3:])
        else:
            out_ref[half, pl.ds(part * 2, 2)] = value.reshape(2, *out_ref.shape[2:])

    loop(total // tile, step)


class Gather:
    def __init__(self, copies, place, buf, order=(0, 1)):
        self.copies, self.place, self.buf, self.order = copies, place, buf, order
        self.flight = {}

    def rows(self, stream, where):
        start = (self.order[stream] * 4 + where) * TOK
        return pl.ds(pl.multiple_of(start, TOK), TOK)

    def pair(self, stream, side):
        start = (self.order[stream] * 4 + side * 2) * TOK
        return pl.ds(pl.multiple_of(start, TOK), 2 * TOK)

    def start(self, stream, block):
        at = self.rows(stream, self.place.t)
        self.buf[at, :] = block
        mine = self.buf.at[at, :]
        across = self.copies.remote(mine, mine, self.place.near)
        beside = self.copies.remote(mine, mine, self.place.core)
        self.flight[stream] = [across, beside]

    def wait_chip(self, stream):
        self.flight[stream][1].wait_recv()

    def forward(self, stream):
        self.flight[stream][0].wait_recv()
        got = self.buf.at[self.rows(stream, self.place.near_t), :]
        self.flight[stream].append(self.copies.remote(got, got, self.place.core))

    def wait_rest(self, stream):
        self.flight[stream][2].wait_recv()


class Scatter:
    def __init__(self, copies, place, ns, name):
        self.copies, self.place = copies, place
        self.away, self.own = ns.terms_away, ns.terms_own
        self.give, self.take, self.send, self.got = (
            getattr(ns, name + part) for part in PASSED
        )
        self.flight = {}

    def push(self, stream, product):
        place, copies = self.place, self.copies
        mine = pl.ds(pl.multiple_of(place.c * TOK, TOK), TOK)
        other = pl.ds(pl.multiple_of((1 - place.c) * TOK, TOK), TOK)

        def to_away(at, value):
            self.away[:, at] = value

        def to_own(at, value):
            self.own[stream, :, at] = value

        product(1 - place.side, to_away)
        self.give[stream, 0] = self.away[other, :].astype(BF)
        first = copies.remote(self.give.at[stream, 0], self.take.at[stream, 0], place.core)
        product(place.side, to_own)
        first.wait_recv()
        self.send[stream] = (self.away[mine, :] + self.take[stream, 0].astype(F32)).astype(BF)
        across = copies.remote(self.send.at[stream], self.got.at[stream], place.near)
        self.give[stream, 1] = self.own[stream, other, :].astype(BF)
        second = copies.remote(self.give.at[stream, 1], self.take.at[stream, 1], place.core)
        self.flight[stream] = (second, across)

    def result(self, stream):
        second, across = self.flight[stream]
        mine = pl.ds(pl.multiple_of(self.place.c * TOK, TOK), TOK)
        second.wait_recv()
        total = self.own[stream, mine, :] + self.take[stream, 1].astype(F32)
        across.wait_recv()
        return total + self.got[stream].astype(F32)


def scatter_scratch(name, width):
    give, take, send, got = (name + part for part in PASSED)
    return {
        "terms_away": pltpu.VMEM((2 * TOK, width), F32),
        "terms_own": pltpu.VMEM((2, 2 * TOK, width), F32),
        give: pltpu.VMEM((2, 2, TOK, width), BF),
        take: pltpu.VMEM((2, 2, TOK, width), BF),
        send: pltpu.VMEM((2, TOK, width), BF),
        got: pltpu.VMEM((2, TOK, width), BF),
    }


def gelu_both(x):
    cubic = x * x * 0.044715
    bent = jnp.tanh(0.7978845608028654 * (x + cubic * x))
    half = 0.5 * (1.0 + bent)
    slope = half + 0.5 * x * (1.0 - bent * bent) * (0.7978845608028654 * (1.0 + 3.0 * cubic))
    return x * half, slope


def norm_back_in(values, gain, grad):
    rstd = lax.rsqrt(jnp.mean(values * values, axis=-1, keepdims=True) + EPS)
    hat = values * rstd
    scaled = grad * gain
    back = rstd * (scaled - hat * jnp.mean(scaled * hat, axis=-1, keepdims=True))
    return back, jnp.sum(grad * hat, axis=0, keepdims=True)


def next_qkv(ns, place, blocks, tick, wait_weights, order=(0, 1), late=None):
    gather = Gather(ns.copies, place, ns.normed_v, order)
    for stream in range(2):
        if late and stream == 1:
            late()
        gather.start(stream, blocks[stream]())
        tick()
    if late:
        for stream in range(2):
            gather.forward(stream)
            tick()
    wait_weights()
    for stream in range(2):

        def project(side):
            at = gather.pair(stream, side)

            def sink(cols, value):
                ns.qkv_v[at, cols] = value.astype(BF)

            times(lambda: ns.normed_v[at, :], ns.wq_v, 384, sink)

        gather.wait_chip(stream)
        project(place.side)
        if not late:
            gather.forward(stream)
        gather.wait_rest(stream)
        project(1 - place.side)
        tick()
        here = pl.ds(pl.multiple_of(order[stream] * 4 * TOK, 4 * TOK), 4 * TOK)
        ns.copies.store(ns.normed_v.at[here, :], ns.normed.at[here, :])
        ns.copies.store(ns.qkv_v.at[here, :], ns.qkv.at[here, :])


def fwd_mid(ns, place, gain, tick, wait_out, wait_up, wait_down):
    copies = ns.copies
    attn = Scatter(copies, place, ns, ATTN)
    down = Scatter(copies, place, ns, DOWN)
    gather = Gather(copies, place, ns.mlp_v)
    wo, wu, wd = ns.wo_v, ns.wu_v, ns.wd_v
    for stream in range(2):

        def product(side, sink):
            at = gather.pair(stream, side)
            times(lambda: ns.mixed_v[at, :], wo, 512, sink)

        attend(ns, stream)
        tick()
        if stream == 0:
            wait_out()
        attn.push(stream, product)
        tick()
    ns.load.hidden.wait()
    for stream in range(2):
        value = attn.result(stream)
        ns.attn_out_v[stream] = value
        resid = ns.hidden_v[stream].astype(F32) + norm(value, gain(1))
        ns.resid_v[stream] = resid
        gather.start(stream, norm(resid, gain(2)).astype(BF))
        tick()
    wait_up()
    for stream in range(2):

        def expand(side):
            at = gather.pair(stream, side)

            def sink(cols, value):
                active, slope = gelu_both(value)
                ns.active_v[at, cols] = active.astype(BF)
                ns.slope_v[at, cols] = slope.astype(BF)

            times(lambda: ns.mlp_v[at, :], wu, 256, sink)

        gather.wait_chip(stream)
        expand(place.side)
        gather.forward(stream)
        gather.wait_rest(stream)
        expand(1 - place.side)
        if stream == 0:
            wait_down()

        def product(side, sink):
            at = gather.pair(stream, side)
            times(lambda: ns.active_v[at, :], wd, 512, sink)

        down.push(stream, product)
        tick()
    return down


def bwd_mid(ns, place, layer, grads, tick, on_down, on_up, order=(0, 1)):
    copies, gain, base = ns.copies, rows_of(ns, layer), layer * 4
    up = Scatter(copies, place, ns, UP)
    first = Gather(copies, place, ns.down_grad_v)
    second = Gather(copies, place, ns.attn_grad_v)
    wo, wu, wd = ns.wo_v, ns.wu_v, ns.wd_v
    for stream in order:
        grad = grads[stream]()
        ns.grad_v[stream] = grad
        back, four = norm_back_in(ns.down_out_v[stream], gain(3), grad)
        ns.dg_v[base + 3 : base + 4, :] += four
        first.start(stream, back.astype(BF))
        tick()
    for stream in order:

        def shrink(side):
            at = first.pair(stream, side)

            def sink(cols, value):
                slope = ns.slope_v[at, cols].astype(F32)
                ns.up_grad_v[at, cols] = (value * slope).astype(BF)

            times_rows(lambda: ns.down_grad_v[at, :], wd, 512, sink)

        first.wait_chip(stream)
        shrink(place.side)
        first.forward(stream)
        first.wait_rest(stream)
        shrink(1 - place.side)

        def product(side, sink):
            at = first.pair(stream, side)
            times_rows(lambda: ns.up_grad_v[at, :], wu, 512, sink)

        up.push(stream, product)
        tick()
    for stream in order:
        back, three = norm_back_in(ns.resid_v[stream], gain(2), up.result(stream))
        grad = ns.grad_v[stream] + back
        ns.grad_v[stream] = grad
        ns.dg_v[base + 2 : base + 3, :] += three
        back, two = norm_back_in(ns.attn_out_v[stream], gain(1), grad)
        ns.dg_v[base + 1 : base + 2, :] += two
        second.start(stream, back.astype(BF))
        tick()
        if stream == order[0]:
            gram(ns.active_v, ns.down_grad_v, ns.gd_v)
            on_down()
        else:
            gram(ns.mlp_v, ns.up_grad_v, ns.gu_v)
            on_up()
            tick()
    copies.store(ns.grad_v, ns.resid_grad)
    for stream in order:

        def project(side):
            at = second.pair(stream, side)
            ns.mixed_grad_v[at, :] = dot_nt(ns.attn_grad_v[at, :], matrix(wo[...])).astype(BF)

        second.wait_chip(stream)
        project(place.side)
        second.forward(stream)
        second.wait_rest(stream)
        project(1 - place.side)
        tick()
        here = pl.ds(stream * 4 * TOK, 4 * TOK)
        copies.store(ns.mixed_grad_v.at[here, :], ns.mixed_grad.at[here, :])
    gram(ns.mixed_v, ns.attn_grad_v, ns.go_v)


def bwd_head(ns, place, layer, tick, on_qkv, weight_first):
    copies, gain = ns.copies, rows_of(ns, layer)
    qkv = Scatter(copies, place, ns, QKV)
    walk = Gather(copies, place, None)

    def weight():
        ns.load.normed.wait()
        gram(ns.normed_v, ns.qkv_grad_v, ns.gq_v)
        on_qkv()
        tick()

    ns.dk_v[...] = jnp.zeros_like(ns.dk_v)
    ns.dv_v[...] = jnp.zeros_like(ns.dv_v)
    for stream in (1, 0):

        def product(side, sink):
            at = walk.pair(stream, side)
            times_rows(lambda: ns.qkv_grad_v[at, :], ns.wq_v, 512, sink)

        attend_back(ns, stream)
        tick()
        if stream == 1:
            ns.load.wq.wait()
        elif weight_first:
            weight()
        qkv.push(stream, product)
        tick()
    if not weight_first:
        weight()
    ns.load.hidden.wait()
    ns.load.grad.wait()

    def result(stream):
        back, one = norm_back_in(ns.hidden_v[stream].astype(F32), gain(0), qkv.result(stream))
        ns.dg_v[layer * 4 : layer * 4 + 1, :] += one
        return ns.grad_v[stream] + back

    return [functools.partial(result, stream) for stream in range(2)]


def kernel_of(body, reach, inputs, outputs, scratch, slot, remotes, locals_, vmem, flops):
    names = [*inputs, *outputs, *scratch]

    def kernel(*refs):
        ns = types.SimpleNamespace(**dict(zip(names, refs)))
        ns.copies = Copies(*refs[len(names) :])
        announce(reach(Place()))
        ns.load = types.SimpleNamespace()
        for name in inputs:
            if name + HELD in scratch:
                copy = ns.copies.local(getattr(ns, name), getattr(ns, name + HELD))
                setattr(ns.load, name, copy)
        body(ns)
        ns.copies.finish()

    moved = sum(v.size * v.dtype.itemsize for v in [*inputs.values(), *outputs.values()])
    return kernel, dict(
        name=body.__name__,
        out_shape=list(outputs.values()),
        in_specs=[pl.BlockSpec(memory_space=pl.ANY)] * len(inputs),
        out_specs=[pl.BlockSpec(memory_space=pl.ANY)] * len(outputs),
        scratch_shapes=[
            *scratch.values(),
            pltpu.SemaphoreType.DMA((remotes,)),
            pltpu.SemaphoreType.DMA((remotes,)),
            pltpu.SemaphoreType.DMA((locals_,)),
        ],
        compiler_params=pltpu.CompilerParams(
            collective_id=slot, has_side_effects=True, vmem_limit_bytes=vmem << 20
        ),
        cost_estimate=pl.CostEstimate(flops=flops, bytes_accessed=moved, transcendentals=0),
    )


def named(outputs, results):
    return types.SimpleNamespace(**dict(zip(outputs, results)))


def held(*groups):
    merged = {name: value for group in groups for name, value in group.items()}
    return {name + HELD: pltpu.VMEM(value.shape, value.dtype) for name, value in merged.items()}


def struct(shape, dtype):
    return jax.ShapeDtypeStruct(shape, dtype)


def rows_of(ns, layer):
    return lambda index, level=layer: ns.gains_v[level * 4 + index : level * 4 + index + 1, :]


def quarter_of(ns, place, weight, layer, target):
    rows = weight.shape[1] // 4
    at = pl.ds(pl.multiple_of(place.rep * rows, rows), rows)
    return ns.copies.local(weight.at[layer, at, :], target)


def arrange(quarter, dealt, groups):
    unit = quarter.shape[1] // (groups * 4)
    for t in range(4):
        for k in range(groups):
            start = (k * 4 + t) * unit
            dealt[t, :, k * unit : (k + 1) * unit] = quarter[:, start : start + unit]


def by_rows(ref, place):
    return lambda half, a, b: ref.at[1 - place.upper, a, b, half]


def by_columns(ref):
    return lambda half, a, b: ref.at[half, :, a, b]


def start_kernel(block, gain_part, w_qkv, w_up, w_out):
    width, part = block.shape[2], w_qkv.shape[2] // 4
    units = w_up.shape[2] // 4
    length, rows = 8 * TOK, width // 32
    inputs = dict(block=block, gain_part=gain_part, w_qkv=w_qkv, w_up=w_up, w_out=w_out)
    gains = struct((gain_part.shape[0], width), F32)
    hidden = struct(block.shape, BF)
    normed = struct((length, width), BF)
    qkv = struct((length, part), BF)
    wq = struct((2, 4, 2, 2, rows, part), BF)
    outputs = dict(
        hidden=hidden,
        gains=gains,
        normed=normed,
        qkv=qkv,
        wq=wq,
        part_u=struct((2, 4, rows, units), BF),
        half_o=struct(w_out.shape[1:], BF),
    )
    kept = dict(
        half_o=struct(w_out.shape[1:], BF),
        hidden=hidden,
        gains=gains,
        normed=normed,
        qkv=qkv,
        wq=wq,
        quarter_q=struct((rows, 4 * part), BF),
        quarter_u=struct((rows, 4 * units), BF),
        deal_q=struct((4, rows, part), BF),
        deal_u=struct((4, rows, units), BF),
    )
    scratch = held(kept)

    def start(ns):
        place, copies = Place(), ns.copies
        upper, y, x = place.upper, place.y, place.x
        columns = pl.ds(pl.multiple_of(place.grp * TOK, TOK), TOK)
        line = [place.line(offset)[0] for offset in range(1, 8)]
        quarter_q = quarter_of(ns, place, ns.w_qkv, 0, ns.quarter_q_v)
        quarter_u = quarter_of(ns, place, ns.w_up, 0, ns.quarter_u_v)
        kept = copies.local(ns.block.at[upper], ns.hidden_v.at[upper])
        gain_own = copies.local(ns.gain_part, ns.gains_v.at[:, columns])
        quarter_q.wait()
        arrange(ns.quarter_q_v, ns.deal_q_v, 6)
        meet(with_line(place))
        gain_rest = [copies.remote(ns.gain_part, ns.gains_v.at[:, columns], at) for at in line]
        wq_dealt = deal(copies, place, ns.deal_q_v, ns.wq_v.at[upper, place.t, y, x])
        next(wq_dealt)
        next(wq_dealt)
        brought = copies.remote(ns.block.at[1 - upper], ns.hidden_v.at[upper], place.far)
        out_in = copies.remote(ns.w_out.at[0, y, x], ns.half_o_v.at[y, x], place.far)
        wq_spread = spread(copies, place, by_columns(ns.wq_v))
        out_spread = spread(copies, place, lambda half, a, b: ns.half_o_v.at[a, b, half])
        up_dealt = deal(copies, place, ns.deal_u_v, ns.part_u.at[upper, place.t])
        quarter_u.wait()
        arrange(ns.quarter_u_v, ns.deal_u_v, 2)
        next(up_dealt)
        kept.wait()
        gain_own.wait()
        for copy in gain_rest:
            copy.wait_recv()

        def late():
            next(wq_spread)
            brought.wait_recv()
            copies.store(ns.hidden_v, ns.hidden)

        def out_arrived():
            out_in.wait_recv()
            next(out_spread)

        def wait_weights():
            next(wq_spread)
            copies.store(ns.wq_v, ns.wq)

        copies.store(ns.gains_v, ns.gains)
        order = (upper, 1 - upper)
        blocks = [
            functools.partial(
                lambda s: norm(ns.hidden_v[s].astype(F32), ns.gains_v[0:1, :]).astype(BF), stream
            )
            for stream in order
        ]
        plan = Plan(
            [stages(wq_dealt), stages(wq_spread)],
            [stages(up_dealt)],
            [out_arrived],
            [stages(out_spread)],
        )
        next_qkv(ns, place, blocks, plan.tick, wait_weights, order, late)
        next(out_spread)
        copies.store(ns.half_o_v, ns.half_o)
        next(up_dealt)

    flops = 2 * length * width * part
    kernel, options = kernel_of(start, with_line, inputs, outputs, scratch, 0, 48, 64, 60, flops)
    results = pl.pallas_call(kernel, **options)(*inputs.values())
    return named(outputs, results)


def forward_kernel(begun, w_qkv, w_up, w_down, w_out):
    hidden, gains = begun.hidden, begun.gains
    length, part = begun.qkv.shape
    width, mixed_width = hidden.shape[2], part // 3
    units, rows = w_up.shape[2] // 4, width // 32
    inputs = dict(
        qkv_in=begun.qkv, hidden=hidden, gains=gains, w_qkv=w_qkv, w_up=w_up, w_down=w_down,
        w_out=w_out, part_u=begun.part_u, half_o=begun.half_o,
    )
    blocks = struct((2, TOK, width), F32)
    wide = struct((length, width), BF)
    next_u, next_o = struct((2, 4, rows, units), BF), struct((2, *w_out.shape[1:]), BF)
    outputs = dict(
        mixed=struct((length, mixed_width), BF),
        lse=struct((length, 128), F32),
        attn_out=blocks,
        resid=blocks,
        mlp=wide,
        active=struct((length, units), BF),
        slope=struct((length, units), BF),
        down_out=blocks,
        hidden_out=blocks,
        normed=wide,
        qkv=struct((length, part), BF),
        wu=struct((2, 4, 2, 2, rows, units), BF),
        wd=struct((2, *w_down.shape[1:]), BF),
        wo=next_o,
        wq=struct((2, 4, 2, 2, rows, part), BF),
    )
    kept = dict(
        qkv_in=begun.qkv,
        hidden=hidden,
        gains=gains,
        quarter_q=struct((rows, 4 * part), BF),
        quarter_u=struct((rows, 4 * units), BF),
        deal_q=struct((4, rows, part), BF),
        deal_u=struct((4, rows, units), BF),
    )
    scratch = held(outputs, kept)
    outputs = dict(outputs, next_u=next_u, next_o=next_o)
    scratch |= scatter_scratch(ATTN, width) | scatter_scratch(DOWN, width)

    def forward(ns):
        place, copies = Place(), ns.copies
        upper, t, y, x = place.upper, place.t, place.y, place.x
        half_o = copies.local(ns.half_o, ns.wo_v.at[1 - upper])
        part_u = copies.local(ns.part_u, ns.wu_v.at[:, :, y, x])
        quarter_q = quarter_of(ns, place, ns.w_qkv, 1, ns.quarter_q_v)
        whole_o = copies.local(ns.w_out.at[0], ns.wo_v.at[upper])
        whole_d = copies.local(ns.w_down.at[0], ns.wd_v.at[upper])
        quarter_u = quarter_of(ns, place, ns.w_up, 1, ns.quarter_u_v)
        line = [place.line(offset)[0] for offset in range(1, 8)]
        meet(with_line(place))
        down_in = copies.remote(ns.w_down.at[0, y, x], ns.wd_v.at[upper, y, x], place.far)
        part_u.wait()
        up_spread = spread(copies, place, by_columns(ns.wu_v))
        down_spread = spread(copies, place, by_rows(ns.wd_v, place))
        next(up_spread)
        quarter_q.wait()
        arrange(ns.quarter_q_v, ns.deal_q_v, 6)
        q_deal = deal(copies, place, ns.deal_q_v, ns.wq_v.at[upper, t, y, x])
        next(q_deal)
        next(q_deal)
        q_spread = spread(copies, place, by_columns(ns.wq_v))
        u_deal = deal(copies, place, ns.deal_u_v, ns.next_u.at[upper, t])
        o_spread = spread(copies, place, by_rows(ns.next_o, place))
        rest = []

        def out_part():
            rest.append(copies.remote(ns.w_out.at[1, y, x], ns.next_o.at[upper, y, x], place.far))

        def deal_up():
            quarter_u.wait()
            arrange(ns.quarter_u_v, ns.deal_u_v, 2)
            next(u_deal)
            next(u_deal)

        def down_arrived():
            down_in.wait_recv()
            next(down_spread)

        def out_arrived():
            rest[0].wait_recv()
            next(o_spread)

        plan = Plan(
            [],
            [],
            [stages(up_spread)],
            [deal_up],
            [down_arrived],
            [stages(down_spread), out_part],
            [stages(q_deal), stages(q_spread)],
            [stages(q_spread)],
            [out_arrived],
            [],
            [stages(o_spread)],
            [stages(o_spread)],
        )
        ns.load.qkv_in.wait()
        ns.load.gains.wait()
        gain = rows_of(ns, 0)

        def wait_out():
            half_o.wait()
            whole_o.wait()
            copies.store(ns.wo_v, ns.wo)

        def wait_down():
            next(down_spread)
            whole_d.wait()
            copies.store(ns.wu_v, ns.wu)
            copies.store(ns.wd_v, ns.wd)

        def wait_next():
            next(q_spread)
            copies.store(ns.wq_v, ns.wq)

        down = fwd_mid(ns, place, gain, plan.tick, wait_out, lambda: next(up_spread), wait_down)
        copies.store(ns.mixed_v, ns.mixed)
        copies.store(ns.lse_v, ns.lse)
        copies.store(ns.attn_out_v, ns.attn_out)
        copies.store(ns.resid_v, ns.resid)
        copies.store(ns.mlp_v, ns.mlp)
        copies.store(ns.active_v, ns.active)
        copies.store(ns.slope_v, ns.slope)

        def block(stream):
            value = down.result(stream)
            ns.down_out_v[stream] = value
            hidden_out = ns.resid_v[stream] + norm(value, gain(3))
            ns.hidden_out_v[stream] = hidden_out
            return norm(hidden_out, gain(0, 1)).astype(BF)

        blocks = [functools.partial(block, stream) for stream in range(2)]
        next_qkv(ns, place, blocks, plan.tick, wait_next)
        copies.store(ns.down_out_v, ns.down_out)
        copies.store(ns.hidden_out_v, ns.hidden_out)
        plan.drain()
        next(u_deal)

    flops = 2 * length * width * (mixed_width + 2 * units + part)
    kernel, options = kernel_of(forward, with_line, inputs, outputs, scratch, 1, 80, 64, 62, flops)
    results = pl.pallas_call(kernel, **options)(*inputs.values())
    return named(outputs, results)


def turn_kernel(lower, gains, w_down, w_out, cotangent):
    hidden = lower.hidden_out
    width = hidden.shape[2]
    length, part = lower.qkv.shape
    mixed_width = part // 3
    inputs = dict(
        qkv_in=lower.qkv, gains=gains, hidden=hidden, cot=cotangent,
        part_u=lower.next_u, part_o=lower.next_o, w_down=w_down, w_out=w_out,
    )
    rows, units = lower.next_u.shape[2:]
    blocks = struct((2, TOK, width), F32)
    outputs = dict(
        out=struct((2, TOK, width), BF),
        lse=struct((length, 128), F32),
        mixed_grad=struct((length, mixed_width), BF),
        gd=by_device((units, width), 1),
        gu=by_device((width, units), 4),
        go=by_device((mixed_width, width), 1),
        dg=struct((8, width), F32),
    )
    kept = dict(
        qkv_in=lower.qkv,
        hidden=hidden,
        gains=gains,
        cot=cotangent,
        wd=struct((2, *w_down.shape[1:]), BF),
        wo=lower.next_o,
        wu=struct((2, 4, 2, 2, rows, units), BF),
        mixed=struct((length, mixed_width), BF),
        attn_out=blocks,
        resid=blocks,
        grad=blocks,
        mlp=struct((length, width), BF),
        active=struct((length, units), BF),
        slope=struct((length, units), BF),
        up_grad=struct((length, units), BF),
        down_out=blocks,
        down_grad=struct((length, width), BF),
        attn_grad=struct((length, width), BF),
    )
    scratch = held(outputs, kept)
    outputs |= dict(resid_grad=blocks)
    for name in (ATTN, DOWN, UP):
        scratch |= scatter_scratch(name, width)
    scratch |= reduce_scratch(D1, 1, units // 8, width, 1)

    def turn(ns):
        place, copies = Place(), ns.copies
        upper, y, x = place.upper, place.y, place.x
        part_u = copies.local(ns.part_u, ns.wu_v.at[:, :, y, x])
        part_o = copies.local(ns.part_o.at[1 - upper], ns.wo_v.at[1 - upper])
        whole_o = copies.local(ns.w_out.at[1], ns.wo_v.at[upper])
        whole_d = copies.local(ns.w_down.at[1], ns.wd_v.at[upper])
        meet(with_few(place))
        down_in = copies.remote(ns.w_down.at[1, y, x], ns.wd_v.at[upper, y, x], place.far)
        part_u.wait()
        up_spread = spread(copies, place, by_columns(ns.wu_v))
        down_spread = spread(copies, place, by_rows(ns.wd_v, place))
        next(up_spread)
        ns.load.qkv_in.wait()
        far_in = []

        def bring():
            ns.load.cot.wait()
            far_in.append(copies.remote(ns.cot.at[1 - upper], ns.cot_far_v, place.far))

        def down_arrived():
            down_in.wait_recv()
            next(down_spread)

        plan = Plan(
            [],
            [],
            [stages(up_spread)],
            [],
            [down_arrived],
            [stages(down_spread), bring],
        )
        ns.load.gains.wait()
        ns.dg_v[...] = jnp.zeros_like(ns.dg_v)
        gain = rows_of(ns, 1)

        def wait_out():
            part_o.wait()
            whole_o.wait()

        def wait_down():
            next(down_spread)
            whole_d.wait()

        down = fwd_mid(
            ns, place, gain, plan.tick, wait_out, lambda: next(up_spread), wait_down
        )
        copies.store(ns.lse_v, ns.lse)
        far_in[0].wait_recv()

        def grad(stream):
            value = down.result(stream)
            ns.down_out_v[stream] = value
            own = jnp.where(upper == stream, ns.cot_v[stream], ns.cot_far_v[...])
            return own.astype(F32)

        def finish():
            for stream in range(2):
                out = ns.resid_v[stream] + norm(ns.down_out_v[stream], gain(3))
                ns.out_v[stream] = out.astype(BF)
            copies.store(ns.out_v, ns.out)

        d_first, unused = reduce_rep(copies, place, ns.gd_v, ns, D1)
        plan = Plan(
            [],
            [finish],
            [],
            [],
            [],
        )
        grads = [functools.partial(grad, stream) for stream in range(2)]
        store_up = functools.partial(copies.store, ns.gu_v, ns.gu)
        bwd_mid(ns, place, 1, grads, plan.tick, stages(d_first), store_up)
        copies.store(ns.go_v, ns.go)
        copies.store(ns.dg_v, ns.dg)
        next(d_first)
        copies.store(ns.gd_v, ns.gd)

    scratch["cot_far_v"] = pltpu.VMEM((TOK, width), BF)
    flops = 6 * length * width * (mixed_width + 2 * units)
    kernel, options = kernel_of(turn, with_few, inputs, outputs, scratch, 2, 64, 64, 63, flops)
    results = pl.pallas_call(kernel, **options)(*inputs.values())
    return named(outputs, results)


def backward_kernel(begun, lower, turned):
    wo, wu, wd, wq = (matrix(value) for value in (lower.wo, lower.wu, lower.wd, lower.wq))
    width, units = wu.shape
    length, part = lower.qkv.shape
    mixed_width = wo.shape[0]
    inputs = dict(
        gu=turned.gu, d1=turned.gd, o1=turned.go, qkv_in=lower.qkv, lse=turned.lse,
        mixed_grad=turned.mixed_grad, dg=turned.dg, gains=begun.gains, wq=wq, normed=lower.normed,
        hidden=lower.hidden_out, grad=turned.resid_grad, down_out=lower.down_out, wd=wd,
        slope=lower.slope, wu=wu, active=lower.active, mlp=lower.mlp, resid=lower.resid,
        attn_out=lower.attn_out, wo=wo, mixed=lower.mixed,
    )
    blocks = struct((2, TOK, width), F32)
    kept = dict(
        gq=by_device(wq.shape, 4),
        gd=by_device(wd.shape, 1),
        gu=by_device(wu.shape, 4),
        go=by_device(wo.shape, 1),
        qkv_grad=struct(lower.qkv.shape, BF),
        dk=struct((length, mixed_width), F32),
        dv=struct((length, mixed_width), F32),
        down_grad=struct((length, width), BF),
        attn_grad=struct((length, width), BF),
    )
    outputs = dict(
        resid_grad=blocks,
        mixed_out=struct((length, mixed_width), BF),
        gd=kept["gd"],
        up_out=kept["gu"],
        go=kept["go"],
        dg_out=turned.dg,
        full_d=struct((2, 2, 2, units // 16, width), BF),
        full_u=struct((2, 2, width // 32, 4 * units), BF),
        full_q=struct((2, 2, width // 32, 4 * part), BF),
        full_o=struct((2, 2, 2, mixed_width // 16, width), BF),
    )
    loaded = dict(inputs)
    del loaded["d1"]
    scratch = held(loaded, kept)
    for name in (QKV, UP):
        scratch |= scatter_scratch(name, width)
    rows = width // 32
    for name, count, high, wide, steps in (
        (D1, 1, units // 8, width, 2),
        (U1, 4, rows, units, 3),
        (Q1, 4, rows, part, 3),
        (O1, 1, mixed_width // 8, width, 3),
    ):
        scratch |= finish_scratch(name, count, high, wide)
        scratch |= reduce_scratch(name, count, high, wide, steps)
    scratch |= reduce_scratch(D0, 1, units // 8, width, 1)

    def backward(ns):
        place, copies = Place(), ns.copies
        ns.up_grad_v = ns.normed_v
        line = [place.line(offset)[0] for offset in range(1, 8)]
        meet(with_line(place))
        unused, d1_second = reduce_rep(copies, place, ns.d1, ns, D1)
        u1_first, u1_second = reduce_rep(copies, place, ns.gu_v, ns, U1)
        o1_first, o1_second = reduce_rep(copies, place, ns.o1_v, ns, O1)
        q1_first, q1_second = reduce_rep(copies, place, ns.gq_v, ns, Q1)
        d0_first, unused = reduce_rep(copies, place, ns.gd_v, ns, D0)
        d1_line = line_rows(copies, place, ns, D1)
        u1_line = line_columns(copies, place, ns, U1)
        o1_line = line_rows(copies, place, ns, O1)
        q1_line = line_columns(copies, place, ns, Q1)
        d1_whole = whole_rows(copies, place, ns, D1, ns.full_d)
        u1_whole = whole_columns(copies, place, ns, U1, ns.full_u, 2)
        q1_whole = whole_columns(copies, place, ns, Q1, ns.full_q, 6)
        o1_whole = whole_rows(copies, place, ns, O1, ns.full_o)
        next(d1_second)
        ns.load.gu.wait()
        next(u1_first)
        ns.load.o1.wait()
        ns.load.qkv_in.wait()
        ns.load.lse.wait()
        ns.load.mixed_grad.wait()
        ns.load.dg.wait()
        plan = Plan(
            [stages(d1_second), stages(d1_line)],
            [],
            [stages(u1_first), stages(u1_second), stages(o1_first)],
            [],
            [],
            [stages(u1_second), stages(u1_line), stages(d1_line), stages(d1_whole)],
            [stages(o1_first), stages(o1_second), stages(q1_first), stages(q1_second)],
            [stages(d1_whole), stages(u1_line), stages(u1_whole)]
            + [stages(q1_second), stages(q1_line)],
            [stages(o1_second), stages(o1_line)],
            [stages(d1_whole), stages(u1_whole), stages(q1_line), stages(q1_whole)],
            [],
            [stages(o1_line), stages(o1_whole), stages(q1_whole)],
            [stages(u1_whole)],
            [stages(d0_first), stages(o1_whole)],
        )
        ns.load.gains.wait()
        grads = bwd_head(ns, place, 1, plan.tick, stages(q1_first), False)
        for copy in (ns.load.down_out, ns.load.wd, ns.load.slope, ns.load.wu, ns.load.active):
            copy.wait()
        for copy in (ns.load.mlp, ns.load.resid, ns.load.attn_out, ns.load.wo, ns.load.mixed):
            copy.wait()
        ns.mixed_grad = ns.mixed_out
        store_up = functools.partial(copies.store, ns.gu_v, ns.up_out)
        bwd_mid(ns, place, 0, grads, plan.tick, stages(d0_first), store_up, (1, 0))
        plan.drain()
        copies.store(ns.go_v, ns.go)
        copies.store(ns.gd_v, ns.gd)
        copies.store(ns.dg_v, ns.dg_out)
        next(q1_whole)
        next(o1_whole)

    flops = 6 * length * width * (mixed_width + 2 * units) + 4 * length * width * part
    kernel, options = kernel_of(backward, with_line, inputs, outputs, scratch, 3, 128, 128, 63, flops)
    results = pl.pallas_call(kernel, **options)(*inputs.values())
    return named(outputs, results)


def last_kernel(begun, lower, turned, back):
    wq = matrix(begun.wq)
    width, part = wq.shape
    length, mixed_width = back.mixed_out.shape
    units, rows = back.up_out.shape[-1], width // 32
    inputs = dict(
        u0=back.up_out, d0=back.gd, o0=back.go, qkv_in=begun.qkv, lse=lower.lse,
        mixed_grad=back.mixed_out, dg=back.dg_out, gains=begun.gains, normed=begun.normed, wq=wq,
        hidden=begun.hidden, grad=back.resid_grad, second=turned.out,
    )
    outputs = dict(
        out=struct((2, TOK, width), BF),
        block_out=struct((2, TOK, width), BF),
        gain_grad=struct((8, TOK), F32),
        full_d=struct(back.full_d.shape, BF),
        full_u=struct(back.full_u.shape, BF),
        full_q=struct(back.full_q.shape, BF),
        full_o=struct(back.full_o.shape, BF),
    )
    kept = dict(
        out=outputs["out"],
        gq=by_device(wq.shape, 4),
        qkv_grad=struct(begun.qkv.shape, BF),
        dk=struct((length, mixed_width), F32),
        dv=struct((length, mixed_width), F32),
        dg_line=struct((8, 8, TOK), F32),
        dg_pass=struct((5, 8, TOK), F32),
    )
    loaded = dict(inputs)
    del loaded["d0"]
    scratch = held(loaded, kept)
    scratch |= scatter_scratch(QKV, width)
    for name, count, high, wide, steps in (
        (D0, 1, units // 8, width, 2),
        (U0, 4, rows, units, 3),
        (Q0, 4, rows, part, 3),
        (O0, 1, mixed_width // 8, width, 3),
    ):
        scratch |= reduce_scratch(name, count, high, wide, steps)
        scratch |= finish_scratch(name, count, high, wide)

    def last(ns):
        place, copies = Place(), ns.copies
        line = [place.line(offset)[0] for offset in range(1, 8)]
        meet(with_line(place))
        unused, d0_second = reduce_rep(copies, place, ns.d0, ns, D0)
        u0_first, u0_second = reduce_rep(copies, place, ns.u0_v, ns, U0)
        o0_first, o0_second = reduce_rep(copies, place, ns.o0_v, ns, O0)
        q0_first, q0_second = reduce_rep(copies, place, ns.gq_v, ns, Q0)
        d0_line = line_rows(copies, place, ns, D0)
        o0_line = line_rows(copies, place, ns, O0)
        u0_line = line_columns(copies, place, ns, U0)
        q0_line = line_columns(copies, place, ns, Q0)
        d0_whole = whole_rows(copies, place, ns, D0, ns.full_d)
        o0_whole = whole_rows(copies, place, ns, O0, ns.full_o)
        u0_whole = whole_columns(copies, place, ns, U0, ns.full_u, 2)
        q0_whole = whole_columns(copies, place, ns, Q0, ns.full_q, 6)
        upper = place.upper
        second = copies.remote(ns.second.at[1 - upper], ns.block_out.at[upper], place.far)
        next(d0_second)
        ns.load.u0.wait()
        next(u0_first)
        ns.load.qkv_in.wait()
        ns.load.lse.wait()
        ns.load.mixed_grad.wait()
        ns.load.dg.wait()
        ns.load.o0.wait()
        plan = Plan(
            [stages(d0_second), stages(d0_line)],
            [],
            [stages(u0_first), stages(u0_second)],
            [stages(d0_line), stages(d0_whole)],
            [],
        )
        ns.load.gains.wait()
        grads = bwd_head(ns, place, 0, plan.tick, stages(q0_first), True)
        ns.load.second.wait()
        copies.store(ns.second_v.at[upper], ns.block_out.at[upper])
        ns.out_v[1] = grads[1]().astype(BF)
        for task in (u0_second, u0_line, q0_first, q0_second, o0_first, d0_whole):
            next(task)
        ns.out_v[0] = grads[0]().astype(BF)
        copies.store(ns.out_v.at[upper], ns.out.at[upper])
        gain_grad = gain_sum(ns, copies, place)
        for task in (
            gain_grad, q0_second, q0_line, o0_first, o0_second, u0_line, u0_whole, d0_whole,
            gain_grad, o0_second, o0_line,
        ):
            next(task)
        moved = copies.remote(ns.out_v.at[1 - upper], ns.out.at[upper], place.far)
        for task in (
            u0_whole, q0_line, q0_whole, o0_line, o0_whole, gain_grad, u0_whole, q0_whole,
            o0_whole, gain_grad, q0_whole, o0_whole,
        ):
            next(task)
        moved.wait_recv()
        second.wait_recv()

    flops = 4 * length * width * part
    kernel, options = kernel_of(last, with_line, inputs, outputs, scratch, 4, 128, 128, 60, flops)
    results = pl.pallas_call(kernel, **options)(*inputs.values())
    return named(outputs, results)


def widen(pairs):
    flat = [value for group in pairs for value in group]
    outs = [struct((len(group), *group[0].shape), F32) for group in pairs]

    def finish(*refs):
        sources, targets = refs[: len(flat)], refs[len(flat) : len(flat) + len(outs)]
        low, wide = refs[len(flat) + len(outs) :][: len(flat)], refs[-len(flat) - 2 : -2]
        sem_in, sem_out = refs[-2:]
        slots = [(g, n) for g, group in enumerate(pairs) for n in range(len(group))]
        loads = [pltpu.make_async_copy(sources[i], low[i], sem_in.at[i]) for i in range(len(flat))]
        for copy in loads:
            copy.start()
        stores = []
        for i, (g, n) in enumerate(slots):
            loads[i].wait()

            def step(index):
                at = tile_of(index, 32)
                wide[i][at, :] = low[i][at, :].astype(F32)

            loop(low[i].shape[0] // 32, step)
            stores.append(pltpu.make_async_copy(wide[i], targets[g].at[n], sem_out.at[i]))
            stores[-1].start()
        for copy in stores:
            copy.wait()

    size = sum(value.size for value in flat)
    return pl.pallas_call(
        finish,
        name=finish.__name__,
        out_shape=outs,
        in_specs=[pl.BlockSpec(memory_space=pl.ANY)] * len(flat),
        out_specs=[pl.BlockSpec(memory_space=pl.ANY)] * len(outs),
        scratch_shapes=[
            *(pltpu.VMEM(value.shape, BF) for value in flat),
            *(pltpu.VMEM(value.shape, F32) for value in flat),
            pltpu.SemaphoreType.DMA((len(flat),)),
            pltpu.SemaphoreType.DMA((len(flat),)),
        ],
        compiler_params=pltpu.CompilerParams(vmem_limit_bytes=63 << 20),
        cost_estimate=pl.CostEstimate(flops=size, bytes_accessed=6 * size, transcendentals=0),
    )(*flat)


def gain_sum(ns, copies, place):
    def columns(grp):
        return pl.ds(pl.multiple_of(grp * TOK, TOK), TOK)

    moved = []
    for offset in range(1, 8):
        device, upper, t = place.line(offset)
        source = ns.dg_v.at[:, columns(upper * 4 + t)]
        moved.append(copies.remote(source, ns.dg_line_v.at[place.grp], device))
    ns.dg_line_v[place.grp] = ns.dg_v[:, columns(place.grp)]
    yield
    for copy in moved:
        copy.wait_recv()
    ns.dg_pass_v[0] = jnp.sum(ns.dg_line_v[...], axis=0)
    moved = copies.remote(ns.dg_pass_v.at[0], ns.dg_pass_v.at[1], place.along_x)
    yield
    moved.wait_recv()
    ns.dg_pass_v[2] = ns.dg_pass_v[0] + ns.dg_pass_v[1]
    moved = copies.remote(ns.dg_pass_v.at[2], ns.dg_pass_v.at[3], place.along_y)
    yield
    moved.wait_recv()
    ns.dg_pass_v[4] = ns.dg_pass_v[2] + ns.dg_pass_v[3]
    copies.store(ns.dg_pass_v.at[4], ns.gain_grad)
    yield


def body_pairs(block_in, cotangent, w_qkv, w_out, w_up, w_down, norm_gains):
    layers, rows, width = w_out.shape
    hidden_unit = w_down.shape[1]
    gain_part = jnp.transpose(norm_gains.astype(F32), (0, 2, 1)).reshape(layers * 4, rows)
    down_parts = w_down.reshape(layers, 2, 2, 2, hidden_unit // 8, width)
    out_parts = w_out.reshape(layers, 2, 2, 2, rows // 8, width)

    begun = start_kernel(block_in[:, 0], gain_part, w_qkv, w_up, out_parts)
    lower = forward_kernel(begun, w_qkv, w_up, down_parts, out_parts)
    turned = turn_kernel(lower, begun.gains, down_parts, out_parts, cotangent[:, 0])
    back = backward_kernel(begun, lower, turned)
    last = last_kernel(begun, lower, turned, back)

    pairs = (
        (last.full_d, back.full_d),
        (last.full_u, back.full_u),
        (last.full_q, back.full_q),
        (last.full_o, back.full_o),
        (last.out,),
    )
    wide = widen([[matrix(value) for value in group] for group in pairs])
    return (
        last.block_out[:, None],
        wide[4].reshape(block_in.shape),
        wide[2],
        wide[3],
        wide[1],
        wide[0],
        jnp.transpose(last.gain_grad.reshape(layers, 4, rows), (0, 2, 1)),
    )


def norm_apply(values, gains):
    return values * lax.rsqrt(jnp.mean(values * values, axis=-1, keepdims=True) + EPS) * gains


def inner_rows(left, right):
    return lax.dot_general(
        left, right, (((0,), (0,)), ((), ())), preferred_element_type=jnp.float32
    )


def times_trans(left, right):
    return lax.dot_general(
        left, right, (((1,), (1,)), ((), ())), preferred_element_type=jnp.float32
    )


def split_blocks(whole):
    length = whole.shape[0]
    width = min(512, length)
    count = length // width
    return (whole.reshape(count, width, HEADS, HDIM), width, count)


def block_at(blocks, index):
    return lax.dynamic_index_in_dim(blocks, index, 0, keepdims=False)


def key_scores(query, key_block, key_start, query_pos):
    scale = HDIM ** (-0.5)
    scores = (
        jnp.einsum("qhd,khd->hqk", query, key_block, preferred_element_type=jnp.float32) * scale
    )
    key_pos = key_start + jnp.arange(key_block.shape[0], dtype=jnp.int32)
    allowed = key_pos[None, :] <= query_pos[:, None]
    return (scores, allowed[None])


def attend_split(query, keys_all, values_all, query_pos):
    key_blocks, width, count = split_blocks(keys_all)
    value_blocks = split_blocks(values_all)[0]
    row_count = query.shape[0]
    upper = query_pos[row_count - 1] // width + 1

    def total_step(index, carry):
        running, total = carry
        scores, allowed = key_scores(query, block_at(key_blocks, index), index * width, query_pos)
        newest = jnp.maximum(running, jnp.max(jnp.where(allowed, scores, NEGATIVE), axis=-1))
        terms = jnp.where(allowed, jnp.exp(scores - newest[..., None]), 0.0)
        total = total * jnp.exp(running - newest) + jnp.sum(terms, axis=-1)
        return (newest, total)

    start_run = jnp.full((HEADS, row_count), NEGATIVE, jnp.float32)
    start_total = jnp.zeros((HEADS, row_count), jnp.float32)
    running, total = lax.fori_loop(0, upper, total_step, (start_run, start_total))
    log_total = running + jnp.log(total)

    def mix_step(index, accum):
        scores, allowed = key_scores(query, block_at(key_blocks, index), index * width, query_pos)
        probs = jnp.where(allowed, jnp.exp(scores - log_total[..., None]), 0.0)
        return accum + jnp.einsum(
            "hqk,khd->qhd",
            probs.astype(jnp.bfloat16),
            block_at(value_blocks, index),
            preferred_element_type=jnp.float32,
        )

    start_mix = jnp.zeros((row_count, HEADS, HDIM), jnp.float32)
    mixed = lax.fori_loop(0, upper, mix_step, start_mix)
    return (mixed.reshape(row_count, HEADS * HDIM), log_total)


def attend_back_split(query, keys_all, values_all, log_total, out_grad, delta, query_pos):
    key_blocks, width, count = split_blocks(keys_all)
    value_blocks = split_blocks(values_all)[0]
    row_count = query.shape[0]
    upper = query_pos[row_count - 1] // width + 1
    scale = HDIM ** (-0.5)

    def back_step(index, carry):
        query_acc, pieces = carry
        key_block = block_at(key_blocks, index)
        value_block = block_at(value_blocks, index)
        scores, allowed = key_scores(query, key_block, index * width, query_pos)
        probs = jnp.where(allowed, jnp.exp(scores - log_total[..., None]), 0.0)
        prob_grad = jnp.einsum(
            "qhd,khd->hqk", out_grad, value_block, preferred_element_type=jnp.float32
        )
        score_grad = (probs * (prob_grad - delta[..., None])).astype(jnp.bfloat16)
        query_acc = (
            query_acc
            + jnp.einsum("hqk,khd->qhd", score_grad, key_block, preferred_element_type=jnp.float32)
            * scale
        )
        key_grad = (
            jnp.einsum("hqk,qhd->khd", score_grad, query, preferred_element_type=jnp.float32)
            * scale
        )
        value_grad = jnp.einsum(
            "hqk,qhd->khd", probs.astype(jnp.bfloat16), out_grad, preferred_element_type=jnp.float32
        )
        joined = jnp.concatenate(
            [key_grad.reshape(width, HEADS * HDIM), value_grad.reshape(width, HEADS * HDIM)], axis=1
        )
        pieces = lax.dynamic_update_index_in_dim(pieces, joined, index, 0)
        return (query_acc, pieces)

    start_acc = jnp.zeros((row_count, HEADS, HDIM), jnp.float32)
    start_pieces = jnp.zeros((count, width, 2 * HEADS * HDIM), jnp.float32)
    query_grad, pieces = lax.fori_loop(0, upper, back_step, (start_acc, start_pieces))
    return (query_grad.reshape(row_count, HEADS * HDIM), pieces.reshape(-1, pieces.shape[-1]))


def layer_forward(hidden_in, weights, query_pos):
    w_qkv_full, w_out_full, w_up_full, w_down_full, gain_full = weights
    gains_f = gain_full.astype(jnp.float32)
    row_count = hidden_in.shape[0]
    width = w_out_full.shape[1]
    normed = norm_apply(hidden_in, gains_f[:, 0]).astype(jnp.bfloat16)
    qkv_low = jnp.dot(normed, w_qkv_full, preferred_element_type=jnp.float32).astype(jnp.bfloat16)
    query = qkv_low[:, :width]
    keys_all, values_all = (
        lax.all_gather(qkv_low[:, width : 2 * width], "grp", axis=0, tiled=True),
        lax.all_gather(qkv_low[:, 2 * width :], "grp", axis=0, tiled=True),
    )
    mixed, log_total = attend_split(
        query.reshape(row_count, HEADS, HDIM),
        keys_all.reshape(-1, HEADS, HDIM),
        values_all.reshape(-1, HEADS, HDIM),
        query_pos,
    )
    mixed_low = mixed.astype(jnp.bfloat16)
    attn_out = jnp.dot(mixed_low, w_out_full, preferred_element_type=jnp.float32)
    resid = hidden_in + norm_apply(attn_out, gains_f[:, 1])
    mlp_in = norm_apply(resid, gains_f[:, 2]).astype(jnp.bfloat16)
    up_out = jnp.dot(mlp_in, w_up_full, preferred_element_type=jnp.float32)
    active = jax.nn.gelu(up_out).astype(jnp.bfloat16)
    down_out = jnp.dot(active, w_down_full, preferred_element_type=jnp.float32)
    result = resid + norm_apply(down_out, gains_f[:, 3])
    kept = (
        hidden_in,
        normed,
        qkv_low,
        mixed,
        mixed_low,
        log_total,
        attn_out,
        resid,
        mlp_in,
        up_out,
        active,
        down_out,
    )
    return (result, kept)


def layer_backward(grad_out, weights, kept, query_pos):
    w_qkv_full, w_out_full, w_up_full, w_down_full, gain_full = weights
    (
        hidden_in,
        normed,
        qkv_low,
        mixed,
        mixed_low,
        log_total,
        attn_out,
        resid,
        mlp_in,
        up_out,
        active,
        down_out,
    ) = kept
    gains_f = gain_full.astype(jnp.float32)
    row_count = hidden_in.shape[0]
    width = w_out_full.shape[1]
    unused, puller = jax.vjp(norm_apply, down_out, gains_f[:, 3])
    down_grad, gain_four = puller(grad_out)
    down_low = down_grad.astype(jnp.bfloat16)
    w_down_grad = inner_rows(active, down_low)
    active_grad = times_trans(down_low, w_down_full)
    unused, puller = jax.vjp(jax.nn.gelu, up_out)
    up_low = puller(active_grad)[0].astype(jnp.bfloat16)
    w_up_grad = inner_rows(mlp_in, up_low)
    mlp_grad = times_trans(up_low, w_up_full)
    unused, puller = jax.vjp(norm_apply, resid, gains_f[:, 2])
    resid_part, gain_three = puller(mlp_grad)
    resid_grad = grad_out + resid_part
    unused, puller = jax.vjp(norm_apply, attn_out, gains_f[:, 1])
    attn_grad, gain_two = puller(resid_grad)
    attn_low = attn_grad.astype(jnp.bfloat16)
    w_out_grad = inner_rows(mixed_low, attn_low)
    mixed_grad = times_trans(attn_low, w_out_full).astype(jnp.bfloat16)
    keys_all, values_all = (
        lax.all_gather(qkv_low[:, width : 2 * width], "grp", axis=0, tiled=True),
        lax.all_gather(qkv_low[:, 2 * width :], "grp", axis=0, tiled=True),
    )
    delta = jnp.sum(
        (mixed_grad.astype(jnp.float32) * mixed).reshape(row_count, HEADS, HDIM), axis=-1
    ).T
    query_low = qkv_low[:, :width]
    query_grad, key_value_terms = attend_back_split(
        query_low.reshape(row_count, HEADS, HDIM),
        keys_all.reshape(-1, HEADS, HDIM),
        values_all.reshape(-1, HEADS, HDIM),
        log_total,
        mixed_grad.reshape(row_count, HEADS, HDIM),
        delta,
        query_pos,
    )
    key_value_grad = lax.psum_scatter(
        key_value_terms.astype(jnp.bfloat16), "grp", scatter_dimension=0, tiled=True
    ).astype(jnp.float32)
    qkv_grad = jnp.concatenate([query_grad, key_value_grad], axis=1).astype(jnp.bfloat16)
    w_qkv_grad = inner_rows(normed, qkv_grad)
    normed_grad = times_trans(qkv_grad, w_qkv_full)
    unused, puller = jax.vjp(norm_apply, hidden_in, gains_f[:, 0])
    input_part, gain_one = puller(normed_grad)
    gain_grad = jnp.stack([gain_one, gain_two, gain_three, gain_four], axis=1)
    return (resid_grad + input_part, (w_qkv_grad, w_out_grad, w_up_grad, w_down_grad, gain_grad))


def body_general(block_in, cotangent, w_qkv, w_out, w_up, w_down, norm_gains):
    layer_count = w_qkv.shape[0]
    micro_count = block_in.shape[0]
    row_count = block_in.shape[2]
    query_pos = lax.axis_index("grp") * row_count + jnp.arange(row_count, dtype=jnp.int32)
    totals = [None] * layer_count
    outputs = []
    input_grads = []
    for micro_idx in range(micro_count):
        hidden = block_in[micro_idx, 0].astype(jnp.float32)
        saved = []
        for layer_idx in range(layer_count):
            hidden, kept = layer_forward(
                hidden,
                (
                    lax.all_gather(w_qkv[layer_idx], "grp", axis=0, tiled=True),
                    lax.all_gather(w_out[layer_idx], "grp", axis=0, tiled=True),
                    lax.all_gather(w_up[layer_idx], "grp", axis=0, tiled=True),
                    lax.all_gather(w_down[layer_idx], "grp", axis=0, tiled=True),
                    lax.all_gather(norm_gains[layer_idx], "grp", axis=0, tiled=True),
                ),
                query_pos,
            )
            saved.append(kept)
        outputs.append(hidden.astype(jnp.bfloat16))
        grad_flow = cotangent[micro_idx, 0].astype(jnp.float32)
        for layer_idx in reversed(range(layer_count)):
            grad_flow, parts = layer_backward(
                grad_flow,
                (
                    lax.all_gather(w_qkv[layer_idx], "grp", axis=0, tiled=True),
                    lax.all_gather(w_out[layer_idx], "grp", axis=0, tiled=True),
                    lax.all_gather(w_up[layer_idx], "grp", axis=0, tiled=True),
                    lax.all_gather(w_down[layer_idx], "grp", axis=0, tiled=True),
                    lax.all_gather(norm_gains[layer_idx], "grp", axis=0, tiled=True),
                ),
                saved[layer_idx],
                query_pos,
            )
            if totals[layer_idx] is None:
                totals[layer_idx] = parts
            else:
                totals[layer_idx] = tuple(
                    (left + right for left, right in zip(totals[layer_idx], parts))
                )
        input_grads.append(grad_flow)
    reduced = []
    for layer_idx in range(layer_count):
        accum = totals[layer_idx]
        shards = (
            lax.psum_scatter(
                accum[0].astype(jnp.bfloat16), "grp", scatter_dimension=0, tiled=True
            ).astype(jnp.float32),
            lax.psum_scatter(
                accum[1].astype(jnp.bfloat16), "grp", scatter_dimension=0, tiled=True
            ).astype(jnp.float32),
            lax.psum_scatter(
                accum[2].astype(jnp.bfloat16), "grp", scatter_dimension=0, tiled=True
            ).astype(jnp.float32),
            lax.psum_scatter(
                accum[3].astype(jnp.bfloat16), "grp", scatter_dimension=0, tiled=True
            ).astype(jnp.float32),
            lax.psum_scatter(
                accum[4].astype(jnp.bfloat16), "grp", scatter_dimension=0, tiled=True
            ).astype(jnp.float32),
        )
        reduced.append(
            (
                lax.psum(shards[0].astype(jnp.bfloat16), "rep").astype(jnp.float32),
                lax.psum(shards[1].astype(jnp.bfloat16), "rep").astype(jnp.float32),
                lax.psum(shards[2].astype(jnp.bfloat16), "rep").astype(jnp.float32),
                lax.psum(shards[3].astype(jnp.bfloat16), "rep").astype(jnp.float32),
                lax.psum(shards[4].astype(jnp.bfloat16), "rep").astype(jnp.float32),
            )
        )
    block_out = jnp.stack(outputs)[:, None]
    block_in_grad = jnp.stack(input_grads)[:, None]
    stacked = [
        jnp.stack([reduced[layer_idx][member] for layer_idx in range(layer_count)])
        for member in range(5)
    ]
    return (block_out, block_in_grad, stacked[0], stacked[1], stacked[2], stacked[3], stacked[4])


def solution(mesh):
    rep_size, grp_size = mesh.shape["rep"], mesh.shape["grp"]

    def body(block_in, cotangent, w_qkv, w_out, w_up, w_down, norm_gains):
        sizes = (rep_size, grp_size, block_in.shape[0], w_qkv.shape[0], block_in.shape[2])
        fits = sizes == (4, 8, 2, 2, TOK)
        chosen = body_pairs if fits else body_general
        return chosen(block_in, cotangent, w_qkv, w_out, w_up, w_down, norm_gains)

    tokens = P(None, "rep", "grp", None)
    rows = P(None, "grp", None)
    return jax.shard_map(
        body,
        mesh=mesh,
        in_specs=(tokens, tokens, rows, rows, rows, rows, rows),
        out_specs=(tokens, tokens, rows, rows, rows, rows, rows),
        check_vma=False,
    )
```

```python
import functools
import types

import jax
import jax.numpy as jnp
from jax import lax
from jax.experimental import pallas as pl
from jax.experimental.pallas import tpu as pltpu
from jax.sharding import PartitionSpec as P

HEADS = 16
HDIM = 64
EPS = 1e-06
NEGATIVE = -1e30
BF = jnp.bfloat16
REP, GRP = "rep", "grp"
F32 = jnp.float32


def dot(left, right):
    return jnp.dot(left, right, preferred_element_type=F32)


def dot_tn(left, right):
    return lax.dot_general(left, right, (((0,), (0,)), ((), ())), preferred_element_type=F32)


def dot_nt(left, right):
    return lax.dot_general(left, right, (((1,), (1,)), ((), ())), preferred_element_type=F32)


def norm(values, gain):
    return values * lax.rsqrt(jnp.mean(values * values, axis=-1, keepdims=True) + EPS) * gain


def head_mask(width, head):
    lanes = lax.broadcasted_iota(jnp.int32, (1, width), 1)
    return (lanes // HDIM) == head


def causal_scores(query, keys, below, start):
    scores = dot_nt(query, keys)
    last = jnp.where(below, scores[:, start:], NEGATIVE)
    return jnp.concatenate([scores[:, :start], last], axis=1) if start else last


def attend(ns, stream, block=256):
    length, width = ns.mixed_v.shape
    qkv_ref, lse_ref, sum_ref = ns.qkv_in_v, ns.lse_v, ns.terms_own.at[stream]
    row = lax.broadcasted_iota(jnp.int32, (block, block), 0)
    col = lax.broadcasted_iota(jnp.int32, (block, block), 1)
    below = col <= row
    zero = jnp.zeros((), BF)
    lane = lax.broadcasted_iota(jnp.int32, (1, 128), 1)
    base, high = stream * length // 2, (stream + 1) * length // 2
    sum_ref[...] = jnp.zeros_like(sum_ref)
    lse_ref[base:high, :] = jnp.zeros((length // 2, 128), F32)

    def one_head(head):
        mask = head_mask(width, head)
        for start in range(base, high, block):
            stop = start + block
            query = qkv_ref[start:stop, :width] * jnp.asarray(HDIM**-0.5, BF)
            query = jnp.where(mask, query, zero)
            scores = causal_scores(query, qkv_ref[:stop, width : 2 * width], below, start)
            top = jnp.max(scores, axis=1, keepdims=True)
            terms = jnp.exp(scores - top)
            sums = jnp.sum(terms, axis=1, keepdims=True)
            mixed = dot(terms.astype(BF), qkv_ref[:stop, 2 * width :]) * (1.0 / sums)
            sum_ref[:, start - base : stop - base] += jnp.where(mask, mixed, 0.0)
            stats = lse_ref[start:stop, :]
            lse_ref[start:stop, :] = jnp.where(lane == head, top + jnp.log(sums), stats)

    loop(width // HDIM, one_head)
    for start in range(base, high, block):
        ns.mixed_v[start : start + block, :] = sum_ref[:, start - base : start - base + width].astype(BF)


def attend_back(ns, stream, block=256):
    length, width = ns.mixed_grad_v.shape
    qkv_ref, grad_ref, sum_ref = ns.qkv_in_v, ns.mixed_grad_v, ns.terms_own.at[stream]
    row = lax.broadcasted_iota(jnp.int32, (block, block), 0)
    col = lax.broadcasted_iota(jnp.int32, (block, block), 1)
    below = col <= row
    zero = jnp.zeros((), BF)
    scale = HDIM**-0.5
    lane = lax.broadcasted_iota(jnp.int32, (1, 128), 1)
    base, high = stream * length // 2, (stream + 1) * length // 2
    sum_ref[...] = jnp.zeros_like(sum_ref)

    def one_head(head):
        mask = head_mask(width, head)
        for start in range(base, high, block):
            stop = start + block
            query = qkv_ref[start:stop, :width] * jnp.asarray(scale, BF)
            query = jnp.where(mask, query, zero)
            grad = jnp.where(mask, grad_ref[start:stop, :], zero)
            keys, vals = qkv_ref[:stop, width : 2 * width], qkv_ref[:stop, 2 * width :]
            scores = causal_scores(query, keys, below, start)
            lse = jnp.where(lane == head, ns.lse_v[start:stop, :], 0.0)
            probs = jnp.exp(scores - jnp.sum(lse, axis=1, keepdims=True))
            prob_grad = dot_nt(grad, vals)
            delta = jnp.sum(probs * prob_grad, axis=1, keepdims=True)
            score_grad = (probs * (prob_grad - delta)).astype(BF)
            query_grad = jnp.where(mask, dot(score_grad, keys), 0.0)
            sum_ref[:, start - base : stop - base] += query_grad
            ns.dk_v[:stop, :] += dot_tn(score_grad, query)
            ns.dv_v[:stop, :] += dot_tn(probs.astype(BF), grad)

    loop(width // HDIM, one_head)
    for start in range(base, high, block):
        value = sum_ref[:, start - base : start - base + width] * scale
        ns.qkv_grad_v[start : start + block, :width] = value.astype(BF)
    ns.qkv_grad_v[base:high, width : 2 * width] = ns.dk_v[base:high, :].astype(BF)
    ns.qkv_grad_v[base:high, 2 * width :] = ns.dv_v[base:high, :].astype(BF)


MESH_ID = pl.DeviceIdType.MESH
HELD, ONE, TWO, SUM, LINE, FULL = "_v", "one", "two", "sum", "line", "full"
PASSED = ("give", "take", "send", "got")
ATTN, DOWN, UP, QKV = "attn", "down", "up", "qkv"
D0, U0, Q0, O0 = "d0", "u0", "q0", "o0"
D1, U1, Q1, O1 = "d1", "u1", "q1", "o1"
TOK = 128


class Place:
    def __init__(self):
        rep, grp = lax.axis_index(REP), lax.axis_index(GRP)
        self.rep, self.grp = rep, grp
        self.x, self.y = lax.rem(rep, 2), lax.div(rep, 2)
        self.t, self.upper = lax.rem(grp, 4), lax.div(grp, 4)
        self.c, self.side = lax.rem(grp, 2), lax.div(self.t, 2)
        base = self.upper * 4
        self.core = (rep, base + self.side * 2 + 1 - self.c)
        self.near = (rep, base + (1 - self.side) * 2 + self.c)
        self.far = (rep, (1 - self.upper) * 4 + self.t)
        self.along_x = (self.y * 2 + 1 - self.x, grp)
        self.along_y = ((1 - self.y) * 2 + self.x, grp)
        self.near_t = (1 - self.side) * 2 + self.c

    def line(self, offset):
        c = 1 - self.c if offset & 1 else self.c
        side = 1 - self.side if offset & 2 else self.side
        upper = 1 - self.upper if offset & 4 else self.upper
        return (self.rep, upper * 4 + side * 2 + c), upper, side * 2 + c


class Copies:
    def __init__(self, send, recv, here):
        self.sems, self.here = (send, recv), here
        self.sent, self.local_count, self.stores, self.done = [], 0, [], set()

    def remote(self, source, target, device):
        at = len(self.sent)
        assert at < self.sems[0].shape[0]
        copy = pltpu.make_async_remote_copy(
            src_ref=source,
            dst_ref=target,
            send_sem=self.sems[0].at[at],
            recv_sem=self.sems[1].at[at],
            device_id=device,
            device_id_type=MESH_ID,
        )
        copy.start()
        self.sent.append(copy)
        return copy

    def local(self, source, target):
        assert self.local_count < self.here.shape[0]
        copy = pltpu.make_async_copy(source, target, self.here.at[self.local_count])
        self.local_count += 1
        copy.start()
        return copy

    def store(self, source, target):
        self.stores.append(self.local(source, target))

    def both(self, *copies):
        for copy in copies:
            copy.wait_recv()
            copy.wait_send()
            self.done.add(id(copy))

    def finish(self):
        for copy in self.sent:
            if id(copy) not in self.done:
                copy.wait_send()
        for copy in self.stores:
            copy.wait()


def announce(devices):
    barrier = pltpu.get_barrier_semaphore()
    for device in devices:
        pl.semaphore_signal(barrier, inc=1, device_id=device, device_id_type=MESH_ID)


def meet(devices):
    pl.semaphore_wait(pltpu.get_barrier_semaphore(), len(devices))


def with_line(place):
    line = [place.line(offset)[0] for offset in range(1, 8)]
    return [*line, place.along_x, place.along_y]


def with_few(place):
    return [place.core, place.near, place.far, place.along_x, place.along_y]


class Plan:
    def __init__(self, *entries):
        self.entries = list(entries)

    def tick(self):
        if self.entries:
            for action in self.entries.pop(0):
                action()

    def drain(self):
        while self.entries:
            self.tick()


def stages(task):
    return lambda: next(task, None)


def spread(copies, place, part, last=True):
    x, y, every = place.x, place.y, slice(None)
    one = copies.remote(part(0, y, x), part(0, y, x), place.along_x)
    two = copies.remote(part(1, y, x), part(1, y, x), place.along_y)
    yield
    one.wait_recv()
    three = copies.remote(part(0, y, every), part(0, y, every), place.along_y)
    two.wait_recv()
    four = copies.remote(part(1, every, x), part(1, every, x), place.along_x)
    yield
    three.wait_recv()
    four.wait_recv()
    if last:
        yield


def deal(copies, place, source, target):
    moved = []
    own = copies.local(source.at[place.t], target)
    for offset in range(1, 8):
        if offset == 4:
            yield
        device, upper, t = place.line(offset)
        moved.append(copies.remote(source.at[t], target, device))
    yield
    own.wait()
    for copy in moved:
        copy.wait_recv()
    yield


def add_low(one, two):
    return (one.astype(F32) + two.astype(F32)).astype(BF)


def reduce_rep(copies, place, grad, ns, name):
    x, y = place.x, place.y
    count = grad.shape[1]

    def step_one():
        one = getattr(ns, name + ONE)
        first = copies.remote(grad.at[0, :, :, 1 - x], one.at[0], place.along_x)
        second = copies.remote(grad.at[1, :, 1 - y], one.at[1], place.along_y)
        yield
        copies.both(first, second)
        for i in range(count):
            for j in range(2):
                grad[0, i, j, x] = add_low(grad[0, i, j, x], one[0, i, j])
                grad[1, i, y, j] = add_low(grad[1, i, y, j], one[1, i, j])
        yield

    def step_two():
        two, total = getattr(ns, name + TWO), getattr(ns, name + SUM)
        first = copies.remote(grad.at[0, :, 1 - y, x], two.at[0], place.along_y)
        second = copies.remote(grad.at[1, :, y, 1 - x], two.at[1], place.along_x)
        own = [copies.local(grad.at[half, :, y, x], total.at[half]) for half in range(2)]
        yield
        copies.both(first, second)
        for half in range(2):
            own[half].wait()
            for i in range(count):
                total[half, i] = add_low(total[half, i], two[half, i])
        yield

    return step_one(), step_two()


def line_columns(copies, place, ns, name):
    total, line, full = (getattr(ns, name + part) for part in (SUM, LINE, FULL))
    moved = []
    for offset in range(1, 8):
        device, upper, t = place.line(offset)
        here = line.at[place.upper, place.t]
        moved.append(copies.remote(total.at[upper, t], here, device))
    line[place.upper, place.t] = total[place.upper, place.t]
    yield
    for copy in moved:
        copy.wait_recv()
    for t in range(4):
        full[place.y, place.x, t] = add_low(line[0, t], line[1, t])
    yield


def line_rows(copies, place, ns, name):
    total, line, full = (getattr(ns, name + part) for part in (SUM, LINE, FULL))
    moved = copies.remote(total.at[1 - place.upper, 0], line, place.far)
    yield
    moved.wait_recv()
    rows = line.shape[0] // 2
    for half in range(2):
        at = pl.ds(half * rows, rows)
        full[place.y, place.x, half] = add_low(total[place.upper, 0, at, :], line[at, :])
    yield


def whole_columns(copies, place, ns, name, target, groups):
    full = getattr(ns, name + FULL)
    yield from spread(copies, place, lambda half, a, b: full.at[a, b, pl.ds(2 * half, 2)], False)
    unit = full.shape[4] // groups
    for t in range(4):
        for k in range(groups):
            source = full.at[:, :, t, :, k * unit : (k + 1) * unit]
            start = (k * 4 + t) * unit
            copies.store(source, target.at[:, :, :, start : start + unit])
    yield


def whole_rows(copies, place, ns, name, target):
    full = getattr(ns, name + FULL)
    yield from spread(copies, place, lambda half, a, b: full.at[a, b, half], False)
    copies.store(full, target)
    yield


def reduce_scratch(name, count, rows, width, steps=3):
    total = {}
    if steps & 1:
        total[name + ONE] = pltpu.VMEM((2, count, 2, rows, width), BF)
    if steps & 2:
        total[name + TWO] = pltpu.VMEM((2, count, rows, width), BF)
        total[name + SUM] = pltpu.VMEM((2, count, rows, width), BF)
    return total


def finish_scratch(name, count, rows, width):
    if count == 1:
        line, full = (rows, width), (2, 2, 2, rows // 2, width)
    else:
        line, full = (2, count, rows, width), (2, 2, count, rows, width)
    return {name + LINE: pltpu.VMEM(line, BF), name + FULL: pltpu.VMEM(full, BF)}


def by_device(shape, count):
    rows, width = shape
    return struct((2, count, 2, 2, rows // (8 * count), width), BF)


def loop(count, step):
    def run(index, carry):
        step(index)
        return carry

    lax.fori_loop(0, count, run, 0)


def tile_of(index, size):
    return pl.ds(pl.multiple_of(index * size, size), size)


def matrix(value):
    return value.reshape(-1, value.shape[-1])


def times(left, right_ref, tile, sink):
    every = (slice(None),) * (len(right_ref.shape) - 1)

    def step(index):
        at = tile_of(index, tile)
        sink(at, dot(left(), matrix(right_ref[(*every, at)])))

    loop(right_ref.shape[-1] // tile, step)


def times_rows(left, right_ref, tile, sink):
    flat = len(right_ref.shape) == 2

    def step(index):
        if flat:
            at = tile_of(index, tile)
            sink(at, dot_nt(left(), right_ref[at, :]))
        else:
            block = matrix(right_ref[index])
            sink(tile_of(index, block.shape[0]), dot_nt(left(), block))

    loop(right_ref.shape[0] // (tile if flat else 1), step)


def gram(left_ref, right_ref, out_ref):
    count, tile = out_ref.shape[1], 256
    total = left_ref.shape[1]
    if total == tile:
        value = dot_tn(left_ref[...], right_ref[...]).astype(BF)
        out_ref[...] = value.reshape(out_ref.shape)
        return

    def step(index):
        value = dot_tn(left_ref[:, tile_of(index, tile)], right_ref[...]).astype(BF)
        half, part = lax.div(index, 2), lax.rem(index, 2)
        if count == 1:
            out_ref[half, 0, part] = value.reshape(out_ref.shape[3:])
        else:
            out_ref[half, pl.ds(part * 2, 2)] = value.reshape(2, *out_ref.shape[2:])

    loop(total // tile, step)


class Gather:
    def __init__(self, copies, place, buf, order=(0, 1)):
        self.copies, self.place, self.buf, self.order = copies, place, buf, order
        self.flight = {}

    def rows(self, stream, where):
        start = (self.order[stream] * 4 + where) * TOK
        return pl.ds(pl.multiple_of(start, TOK), TOK)

    def pair(self, stream, side):
        start = (self.order[stream] * 4 + side * 2) * TOK
        return pl.ds(pl.multiple_of(start, TOK), 2 * TOK)

    def start(self, stream, block):
        at = self.rows(stream, self.place.t)
        self.buf[at, :] = block
        mine = self.buf.at[at, :]
        across = self.copies.remote(mine, mine, self.place.near)
        beside = self.copies.remote(mine, mine, self.place.core)
        self.flight[stream] = [across, beside]

    def wait_chip(self, stream):
        self.flight[stream][1].wait_recv()

    def forward(self, stream):
        self.flight[stream][0].wait_recv()
        got = self.buf.at[self.rows(stream, self.place.near_t), :]
        self.flight[stream].append(self.copies.remote(got, got, self.place.core))

    def wait_rest(self, stream):
        self.flight[stream][2].wait_recv()


class Scatter:
    def __init__(self, copies, place, ns, name):
        self.copies, self.place = copies, place
        self.away, self.own = ns.terms_away, ns.terms_own
        self.give, self.take, self.send, self.got = (
            getattr(ns, name + part) for part in PASSED
        )
        self.flight = {}

    def push(self, stream, product):
        place, copies = self.place, self.copies
        mine = pl.ds(pl.multiple_of(place.c * TOK, TOK), TOK)
        other = pl.ds(pl.multiple_of((1 - place.c) * TOK, TOK), TOK)

        def to_away(at, value):
            self.away[:, at] = value

        def to_own(at, value):
            self.own[stream, :, at] = value

        product(1 - place.side, to_away)
        self.give[stream, 0] = self.away[other, :].astype(BF)
        first = copies.remote(self.give.at[stream, 0], self.take.at[stream, 0], place.core)
        product(place.side, to_own)
        first.wait_recv()
        self.send[stream] = (self.away[mine, :] + self.take[stream, 0].astype(F32)).astype(BF)
        across = copies.remote(self.send.at[stream], self.got.at[stream], place.near)
        self.give[stream, 1] = self.own[stream, other, :].astype(BF)
        second = copies.remote(self.give.at[stream, 1], self.take.at[stream, 1], place.core)
        self.flight[stream] = (second, across)

    def result(self, stream):
        second, across = self.flight[stream]
        mine = pl.ds(pl.multiple_of(self.place.c * TOK, TOK), TOK)
        second.wait_recv()
        total = self.own[stream, mine, :] + self.take[stream, 1].astype(F32)
        across.wait_recv()
        return total + self.got[stream].astype(F32)


def scatter_scratch(name, width):
    give, take, send, got = (name + part for part in PASSED)
    return {
        "terms_away": pltpu.VMEM((2 * TOK, width), F32),
        "terms_own": pltpu.VMEM((2, 2 * TOK, width), F32),
        give: pltpu.VMEM((2, 2, TOK, width), BF),
        take: pltpu.VMEM((2, 2, TOK, width), BF),
        send: pltpu.VMEM((2, TOK, width), BF),
        got: pltpu.VMEM((2, TOK, width), BF),
    }


def gelu_both(x):
    cubic = x * x * 0.044715
    bent = jnp.tanh(0.7978845608028654 * (x + cubic * x))
    half = 0.5 * (1.0 + bent)
    slope = half + 0.5 * x * (1.0 - bent * bent) * (0.7978845608028654 * (1.0 + 3.0 * cubic))
    return x * half, slope


def norm_back_in(values, gain, grad):
    rstd = lax.rsqrt(jnp.mean(values * values, axis=-1, keepdims=True) + EPS)
    hat = values * rstd
    scaled = grad * gain
    back = rstd * (scaled - hat * jnp.mean(scaled * hat, axis=-1, keepdims=True))
    return back, jnp.sum(grad * hat, axis=0, keepdims=True)


def next_qkv(ns, place, blocks, tick, wait_weights, order=(0, 1), late=None):
    gather = Gather(ns.copies, place, ns.normed_v, order)
    for stream in range(2):
        if late and stream == 1:
            late()
        gather.start(stream, blocks[stream]())
        tick()
    if late:
        for stream in range(2):
            gather.forward(stream)
            tick()
    wait_weights()
    for stream in range(2):

        def project(side):
            at = gather.pair(stream, side)

            def sink(cols, value):
                ns.qkv_v[at, cols] = value.astype(BF)

            times(lambda: ns.normed_v[at, :], ns.wq_v, 384, sink)

        gather.wait_chip(stream)
        project(place.side)
        if not late:
            gather.forward(stream)
        gather.wait_rest(stream)
        project(1 - place.side)
        tick()
        here = pl.ds(pl.multiple_of(order[stream] * 4 * TOK, 4 * TOK), 4 * TOK)
        ns.copies.store(ns.normed_v.at[here, :], ns.normed.at[here, :])
        ns.copies.store(ns.qkv_v.at[here, :], ns.qkv.at[here, :])


def fwd_mid(ns, place, gain, tick, wait_out, wait_up, wait_down):
    copies = ns.copies
    attn = Scatter(copies, place, ns, ATTN)
    down = Scatter(copies, place, ns, DOWN)
    gather = Gather(copies, place, ns.mlp_v)
    wo, wu, wd = ns.wo_v, ns.wu_v, ns.wd_v
    for stream in range(2):

        def product(side, sink):
            at = gather.pair(stream, side)
            times(lambda: ns.mixed_v[at, :], wo, 512, sink)

        attend(ns, stream)
        tick()
        if stream == 0:
            wait_out()
        attn.push(stream, product)
        tick()
    ns.load.hidden.wait()
    for stream in range(2):
        value = attn.result(stream)
        ns.attn_out_v[stream] = value
        resid = ns.hidden_v[stream].astype(F32) + norm(value, gain(1))
        ns.resid_v[stream] = resid
        gather.start(stream, norm(resid, gain(2)).astype(BF))
        tick()
    wait_up()
    for stream in range(2):

        def expand(side):
            at = gather.pair(stream, side)

            def sink(cols, value):
                active, slope = gelu_both(value)
                ns.active_v[at, cols] = active.astype(BF)
                ns.slope_v[at, cols] = slope.astype(BF)

            times(lambda: ns.mlp_v[at, :], wu, 256, sink)

        gather.wait_chip(stream)
        expand(place.side)
        gather.forward(stream)
        gather.wait_rest(stream)
        expand(1 - place.side)
        if stream == 0:
            wait_down()

        def product(side, sink):
            at = gather.pair(stream, side)
            times(lambda: ns.active_v[at, :], wd, 512, sink)

        down.push(stream, product)
        tick()
    return down


def bwd_mid(ns, place, layer, grads, tick, on_down, on_up, order=(0, 1)):
    copies, gain, base = ns.copies, rows_of(ns, layer), layer * 4
    up = Scatter(copies, place, ns, UP)
    first = Gather(copies, place, ns.down_grad_v)
    second = Gather(copies, place, ns.attn_grad_v)
    wo, wu, wd = ns.wo_v, ns.wu_v, ns.wd_v
    for stream in order:
        grad = grads[stream]()
        ns.grad_v[stream] = grad
        back, four = norm_back_in(ns.down_out_v[stream], gain(3), grad)
        ns.dg_v[base + 3 : base + 4, :] += four
        first.start(stream, back.astype(BF))
        tick()
    for stream in order:

        def shrink(side):
            at = first.pair(stream, side)

            def sink(cols, value):
                slope = ns.slope_v[at, cols].astype(F32)
                ns.up_grad_v[at, cols] = (value * slope).astype(BF)

            times_rows(lambda: ns.down_grad_v[at, :], wd, 512, sink)

        first.wait_chip(stream)
        shrink(place.side)
        first.forward(stream)
        first.wait_rest(stream)
        shrink(1 - place.side)

        def product(side, sink):
            at = first.pair(stream, side)
            times_rows(lambda: ns.up_grad_v[at, :], wu, 512, sink)

        up.push(stream, product)
        tick()
    for stream in order:
        back, three = norm_back_in(ns.resid_v[stream], gain(2), up.result(stream))
        grad = ns.grad_v[stream] + back
        ns.grad_v[stream] = grad
        ns.dg_v[base + 2 : base + 3, :] += three
        back, two = norm_back_in(ns.attn_out_v[stream], gain(1), grad)
        ns.dg_v[base + 1 : base + 2, :] += two
        second.start(stream, back.astype(BF))
        tick()
        if stream == order[0]:
            gram(ns.active_v, ns.down_grad_v, ns.gd_v)
            on_down()
        else:
            gram(ns.mlp_v, ns.up_grad_v, ns.gu_v)
            on_up()
            tick()
    copies.store(ns.grad_v, ns.resid_grad)
    for stream in order:

        def project(side):
            at = second.pair(stream, side)
            ns.mixed_grad_v[at, :] = dot_nt(ns.attn_grad_v[at, :], matrix(wo[...])).astype(BF)

        second.wait_chip(stream)
        project(place.side)
        second.forward(stream)
        second.wait_rest(stream)
        project(1 - place.side)
        tick()
        here = pl.ds(stream * 4 * TOK, 4 * TOK)
        copies.store(ns.mixed_grad_v.at[here, :], ns.mixed_grad.at[here, :])
    gram(ns.mixed_v, ns.attn_grad_v, ns.go_v)


def bwd_head(ns, place, layer, tick, on_qkv, weight_first):
    copies, gain = ns.copies, rows_of(ns, layer)
    qkv = Scatter(copies, place, ns, QKV)
    walk = Gather(copies, place, None)

    def weight():
        ns.load.normed.wait()
        gram(ns.normed_v, ns.qkv_grad_v, ns.gq_v)
        on_qkv()
        tick()

    ns.dk_v[...] = jnp.zeros_like(ns.dk_v)
    ns.dv_v[...] = jnp.zeros_like(ns.dv_v)
    for stream in (1, 0):

        def product(side, sink):
            at = walk.pair(stream, side)
            times_rows(lambda: ns.qkv_grad_v[at, :], ns.wq_v, 512, sink)

        attend_back(ns, stream)
        tick()
        if stream == 1:
            ns.load.wq.wait()
        elif weight_first:
            weight()
        qkv.push(stream, product)
        tick()
    if not weight_first:
        weight()
    ns.load.hidden.wait()
    ns.load.grad.wait()

    def result(stream):
        back, one = norm_back_in(ns.hidden_v[stream].astype(F32), gain(0), qkv.result(stream))
        ns.dg_v[layer * 4 : layer * 4 + 1, :] += one
        return ns.grad_v[stream] + back

    return [functools.partial(result, stream) for stream in range(2)]


def kernel_of(body, reach, inputs, outputs, scratch, slot, remotes, locals_, vmem, flops):
    names = [*inputs, *outputs, *scratch]

    def kernel(*refs):
        ns = types.SimpleNamespace(**dict(zip(names, refs)))
        ns.copies = Copies(*refs[len(names) :])
        announce(reach(Place()))
        ns.load = types.SimpleNamespace()
        for name in inputs:
            if name + HELD in scratch:
                copy = ns.copies.local(getattr(ns, name), getattr(ns, name + HELD))
                setattr(ns.load, name, copy)
        body(ns)
        ns.copies.finish()

    moved = sum(v.size * v.dtype.itemsize for v in [*inputs.values(), *outputs.values()])
    return kernel, dict(
        name=body.__name__,
        out_shape=list(outputs.values()),
        in_specs=[pl.BlockSpec(memory_space=pl.ANY)] * len(inputs),
        out_specs=[pl.BlockSpec(memory_space=pl.ANY)] * len(outputs),
        scratch_shapes=[
            *scratch.values(),
            pltpu.SemaphoreType.DMA((remotes,)),
            pltpu.SemaphoreType.DMA((remotes,)),
            pltpu.SemaphoreType.DMA((locals_,)),
        ],
        compiler_params=pltpu.CompilerParams(
            collective_id=slot, has_side_effects=True, vmem_limit_bytes=vmem << 20
        ),
        cost_estimate=pl.CostEstimate(flops=flops, bytes_accessed=moved, transcendentals=0),
    )


def named(outputs, results):
    return types.SimpleNamespace(**dict(zip(outputs, results)))


def held(*groups):
    merged = {name: value for group in groups for name, value in group.items()}
    return {name + HELD: pltpu.VMEM(value.shape, value.dtype) for name, value in merged.items()}


def struct(shape, dtype):
    return jax.ShapeDtypeStruct(shape, dtype)


def rows_of(ns, layer):
    return lambda index, level=layer: ns.gains_v[level * 4 + index : level * 4 + index + 1, :]


def quarter_of(ns, place, weight, layer, target):
    rows = weight.shape[1] // 4
    at = pl.ds(pl.multiple_of(place.rep * rows, rows), rows)
    return ns.copies.local(weight.at[layer, at, :], target)


def arrange(quarter, dealt, groups):
    unit = quarter.shape[1] // (groups * 4)
    for t in range(4):
        for k in range(groups):
            start = (k * 4 + t) * unit
            dealt[t, :, k * unit : (k + 1) * unit] = quarter[:, start : start + unit]


def by_rows(ref, place):
    return lambda half, a, b: ref.at[1 - place.upper, a, b, half]


def by_columns(ref):
    return lambda half, a, b: ref.at[half, :, a, b]


def first_kernel(block, gain_part, w_qkv, w_up, w_down, w_out):
    width, part = block.shape[2], w_qkv.shape[2] // 4
    length, mixed_width = 8 * TOK, part // 3
    units, rows = w_up.shape[2] // 4, width // 32
    inputs = dict(
        block=block, gain_part=gain_part, w_qkv=w_qkv, w_up=w_up, w_down=w_down, w_out=w_out
    )
    blocks = struct((2, TOK, width), F32)
    wide = struct((length, width), BF)
    next_u, next_o = struct((2, 4, rows, units), BF), struct((2, *w_out.shape[1:]), BF)
    early = dict(
        hidden=struct(block.shape, BF),
        gains=struct((gain_part.shape[0], width), F32),
        normed_0=wide,
        qkv_0=struct((length, part), BF),
        wq_0=struct((2, 4, 2, 2, rows, part), BF),
    )
    outputs = dict(
        early,
        mixed=struct((length, mixed_width), BF),
        lse=struct((length, 128), F32),
        attn_out=blocks,
        resid=blocks,
        mlp=wide,
        active=struct((length, units), BF),
        slope=struct((length, units), BF),
        down_out=blocks,
        hidden_out=blocks,
        normed=wide,
        qkv=struct((length, part), BF),
        wu=struct((2, 4, 2, 2, rows, units), BF),
        wd=struct((2, *w_down.shape[1:]), BF),
        wo=next_o,
        wq=struct((2, 4, 2, 2, rows, part), BF),
    )
    kept = dict(
        quarter_q=struct((rows, 4 * part), BF),
        quarter_u=struct((rows, 4 * units), BF),
        deal_q=struct((4, rows, part), BF),
        deal_u=struct((4, rows, units), BF),
        quarter_q0=struct((rows, 4 * part), BF),
        quarter_u0=struct((rows, 4 * units), BF),
        deal_q0=struct((4, rows, part), BF),
        deal_u0=struct((4, rows, units), BF),
    )
    scratch = held(outputs, kept)
    outputs = dict(outputs, next_u=next_u, next_o=next_o)
    scratch |= scatter_scratch(ATTN, width) | scatter_scratch(DOWN, width)

    def tokens_in(ns, place):
        copies = ns.copies
        upper, y, x = place.upper, place.y, place.x
        columns = pl.ds(pl.multiple_of(place.grp * TOK, TOK), TOK)
        line = [place.line(offset)[0] for offset in range(1, 8)]
        quarter_q = quarter_of(ns, place, ns.w_qkv, 0, ns.quarter_q_v)
        quarter_u = quarter_of(ns, place, ns.w_up, 0, ns.quarter_u_v)
        kept = copies.local(ns.block.at[upper], ns.hidden_v.at[upper])
        gain_own = copies.local(ns.gain_part, ns.gains_v.at[:, columns])
        quarter_q.wait()
        arrange(ns.quarter_q_v, ns.deal_q_v, 6)
        meet(with_line(place))
        gain_rest = [copies.remote(ns.gain_part, ns.gains_v.at[:, columns], at) for at in line]
        wq_dealt = deal(copies, place, ns.deal_q_v, ns.wq_v.at[upper, place.t, y, x])
        next(wq_dealt)
        next(wq_dealt)
        brought = copies.remote(ns.block.at[1 - upper], ns.hidden_v.at[upper], place.far)
        out_in = copies.remote(ns.w_out.at[0, y, x], ns.wo_v.at[upper, y, x], place.far)
        wq_spread = spread(copies, place, by_columns(ns.wq_v))
        out_spread = spread(copies, place, by_rows(ns.wo_v, place))
        up_dealt = deal(copies, place, ns.deal_u_v, ns.wu_v.at[upper, place.t, y, x])
        quarter_u.wait()
        arrange(ns.quarter_u_v, ns.deal_u_v, 2)
        next(up_dealt)
        kept.wait()
        gain_own.wait()
        for copy in gain_rest:
            copy.wait_recv()

        def late():
            next(wq_spread)
            brought.wait_recv()
            copies.store(ns.hidden_v, ns.hidden)

        def out_arrived():
            out_in.wait_recv()
            next(out_spread)

        def wait_weights():
            next(wq_spread)
            copies.store(ns.wq_v, ns.wq)

        copies.store(ns.gains_v, ns.gains)
        order = (upper, 1 - upper)
        blocks = [
            functools.partial(
                lambda s: norm(ns.hidden_v[s].astype(F32), ns.gains_v[0:1, :]).astype(BF), stream
            )
            for stream in order
        ]
        plan = Plan(
            [stages(wq_dealt), stages(wq_spread)],
            [stages(up_dealt)],
            [out_arrived],
            [stages(out_spread)],
        )
        next_qkv(ns, place, blocks, plan.tick, wait_weights, order, late)
        next(out_spread)
        return up_dealt

    def rest_of(ns, place, up_dealt):
        copies = ns.copies
        upper, t, y, x = place.upper, place.t, place.y, place.x
        quarter_q = quarter_of(ns, place, ns.w_qkv, 1, ns.quarter_q_v)
        whole_o = copies.local(ns.w_out.at[0], ns.wo_v.at[upper])
        whole_d = copies.local(ns.w_down.at[0], ns.wd_v.at[upper])
        quarter_u = quarter_of(ns, place, ns.w_up, 1, ns.quarter_u_v)
        down_in = copies.remote(ns.w_down.at[0, y, x], ns.wd_v.at[upper, y, x], place.far)
        next(up_dealt)
        up_spread = spread(copies, place, by_columns(ns.wu_v))
        down_spread = spread(copies, place, by_rows(ns.wd_v, place))
        next(up_spread)
        quarter_q.wait()
        arrange(ns.quarter_q_v, ns.deal_q_v, 6)
        q_deal = deal(copies, place, ns.deal_q_v, ns.wq_v.at[upper, t, y, x])
        next(q_deal)
        next(q_deal)
        q_spread = spread(copies, place, by_columns(ns.wq_v))
        u_deal = deal(copies, place, ns.deal_u_v, ns.next_u.at[upper, t])
        o_spread = spread(copies, place, by_rows(ns.next_o, place))
        rest = []

        def out_part():
            rest.append(copies.remote(ns.w_out.at[1, y, x], ns.next_o.at[upper, y, x], place.far))

        def deal_up():
            quarter_u.wait()
            arrange(ns.quarter_u_v, ns.deal_u_v, 2)
            next(u_deal)
            next(u_deal)

        def down_arrived():
            down_in.wait_recv()
            next(down_spread)

        def out_arrived():
            rest[0].wait_recv()
            next(o_spread)

        plan = Plan(
            [],
            [],
            [stages(up_spread)],
            [deal_up],
            [down_arrived],
            [stages(down_spread), out_part],
            [stages(q_deal), stages(q_spread)],
            [stages(q_spread)],
            [out_arrived],
            [],
            [stages(o_spread)],
            [stages(o_spread)],
        )
        gain = rows_of(ns, 0)

        def wait_out():
            whole_o.wait()
            copies.store(ns.wo_v, ns.wo)

        def wait_down():
            next(down_spread)
            whole_d.wait()
            copies.store(ns.wu_v, ns.wu)
            copies.store(ns.wd_v, ns.wd)

        def wait_next():
            next(q_spread)
            copies.store(ns.wq_v, ns.wq)

        down = fwd_mid(ns, place, gain, plan.tick, wait_out, lambda: next(up_spread), wait_down)
        copies.store(ns.mixed_v, ns.mixed)
        copies.store(ns.lse_v, ns.lse)
        copies.store(ns.attn_out_v, ns.attn_out)
        copies.store(ns.resid_v, ns.resid)
        copies.store(ns.mlp_v, ns.mlp)
        copies.store(ns.active_v, ns.active)
        copies.store(ns.slope_v, ns.slope)

        def block(stream):
            value = down.result(stream)
            ns.down_out_v[stream] = value
            hidden_out = ns.resid_v[stream] + norm(value, gain(3))
            ns.hidden_out_v[stream] = hidden_out
            return norm(hidden_out, gain(0, 1)).astype(BF)

        blocks = [functools.partial(block, stream) for stream in range(2)]
        next_qkv(ns, place, blocks, plan.tick, wait_next)
        copies.store(ns.down_out_v, ns.down_out)
        copies.store(ns.hidden_out_v, ns.hidden_out)
        plan.drain()
        next(u_deal)

    def first(ns):
        place = Place()
        initial = types.SimpleNamespace(**vars(ns))
        initial.normed, initial.normed_v = ns.normed_0, ns.normed_0_v
        initial.qkv, initial.qkv_v = ns.qkv_0, ns.qkv_0_v
        initial.wq, initial.wq_v = ns.wq_0, ns.wq_0_v
        initial.quarter_q_v, initial.quarter_u_v = ns.quarter_q0_v, ns.quarter_u0_v
        initial.deal_q_v, initial.deal_u_v = ns.deal_q0_v, ns.deal_u0_v
        up_dealt = tokens_in(initial, place)
        ns.qkv_in_v = ns.qkv_0_v
        ns.load.hidden = types.SimpleNamespace(wait=lambda: None)
        rest_of(ns, place, up_dealt)

    flops = 2 * length * width * (mixed_width + 2 * units + 2 * part)
    kernel, options = kernel_of(first, with_line, inputs, outputs, scratch, 0, 128, 96, 62, flops)
    results = pl.pallas_call(kernel, **options)(*inputs.values())
    return named(outputs, results)


def turn_kernel(lower, gains, w_down, w_out, cotangent):
    hidden = lower.hidden_out
    width = hidden.shape[2]
    length, part = lower.qkv.shape
    mixed_width = part // 3
    inputs = dict(
        qkv_in=lower.qkv, gains=gains, hidden=hidden, cot=cotangent,
        part_u=lower.next_u, part_o=lower.next_o, w_down=w_down, w_out=w_out,
    )
    rows, units = lower.next_u.shape[2:]
    blocks = struct((2, TOK, width), F32)
    outputs = dict(
        out=struct((2, TOK, width), BF),
        lse=struct((length, 128), F32),
        mixed_grad=struct((length, mixed_width), BF),
        gd=by_device((units, width), 1),
        gu=by_device((width, units), 4),
        go=by_device((mixed_width, width), 1),
        dg=struct((8, width), F32),
    )
    kept = dict(
        qkv_in=lower.qkv,
        hidden=hidden,
        gains=gains,
        cot=cotangent,
        wd=struct((2, *w_down.shape[1:]), BF),
        wo=lower.next_o,
        wu=struct((2, 4, 2, 2, rows, units), BF),
        mixed=struct((length, mixed_width), BF),
        attn_out=blocks,
        resid=blocks,
        grad=blocks,
        mlp=struct((length, width), BF),
        active=struct((length, units), BF),
        slope=struct((length, units), BF),
        up_grad=struct((length, units), BF),
        down_out=blocks,
        down_grad=struct((length, width), BF),
        attn_grad=struct((length, width), BF),
    )
    scratch = held(outputs, kept)
    outputs |= dict(resid_grad=blocks)
    for name in (ATTN, DOWN, UP):
        scratch |= scatter_scratch(name, width)
    scratch |= reduce_scratch(D1, 1, units // 8, width, 1)

    def turn(ns):
        place, copies = Place(), ns.copies
        upper, y, x = place.upper, place.y, place.x
        part_u = copies.local(ns.part_u, ns.wu_v.at[:, :, y, x])
        part_o = copies.local(ns.part_o.at[1 - upper], ns.wo_v.at[1 - upper])
        whole_o = copies.local(ns.w_out.at[1], ns.wo_v.at[upper])
        whole_d = copies.local(ns.w_down.at[1], ns.wd_v.at[upper])
        meet(with_few(place))
        down_in = copies.remote(ns.w_down.at[1, y, x], ns.wd_v.at[upper, y, x], place.far)
        part_u.wait()
        up_spread = spread(copies, place, by_columns(ns.wu_v))
        down_spread = spread(copies, place, by_rows(ns.wd_v, place))
        next(up_spread)
        ns.load.qkv_in.wait()
        far_in = []

        def bring():
            ns.load.cot.wait()
            far_in.append(copies.remote(ns.cot.at[1 - upper], ns.cot_far_v, place.far))

        def down_arrived():
            down_in.wait_recv()
            next(down_spread)

        plan = Plan(
            [],
            [],
            [stages(up_spread)],
            [],
            [down_arrived],
            [stages(down_spread), bring],
        )
        ns.load.gains.wait()
        ns.dg_v[...] = jnp.zeros_like(ns.dg_v)
        gain = rows_of(ns, 1)

        def wait_out():
            part_o.wait()
            whole_o.wait()

        def wait_down():
            next(down_spread)
            whole_d.wait()

        down = fwd_mid(
            ns, place, gain, plan.tick, wait_out, lambda: next(up_spread), wait_down
        )
        copies.store(ns.lse_v, ns.lse)
        far_in[0].wait_recv()

        def grad(stream):
            value = down.result(stream)
            ns.down_out_v[stream] = value
            own = jnp.where(upper == stream, ns.cot_v[stream], ns.cot_far_v[...])
            return own.astype(F32)

        def finish():
            for stream in range(2):
                out = ns.resid_v[stream] + norm(ns.down_out_v[stream], gain(3))
                ns.out_v[stream] = out.astype(BF)
            copies.store(ns.out_v, ns.out)

        d_first, unused = reduce_rep(copies, place, ns.gd_v, ns, D1)
        plan = Plan(
            [],
            [finish],
            [],
            [],
            [],
        )
        grads = [functools.partial(grad, stream) for stream in range(2)]
        store_up = functools.partial(copies.store, ns.gu_v, ns.gu)
        bwd_mid(ns, place, 1, grads, plan.tick, stages(d_first), store_up)
        copies.store(ns.go_v, ns.go)
        copies.store(ns.dg_v, ns.dg)
        next(d_first)
        copies.store(ns.gd_v, ns.gd)

    scratch["cot_far_v"] = pltpu.VMEM((TOK, width), BF)
    flops = 6 * length * width * (mixed_width + 2 * units)
    kernel, options = kernel_of(turn, with_few, inputs, outputs, scratch, 2, 64, 64, 63, flops)
    results = pl.pallas_call(kernel, **options)(*inputs.values())
    return named(outputs, results)


def backward_kernel(lower, turned):
    wo, wu, wd, wq = (matrix(value) for value in (lower.wo, lower.wu, lower.wd, lower.wq))
    width, units = wu.shape
    length, part = lower.qkv.shape
    mixed_width = wo.shape[0]
    inputs = dict(
        gu=turned.gu, d1=turned.gd, o1=turned.go, qkv_in=lower.qkv, lse=turned.lse,
        mixed_grad=turned.mixed_grad, dg=turned.dg, gains=lower.gains, wq=wq, normed=lower.normed,
        hidden=lower.hidden_out, grad=turned.resid_grad, down_out=lower.down_out, wd=wd,
        slope=lower.slope, wu=wu, active=lower.active, mlp=lower.mlp, resid=lower.resid,
        attn_out=lower.attn_out, wo=wo, mixed=lower.mixed,
    )
    blocks = struct((2, TOK, width), F32)
    kept = dict(
        gq=by_device(wq.shape, 4),
        gd=by_device(wd.shape, 1),
        gu=by_device(wu.shape, 4),
        go=by_device(wo.shape, 1),
        qkv_grad=struct(lower.qkv.shape, BF),
        dk=struct((length, mixed_width), F32),
        dv=struct((length, mixed_width), F32),
        down_grad=struct((length, width), BF),
        attn_grad=struct((length, width), BF),
    )
    outputs = dict(
        resid_grad=blocks,
        mixed_out=struct((length, mixed_width), BF),
        gd=kept["gd"],
        up_out=kept["gu"],
        go=kept["go"],
        dg_out=turned.dg,
        full_d=struct((2, 2, 2, units // 16, width), BF),
        full_u=struct((2, 2, width // 32, 4 * units), BF),
        full_q=struct((2, 2, width // 32, 4 * part), BF),
        full_o=struct((2, 2, 2, mixed_width // 16, width), BF),
    )
    loaded = dict(inputs)
    del loaded["d1"]
    scratch = held(loaded, kept)
    for name in (QKV, UP):
        scratch |= scatter_scratch(name, width)
    rows = width // 32
    for name, count, high, wide, steps in (
        (D1, 1, units // 8, width, 2),
        (U1, 4, rows, units, 3),
        (Q1, 4, rows, part, 3),
        (O1, 1, mixed_width // 8, width, 3),
    ):
        scratch |= finish_scratch(name, count, high, wide)
        scratch |= reduce_scratch(name, count, high, wide, steps)
    scratch |= reduce_scratch(D0, 1, units // 8, width, 1)

    def backward(ns):
        place, copies = Place(), ns.copies
        ns.up_grad_v = ns.normed_v
        line = [place.line(offset)[0] for offset in range(1, 8)]
        meet(with_line(place))
        unused, d1_second = reduce_rep(copies, place, ns.d1, ns, D1)
        u1_first, u1_second = reduce_rep(copies, place, ns.gu_v, ns, U1)
        o1_first, o1_second = reduce_rep(copies, place, ns.o1_v, ns, O1)
        q1_first, q1_second = reduce_rep(copies, place, ns.gq_v, ns, Q1)
        d0_first, unused = reduce_rep(copies, place, ns.gd_v, ns, D0)
        d1_line = line_rows(copies, place, ns, D1)
        u1_line = line_columns(copies, place, ns, U1)
        o1_line = line_rows(copies, place, ns, O1)
        q1_line = line_columns(copies, place, ns, Q1)
        d1_whole = whole_rows(copies, place, ns, D1, ns.full_d)
        u1_whole = whole_columns(copies, place, ns, U1, ns.full_u, 2)
        q1_whole = whole_columns(copies, place, ns, Q1, ns.full_q, 6)
        o1_whole = whole_rows(copies, place, ns, O1, ns.full_o)
        next(d1_second)
        ns.load.gu.wait()
        next(u1_first)
        ns.load.o1.wait()
        ns.load.qkv_in.wait()
        ns.load.lse.wait()
        ns.load.mixed_grad.wait()
        ns.load.dg.wait()
        plan = Plan(
            [stages(d1_second), stages(d1_line)],
            [],
            [stages(u1_first), stages(u1_second), stages(o1_first)],
            [],
            [],
            [stages(u1_second), stages(u1_line), stages(d1_line), stages(d1_whole)],
            [stages(o1_first), stages(o1_second), stages(q1_first), stages(q1_second)],
            [stages(d1_whole), stages(u1_line), stages(u1_whole)]
            + [stages(q1_second), stages(q1_line)],
            [stages(o1_second), stages(o1_line)],
            [stages(d1_whole), stages(u1_whole), stages(q1_line), stages(q1_whole)],
            [],
            [stages(o1_line), stages(o1_whole), stages(q1_whole)],
            [stages(u1_whole)],
            [stages(d0_first), stages(o1_whole)],
        )
        ns.load.gains.wait()
        grads = bwd_head(ns, place, 1, plan.tick, stages(q1_first), False)
        for copy in (ns.load.down_out, ns.load.wd, ns.load.slope, ns.load.wu, ns.load.active):
            copy.wait()
        for copy in (ns.load.mlp, ns.load.resid, ns.load.attn_out, ns.load.wo, ns.load.mixed):
            copy.wait()
        ns.mixed_grad = ns.mixed_out
        store_up = functools.partial(copies.store, ns.gu_v, ns.up_out)
        bwd_mid(ns, place, 0, grads, plan.tick, stages(d0_first), store_up, (1, 0))
        plan.drain()
        copies.store(ns.go_v, ns.go)
        copies.store(ns.gd_v, ns.gd)
        copies.store(ns.dg_v, ns.dg_out)
        next(q1_whole)
        next(o1_whole)

    flops = 6 * length * width * (mixed_width + 2 * units) + 4 * length * width * part
    kernel, options = kernel_of(backward, with_line, inputs, outputs, scratch, 3, 128, 128, 63, flops)
    results = pl.pallas_call(kernel, **options)(*inputs.values())
    return named(outputs, results)


def last_kernel(lower, turned, back):
    wq = matrix(lower.wq_0)
    width, part = wq.shape
    length, mixed_width = back.mixed_out.shape
    units, rows = back.up_out.shape[-1], width // 32
    inputs = dict(
        u0=back.up_out, d0=back.gd, o0=back.go, qkv_in=lower.qkv_0, lse=lower.lse,
        mixed_grad=back.mixed_out, dg=back.dg_out, gains=lower.gains, normed=lower.normed_0, wq=wq,
        hidden=lower.hidden, grad=back.resid_grad, second=turned.out,
    )
    outputs = dict(
        out=struct((2, TOK, width), BF),
        block_out=struct((2, TOK, width), BF),
        gain_grad=struct((8, TOK), F32),
        full_d=struct(back.full_d.shape, BF),
        full_u=struct(back.full_u.shape, BF),
        full_q=struct(back.full_q.shape, BF),
        full_o=struct(back.full_o.shape, BF),
    )
    kept = dict(
        out=outputs["out"],
        gq=by_device(wq.shape, 4),
        qkv_grad=struct(lower.qkv_0.shape, BF),
        dk=struct((length, mixed_width), F32),
        dv=struct((length, mixed_width), F32),
        dg_line=struct((8, 8, TOK), F32),
        dg_pass=struct((5, 8, TOK), F32),
    )
    loaded = dict(inputs)
    del loaded["d0"]
    scratch = held(loaded, kept)
    scratch |= scatter_scratch(QKV, width)
    for name, count, high, wide, steps in (
        (D0, 1, units // 8, width, 2),
        (U0, 4, rows, units, 3),
        (Q0, 4, rows, part, 3),
        (O0, 1, mixed_width // 8, width, 3),
    ):
        scratch |= reduce_scratch(name, count, high, wide, steps)
        scratch |= finish_scratch(name, count, high, wide)

    def last(ns):
        place, copies = Place(), ns.copies
        line = [place.line(offset)[0] for offset in range(1, 8)]
        meet(with_line(place))
        unused, d0_second = reduce_rep(copies, place, ns.d0, ns, D0)
        u0_first, u0_second = reduce_rep(copies, place, ns.u0_v, ns, U0)
        o0_first, o0_second = reduce_rep(copies, place, ns.o0_v, ns, O0)
        q0_first, q0_second = reduce_rep(copies, place, ns.gq_v, ns, Q0)
        d0_line = line_rows(copies, place, ns, D0)
        o0_line = line_rows(copies, place, ns, O0)
        u0_line = line_columns(copies, place, ns, U0)
        q0_line = line_columns(copies, place, ns, Q0)
        d0_whole = whole_rows(copies, place, ns, D0, ns.full_d)
        o0_whole = whole_rows(copies, place, ns, O0, ns.full_o)
        u0_whole = whole_columns(copies, place, ns, U0, ns.full_u, 2)
        q0_whole = whole_columns(copies, place, ns, Q0, ns.full_q, 6)
        upper = place.upper
        second = copies.remote(ns.second.at[1 - upper], ns.block_out.at[upper], place.far)
        next(d0_second)
        ns.load.u0.wait()
        next(u0_first)
        ns.load.qkv_in.wait()
        ns.load.lse.wait()
        ns.load.mixed_grad.wait()
        ns.load.dg.wait()
        ns.load.o0.wait()
        plan = Plan(
            [stages(d0_second), stages(d0_line)],
            [],
            [stages(u0_first), stages(u0_second)],
            [stages(d0_line), stages(d0_whole)],
            [],
        )
        ns.load.gains.wait()
        grads = bwd_head(ns, place, 0, plan.tick, stages(q0_first), True)
        ns.load.second.wait()
        copies.store(ns.second_v.at[upper], ns.block_out.at[upper])
        ns.out_v[1] = grads[1]().astype(BF)
        for task in (u0_second, u0_line, q0_first, q0_second, o0_first, d0_whole):
            next(task)
        ns.out_v[0] = grads[0]().astype(BF)
        copies.store(ns.out_v.at[upper], ns.out.at[upper])
        gain_grad = gain_sum(ns, copies, place)
        for task in (
            gain_grad, q0_second, q0_line, o0_first, o0_second, u0_line, u0_whole, d0_whole,
            gain_grad, o0_second, o0_line,
        ):
            next(task)
        moved = copies.remote(ns.out_v.at[1 - upper], ns.out.at[upper], place.far)
        for task in (
            u0_whole, q0_line, q0_whole, o0_line, o0_whole, gain_grad, u0_whole, q0_whole,
            o0_whole, gain_grad, q0_whole, o0_whole,
        ):
            next(task)
        moved.wait_recv()
        second.wait_recv()

    flops = 4 * length * width * part
    kernel, options = kernel_of(last, with_line, inputs, outputs, scratch, 4, 128, 128, 60, flops)
    results = pl.pallas_call(kernel, **options)(*inputs.values())
    return named(outputs, results)


def widen(pairs):
    flat = [value for group in pairs for value in group]
    outs = [struct((len(group), *group[0].shape), F32) for group in pairs]

    def finish(*refs):
        sources, targets = refs[: len(flat)], refs[len(flat) : len(flat) + len(outs)]
        low, wide = refs[len(flat) + len(outs) :][: len(flat)], refs[-len(flat) - 2 : -2]
        sem_in, sem_out = refs[-2:]
        slots = [(g, n) for g, group in enumerate(pairs) for n in range(len(group))]
        loads = [pltpu.make_async_copy(sources[i], low[i], sem_in.at[i]) for i in range(len(flat))]
        for copy in loads:
            copy.start()
        stores = []
        for i, (g, n) in enumerate(slots):
            loads[i].wait()

            def step(index):
                at = tile_of(index, 32)
                wide[i][at, :] = low[i][at, :].astype(F32)

            loop(low[i].shape[0] // 32, step)
            stores.append(pltpu.make_async_copy(wide[i], targets[g].at[n], sem_out.at[i]))
            stores[-1].start()
        for copy in stores:
            copy.wait()

    size = sum(value.size for value in flat)
    return pl.pallas_call(
        finish,
        name=finish.__name__,
        out_shape=outs,
        in_specs=[pl.BlockSpec(memory_space=pl.ANY)] * len(flat),
        out_specs=[pl.BlockSpec(memory_space=pl.ANY)] * len(outs),
        scratch_shapes=[
            *(pltpu.VMEM(value.shape, BF) for value in flat),
            *(pltpu.VMEM(value.shape, F32) for value in flat),
            pltpu.SemaphoreType.DMA((len(flat),)),
            pltpu.SemaphoreType.DMA((len(flat),)),
        ],
        compiler_params=pltpu.CompilerParams(vmem_limit_bytes=63 << 20),
        cost_estimate=pl.CostEstimate(flops=size, bytes_accessed=6 * size, transcendentals=0),
    )(*flat)


def gain_sum(ns, copies, place):
    def columns(grp):
        return pl.ds(pl.multiple_of(grp * TOK, TOK), TOK)

    moved = []
    for offset in range(1, 8):
        device, upper, t = place.line(offset)
        source = ns.dg_v.at[:, columns(upper * 4 + t)]
        moved.append(copies.remote(source, ns.dg_line_v.at[place.grp], device))
    ns.dg_line_v[place.grp] = ns.dg_v[:, columns(place.grp)]
    yield
    for copy in moved:
        copy.wait_recv()
    ns.dg_pass_v[0] = jnp.sum(ns.dg_line_v[...], axis=0)
    moved = copies.remote(ns.dg_pass_v.at[0], ns.dg_pass_v.at[1], place.along_x)
    yield
    moved.wait_recv()
    ns.dg_pass_v[2] = ns.dg_pass_v[0] + ns.dg_pass_v[1]
    moved = copies.remote(ns.dg_pass_v.at[2], ns.dg_pass_v.at[3], place.along_y)
    yield
    moved.wait_recv()
    ns.dg_pass_v[4] = ns.dg_pass_v[2] + ns.dg_pass_v[3]
    copies.store(ns.dg_pass_v.at[4], ns.gain_grad)
    yield


def body_pairs(block_in, cotangent, w_qkv, w_out, w_up, w_down, norm_gains):
    layers, rows, width = w_out.shape
    hidden_unit = w_down.shape[1]
    gain_part = jnp.transpose(norm_gains.astype(F32), (0, 2, 1)).reshape(layers * 4, rows)
    down_parts = w_down.reshape(layers, 2, 2, 2, hidden_unit // 8, width)
    out_parts = w_out.reshape(layers, 2, 2, 2, rows // 8, width)

    lower = first_kernel(block_in[:, 0], gain_part, w_qkv, w_up, down_parts, out_parts)
    turned = turn_kernel(lower, lower.gains, down_parts, out_parts, cotangent[:, 0])
    back = backward_kernel(lower, turned)
    last = last_kernel(lower, turned, back)

    pairs = (
        (last.full_d, back.full_d),
        (last.full_u, back.full_u),
        (last.full_q, back.full_q),
        (last.full_o, back.full_o),
        (last.out,),
    )
    wide = widen([[matrix(value) for value in group] for group in pairs])
    return (
        last.block_out[:, None],
        wide[4].reshape(block_in.shape),
        wide[2],
        wide[3],
        wide[1],
        wide[0],
        jnp.transpose(last.gain_grad.reshape(layers, 4, rows), (0, 2, 1)),
    )


def norm_apply(values, gains):
    return values * lax.rsqrt(jnp.mean(values * values, axis=-1, keepdims=True) + EPS) * gains


def inner_rows(left, right):
    return lax.dot_general(
        left, right, (((0,), (0,)), ((), ())), preferred_element_type=jnp.float32
    )


def times_trans(left, right):
    return lax.dot_general(
        left, right, (((1,), (1,)), ((), ())), preferred_element_type=jnp.float32
    )


def split_blocks(whole):
    length = whole.shape[0]
    width = min(512, length)
    count = length // width
    return (whole.reshape(count, width, HEADS, HDIM), width, count)


def block_at(blocks, index):
    return lax.dynamic_index_in_dim(blocks, index, 0, keepdims=False)


def key_scores(query, key_block, key_start, query_pos):
    scale = HDIM ** (-0.5)
    scores = (
        jnp.einsum("qhd,khd->hqk", query, key_block, preferred_element_type=jnp.float32) * scale
    )
    key_pos = key_start + jnp.arange(key_block.shape[0], dtype=jnp.int32)
    allowed = key_pos[None, :] <= query_pos[:, None]
    return (scores, allowed[None])


def attend_split(query, keys_all, values_all, query_pos):
    key_blocks, width, count = split_blocks(keys_all)
    value_blocks = split_blocks(values_all)[0]
    row_count = query.shape[0]
    upper = query_pos[row_count - 1] // width + 1

    def total_step(index, carry):
        running, total = carry
        scores, allowed = key_scores(query, block_at(key_blocks, index), index * width, query_pos)
        newest = jnp.maximum(running, jnp.max(jnp.where(allowed, scores, NEGATIVE), axis=-1))
        terms = jnp.where(allowed, jnp.exp(scores - newest[..., None]), 0.0)
        total = total * jnp.exp(running - newest) + jnp.sum(terms, axis=-1)
        return (newest, total)

    start_run = jnp.full((HEADS, row_count), NEGATIVE, jnp.float32)
    start_total = jnp.zeros((HEADS, row_count), jnp.float32)
    running, total = lax.fori_loop(0, upper, total_step, (start_run, start_total))
    log_total = running + jnp.log(total)

    def mix_step(index, accum):
        scores, allowed = key_scores(query, block_at(key_blocks, index), index * width, query_pos)
        probs = jnp.where(allowed, jnp.exp(scores - log_total[..., None]), 0.0)
        return accum + jnp.einsum(
            "hqk,khd->qhd",
            probs.astype(jnp.bfloat16),
            block_at(value_blocks, index),
            preferred_element_type=jnp.float32,
        )

    start_mix = jnp.zeros((row_count, HEADS, HDIM), jnp.float32)
    mixed = lax.fori_loop(0, upper, mix_step, start_mix)
    return (mixed.reshape(row_count, HEADS * HDIM), log_total)


def attend_back_split(query, keys_all, values_all, log_total, out_grad, delta, query_pos):
    key_blocks, width, count = split_blocks(keys_all)
    value_blocks = split_blocks(values_all)[0]
    row_count = query.shape[0]
    upper = query_pos[row_count - 1] // width + 1
    scale = HDIM ** (-0.5)

    def back_step(index, carry):
        query_acc, pieces = carry
        key_block = block_at(key_blocks, index)
        value_block = block_at(value_blocks, index)
        scores, allowed = key_scores(query, key_block, index * width, query_pos)
        probs = jnp.where(allowed, jnp.exp(scores - log_total[..., None]), 0.0)
        prob_grad = jnp.einsum(
            "qhd,khd->hqk", out_grad, value_block, preferred_element_type=jnp.float32
        )
        score_grad = (probs * (prob_grad - delta[..., None])).astype(jnp.bfloat16)
        query_acc = (
            query_acc
            + jnp.einsum("hqk,khd->qhd", score_grad, key_block, preferred_element_type=jnp.float32)
            * scale
        )
        key_grad = (
            jnp.einsum("hqk,qhd->khd", score_grad, query, preferred_element_type=jnp.float32)
            * scale
        )
        value_grad = jnp.einsum(
            "hqk,qhd->khd", probs.astype(jnp.bfloat16), out_grad, preferred_element_type=jnp.float32
        )
        joined = jnp.concatenate(
            [key_grad.reshape(width, HEADS * HDIM), value_grad.reshape(width, HEADS * HDIM)], axis=1
        )
        pieces = lax.dynamic_update_index_in_dim(pieces, joined, index, 0)
        return (query_acc, pieces)

    start_acc = jnp.zeros((row_count, HEADS, HDIM), jnp.float32)
    start_pieces = jnp.zeros((count, width, 2 * HEADS * HDIM), jnp.float32)
    query_grad, pieces = lax.fori_loop(0, upper, back_step, (start_acc, start_pieces))
    return (query_grad.reshape(row_count, HEADS * HDIM), pieces.reshape(-1, pieces.shape[-1]))


def layer_forward(hidden_in, weights, query_pos):
    w_qkv_full, w_out_full, w_up_full, w_down_full, gain_full = weights
    gains_f = gain_full.astype(jnp.float32)
    row_count = hidden_in.shape[0]
    width = w_out_full.shape[1]
    normed = norm_apply(hidden_in, gains_f[:, 0]).astype(jnp.bfloat16)
    qkv_low = jnp.dot(normed, w_qkv_full, preferred_element_type=jnp.float32).astype(jnp.bfloat16)
    query = qkv_low[:, :width]
    keys_all, values_all = (
        lax.all_gather(qkv_low[:, width : 2 * width], "grp", axis=0, tiled=True),
        lax.all_gather(qkv_low[:, 2 * width :], "grp", axis=0, tiled=True),
    )
    mixed, log_total = attend_split(
        query.reshape(row_count, HEADS, HDIM),
        keys_all.reshape(-1, HEADS, HDIM),
        values_all.reshape(-1, HEADS, HDIM),
        query_pos,
    )
    mixed_low = mixed.astype(jnp.bfloat16)
    attn_out = jnp.dot(mixed_low, w_out_full, preferred_element_type=jnp.float32)
    resid = hidden_in + norm_apply(attn_out, gains_f[:, 1])
    mlp_in = norm_apply(resid, gains_f[:, 2]).astype(jnp.bfloat16)
    up_out = jnp.dot(mlp_in, w_up_full, preferred_element_type=jnp.float32)
    active = jax.nn.gelu(up_out).astype(jnp.bfloat16)
    down_out = jnp.dot(active, w_down_full, preferred_element_type=jnp.float32)
    result = resid + norm_apply(down_out, gains_f[:, 3])
    kept = (
        hidden_in,
        normed,
        qkv_low,
        mixed,
        mixed_low,
        log_total,
        attn_out,
        resid,
        mlp_in,
        up_out,
        active,
        down_out,
    )
    return (result, kept)


def layer_backward(grad_out, weights, kept, query_pos):
    w_qkv_full, w_out_full, w_up_full, w_down_full, gain_full = weights
    (
        hidden_in,
        normed,
        qkv_low,
        mixed,
        mixed_low,
        log_total,
        attn_out,
        resid,
        mlp_in,
        up_out,
        active,
        down_out,
    ) = kept
    gains_f = gain_full.astype(jnp.float32)
    row_count = hidden_in.shape[0]
    width = w_out_full.shape[1]
    unused, puller = jax.vjp(norm_apply, down_out, gains_f[:, 3])
    down_grad, gain_four = puller(grad_out)
    down_low = down_grad.astype(jnp.bfloat16)
    w_down_grad = inner_rows(active, down_low)
    active_grad = times_trans(down_low, w_down_full)
    unused, puller = jax.vjp(jax.nn.gelu, up_out)
    up_low = puller(active_grad)[0].astype(jnp.bfloat16)
    w_up_grad = inner_rows(mlp_in, up_low)
    mlp_grad = times_trans(up_low, w_up_full)
    unused, puller = jax.vjp(norm_apply, resid, gains_f[:, 2])
    resid_part, gain_three = puller(mlp_grad)
    resid_grad = grad_out + resid_part
    unused, puller = jax.vjp(norm_apply, attn_out, gains_f[:, 1])
    attn_grad, gain_two = puller(resid_grad)
    attn_low = attn_grad.astype(jnp.bfloat16)
    w_out_grad = inner_rows(mixed_low, attn_low)
    mixed_grad = times_trans(attn_low, w_out_full).astype(jnp.bfloat16)
    keys_all, values_all = (
        lax.all_gather(qkv_low[:, width : 2 * width], "grp", axis=0, tiled=True),
        lax.all_gather(qkv_low[:, 2 * width :], "grp", axis=0, tiled=True),
    )
    delta = jnp.sum(
        (mixed_grad.astype(jnp.float32) * mixed).reshape(row_count, HEADS, HDIM), axis=-1
    ).T
    query_low = qkv_low[:, :width]
    query_grad, key_value_terms = attend_back_split(
        query_low.reshape(row_count, HEADS, HDIM),
        keys_all.reshape(-1, HEADS, HDIM),
        values_all.reshape(-1, HEADS, HDIM),
        log_total,
        mixed_grad.reshape(row_count, HEADS, HDIM),
        delta,
        query_pos,
    )
    key_value_grad = lax.psum_scatter(
        key_value_terms.astype(jnp.bfloat16), "grp", scatter_dimension=0, tiled=True
    ).astype(jnp.float32)
    qkv_grad = jnp.concatenate([query_grad, key_value_grad], axis=1).astype(jnp.bfloat16)
    w_qkv_grad = inner_rows(normed, qkv_grad)
    normed_grad = times_trans(qkv_grad, w_qkv_full)
    unused, puller = jax.vjp(norm_apply, hidden_in, gains_f[:, 0])
    input_part, gain_one = puller(normed_grad)
    gain_grad = jnp.stack([gain_one, gain_two, gain_three, gain_four], axis=1)
    return (resid_grad + input_part, (w_qkv_grad, w_out_grad, w_up_grad, w_down_grad, gain_grad))


def body_general(block_in, cotangent, w_qkv, w_out, w_up, w_down, norm_gains):
    layer_count = w_qkv.shape[0]
    micro_count = block_in.shape[0]
    row_count = block_in.shape[2]
    query_pos = lax.axis_index("grp") * row_count + jnp.arange(row_count, dtype=jnp.int32)
    totals = [None] * layer_count
    outputs = []
    input_grads = []
    for micro_idx in range(micro_count):
        hidden = block_in[micro_idx, 0].astype(jnp.float32)
        saved = []
        for layer_idx in range(layer_count):
            hidden, kept = layer_forward(
                hidden,
                (
                    lax.all_gather(w_qkv[layer_idx], "grp", axis=0, tiled=True),
                    lax.all_gather(w_out[layer_idx], "grp", axis=0, tiled=True),
                    lax.all_gather(w_up[layer_idx], "grp", axis=0, tiled=True),
                    lax.all_gather(w_down[layer_idx], "grp", axis=0, tiled=True),
                    lax.all_gather(norm_gains[layer_idx], "grp", axis=0, tiled=True),
                ),
                query_pos,
            )
            saved.append(kept)
        outputs.append(hidden.astype(jnp.bfloat16))
        grad_flow = cotangent[micro_idx, 0].astype(jnp.float32)
        for layer_idx in reversed(range(layer_count)):
            grad_flow, parts = layer_backward(
                grad_flow,
                (
                    lax.all_gather(w_qkv[layer_idx], "grp", axis=0, tiled=True),
                    lax.all_gather(w_out[layer_idx], "grp", axis=0, tiled=True),
                    lax.all_gather(w_up[layer_idx], "grp", axis=0, tiled=True),
                    lax.all_gather(w_down[layer_idx], "grp", axis=0, tiled=True),
                    lax.all_gather(norm_gains[layer_idx], "grp", axis=0, tiled=True),
                ),
                saved[layer_idx],
                query_pos,
            )
            if totals[layer_idx] is None:
                totals[layer_idx] = parts
            else:
                totals[layer_idx] = tuple(
                    (left + right for left, right in zip(totals[layer_idx], parts))
                )
        input_grads.append(grad_flow)
    reduced = []
    for layer_idx in range(layer_count):
        accum = totals[layer_idx]
        shards = (
            lax.psum_scatter(
                accum[0].astype(jnp.bfloat16), "grp", scatter_dimension=0, tiled=True
            ).astype(jnp.float32),
            lax.psum_scatter(
                accum[1].astype(jnp.bfloat16), "grp", scatter_dimension=0, tiled=True
            ).astype(jnp.float32),
            lax.psum_scatter(
                accum[2].astype(jnp.bfloat16), "grp", scatter_dimension=0, tiled=True
            ).astype(jnp.float32),
            lax.psum_scatter(
                accum[3].astype(jnp.bfloat16), "grp", scatter_dimension=0, tiled=True
            ).astype(jnp.float32),
            lax.psum_scatter(
                accum[4].astype(jnp.bfloat16), "grp", scatter_dimension=0, tiled=True
            ).astype(jnp.float32),
        )
        reduced.append(
            (
                lax.psum(shards[0].astype(jnp.bfloat16), "rep").astype(jnp.float32),
                lax.psum(shards[1].astype(jnp.bfloat16), "rep").astype(jnp.float32),
                lax.psum(shards[2].astype(jnp.bfloat16), "rep").astype(jnp.float32),
                lax.psum(shards[3].astype(jnp.bfloat16), "rep").astype(jnp.float32),
                lax.psum(shards[4].astype(jnp.bfloat16), "rep").astype(jnp.float32),
            )
        )
    block_out = jnp.stack(outputs)[:, None]
    block_in_grad = jnp.stack(input_grads)[:, None]
    stacked = [
        jnp.stack([reduced[layer_idx][member] for layer_idx in range(layer_count)])
        for member in range(5)
    ]
    return (block_out, block_in_grad, stacked[0], stacked[1], stacked[2], stacked[3], stacked[4])


def solution(mesh):
    rep_size, grp_size = mesh.shape["rep"], mesh.shape["grp"]

    def body(block_in, cotangent, w_qkv, w_out, w_up, w_down, norm_gains):
        sizes = (rep_size, grp_size, block_in.shape[0], w_qkv.shape[0], block_in.shape[2])
        fits = sizes == (4, 8, 2, 2, TOK)
        chosen = body_pairs if fits else body_general
        return chosen(block_in, cotangent, w_qkv, w_out, w_up, w_down, norm_gains)

    tokens = P(None, "rep", "grp", None)
    rows = P(None, "grp", None)
    return jax.shard_map(
        body,
        mesh=mesh,
        in_specs=(tokens, tokens, rows, rows, rows, rows, rows),
        out_specs=(tokens, tokens, rows, rows, rows, rows, rows),
        check_vma=False,
    )
```

```python
import functools
import types

import jax
import jax.numpy as jnp
from jax import lax
from jax.experimental import pallas as pl
from jax.experimental.pallas import tpu as pltpu
from jax.sharding import PartitionSpec as P

HEADS = 16
HDIM = 64
EPS = 1e-06
NEGATIVE = -1e30
BF = jnp.bfloat16
REP, GRP = "rep", "grp"
F32 = jnp.float32


def dot(left, right):
    return jnp.dot(left, right, preferred_element_type=F32)


def dot_tn(left, right):
    return lax.dot_general(left, right, (((0,), (0,)), ((), ())), preferred_element_type=F32)


def dot_nt(left, right):
    return lax.dot_general(left, right, (((1,), (1,)), ((), ())), preferred_element_type=F32)


def norm(values, gain):
    return values * lax.rsqrt(jnp.mean(values * values, axis=-1, keepdims=True) + EPS) * gain


def head_mask(width, head):
    lanes = lax.broadcasted_iota(jnp.int32, (1, width), 1)
    return (lanes // HDIM) == head


def causal_scores(query, keys, below, start):
    scores = dot_nt(query, keys)
    last = jnp.where(below, scores[:, start:], NEGATIVE)
    return jnp.concatenate([scores[:, :start], last], axis=1) if start else last


def attend(ns, stream, block=256):
    length, width = ns.mixed_v.shape
    qkv_ref, lse_ref, sum_ref = ns.qkv_in_v, ns.lse_v, ns.terms_own.at[stream]
    row = lax.broadcasted_iota(jnp.int32, (block, block), 0)
    col = lax.broadcasted_iota(jnp.int32, (block, block), 1)
    below = col <= row
    zero = jnp.zeros((), BF)
    lane = lax.broadcasted_iota(jnp.int32, (1, 128), 1)
    base, high = stream * length // 2, (stream + 1) * length // 2
    sum_ref[...] = jnp.zeros_like(sum_ref)
    lse_ref[base:high, :] = jnp.zeros((length // 2, 128), F32)

    def one_head(head):
        mask = head_mask(width, head)
        for start in range(base, high, block):
            stop = start + block
            query = qkv_ref[start:stop, :width] * jnp.asarray(HDIM**-0.5, BF)
            query = jnp.where(mask, query, zero)
            scores = causal_scores(query, qkv_ref[:stop, width : 2 * width], below, start)
            top = jnp.max(scores, axis=1, keepdims=True)
            terms = jnp.exp(scores - top)
            sums = jnp.sum(terms, axis=1, keepdims=True)
            mixed = dot(terms.astype(BF), qkv_ref[:stop, 2 * width :]) * (1.0 / sums)
            sum_ref[:, start - base : stop - base] += jnp.where(mask, mixed, 0.0)
            stats = lse_ref[start:stop, :]
            lse_ref[start:stop, :] = jnp.where(lane == head, top + jnp.log(sums), stats)

    loop(width // HDIM, one_head)
    for start in range(base, high, block):
        ns.mixed_v[start : start + block, :] = sum_ref[:, start - base : start - base + width].astype(BF)


def attend_back(ns, stream, block=256):
    length, width = ns.mixed_grad_v.shape
    qkv_ref, grad_ref, sum_ref = ns.qkv_in_v, ns.mixed_grad_v, ns.terms_own.at[stream]
    row = lax.broadcasted_iota(jnp.int32, (block, block), 0)
    col = lax.broadcasted_iota(jnp.int32, (block, block), 1)
    below = col <= row
    zero = jnp.zeros((), BF)
    scale = HDIM**-0.5
    lane = lax.broadcasted_iota(jnp.int32, (1, 128), 1)
    base, high = stream * length // 2, (stream + 1) * length // 2
    sum_ref[...] = jnp.zeros_like(sum_ref)

    def one_head(head):
        mask = head_mask(width, head)
        for start in range(base, high, block):
            stop = start + block
            query = qkv_ref[start:stop, :width] * jnp.asarray(scale, BF)
            query = jnp.where(mask, query, zero)
            grad = jnp.where(mask, grad_ref[start:stop, :], zero)
            keys, vals = qkv_ref[:stop, width : 2 * width], qkv_ref[:stop, 2 * width :]
            scores = causal_scores(query, keys, below, start)
            lse = jnp.where(lane == head, ns.lse_v[start:stop, :], 0.0)
            probs = jnp.exp(scores - jnp.sum(lse, axis=1, keepdims=True))
            prob_grad = dot_nt(grad, vals)
            delta = jnp.sum(probs * prob_grad, axis=1, keepdims=True)
            score_grad = (probs * (prob_grad - delta)).astype(BF)
            query_grad = jnp.where(mask, dot(score_grad, keys), 0.0)
            sum_ref[:, start - base : stop - base] += query_grad
            ns.dk_v[:stop, :] += dot_tn(score_grad, query)
            ns.dv_v[:stop, :] += dot_tn(probs.astype(BF), grad)

    loop(width // HDIM, one_head)
    for start in range(base, high, block):
        value = sum_ref[:, start - base : start - base + width] * scale
        ns.qkv_grad_v[start : start + block, :width] = value.astype(BF)
    ns.qkv_grad_v[base:high, width : 2 * width] = ns.dk_v[base:high, :].astype(BF)
    ns.qkv_grad_v[base:high, 2 * width :] = ns.dv_v[base:high, :].astype(BF)


MESH_ID = pl.DeviceIdType.MESH
HELD, ONE, TWO, SUM, LINE, FULL = "_v", "one", "two", "sum", "line", "full"
PASSED = ("give", "take", "send", "got")
ATTN, DOWN, UP, QKV = "attn", "down", "up", "qkv"
D0, U0, Q0, O0 = "d0", "u0", "q0", "o0"
D1, U1, Q1, O1 = "d1", "u1", "q1", "o1"
TOK = 128


class Place:
    def __init__(self):
        rep, grp = lax.axis_index(REP), lax.axis_index(GRP)
        self.rep, self.grp = rep, grp
        self.x, self.y = lax.rem(rep, 2), lax.div(rep, 2)
        self.t, self.upper = lax.rem(grp, 4), lax.div(grp, 4)
        self.c, self.side = lax.rem(grp, 2), lax.div(self.t, 2)
        base = self.upper * 4
        self.core = (rep, base + self.side * 2 + 1 - self.c)
        self.near = (rep, base + (1 - self.side) * 2 + self.c)
        self.far = (rep, (1 - self.upper) * 4 + self.t)
        self.along_x = (self.y * 2 + 1 - self.x, grp)
        self.along_y = ((1 - self.y) * 2 + self.x, grp)
        self.near_t = (1 - self.side) * 2 + self.c

    def line(self, offset):
        c = 1 - self.c if offset & 1 else self.c
        side = 1 - self.side if offset & 2 else self.side
        upper = 1 - self.upper if offset & 4 else self.upper
        return (self.rep, upper * 4 + side * 2 + c), upper, side * 2 + c


class Copies:
    def __init__(self, send, recv, here):
        self.sems, self.here = (send, recv), here
        self.sent, self.local_count, self.stores, self.done = [], 0, [], set()

    def remote(self, source, target, device):
        at = len(self.sent)
        assert at < self.sems[0].shape[0]
        copy = pltpu.make_async_remote_copy(
            src_ref=source,
            dst_ref=target,
            send_sem=self.sems[0].at[at],
            recv_sem=self.sems[1].at[at],
            device_id=device,
            device_id_type=MESH_ID,
        )
        copy.start()
        self.sent.append(copy)
        return copy

    def local(self, source, target):
        assert self.local_count < self.here.shape[0]
        copy = pltpu.make_async_copy(source, target, self.here.at[self.local_count])
        self.local_count += 1
        copy.start()
        return copy

    def store(self, source, target):
        self.stores.append(self.local(source, target))

    def both(self, *copies):
        for copy in copies:
            copy.wait_recv()
            copy.wait_send()
            self.done.add(id(copy))

    def finish(self):
        for copy in self.sent:
            if id(copy) not in self.done:
                copy.wait_send()
        for copy in self.stores:
            copy.wait()


def announce(devices):
    barrier = pltpu.get_barrier_semaphore()
    for device in devices:
        pl.semaphore_signal(barrier, inc=1, device_id=device, device_id_type=MESH_ID)


def meet(devices):
    pl.semaphore_wait(pltpu.get_barrier_semaphore(), len(devices))


def with_line(place):
    line = [place.line(offset)[0] for offset in range(1, 8)]
    return [*line, place.along_x, place.along_y]


def with_few(place):
    return [place.core, place.near, place.far, place.along_x, place.along_y]


class Plan:
    def __init__(self, *entries):
        self.entries = list(entries)

    def tick(self):
        if self.entries:
            for action in self.entries.pop(0):
                action()

    def drain(self):
        while self.entries:
            self.tick()


def stages(task):
    return lambda: next(task, None)


def spread(copies, place, part, last=True):
    x, y, every = place.x, place.y, slice(None)
    one = copies.remote(part(0, y, x), part(0, y, x), place.along_x)
    two = copies.remote(part(1, y, x), part(1, y, x), place.along_y)
    yield
    one.wait_recv()
    three = copies.remote(part(0, y, every), part(0, y, every), place.along_y)
    two.wait_recv()
    four = copies.remote(part(1, every, x), part(1, every, x), place.along_x)
    yield
    three.wait_recv()
    four.wait_recv()
    if last:
        yield


def deal(copies, place, source, target):
    moved = []
    own = copies.local(source.at[place.t], target)
    for offset in range(1, 8):
        if offset == 4:
            yield
        device, upper, t = place.line(offset)
        moved.append(copies.remote(source.at[t], target, device))
    yield
    own.wait()
    for copy in moved:
        copy.wait_recv()
    yield


def add_low(one, two):
    return (one.astype(F32) + two.astype(F32)).astype(BF)


def reduce_rep(copies, place, grad, ns, name):
    x, y = place.x, place.y
    count = grad.shape[1]

    def step_one():
        one = getattr(ns, name + ONE)
        first = copies.remote(grad.at[0, :, :, 1 - x], one.at[0], place.along_x)
        second = copies.remote(grad.at[1, :, 1 - y], one.at[1], place.along_y)
        yield
        copies.both(first, second)
        for i in range(count):
            for j in range(2):
                grad[0, i, j, x] = add_low(grad[0, i, j, x], one[0, i, j])
                grad[1, i, y, j] = add_low(grad[1, i, y, j], one[1, i, j])
        yield

    def step_two():
        two, total = getattr(ns, name + TWO), getattr(ns, name + SUM)
        first = copies.remote(grad.at[0, :, 1 - y, x], two.at[0], place.along_y)
        second = copies.remote(grad.at[1, :, y, 1 - x], two.at[1], place.along_x)
        own = [copies.local(grad.at[half, :, y, x], total.at[half]) for half in range(2)]
        yield
        copies.both(first, second)
        for half in range(2):
            own[half].wait()
            for i in range(count):
                total[half, i] = add_low(total[half, i], two[half, i])
        yield

    return step_one(), step_two()


def line_columns(copies, place, ns, name):
    total, line, full = (getattr(ns, name + part) for part in (SUM, LINE, FULL))
    moved = []
    for offset in range(1, 8):
        device, upper, t = place.line(offset)
        here = line.at[place.upper, place.t]
        moved.append(copies.remote(total.at[upper, t], here, device))
    line[place.upper, place.t] = total[place.upper, place.t]
    yield
    for copy in moved:
        copy.wait_recv()
    for t in range(4):
        full[place.y, place.x, t] = add_low(line[0, t], line[1, t])
    yield


def line_rows(copies, place, ns, name):
    total, line, full = (getattr(ns, name + part) for part in (SUM, LINE, FULL))
    moved = copies.remote(total.at[1 - place.upper, 0], line, place.far)
    yield
    moved.wait_recv()
    rows = line.shape[0] // 2
    for half in range(2):
        at = pl.ds(half * rows, rows)
        full[place.y, place.x, half] = add_low(total[place.upper, 0, at, :], line[at, :])
    yield


def whole_columns(copies, place, ns, name, target, groups):
    full = getattr(ns, name + FULL)
    yield from spread(copies, place, lambda half, a, b: full.at[a, b, pl.ds(2 * half, 2)], False)
    unit = full.shape[4] // groups
    for t in range(4):
        for k in range(groups):
            source = full.at[:, :, t, :, k * unit : (k + 1) * unit]
            start = (k * 4 + t) * unit
            copies.store(source, target.at[:, :, :, start : start + unit])
    yield


def whole_rows(copies, place, ns, name, target):
    full = getattr(ns, name + FULL)
    yield from spread(copies, place, lambda half, a, b: full.at[a, b, half], False)
    copies.store(full, target)
    yield


def reduce_scratch(name, count, rows, width, steps=3):
    total = {}
    if steps & 1:
        total[name + ONE] = pltpu.VMEM((2, count, 2, rows, width), BF)
    if steps & 2:
        total[name + TWO] = pltpu.VMEM((2, count, rows, width), BF)
        total[name + SUM] = pltpu.VMEM((2, count, rows, width), BF)
    return total


def finish_scratch(name, count, rows, width):
    if count == 1:
        line, full = (rows, width), (2, 2, 2, rows // 2, width)
    else:
        line, full = (2, count, rows, width), (2, 2, count, rows, width)
    return {name + LINE: pltpu.VMEM(line, BF), name + FULL: pltpu.VMEM(full, BF)}


def by_device(shape, count):
    rows, width = shape
    return struct((2, count, 2, 2, rows // (8 * count), width), BF)


def loop(count, step):
    def run(index, carry):
        step(index)
        return carry

    lax.fori_loop(0, count, run, 0)


def tile_of(index, size):
    return pl.ds(pl.multiple_of(index * size, size), size)


def matrix(value):
    return value.reshape(-1, value.shape[-1])


def times(left, right_ref, tile, sink):
    every = (slice(None),) * (len(right_ref.shape) - 1)

    def step(index):
        at = tile_of(index, tile)
        sink(at, dot(left(), matrix(right_ref[(*every, at)])))

    loop(right_ref.shape[-1] // tile, step)


def times_rows(left, right_ref, tile, sink):
    flat = len(right_ref.shape) == 2

    def step(index):
        if flat:
            at = tile_of(index, tile)
            sink(at, dot_nt(left(), right_ref[at, :]))
        else:
            block = matrix(right_ref[index])
            sink(tile_of(index, block.shape[0]), dot_nt(left(), block))

    loop(right_ref.shape[0] // (tile if flat else 1), step)


def gram(left_ref, right_ref, out_ref):
    count, tile = out_ref.shape[1], 256
    total = left_ref.shape[1]
    if total == tile:
        value = dot_tn(left_ref[...], right_ref[...]).astype(BF)
        out_ref[...] = value.reshape(out_ref.shape)
        return

    def step(index):
        value = dot_tn(left_ref[:, tile_of(index, tile)], right_ref[...]).astype(BF)
        half, part = lax.div(index, 2), lax.rem(index, 2)
        if count == 1:
            out_ref[half, 0, part] = value.reshape(out_ref.shape[3:])
        else:
            out_ref[half, pl.ds(part * 2, 2)] = value.reshape(2, *out_ref.shape[2:])

    loop(total // tile, step)


class Gather:
    def __init__(self, copies, place, buf, order=(0, 1)):
        self.copies, self.place, self.buf, self.order = copies, place, buf, order
        self.flight = {}

    def rows(self, stream, where):
        start = (self.order[stream] * 4 + where) * TOK
        return pl.ds(pl.multiple_of(start, TOK), TOK)

    def pair(self, stream, side):
        start = (self.order[stream] * 4 + side * 2) * TOK
        return pl.ds(pl.multiple_of(start, TOK), 2 * TOK)

    def start(self, stream, block):
        at = self.rows(stream, self.place.t)
        self.buf[at, :] = block
        mine = self.buf.at[at, :]
        across = self.copies.remote(mine, mine, self.place.near)
        beside = self.copies.remote(mine, mine, self.place.core)
        self.flight[stream] = [across, beside]

    def wait_chip(self, stream):
        self.flight[stream][1].wait_recv()

    def forward(self, stream):
        self.flight[stream][0].wait_recv()
        got = self.buf.at[self.rows(stream, self.place.near_t), :]
        self.flight[stream].append(self.copies.remote(got, got, self.place.core))

    def wait_rest(self, stream):
        self.flight[stream][2].wait_recv()


class Scatter:
    def __init__(self, copies, place, ns, name):
        self.copies, self.place = copies, place
        self.away, self.own = ns.terms_away, ns.terms_own
        self.give, self.take, self.send, self.got = (
            getattr(ns, name + part) for part in PASSED
        )
        self.flight = {}

    def push(self, stream, product):
        place, copies = self.place, self.copies
        mine = pl.ds(pl.multiple_of(place.c * TOK, TOK), TOK)
        other = pl.ds(pl.multiple_of((1 - place.c) * TOK, TOK), TOK)

        def to_away(at, value):
            self.away[:, at] = value

        def to_own(at, value):
            self.own[stream, :, at] = value

        product(1 - place.side, to_away)
        self.give[stream, 0] = self.away[other, :].astype(BF)
        first = copies.remote(self.give.at[stream, 0], self.take.at[stream, 0], place.core)
        product(place.side, to_own)
        first.wait_recv()
        self.send[stream] = (self.away[mine, :] + self.take[stream, 0].astype(F32)).astype(BF)
        across = copies.remote(self.send.at[stream], self.got.at[stream], place.near)
        self.give[stream, 1] = self.own[stream, other, :].astype(BF)
        second = copies.remote(self.give.at[stream, 1], self.take.at[stream, 1], place.core)
        self.flight[stream] = (second, across)

    def result(self, stream):
        second, across = self.flight[stream]
        mine = pl.ds(pl.multiple_of(self.place.c * TOK, TOK), TOK)
        second.wait_recv()
        total = self.own[stream, mine, :] + self.take[stream, 1].astype(F32)
        across.wait_recv()
        return total + self.got[stream].astype(F32)


def scatter_scratch(name, width):
    give, take, send, got = (name + part for part in PASSED)
    return {
        "terms_away": pltpu.VMEM((2 * TOK, width), F32),
        "terms_own": pltpu.VMEM((2, 2 * TOK, width), F32),
        give: pltpu.VMEM((2, 2, TOK, width), BF),
        take: pltpu.VMEM((2, 2, TOK, width), BF),
        send: pltpu.VMEM((2, TOK, width), BF),
        got: pltpu.VMEM((2, TOK, width), BF),
    }


def gelu_both(x):
    cubic = x * x * 0.044715
    bent = jnp.tanh(0.7978845608028654 * (x + cubic * x))
    half = 0.5 * (1.0 + bent)
    slope = half + 0.5 * x * (1.0 - bent * bent) * (0.7978845608028654 * (1.0 + 3.0 * cubic))
    return x * half, slope


def norm_back_in(values, gain, grad):
    rstd = lax.rsqrt(jnp.mean(values * values, axis=-1, keepdims=True) + EPS)
    hat = values * rstd
    scaled = grad * gain
    back = rstd * (scaled - hat * jnp.mean(scaled * hat, axis=-1, keepdims=True))
    return back, jnp.sum(grad * hat, axis=0, keepdims=True)


def next_qkv(ns, place, blocks, tick, wait_weights, order=(0, 1), late=None):
    gather = Gather(ns.copies, place, ns.normed_v, order)
    for stream in range(2):
        if late and stream == 1:
            late()
        gather.start(stream, blocks[stream]())
        tick()
    if late:
        for stream in range(2):
            gather.forward(stream)
            tick()
    wait_weights()
    for stream in range(2):

        def project(side):
            at = gather.pair(stream, side)

            def sink(cols, value):
                ns.qkv_v[at, cols] = value.astype(BF)

            times(lambda: ns.normed_v[at, :], ns.wq_v, 384, sink)

        gather.wait_chip(stream)
        project(place.side)
        if not late:
            gather.forward(stream)
        gather.wait_rest(stream)
        project(1 - place.side)
        tick()
        here = pl.ds(pl.multiple_of(order[stream] * 4 * TOK, 4 * TOK), 4 * TOK)
        ns.copies.store(ns.normed_v.at[here, :], ns.normed.at[here, :])
        ns.copies.store(ns.qkv_v.at[here, :], ns.qkv.at[here, :])


def fwd_mid(ns, place, gain, tick, wait_out, wait_up, wait_down):
    copies = ns.copies
    attn = Scatter(copies, place, ns, ATTN)
    down = Scatter(copies, place, ns, DOWN)
    gather = Gather(copies, place, ns.mlp_v)
    wo, wu, wd = ns.wo_v, ns.wu_v, ns.wd_v
    for stream in range(2):

        def product(side, sink):
            at = gather.pair(stream, side)
            times(lambda: ns.mixed_v[at, :], wo, 512, sink)

        attend(ns, stream)
        tick()
        if stream == 0:
            wait_out()
        attn.push(stream, product)
        tick()
    ns.load.hidden.wait()
    for stream in range(2):
        value = attn.result(stream)
        ns.attn_out_v[stream] = value
        resid = ns.hidden_v[stream].astype(F32) + norm(value, gain(1))
        ns.resid_v[stream] = resid
        gather.start(stream, norm(resid, gain(2)).astype(BF))
        tick()
    wait_up()
    for stream in range(2):

        def expand(side):
            at = gather.pair(stream, side)

            def sink(cols, value):
                active, slope = gelu_both(value)
                ns.active_v[at, cols] = active.astype(BF)
                ns.slope_v[at, cols] = slope.astype(BF)

            times(lambda: ns.mlp_v[at, :], wu, 256, sink)

        gather.wait_chip(stream)
        expand(place.side)
        gather.forward(stream)
        gather.wait_rest(stream)
        expand(1 - place.side)
        if stream == 0:
            wait_down()

        def product(side, sink):
            at = gather.pair(stream, side)
            times(lambda: ns.active_v[at, :], wd, 512, sink)

        down.push(stream, product)
        tick()
    return down


def bwd_mid(ns, place, layer, grads, tick, on_down, on_up, order=(0, 1)):
    copies, gain, base = ns.copies, rows_of(ns, layer), layer * 4
    up = Scatter(copies, place, ns, UP)
    first = Gather(copies, place, ns.down_grad_v)
    second = Gather(copies, place, ns.attn_grad_v)
    wo, wu, wd = ns.wo_v, ns.wu_v, ns.wd_v
    for stream in order:
        grad = grads[stream]()
        ns.grad_v[stream] = grad
        back, four = norm_back_in(ns.down_out_v[stream], gain(3), grad)
        ns.dg_v[base + 3 : base + 4, :] += four
        first.start(stream, back.astype(BF))
        tick()
    for stream in order:

        def shrink(side):
            at = first.pair(stream, side)

            def sink(cols, value):
                slope = ns.slope_v[at, cols].astype(F32)
                ns.up_grad_v[at, cols] = (value * slope).astype(BF)

            times_rows(lambda: ns.down_grad_v[at, :], wd, 512, sink)

        first.wait_chip(stream)
        shrink(place.side)
        first.forward(stream)
        first.wait_rest(stream)
        shrink(1 - place.side)

        def product(side, sink):
            at = first.pair(stream, side)
            times_rows(lambda: ns.up_grad_v[at, :], wu, 512, sink)

        up.push(stream, product)
        tick()
    for stream in order:
        back, three = norm_back_in(ns.resid_v[stream], gain(2), up.result(stream))
        grad = ns.grad_v[stream] + back
        ns.grad_v[stream] = grad
        ns.dg_v[base + 2 : base + 3, :] += three
        back, two = norm_back_in(ns.attn_out_v[stream], gain(1), grad)
        ns.dg_v[base + 1 : base + 2, :] += two
        second.start(stream, back.astype(BF))
        tick()
        if stream == order[0]:
            gram(ns.active_v, ns.down_grad_v, ns.gd_v)
            on_down()
        else:
            gram(ns.mlp_v, ns.up_grad_v, ns.gu_v)
            on_up()
            tick()
    copies.store(ns.grad_v, ns.resid_grad)
    for stream in order:

        def project(side):
            at = second.pair(stream, side)
            ns.mixed_grad_v[at, :] = dot_nt(ns.attn_grad_v[at, :], matrix(wo[...])).astype(BF)

        second.wait_chip(stream)
        project(place.side)
        second.forward(stream)
        second.wait_rest(stream)
        project(1 - place.side)
        tick()
        here = pl.ds(stream * 4 * TOK, 4 * TOK)
        copies.store(ns.mixed_grad_v.at[here, :], ns.mixed_grad.at[here, :])
    gram(ns.mixed_v, ns.attn_grad_v, ns.go_v)


def bwd_head(ns, place, layer, tick, on_qkv, weight_first):
    copies, gain = ns.copies, rows_of(ns, layer)
    qkv = Scatter(copies, place, ns, QKV)
    walk = Gather(copies, place, None)

    def weight():
        ns.load.normed.wait()
        gram(ns.normed_v, ns.qkv_grad_v, ns.gq_v)
        on_qkv()
        tick()

    ns.dk_v[...] = jnp.zeros_like(ns.dk_v)
    ns.dv_v[...] = jnp.zeros_like(ns.dv_v)
    for stream in (1, 0):

        def product(side, sink):
            at = walk.pair(stream, side)
            times_rows(lambda: ns.qkv_grad_v[at, :], ns.wq_v, 512, sink)

        attend_back(ns, stream)
        tick()
        if stream == 1:
            ns.load.wq.wait()
        elif weight_first:
            weight()
        qkv.push(stream, product)
        tick()
    if not weight_first:
        weight()
    ns.load.hidden.wait()
    ns.load.grad.wait()

    def result(stream):
        back, one = norm_back_in(ns.hidden_v[stream].astype(F32), gain(0), qkv.result(stream))
        ns.dg_v[layer * 4 : layer * 4 + 1, :] += one
        return ns.grad_v[stream] + back

    return [functools.partial(result, stream) for stream in range(2)]


def kernel_of(body, reach, inputs, outputs, scratch, slot, remotes, locals_, vmem, flops):
    names = [*inputs, *outputs, *scratch]

    def kernel(*refs):
        ns = types.SimpleNamespace(**dict(zip(names, refs)))
        ns.copies = Copies(*refs[len(names) :])
        announce(reach(Place()))
        ns.load = types.SimpleNamespace()
        for name in inputs:
            if name + HELD in scratch:
                copy = ns.copies.local(getattr(ns, name), getattr(ns, name + HELD))
                setattr(ns.load, name, copy)
        body(ns)
        ns.copies.finish()

    moved = sum(v.size * v.dtype.itemsize for v in [*inputs.values(), *outputs.values()])
    return kernel, dict(
        name=body.__name__,
        out_shape=list(outputs.values()),
        in_specs=[pl.BlockSpec(memory_space=pl.ANY)] * len(inputs),
        out_specs=[pl.BlockSpec(memory_space=pl.ANY)] * len(outputs),
        scratch_shapes=[
            *scratch.values(),
            pltpu.SemaphoreType.DMA((remotes,)),
            pltpu.SemaphoreType.DMA((remotes,)),
            pltpu.SemaphoreType.DMA((locals_,)),
        ],
        compiler_params=pltpu.CompilerParams(
            collective_id=slot, has_side_effects=True, vmem_limit_bytes=vmem << 20
        ),
        cost_estimate=pl.CostEstimate(flops=flops, bytes_accessed=moved, transcendentals=0),
    )


def named(outputs, results):
    return types.SimpleNamespace(**dict(zip(outputs, results)))


def held(*groups):
    merged = {name: value for group in groups for name, value in group.items()}
    return {name + HELD: pltpu.VMEM(value.shape, value.dtype) for name, value in merged.items()}


def struct(shape, dtype):
    return jax.ShapeDtypeStruct(shape, dtype)


def rows_of(ns, layer):
    return lambda index, level=layer: ns.gains_v[level * 4 + index : level * 4 + index + 1, :]


def quarter_of(ns, place, weight, layer, target):
    rows = weight.shape[1] // 4
    at = pl.ds(pl.multiple_of(place.rep * rows, rows), rows)
    return ns.copies.local(weight.at[layer, at, :], target)


def arrange(quarter, dealt, groups):
    unit = quarter.shape[1] // (groups * 4)
    for t in range(4):
        for k in range(groups):
            start = (k * 4 + t) * unit
            dealt[t, :, k * unit : (k + 1) * unit] = quarter[:, start : start + unit]


def by_rows(ref, place):
    return lambda half, a, b: ref.at[1 - place.upper, a, b, half]


def by_columns(ref):
    return lambda half, a, b: ref.at[half, :, a, b]


def first_kernel(block, gain_part, w_qkv, w_up, w_down, w_out):
    width, part = block.shape[2], w_qkv.shape[2] // 4
    length, mixed_width = 8 * TOK, part // 3
    units, rows = w_up.shape[2] // 4, width // 32
    inputs = dict(
        block=block, gain_part=gain_part, w_qkv=w_qkv, w_up=w_up, w_down=w_down, w_out=w_out
    )
    blocks = struct((2, TOK, width), F32)
    wide = struct((length, width), BF)
    next_u, next_o = struct((2, 4, rows, units), BF), struct((2, *w_out.shape[1:]), BF)
    early = dict(
        hidden=struct(block.shape, BF),
        gains=struct((gain_part.shape[0], width), F32),
        normed_0=wide,
        qkv_0=struct((length, part), BF),
        wq_0=struct((2, 4, 2, 2, rows, part), BF),
    )
    outputs = dict(
        early,
        mixed=struct((length, mixed_width), BF),
        lse=struct((length, 128), F32),
        attn_out=blocks,
        resid=blocks,
        mlp=wide,
        active=struct((length, units), BF),
        slope=struct((length, units), BF),
        down_out=blocks,
        hidden_out=blocks,
        normed=wide,
        qkv=struct((length, part), BF),
        wu=struct((2, 4, 2, 2, rows, units), BF),
        wd=struct((2, *w_down.shape[1:]), BF),
        wo=next_o,
        wq=struct((2, 4, 2, 2, rows, part), BF),
    )
    kept = dict(
        quarter_q=struct((rows, 4 * part), BF),
        quarter_u=struct((rows, 4 * units), BF),
        deal_q=struct((4, rows, part), BF),
        deal_u=struct((4, rows, units), BF),
        quarter_q0=struct((rows, 4 * part), BF),
        quarter_u0=struct((rows, 4 * units), BF),
        deal_q0=struct((4, rows, part), BF),
        deal_u0=struct((4, rows, units), BF),
    )
    scratch = held(outputs, kept)
    outputs = dict(outputs, next_u=next_u, next_o=next_o)
    scratch |= scatter_scratch(ATTN, width) | scatter_scratch(DOWN, width)

    def tokens_in(ns, place, ahead):
        copies = ns.copies
        upper, y, x = place.upper, place.y, place.x
        columns = pl.ds(pl.multiple_of(place.grp * TOK, TOK), TOK)
        line = [place.line(offset)[0] for offset in range(1, 8)]
        quarter_q = quarter_of(ns, place, ns.w_qkv, 0, ns.quarter_q_v)
        quarter_u = quarter_of(ns, place, ns.w_up, 0, ns.quarter_u_v)
        kept = copies.local(ns.block.at[upper], ns.hidden_v.at[upper])
        gain_own = copies.local(ns.gain_part, ns.gains_v.at[:, columns])
        quarter_q.wait()
        arrange(ns.quarter_q_v, ns.deal_q_v, 6)
        meet(with_line(place))
        gain_rest = [copies.remote(ns.gain_part, ns.gains_v.at[:, columns], at) for at in line]
        wq_dealt = deal(copies, place, ns.deal_q_v, ns.wq_v.at[upper, place.t, y, x])
        next(wq_dealt)
        next(wq_dealt)
        brought = copies.remote(ns.block.at[1 - upper], ns.hidden_v.at[upper], place.far)
        next(ahead)
        out_in = copies.remote(ns.w_out.at[0, y, x], ns.wo_v.at[upper, y, x], place.far)
        wq_spread = spread(copies, place, by_columns(ns.wq_v))
        out_spread = spread(copies, place, by_rows(ns.wo_v, place))
        up_dealt = deal(copies, place, ns.deal_u_v, ns.wu_v.at[upper, place.t, y, x])
        quarter_u.wait()
        arrange(ns.quarter_u_v, ns.deal_u_v, 2)
        next(up_dealt)
        kept.wait()
        gain_own.wait()
        for copy in gain_rest:
            copy.wait_recv()

        def late():
            next(wq_spread)
            brought.wait_recv()
            copies.store(ns.hidden_v, ns.hidden)

        def out_arrived():
            out_in.wait_recv()
            next(out_spread)

        def wait_weights():
            next(ahead)
            next(wq_spread)
            copies.store(ns.wq_v, ns.wq)

        copies.store(ns.gains_v, ns.gains)
        order = (upper, 1 - upper)
        blocks = [
            functools.partial(
                lambda s: norm(ns.hidden_v[s].astype(F32), ns.gains_v[0:1, :]).astype(BF), stream
            )
            for stream in order
        ]
        plan = Plan(
            [stages(wq_dealt), stages(wq_spread)],
            [stages(up_dealt)],
            [out_arrived],
            [stages(out_spread)],
        )
        next_qkv(ns, place, blocks, plan.tick, wait_weights, order, late)
        next(out_spread)
        return up_dealt

    def rest_of(ns, place, up_dealt, loads, down_in, q_deal):
        copies = ns.copies
        upper, t, y, x = place.upper, place.t, place.y, place.x
        unused, whole_o, whole_d, quarter_u = loads
        next(up_dealt)
        up_spread = spread(copies, place, by_columns(ns.wu_v))
        down_spread = spread(copies, place, by_rows(ns.wd_v, place))
        next(up_spread)
        q_spread = spread(copies, place, by_columns(ns.wq_v))
        u_deal = deal(copies, place, ns.deal_u_v, ns.next_u.at[upper, t])
        o_spread = spread(copies, place, by_rows(ns.next_o, place))
        rest = []

        def out_part():
            rest.append(copies.remote(ns.w_out.at[1, y, x], ns.next_o.at[upper, y, x], place.far))

        def deal_up():
            quarter_u.wait()
            arrange(ns.quarter_u_v, ns.deal_u_v, 2)
            next(u_deal)
            next(u_deal)

        def down_arrived():
            down_in.wait_recv()
            next(down_spread)

        def out_arrived():
            rest[0].wait_recv()
            next(o_spread)

        plan = Plan(
            [],
            [],
            [stages(up_spread)],
            [deal_up],
            [down_arrived],
            [stages(down_spread), out_part],
            [stages(q_deal), stages(q_spread)],
            [stages(q_spread)],
            [out_arrived],
            [],
            [stages(o_spread)],
            [stages(o_spread)],
        )
        gain = rows_of(ns, 0)

        def wait_out():
            whole_o.wait()
            copies.store(ns.wo_v, ns.wo)

        def wait_down():
            next(down_spread)
            whole_d.wait()
            copies.store(ns.wu_v, ns.wu)
            copies.store(ns.wd_v, ns.wd)

        def wait_next():
            next(q_spread)
            copies.store(ns.wq_v, ns.wq)

        down = fwd_mid(ns, place, gain, plan.tick, wait_out, lambda: next(up_spread), wait_down)
        copies.store(ns.mixed_v, ns.mixed)
        copies.store(ns.lse_v, ns.lse)
        copies.store(ns.attn_out_v, ns.attn_out)
        copies.store(ns.resid_v, ns.resid)
        copies.store(ns.mlp_v, ns.mlp)
        copies.store(ns.active_v, ns.active)
        copies.store(ns.slope_v, ns.slope)

        def block(stream):
            value = down.result(stream)
            ns.down_out_v[stream] = value
            hidden_out = ns.resid_v[stream] + norm(value, gain(3))
            ns.hidden_out_v[stream] = hidden_out
            return norm(hidden_out, gain(0, 1)).astype(BF)

        blocks = [functools.partial(block, stream) for stream in range(2)]
        next_qkv(ns, place, blocks, plan.tick, wait_next)
        copies.store(ns.down_out_v, ns.down_out)
        copies.store(ns.hidden_out_v, ns.hidden_out)
        plan.drain()
        next(u_deal)

    def first(ns):
        place = Place()
        initial = types.SimpleNamespace(**vars(ns))
        initial.normed, initial.normed_v = ns.normed_0, ns.normed_0_v
        initial.qkv, initial.qkv_v = ns.qkv_0, ns.qkv_0_v
        initial.wq, initial.wq_v = ns.wq_0, ns.wq_0_v
        initial.quarter_q_v, initial.quarter_u_v = ns.quarter_q0_v, ns.quarter_u0_v
        initial.deal_q_v, initial.deal_u_v = ns.deal_q0_v, ns.deal_u0_v
        upper, y, x = place.upper, place.y, place.x
        copies = ns.copies
        q_deal = deal(copies, place, ns.deal_q_v, ns.wq_v.at[upper, place.t, y, x])
        loads, down_in = [], []

        def ahead():
            loads.append(quarter_of(ns, place, ns.w_qkv, 1, ns.quarter_q_v))
            loads.append(copies.local(ns.w_out.at[0], ns.wo_v.at[upper]))
            loads.append(copies.local(ns.w_down.at[0], ns.wd_v.at[upper]))
            loads.append(quarter_of(ns, place, ns.w_up, 1, ns.quarter_u_v))
            yield
            loads[0].wait()
            arrange(ns.quarter_q_v, ns.deal_q_v, 6)
            target = ns.wd_v.at[upper, y, x]
            down_in.append(copies.remote(ns.w_down.at[0, y, x], target, place.far))
            next(q_deal)
            next(q_deal)
            yield

        up_dealt = tokens_in(initial, place, ahead())
        ns.qkv_in_v = ns.qkv_0_v
        ns.load.hidden = types.SimpleNamespace(wait=lambda: None)
        rest_of(ns, place, up_dealt, loads, down_in[0], q_deal)

    flops = 2 * length * width * (mixed_width + 2 * units + 2 * part)
    kernel, options = kernel_of(first, with_line, inputs, outputs, scratch, 0, 128, 96, 62, flops)
    results = pl.pallas_call(kernel, **options)(*inputs.values())
    return named(outputs, results)


def turn_kernel(lower, gains, w_down, w_out, cotangent):
    hidden = lower.hidden_out
    width = hidden.shape[2]
    length, part = lower.qkv.shape
    mixed_width = part // 3
    inputs = dict(
        qkv_in=lower.qkv, gains=gains, hidden=hidden, cot=cotangent,
        part_u=lower.next_u, part_o=lower.next_o, w_down=w_down, w_out=w_out,
    )
    rows, units = lower.next_u.shape[2:]
    blocks = struct((2, TOK, width), F32)
    outputs = dict(
        out=struct((2, TOK, width), BF),
        lse=struct((length, 128), F32),
        mixed_grad=struct((length, mixed_width), BF),
        gd=by_device((units, width), 1),
        gu=by_device((width, units), 4),
        go=by_device((mixed_width, width), 1),
        dg=struct((8, width), F32),
    )
    kept = dict(
        qkv_in=lower.qkv,
        hidden=hidden,
        gains=gains,
        cot=cotangent,
        wd=struct((2, *w_down.shape[1:]), BF),
        wo=lower.next_o,
        wu=struct((2, 4, 2, 2, rows, units), BF),
        mixed=struct((length, mixed_width), BF),
        attn_out=blocks,
        resid=blocks,
        grad=blocks,
        mlp=struct((length, width), BF),
        active=struct((length, units), BF),
        slope=struct((length, units), BF),
        up_grad=struct((length, units), BF),
        down_out=blocks,
        down_grad=struct((length, width), BF),
        attn_grad=struct((length, width), BF),
    )
    scratch = held(outputs, kept)
    outputs |= dict(resid_grad=blocks)
    for name in (ATTN, DOWN, UP):
        scratch |= scatter_scratch(name, width)
    scratch |= reduce_scratch(D1, 1, units // 8, width, 1)

    def turn(ns):
        place, copies = Place(), ns.copies
        upper, y, x = place.upper, place.y, place.x
        part_u = copies.local(ns.part_u, ns.wu_v.at[:, :, y, x])
        part_o = copies.local(ns.part_o.at[1 - upper], ns.wo_v.at[1 - upper])
        whole_o = copies.local(ns.w_out.at[1], ns.wo_v.at[upper])
        whole_d = copies.local(ns.w_down.at[1], ns.wd_v.at[upper])
        meet(with_few(place))
        down_in = copies.remote(ns.w_down.at[1, y, x], ns.wd_v.at[upper, y, x], place.far)
        part_u.wait()
        up_spread = spread(copies, place, by_columns(ns.wu_v))
        down_spread = spread(copies, place, by_rows(ns.wd_v, place))
        next(up_spread)
        ns.load.qkv_in.wait()
        far_in = []

        def bring():
            ns.load.cot.wait()
            far_in.append(copies.remote(ns.cot.at[1 - upper], ns.cot_far_v, place.far))

        def down_arrived():
            down_in.wait_recv()
            next(down_spread)

        plan = Plan(
            [],
            [],
            [stages(up_spread)],
            [],
            [down_arrived],
            [stages(down_spread), bring],
        )
        ns.load.gains.wait()
        ns.dg_v[...] = jnp.zeros_like(ns.dg_v)
        gain = rows_of(ns, 1)

        def wait_out():
            part_o.wait()
            whole_o.wait()

        def wait_down():
            next(down_spread)
            whole_d.wait()

        down = fwd_mid(
            ns, place, gain, plan.tick, wait_out, lambda: next(up_spread), wait_down
        )
        copies.store(ns.lse_v, ns.lse)
        far_in[0].wait_recv()

        def grad(stream):
            value = down.result(stream)
            ns.down_out_v[stream] = value
            own = jnp.where(upper == stream, ns.cot_v[stream], ns.cot_far_v[...])
            return own.astype(F32)

        def finish():
            for stream in range(2):
                out = ns.resid_v[stream] + norm(ns.down_out_v[stream], gain(3))
                ns.out_v[stream] = out.astype(BF)
            copies.store(ns.out_v, ns.out)

        d_first, unused = reduce_rep(copies, place, ns.gd_v, ns, D1)
        plan = Plan(
            [],
            [finish],
            [],
            [],
            [],
        )
        grads = [functools.partial(grad, stream) for stream in range(2)]
        store_up = functools.partial(copies.store, ns.gu_v, ns.gu)
        bwd_mid(ns, place, 1, grads, plan.tick, stages(d_first), store_up)
        copies.store(ns.go_v, ns.go)
        copies.store(ns.dg_v, ns.dg)
        next(d_first)
        copies.store(ns.gd_v, ns.gd)

    scratch["cot_far_v"] = pltpu.VMEM((TOK, width), BF)
    flops = 6 * length * width * (mixed_width + 2 * units)
    kernel, options = kernel_of(turn, with_few, inputs, outputs, scratch, 2, 64, 64, 63, flops)
    results = pl.pallas_call(kernel, **options)(*inputs.values())
    return named(outputs, results)


def backward_kernel(lower, turned):
    wo, wu, wd, wq = (matrix(value) for value in (lower.wo, lower.wu, lower.wd, lower.wq))
    width, units = wu.shape
    length, part = lower.qkv.shape
    mixed_width = wo.shape[0]
    inputs = dict(
        gu=turned.gu, d1=turned.gd, o1=turned.go, qkv_in=lower.qkv, lse=turned.lse,
        mixed_grad=turned.mixed_grad, dg=turned.dg, gains=lower.gains, wq=wq, normed=lower.normed,
        hidden=lower.hidden_out, grad=turned.resid_grad, down_out=lower.down_out, wd=wd,
        slope=lower.slope, wu=wu, active=lower.active, mlp=lower.mlp, resid=lower.resid,
        attn_out=lower.attn_out, wo=wo, mixed=lower.mixed,
    )
    blocks = struct((2, TOK, width), F32)
    kept = dict(
        gq=by_device(wq.shape, 4),
        gd=by_device(wd.shape, 1),
        gu=by_device(wu.shape, 4),
        go=by_device(wo.shape, 1),
        qkv_grad=struct(lower.qkv.shape, BF),
        dk=struct((length, mixed_width), F32),
        dv=struct((length, mixed_width), F32),
        down_grad=struct((length, width), BF),
        attn_grad=struct((length, width), BF),
    )
    outputs = dict(
        resid_grad=blocks,
        mixed_out=struct((length, mixed_width), BF),
        gd=kept["gd"],
        up_out=kept["gu"],
        go=kept["go"],
        dg_out=turned.dg,
        full_d=struct((2, 2, 2, units // 16, width), BF),
        full_u=struct((2, 2, width // 32, 4 * units), BF),
        full_q=struct((2, 2, width // 32, 4 * part), BF),
        full_o=struct((2, 2, 2, mixed_width // 16, width), BF),
    )
    loaded = dict(inputs)
    del loaded["d1"]
    scratch = held(loaded, kept)
    for name in (QKV, UP):
        scratch |= scatter_scratch(name, width)
    rows = width // 32
    for name, count, high, wide, steps in (
        (D1, 1, units // 8, width, 2),
        (U1, 4, rows, units, 3),
        (Q1, 4, rows, part, 3),
        (O1, 1, mixed_width // 8, width, 3),
    ):
        scratch |= finish_scratch(name, count, high, wide)
        scratch |= reduce_scratch(name, count, high, wide, steps)
    scratch |= reduce_scratch(D0, 1, units // 8, width, 1)

    def backward(ns):
        place, copies = Place(), ns.copies
        ns.up_grad_v = ns.normed_v
        line = [place.line(offset)[0] for offset in range(1, 8)]
        meet(with_line(place))
        unused, d1_second = reduce_rep(copies, place, ns.d1, ns, D1)
        u1_first, u1_second = reduce_rep(copies, place, ns.gu_v, ns, U1)
        o1_first, o1_second = reduce_rep(copies, place, ns.o1_v, ns, O1)
        q1_first, q1_second = reduce_rep(copies, place, ns.gq_v, ns, Q1)
        d0_first, unused = reduce_rep(copies, place, ns.gd_v, ns, D0)
        d1_line = line_rows(copies, place, ns, D1)
        u1_line = line_columns(copies, place, ns, U1)
        o1_line = line_rows(copies, place, ns, O1)
        q1_line = line_columns(copies, place, ns, Q1)
        d1_whole = whole_rows(copies, place, ns, D1, ns.full_d)
        u1_whole = whole_columns(copies, place, ns, U1, ns.full_u, 2)
        q1_whole = whole_columns(copies, place, ns, Q1, ns.full_q, 6)
        o1_whole = whole_rows(copies, place, ns, O1, ns.full_o)
        next(d1_second)
        ns.load.gu.wait()
        next(u1_first)
        ns.load.o1.wait()
        ns.load.qkv_in.wait()
        ns.load.lse.wait()
        ns.load.mixed_grad.wait()
        ns.load.dg.wait()
        plan = Plan(
            [stages(d1_second), stages(d1_line)],
            [],
            [stages(u1_first), stages(u1_second), stages(o1_first)],
            [],
            [],
            [stages(u1_second), stages(u1_line), stages(d1_line), stages(d1_whole)],
            [stages(o1_first), stages(o1_second), stages(q1_first), stages(q1_second)],
            [stages(d1_whole), stages(u1_line), stages(u1_whole)]
            + [stages(q1_second), stages(q1_line)],
            [stages(o1_second), stages(o1_line)],
            [stages(d1_whole), stages(u1_whole), stages(q1_line), stages(q1_whole)],
            [],
            [stages(o1_line), stages(o1_whole), stages(q1_whole)],
            [stages(u1_whole)],
            [stages(d0_first), stages(o1_whole)],
        )
        ns.load.gains.wait()
        grads = bwd_head(ns, place, 1, plan.tick, stages(q1_first), False)
        for copy in (ns.load.down_out, ns.load.wd, ns.load.slope, ns.load.wu, ns.load.active):
            copy.wait()
        for copy in (ns.load.mlp, ns.load.resid, ns.load.attn_out, ns.load.wo, ns.load.mixed):
            copy.wait()
        ns.mixed_grad = ns.mixed_out
        store_up = functools.partial(copies.store, ns.gu_v, ns.up_out)
        bwd_mid(ns, place, 0, grads, plan.tick, stages(d0_first), store_up, (1, 0))
        plan.drain()
        copies.store(ns.go_v, ns.go)
        copies.store(ns.gd_v, ns.gd)
        copies.store(ns.dg_v, ns.dg_out)
        next(q1_whole)
        next(o1_whole)

    flops = 6 * length * width * (mixed_width + 2 * units) + 4 * length * width * part
    kernel, options = kernel_of(backward, with_line, inputs, outputs, scratch, 3, 128, 128, 63, flops)
    results = pl.pallas_call(kernel, **options)(*inputs.values())
    return named(outputs, results)


def last_kernel(lower, turned, back):
    wq = matrix(lower.wq_0)
    width, part = wq.shape
    length, mixed_width = back.mixed_out.shape
    units, rows = back.up_out.shape[-1], width // 32
    inputs = dict(
        u0=back.up_out, d0=back.gd, o0=back.go, qkv_in=lower.qkv_0, lse=lower.lse,
        mixed_grad=back.mixed_out, dg=back.dg_out, gains=lower.gains, normed=lower.normed_0, wq=wq,
        hidden=lower.hidden, grad=back.resid_grad, second=turned.out,
    )
    outputs = dict(
        out=struct((2, TOK, width), BF),
        block_out=struct((2, TOK, width), BF),
        gain_grad=struct((8, TOK), F32),
        full_d=struct(back.full_d.shape, BF),
        full_u=struct(back.full_u.shape, BF),
        full_q=struct(back.full_q.shape, BF),
        full_o=struct(back.full_o.shape, BF),
    )
    kept = dict(
        out=outputs["out"],
        gq=by_device(wq.shape, 4),
        qkv_grad=struct(lower.qkv_0.shape, BF),
        dk=struct((length, mixed_width), F32),
        dv=struct((length, mixed_width), F32),
        dg_line=struct((8, 8, TOK), F32),
        dg_pass=struct((5, 8, TOK), F32),
    )
    loaded = dict(inputs)
    del loaded["d0"]
    scratch = held(loaded, kept)
    scratch |= scatter_scratch(QKV, width)
    for name, count, high, wide, steps in (
        (D0, 1, units // 8, width, 2),
        (U0, 4, rows, units, 3),
        (Q0, 4, rows, part, 3),
        (O0, 1, mixed_width // 8, width, 3),
    ):
        scratch |= reduce_scratch(name, count, high, wide, steps)
        scratch |= finish_scratch(name, count, high, wide)

    def last(ns):
        place, copies = Place(), ns.copies
        line = [place.line(offset)[0] for offset in range(1, 8)]
        meet(with_line(place))
        unused, d0_second = reduce_rep(copies, place, ns.d0, ns, D0)
        u0_first, u0_second = reduce_rep(copies, place, ns.u0_v, ns, U0)
        o0_first, o0_second = reduce_rep(copies, place, ns.o0_v, ns, O0)
        q0_first, q0_second = reduce_rep(copies, place, ns.gq_v, ns, Q0)
        d0_line = line_rows(copies, place, ns, D0)
        o0_line = line_rows(copies, place, ns, O0)
        u0_line = line_columns(copies, place, ns, U0)
        q0_line = line_columns(copies, place, ns, Q0)
        d0_whole = whole_rows(copies, place, ns, D0, ns.full_d)
        o0_whole = whole_rows(copies, place, ns, O0, ns.full_o)
        u0_whole = whole_columns(copies, place, ns, U0, ns.full_u, 2)
        q0_whole = whole_columns(copies, place, ns, Q0, ns.full_q, 6)
        upper = place.upper
        second = copies.remote(ns.second.at[1 - upper], ns.block_out.at[upper], place.far)
        next(d0_second)
        ns.load.u0.wait()
        next(u0_first)
        ns.load.qkv_in.wait()
        ns.load.lse.wait()
        ns.load.mixed_grad.wait()
        ns.load.dg.wait()
        ns.load.o0.wait()
        plan = Plan(
            [stages(d0_second), stages(d0_line)],
            [],
            [stages(u0_first), stages(u0_second)],
            [stages(d0_line), stages(d0_whole)],
            [],
        )
        ns.load.gains.wait()
        grads = bwd_head(ns, place, 0, plan.tick, stages(q0_first), True)
        ns.load.second.wait()
        copies.store(ns.second_v.at[upper], ns.block_out.at[upper])
        ns.out_v[1] = grads[1]().astype(BF)
        for task in (u0_second, u0_line, q0_first, q0_second, o0_first, d0_whole):
            next(task)
        ns.out_v[0] = grads[0]().astype(BF)
        copies.store(ns.out_v.at[upper], ns.out.at[upper])
        gain_grad = gain_sum(ns, copies, place)
        for task in (
            gain_grad, q0_second, q0_line, o0_first, o0_second, u0_line, u0_whole, d0_whole,
            gain_grad, o0_second, o0_line,
        ):
            next(task)
        moved = copies.remote(ns.out_v.at[1 - upper], ns.out.at[upper], place.far)
        for task in (
            u0_whole, q0_line, q0_whole, o0_line, o0_whole, gain_grad, u0_whole, q0_whole,
            o0_whole, gain_grad, q0_whole, o0_whole,
        ):
            next(task)
        moved.wait_recv()
        second.wait_recv()

    flops = 4 * length * width * part
    kernel, options = kernel_of(last, with_line, inputs, outputs, scratch, 4, 128, 128, 60, flops)
    results = pl.pallas_call(kernel, **options)(*inputs.values())
    return named(outputs, results)


def widen(pairs):
    flat = [value for group in pairs for value in group]
    outs = [struct((len(group), *group[0].shape), F32) for group in pairs]

    def finish(*refs):
        sources, targets = refs[: len(flat)], refs[len(flat) : len(flat) + len(outs)]
        low, wide = refs[len(flat) + len(outs) :][: len(flat)], refs[-len(flat) - 2 : -2]
        sem_in, sem_out = refs[-2:]
        slots = [(g, n) for g, group in enumerate(pairs) for n in range(len(group))]
        loads = [pltpu.make_async_copy(sources[i], low[i], sem_in.at[i]) for i in range(len(flat))]
        for copy in loads:
            copy.start()
        stores = []
        for i, (g, n) in enumerate(slots):
            loads[i].wait()

            def step(index):
                at = tile_of(index, 32)
                wide[i][at, :] = low[i][at, :].astype(F32)

            loop(low[i].shape[0] // 32, step)
            stores.append(pltpu.make_async_copy(wide[i], targets[g].at[n], sem_out.at[i]))
            stores[-1].start()
        for copy in stores:
            copy.wait()

    size = sum(value.size for value in flat)
    return pl.pallas_call(
        finish,
        name=finish.__name__,
        out_shape=outs,
        in_specs=[pl.BlockSpec(memory_space=pl.ANY)] * len(flat),
        out_specs=[pl.BlockSpec(memory_space=pl.ANY)] * len(outs),
        scratch_shapes=[
            *(pltpu.VMEM(value.shape, BF) for value in flat),
            *(pltpu.VMEM(value.shape, F32) for value in flat),
            pltpu.SemaphoreType.DMA((len(flat),)),
            pltpu.SemaphoreType.DMA((len(flat),)),
        ],
        compiler_params=pltpu.CompilerParams(vmem_limit_bytes=63 << 20),
        cost_estimate=pl.CostEstimate(flops=size, bytes_accessed=6 * size, transcendentals=0),
    )(*flat)


def gain_sum(ns, copies, place):
    def columns(grp):
        return pl.ds(pl.multiple_of(grp * TOK, TOK), TOK)

    moved = []
    for offset in range(1, 8):
        device, upper, t = place.line(offset)
        source = ns.dg_v.at[:, columns(upper * 4 + t)]
        moved.append(copies.remote(source, ns.dg_line_v.at[place.grp], device))
    ns.dg_line_v[place.grp] = ns.dg_v[:, columns(place.grp)]
    yield
    for copy in moved:
        copy.wait_recv()
    ns.dg_pass_v[0] = jnp.sum(ns.dg_line_v[...], axis=0)
    moved = copies.remote(ns.dg_pass_v.at[0], ns.dg_pass_v.at[1], place.along_x)
    yield
    moved.wait_recv()
    ns.dg_pass_v[2] = ns.dg_pass_v[0] + ns.dg_pass_v[1]
    moved = copies.remote(ns.dg_pass_v.at[2], ns.dg_pass_v.at[3], place.along_y)
    yield
    moved.wait_recv()
    ns.dg_pass_v[4] = ns.dg_pass_v[2] + ns.dg_pass_v[3]
    copies.store(ns.dg_pass_v.at[4], ns.gain_grad)
    yield


def body_pairs(block_in, cotangent, w_qkv, w_out, w_up, w_down, norm_gains):
    layers, rows, width = w_out.shape
    hidden_unit = w_down.shape[1]
    gain_part = jnp.transpose(norm_gains.astype(F32), (0, 2, 1)).reshape(layers * 4, rows)
    down_parts = w_down.reshape(layers, 2, 2, 2, hidden_unit // 8, width)
    out_parts = w_out.reshape(layers, 2, 2, 2, rows // 8, width)

    lower = first_kernel(block_in[:, 0], gain_part, w_qkv, w_up, down_parts, out_parts)
    turned = turn_kernel(lower, lower.gains, down_parts, out_parts, cotangent[:, 0])
    back = backward_kernel(lower, turned)
    last = last_kernel(lower, turned, back)

    pairs = (
        (last.full_d, back.full_d),
        (last.full_u, back.full_u),
        (last.full_q, back.full_q),
        (last.full_o, back.full_o),
        (last.out,),
    )
    wide = widen([[matrix(value) for value in group] for group in pairs])
    return (
        last.block_out[:, None],
        wide[4].reshape(block_in.shape),
        wide[2],
        wide[3],
        wide[1],
        wide[0],
        jnp.transpose(last.gain_grad.reshape(layers, 4, rows), (0, 2, 1)),
    )


def norm_apply(values, gains):
    return values * lax.rsqrt(jnp.mean(values * values, axis=-1, keepdims=True) + EPS) * gains


def inner_rows(left, right):
    return lax.dot_general(
        left, right, (((0,), (0,)), ((), ())), preferred_element_type=jnp.float32
    )


def times_trans(left, right):
    return lax.dot_general(
        left, right, (((1,), (1,)), ((), ())), preferred_element_type=jnp.float32
    )


def split_blocks(whole):
    length = whole.shape[0]
    width = min(512, length)
    count = length // width
    return (whole.reshape(count, width, HEADS, HDIM), width, count)


def block_at(blocks, index):
    return lax.dynamic_index_in_dim(blocks, index, 0, keepdims=False)


def key_scores(query, key_block, key_start, query_pos):
    scale = HDIM ** (-0.5)
    scores = (
        jnp.einsum("qhd,khd->hqk", query, key_block, preferred_element_type=jnp.float32) * scale
    )
    key_pos = key_start + jnp.arange(key_block.shape[0], dtype=jnp.int32)
    allowed = key_pos[None, :] <= query_pos[:, None]
    return (scores, allowed[None])


def attend_split(query, keys_all, values_all, query_pos):
    key_blocks, width, count = split_blocks(keys_all)
    value_blocks = split_blocks(values_all)[0]
    row_count = query.shape[0]
    upper = query_pos[row_count - 1] // width + 1

    def total_step(index, carry):
        running, total = carry
        scores, allowed = key_scores(query, block_at(key_blocks, index), index * width, query_pos)
        newest = jnp.maximum(running, jnp.max(jnp.where(allowed, scores, NEGATIVE), axis=-1))
        terms = jnp.where(allowed, jnp.exp(scores - newest[..., None]), 0.0)
        total = total * jnp.exp(running - newest) + jnp.sum(terms, axis=-1)
        return (newest, total)

    start_run = jnp.full((HEADS, row_count), NEGATIVE, jnp.float32)
    start_total = jnp.zeros((HEADS, row_count), jnp.float32)
    running, total = lax.fori_loop(0, upper, total_step, (start_run, start_total))
    log_total = running + jnp.log(total)

    def mix_step(index, accum):
        scores, allowed = key_scores(query, block_at(key_blocks, index), index * width, query_pos)
        probs = jnp.where(allowed, jnp.exp(scores - log_total[..., None]), 0.0)
        return accum + jnp.einsum(
            "hqk,khd->qhd",
            probs.astype(jnp.bfloat16),
            block_at(value_blocks, index),
            preferred_element_type=jnp.float32,
        )

    start_mix = jnp.zeros((row_count, HEADS, HDIM), jnp.float32)
    mixed = lax.fori_loop(0, upper, mix_step, start_mix)
    return (mixed.reshape(row_count, HEADS * HDIM), log_total)


def attend_back_split(query, keys_all, values_all, log_total, out_grad, delta, query_pos):
    key_blocks, width, count = split_blocks(keys_all)
    value_blocks = split_blocks(values_all)[0]
    row_count = query.shape[0]
    upper = query_pos[row_count - 1] // width + 1
    scale = HDIM ** (-0.5)

    def back_step(index, carry):
        query_acc, pieces = carry
        key_block = block_at(key_blocks, index)
        value_block = block_at(value_blocks, index)
        scores, allowed = key_scores(query, key_block, index * width, query_pos)
        probs = jnp.where(allowed, jnp.exp(scores - log_total[..., None]), 0.0)
        prob_grad = jnp.einsum(
            "qhd,khd->hqk", out_grad, value_block, preferred_element_type=jnp.float32
        )
        score_grad = (probs * (prob_grad - delta[..., None])).astype(jnp.bfloat16)
        query_acc = (
            query_acc
            + jnp.einsum("hqk,khd->qhd", score_grad, key_block, preferred_element_type=jnp.float32)
            * scale
        )
        key_grad = (
            jnp.einsum("hqk,qhd->khd", score_grad, query, preferred_element_type=jnp.float32)
            * scale
        )
        value_grad = jnp.einsum(
            "hqk,qhd->khd", probs.astype(jnp.bfloat16), out_grad, preferred_element_type=jnp.float32
        )
        joined = jnp.concatenate(
            [key_grad.reshape(width, HEADS * HDIM), value_grad.reshape(width, HEADS * HDIM)], axis=1
        )
        pieces = lax.dynamic_update_index_in_dim(pieces, joined, index, 0)
        return (query_acc, pieces)

    start_acc = jnp.zeros((row_count, HEADS, HDIM), jnp.float32)
    start_pieces = jnp.zeros((count, width, 2 * HEADS * HDIM), jnp.float32)
    query_grad, pieces = lax.fori_loop(0, upper, back_step, (start_acc, start_pieces))
    return (query_grad.reshape(row_count, HEADS * HDIM), pieces.reshape(-1, pieces.shape[-1]))


def layer_forward(hidden_in, weights, query_pos):
    w_qkv_full, w_out_full, w_up_full, w_down_full, gain_full = weights
    gains_f = gain_full.astype(jnp.float32)
    row_count = hidden_in.shape[0]
    width = w_out_full.shape[1]
    normed = norm_apply(hidden_in, gains_f[:, 0]).astype(jnp.bfloat16)
    qkv_low = jnp.dot(normed, w_qkv_full, preferred_element_type=jnp.float32).astype(jnp.bfloat16)
    query = qkv_low[:, :width]
    keys_all, values_all = (
        lax.all_gather(qkv_low[:, width : 2 * width], "grp", axis=0, tiled=True),
        lax.all_gather(qkv_low[:, 2 * width :], "grp", axis=0, tiled=True),
    )
    mixed, log_total = attend_split(
        query.reshape(row_count, HEADS, HDIM),
        keys_all.reshape(-1, HEADS, HDIM),
        values_all.reshape(-1, HEADS, HDIM),
        query_pos,
    )
    mixed_low = mixed.astype(jnp.bfloat16)
    attn_out = jnp.dot(mixed_low, w_out_full, preferred_element_type=jnp.float32)
    resid = hidden_in + norm_apply(attn_out, gains_f[:, 1])
    mlp_in = norm_apply(resid, gains_f[:, 2]).astype(jnp.bfloat16)
    up_out = jnp.dot(mlp_in, w_up_full, preferred_element_type=jnp.float32)
    active = jax.nn.gelu(up_out).astype(jnp.bfloat16)
    down_out = jnp.dot(active, w_down_full, preferred_element_type=jnp.float32)
    result = resid + norm_apply(down_out, gains_f[:, 3])
    kept = (
        hidden_in,
        normed,
        qkv_low,
        mixed,
        mixed_low,
        log_total,
        attn_out,
        resid,
        mlp_in,
        up_out,
        active,
        down_out,
    )
    return (result, kept)


def layer_backward(grad_out, weights, kept, query_pos):
    w_qkv_full, w_out_full, w_up_full, w_down_full, gain_full = weights
    (
        hidden_in,
        normed,
        qkv_low,
        mixed,
        mixed_low,
        log_total,
        attn_out,
        resid,
        mlp_in,
        up_out,
        active,
        down_out,
    ) = kept
    gains_f = gain_full.astype(jnp.float32)
    row_count = hidden_in.shape[0]
    width = w_out_full.shape[1]
    unused, puller = jax.vjp(norm_apply, down_out, gains_f[:, 3])
    down_grad, gain_four = puller(grad_out)
    down_low = down_grad.astype(jnp.bfloat16)
    w_down_grad = inner_rows(active, down_low)
    active_grad = times_trans(down_low, w_down_full)
    unused, puller = jax.vjp(jax.nn.gelu, up_out)
    up_low = puller(active_grad)[0].astype(jnp.bfloat16)
    w_up_grad = inner_rows(mlp_in, up_low)
    mlp_grad = times_trans(up_low, w_up_full)
    unused, puller = jax.vjp(norm_apply, resid, gains_f[:, 2])
    resid_part, gain_three = puller(mlp_grad)
    resid_grad = grad_out + resid_part
    unused, puller = jax.vjp(norm_apply, attn_out, gains_f[:, 1])
    attn_grad, gain_two = puller(resid_grad)
    attn_low = attn_grad.astype(jnp.bfloat16)
    w_out_grad = inner_rows(mixed_low, attn_low)
    mixed_grad = times_trans(attn_low, w_out_full).astype(jnp.bfloat16)
    keys_all, values_all = (
        lax.all_gather(qkv_low[:, width : 2 * width], "grp", axis=0, tiled=True),
        lax.all_gather(qkv_low[:, 2 * width :], "grp", axis=0, tiled=True),
    )
    delta = jnp.sum(
        (mixed_grad.astype(jnp.float32) * mixed).reshape(row_count, HEADS, HDIM), axis=-1
    ).T
    query_low = qkv_low[:, :width]
    query_grad, key_value_terms = attend_back_split(
        query_low.reshape(row_count, HEADS, HDIM),
        keys_all.reshape(-1, HEADS, HDIM),
        values_all.reshape(-1, HEADS, HDIM),
        log_total,
        mixed_grad.reshape(row_count, HEADS, HDIM),
        delta,
        query_pos,
    )
    key_value_grad = lax.psum_scatter(
        key_value_terms.astype(jnp.bfloat16), "grp", scatter_dimension=0, tiled=True
    ).astype(jnp.float32)
    qkv_grad = jnp.concatenate([query_grad, key_value_grad], axis=1).astype(jnp.bfloat16)
    w_qkv_grad = inner_rows(normed, qkv_grad)
    normed_grad = times_trans(qkv_grad, w_qkv_full)
    unused, puller = jax.vjp(norm_apply, hidden_in, gains_f[:, 0])
    input_part, gain_one = puller(normed_grad)
    gain_grad = jnp.stack([gain_one, gain_two, gain_three, gain_four], axis=1)
    return (resid_grad + input_part, (w_qkv_grad, w_out_grad, w_up_grad, w_down_grad, gain_grad))


def body_general(block_in, cotangent, w_qkv, w_out, w_up, w_down, norm_gains):
    layer_count = w_qkv.shape[0]
    micro_count = block_in.shape[0]
    row_count = block_in.shape[2]
    query_pos = lax.axis_index("grp") * row_count + jnp.arange(row_count, dtype=jnp.int32)
    totals = [None] * layer_count
    outputs = []
    input_grads = []
    for micro_idx in range(micro_count):
        hidden = block_in[micro_idx, 0].astype(jnp.float32)
        saved = []
        for layer_idx in range(layer_count):
            hidden, kept = layer_forward(
                hidden,
                (
                    lax.all_gather(w_qkv[layer_idx], "grp", axis=0, tiled=True),
                    lax.all_gather(w_out[layer_idx], "grp", axis=0, tiled=True),
                    lax.all_gather(w_up[layer_idx], "grp", axis=0, tiled=True),
                    lax.all_gather(w_down[layer_idx], "grp", axis=0, tiled=True),
                    lax.all_gather(norm_gains[layer_idx], "grp", axis=0, tiled=True),
                ),
                query_pos,
            )
            saved.append(kept)
        outputs.append(hidden.astype(jnp.bfloat16))
        grad_flow = cotangent[micro_idx, 0].astype(jnp.float32)
        for layer_idx in reversed(range(layer_count)):
            grad_flow, parts = layer_backward(
                grad_flow,
                (
                    lax.all_gather(w_qkv[layer_idx], "grp", axis=0, tiled=True),
                    lax.all_gather(w_out[layer_idx], "grp", axis=0, tiled=True),
                    lax.all_gather(w_up[layer_idx], "grp", axis=0, tiled=True),
                    lax.all_gather(w_down[layer_idx], "grp", axis=0, tiled=True),
                    lax.all_gather(norm_gains[layer_idx], "grp", axis=0, tiled=True),
                ),
                saved[layer_idx],
                query_pos,
            )
            if totals[layer_idx] is None:
                totals[layer_idx] = parts
            else:
                totals[layer_idx] = tuple(
                    (left + right for left, right in zip(totals[layer_idx], parts))
                )
        input_grads.append(grad_flow)
    reduced = []
    for layer_idx in range(layer_count):
        accum = totals[layer_idx]
        shards = (
            lax.psum_scatter(
                accum[0].astype(jnp.bfloat16), "grp", scatter_dimension=0, tiled=True
            ).astype(jnp.float32),
            lax.psum_scatter(
                accum[1].astype(jnp.bfloat16), "grp", scatter_dimension=0, tiled=True
            ).astype(jnp.float32),
            lax.psum_scatter(
                accum[2].astype(jnp.bfloat16), "grp", scatter_dimension=0, tiled=True
            ).astype(jnp.float32),
            lax.psum_scatter(
                accum[3].astype(jnp.bfloat16), "grp", scatter_dimension=0, tiled=True
            ).astype(jnp.float32),
            lax.psum_scatter(
                accum[4].astype(jnp.bfloat16), "grp", scatter_dimension=0, tiled=True
            ).astype(jnp.float32),
        )
        reduced.append(
            (
                lax.psum(shards[0].astype(jnp.bfloat16), "rep").astype(jnp.float32),
                lax.psum(shards[1].astype(jnp.bfloat16), "rep").astype(jnp.float32),
                lax.psum(shards[2].astype(jnp.bfloat16), "rep").astype(jnp.float32),
                lax.psum(shards[3].astype(jnp.bfloat16), "rep").astype(jnp.float32),
                lax.psum(shards[4].astype(jnp.bfloat16), "rep").astype(jnp.float32),
            )
        )
    block_out = jnp.stack(outputs)[:, None]
    block_in_grad = jnp.stack(input_grads)[:, None]
    stacked = [
        jnp.stack([reduced[layer_idx][member] for layer_idx in range(layer_count)])
        for member in range(5)
    ]
    return (block_out, block_in_grad, stacked[0], stacked[1], stacked[2], stacked[3], stacked[4])


def solution(mesh):
    rep_size, grp_size = mesh.shape["rep"], mesh.shape["grp"]

    def body(block_in, cotangent, w_qkv, w_out, w_up, w_down, norm_gains):
        sizes = (rep_size, grp_size, block_in.shape[0], w_qkv.shape[0], block_in.shape[2])
        fits = sizes == (4, 8, 2, 2, TOK)
        chosen = body_pairs if fits else body_general
        return chosen(block_in, cotangent, w_qkv, w_out, w_up, w_down, norm_gains)

    tokens = P(None, "rep", "grp", None)
    rows = P(None, "grp", None)
    return jax.shard_map(
        body,
        mesh=mesh,
        in_specs=(tokens, tokens, rows, rows, rows, rows, rows),
        out_specs=(tokens, tokens, rows, rows, rows, rows, rows),
        check_vma=False,
    )
```

```python
import functools
import types

import jax
import jax.numpy as jnp
from jax import lax
from jax.experimental import pallas as pl
from jax.experimental.pallas import tpu as pltpu
from jax.sharding import PartitionSpec as P

HEADS = 16
HDIM = 64
EPS = 1e-06
NEGATIVE = -1e30
BF = jnp.bfloat16
REP, GRP = "rep", "grp"
F32 = jnp.float32


def dot(left, right):
    return jnp.dot(left, right, preferred_element_type=F32)


def dot_tn(left, right):
    return lax.dot_general(left, right, (((0,), (0,)), ((), ())), preferred_element_type=F32)


def dot_nt(left, right):
    return lax.dot_general(left, right, (((1,), (1,)), ((), ())), preferred_element_type=F32)


def norm(values, gain):
    return values * lax.rsqrt(jnp.mean(values * values, axis=-1, keepdims=True) + EPS) * gain


def head_mask(width, head):
    lanes = lax.broadcasted_iota(jnp.int32, (1, width), 1)
    return (lanes // HDIM) == head


def causal_scores(query, keys, below, start):
    scores = dot_nt(query, keys)
    last = jnp.where(below, scores[:, start:], NEGATIVE)
    return jnp.concatenate([scores[:, :start], last], axis=1) if start else last


def attend(ns, stream, block=256):
    length, width = ns.mixed_v.shape
    qkv_ref, lse_ref, sum_ref = ns.qkv_in_v, ns.lse_v, ns.terms_own.at[stream]
    row = lax.broadcasted_iota(jnp.int32, (block, block), 0)
    col = lax.broadcasted_iota(jnp.int32, (block, block), 1)
    below = col <= row
    zero = jnp.zeros((), BF)
    lane = lax.broadcasted_iota(jnp.int32, (1, 128), 1)
    base, high = stream * length // 2, (stream + 1) * length // 2
    sum_ref[...] = jnp.zeros_like(sum_ref)
    lse_ref[base:high, :] = jnp.zeros((length // 2, 128), F32)

    def one_head(head):
        mask = head_mask(width, head)
        for start in range(base, high, block):
            stop = start + block
            query = qkv_ref[start:stop, :width] * jnp.asarray(HDIM**-0.5, BF)
            query = jnp.where(mask, query, zero)
            scores = causal_scores(query, qkv_ref[:stop, width : 2 * width], below, start)
            top = jnp.max(scores, axis=1, keepdims=True)
            terms = jnp.exp(scores - top)
            sums = jnp.sum(terms, axis=1, keepdims=True)
            mixed = dot(terms.astype(BF), qkv_ref[:stop, 2 * width :]) * (1.0 / sums)
            sum_ref[:, start - base : stop - base] += jnp.where(mask, mixed, 0.0)
            stats = lse_ref[start:stop, :]
            lse_ref[start:stop, :] = jnp.where(lane == head, top + jnp.log(sums), stats)

    loop(width // HDIM, one_head)
    for start in range(base, high, block):
        ns.mixed_v[start : start + block, :] = sum_ref[:, start - base : start - base + width].astype(BF)


def attend_back(ns, stream, block=256):
    length, width = ns.mixed_grad_v.shape
    qkv_ref, grad_ref, sum_ref = ns.qkv_in_v, ns.mixed_grad_v, ns.terms_own.at[stream]
    row = lax.broadcasted_iota(jnp.int32, (block, block), 0)
    col = lax.broadcasted_iota(jnp.int32, (block, block), 1)
    below = col <= row
    zero = jnp.zeros((), BF)
    scale = HDIM**-0.5
    lane = lax.broadcasted_iota(jnp.int32, (1, 128), 1)
    base, high = stream * length // 2, (stream + 1) * length // 2
    sum_ref[...] = jnp.zeros_like(sum_ref)

    def one_head(head):
        mask = head_mask(width, head)
        for start in range(base, high, block):
            stop = start + block
            query = qkv_ref[start:stop, :width] * jnp.asarray(scale, BF)
            query = jnp.where(mask, query, zero)
            grad = jnp.where(mask, grad_ref[start:stop, :], zero)
            keys, vals = qkv_ref[:stop, width : 2 * width], qkv_ref[:stop, 2 * width :]
            scores = causal_scores(query, keys, below, start)
            lse = jnp.where(lane == head, ns.lse_v[start:stop, :], 0.0)
            probs = jnp.exp(scores - jnp.sum(lse, axis=1, keepdims=True))
            prob_grad = dot_nt(grad, vals)
            delta = jnp.sum(probs * prob_grad, axis=1, keepdims=True)
            score_grad = (probs * (prob_grad - delta)).astype(BF)
            query_grad = jnp.where(mask, dot(score_grad, keys), 0.0)
            sum_ref[:, start - base : stop - base] += query_grad
            ns.dk_v[:stop, :] += dot_tn(score_grad, query)
            ns.dv_v[:stop, :] += dot_tn(probs.astype(BF), grad)

    loop(width // HDIM, one_head)
    for start in range(base, high, block):
        value = sum_ref[:, start - base : start - base + width] * scale
        ns.qkv_grad_v[start : start + block, :width] = value.astype(BF)
    ns.qkv_grad_v[base:high, width : 2 * width] = ns.dk_v[base:high, :].astype(BF)
    ns.qkv_grad_v[base:high, 2 * width :] = ns.dv_v[base:high, :].astype(BF)


MESH_ID = pl.DeviceIdType.MESH
HELD, ONE, TWO, SUM, LINE, FULL = "_v", "one", "two", "sum", "line", "full"
PASSED = ("give", "take", "send", "got")
ATTN, DOWN, UP, QKV = "attn", "down", "up", "qkv"
D0, U0, Q0, O0 = "d0", "u0", "q0", "o0"
D1, U1, Q1, O1 = "d1", "u1", "q1", "o1"
TOK = 128


class Place:
    def __init__(self):
        rep, grp = lax.axis_index(REP), lax.axis_index(GRP)
        self.rep, self.grp = rep, grp
        self.x, self.y = lax.rem(rep, 2), lax.div(rep, 2)
        self.t, self.upper = lax.rem(grp, 4), lax.div(grp, 4)
        self.c, self.side = lax.rem(grp, 2), lax.div(self.t, 2)
        base = self.upper * 4
        self.core = (rep, base + self.side * 2 + 1 - self.c)
        self.near = (rep, base + (1 - self.side) * 2 + self.c)
        self.far = (rep, (1 - self.upper) * 4 + self.t)
        self.along_x = (self.y * 2 + 1 - self.x, grp)
        self.along_y = ((1 - self.y) * 2 + self.x, grp)
        self.near_t = (1 - self.side) * 2 + self.c

    def line(self, offset):
        c = 1 - self.c if offset & 1 else self.c
        side = 1 - self.side if offset & 2 else self.side
        upper = 1 - self.upper if offset & 4 else self.upper
        return (self.rep, upper * 4 + side * 2 + c), upper, side * 2 + c


class Copies:
    def __init__(self, send, recv, here):
        self.sems, self.here = (send, recv), here
        self.sent, self.local_count, self.stores, self.done = [], 0, [], set()

    def remote(self, source, target, device):
        at = len(self.sent)
        assert at < self.sems[0].shape[0]
        copy = pltpu.make_async_remote_copy(
            src_ref=source,
            dst_ref=target,
            send_sem=self.sems[0].at[at],
            recv_sem=self.sems[1].at[at],
            device_id=device,
            device_id_type=MESH_ID,
        )
        copy.start()
        self.sent.append(copy)
        return copy

    def local(self, source, target):
        assert self.local_count < self.here.shape[0]
        copy = pltpu.make_async_copy(source, target, self.here.at[self.local_count])
        self.local_count += 1
        copy.start()
        return copy

    def store(self, source, target):
        self.stores.append(self.local(source, target))

    def both(self, *copies):
        for copy in copies:
            copy.wait_recv()
            copy.wait_send()
            self.done.add(id(copy))

    def finish(self):
        for copy in self.sent:
            if id(copy) not in self.done:
                copy.wait_send()
        for copy in self.stores:
            copy.wait()


def announce(devices):
    barrier = pltpu.get_barrier_semaphore()
    for device in devices:
        pl.semaphore_signal(barrier, inc=1, device_id=device, device_id_type=MESH_ID)


def meet(devices):
    pl.semaphore_wait(pltpu.get_barrier_semaphore(), len(devices))


def with_line(place):
    line = [place.line(offset)[0] for offset in range(1, 8)]
    return [*line, place.along_x, place.along_y]


def with_few(place):
    return [place.core, place.near, place.far, place.along_x, place.along_y]


class Plan:
    def __init__(self, *entries):
        self.entries = list(entries)

    def tick(self):
        if self.entries:
            for action in self.entries.pop(0):
                action()

    def drain(self):
        while self.entries:
            self.tick()


def stages(task):
    return lambda: next(task, None)


def spread(copies, place, part, last=True):
    x, y, every = place.x, place.y, slice(None)
    one = copies.remote(part(0, y, x), part(0, y, x), place.along_x)
    two = copies.remote(part(1, y, x), part(1, y, x), place.along_y)
    yield
    one.wait_recv()
    three = copies.remote(part(0, y, every), part(0, y, every), place.along_y)
    two.wait_recv()
    four = copies.remote(part(1, every, x), part(1, every, x), place.along_x)
    yield
    three.wait_recv()
    four.wait_recv()
    if last:
        yield


def deal(copies, place, source, target):
    moved = []
    own = copies.local(source.at[place.t], target)
    for offset in range(1, 8):
        if offset == 4:
            yield
        device, upper, t = place.line(offset)
        moved.append(copies.remote(source.at[t], target, device))
    yield
    own.wait()
    for copy in moved:
        copy.wait_recv()
    yield


def add_low(one, two):
    return (one.astype(F32) + two.astype(F32)).astype(BF)


def reduce_rep(copies, place, grad, ns, name):
    x, y = place.x, place.y
    count = grad.shape[1]

    def step_one():
        one = getattr(ns, name + ONE)
        first = copies.remote(grad.at[0, :, :, 1 - x], one.at[0], place.along_x)
        second = copies.remote(grad.at[1, :, 1 - y], one.at[1], place.along_y)
        yield
        copies.both(first, second)
        for i in range(count):
            for j in range(2):
                grad[0, i, j, x] = add_low(grad[0, i, j, x], one[0, i, j])
                grad[1, i, y, j] = add_low(grad[1, i, y, j], one[1, i, j])
        yield

    def step_two():
        two, total = getattr(ns, name + TWO), getattr(ns, name + SUM)
        first = copies.remote(grad.at[0, :, 1 - y, x], two.at[0], place.along_y)
        second = copies.remote(grad.at[1, :, y, 1 - x], two.at[1], place.along_x)
        own = [copies.local(grad.at[half, :, y, x], total.at[half]) for half in range(2)]
        yield
        copies.both(first, second)
        for half in range(2):
            own[half].wait()
            for i in range(count):
                total[half, i] = add_low(total[half, i], two[half, i])
        yield

    return step_one(), step_two()


def line_columns(copies, place, ns, name):
    total, line, full = (getattr(ns, name + part) for part in (SUM, LINE, FULL))
    moved = []
    for offset in range(1, 8):
        device, upper, t = place.line(offset)
        here = line.at[place.upper, place.t]
        moved.append(copies.remote(total.at[upper, t], here, device))
    line[place.upper, place.t] = total[place.upper, place.t]
    yield
    for copy in moved:
        copy.wait_recv()
    for t in range(4):
        full[place.y, place.x, t] = add_low(line[0, t], line[1, t])
    yield


def line_rows(copies, place, ns, name):
    total, line, full = (getattr(ns, name + part) for part in (SUM, LINE, FULL))
    moved = copies.remote(total.at[1 - place.upper, 0], line, place.far)
    yield
    moved.wait_recv()
    rows = line.shape[0] // 2
    for half in range(2):
        at = pl.ds(half * rows, rows)
        full[place.y, place.x, half] = add_low(total[place.upper, 0, at, :], line[at, :])
    yield


def whole_columns(copies, place, ns, name, target, groups):
    full = getattr(ns, name + FULL)
    yield from spread(copies, place, lambda half, a, b: full.at[a, b, pl.ds(2 * half, 2)], False)
    unit = full.shape[4] // groups
    for t in range(4):
        for k in range(groups):
            source = full.at[:, :, t, :, k * unit : (k + 1) * unit]
            start = (k * 4 + t) * unit
            copies.store(source, target.at[:, :, :, start : start + unit])
    yield


def whole_rows(copies, place, ns, name, target):
    full = getattr(ns, name + FULL)
    yield from spread(copies, place, lambda half, a, b: full.at[a, b, half], False)
    copies.store(full, target)
    yield


def reduce_scratch(name, count, rows, width, steps=3):
    total = {}
    if steps & 1:
        total[name + ONE] = pltpu.VMEM((2, count, 2, rows, width), BF)
    if steps & 2:
        total[name + TWO] = pltpu.VMEM((2, count, rows, width), BF)
        total[name + SUM] = pltpu.VMEM((2, count, rows, width), BF)
    return total


def finish_scratch(name, count, rows, width):
    if count == 1:
        line, full = (rows, width), (2, 2, 2, rows // 2, width)
    else:
        line, full = (2, count, rows, width), (2, 2, count, rows, width)
    return {name + LINE: pltpu.VMEM(line, BF), name + FULL: pltpu.VMEM(full, BF)}


def by_device(shape, count):
    rows, width = shape
    return struct((2, count, 2, 2, rows // (8 * count), width), BF)


def loop(count, step):
    def run(index, carry):
        step(index)
        return carry

    lax.fori_loop(0, count, run, 0)


def tile_of(index, size):
    return pl.ds(pl.multiple_of(index * size, size), size)


def matrix(value):
    return value.reshape(-1, value.shape[-1])


def times(left, right_ref, tile, sink):
    every = (slice(None),) * (len(right_ref.shape) - 1)

    def step(index):
        at = tile_of(index, tile)
        sink(at, dot(left(), matrix(right_ref[(*every, at)])))

    loop(right_ref.shape[-1] // tile, step)


def times_rows(left, right_ref, tile, sink):
    flat = len(right_ref.shape) == 2

    def step(index):
        if flat:
            at = tile_of(index, tile)
            sink(at, dot_nt(left(), right_ref[at, :]))
        else:
            block = matrix(right_ref[index])
            sink(tile_of(index, block.shape[0]), dot_nt(left(), block))

    loop(right_ref.shape[0] // (tile if flat else 1), step)


def gram(left_ref, right_ref, out_ref):
    count, tile = out_ref.shape[1], 256
    total = left_ref.shape[1]
    if total == tile:
        value = dot_tn(left_ref[...], right_ref[...]).astype(BF)
        out_ref[...] = value.reshape(out_ref.shape)
        return

    def step(index):
        value = dot_tn(left_ref[:, tile_of(index, tile)], right_ref[...]).astype(BF)
        half, part = lax.div(index, 2), lax.rem(index, 2)
        if count == 1:
            out_ref[half, 0, part] = value.reshape(out_ref.shape[3:])
        else:
            out_ref[half, pl.ds(part * 2, 2)] = value.reshape(2, *out_ref.shape[2:])

    loop(total // tile, step)


class Gather:
    def __init__(self, copies, place, buf, order=(0, 1)):
        self.copies, self.place, self.buf, self.order = copies, place, buf, order
        self.flight = {}

    def rows(self, stream, where):
        start = (self.order[stream] * 4 + where) * TOK
        return pl.ds(pl.multiple_of(start, TOK), TOK)

    def pair(self, stream, side):
        start = (self.order[stream] * 4 + side * 2) * TOK
        return pl.ds(pl.multiple_of(start, TOK), 2 * TOK)

    def start(self, stream, block):
        at = self.rows(stream, self.place.t)
        self.buf[at, :] = block
        mine = self.buf.at[at, :]
        across = self.copies.remote(mine, mine, self.place.near)
        beside = self.copies.remote(mine, mine, self.place.core)
        self.flight[stream] = [across, beside]

    def wait_chip(self, stream):
        self.flight[stream][1].wait_recv()

    def forward(self, stream):
        self.flight[stream][0].wait_recv()
        got = self.buf.at[self.rows(stream, self.place.near_t), :]
        self.flight[stream].append(self.copies.remote(got, got, self.place.core))

    def wait_rest(self, stream):
        self.flight[stream][2].wait_recv()


class Scatter:
    def __init__(self, copies, place, ns, name):
        self.copies, self.place = copies, place
        self.away, self.own = ns.terms_away, ns.terms_own
        self.give, self.take, self.send, self.got = (
            getattr(ns, name + part) for part in PASSED
        )
        self.flight = {}

    def push(self, stream, product):
        place, copies = self.place, self.copies
        mine = pl.ds(pl.multiple_of(place.c * TOK, TOK), TOK)
        other = pl.ds(pl.multiple_of((1 - place.c) * TOK, TOK), TOK)

        def to_away(at, value):
            self.away[:, at] = value

        def to_own(at, value):
            self.own[stream, :, at] = value

        product(1 - place.side, to_away)
        self.give[stream, 0] = self.away[other, :].astype(BF)
        first = copies.remote(self.give.at[stream, 0], self.take.at[stream, 0], place.core)
        product(place.side, to_own)
        first.wait_recv()
        self.send[stream] = (self.away[mine, :] + self.take[stream, 0].astype(F32)).astype(BF)
        across = copies.remote(self.send.at[stream], self.got.at[stream], place.near)
        self.give[stream, 1] = self.own[stream, other, :].astype(BF)
        second = copies.remote(self.give.at[stream, 1], self.take.at[stream, 1], place.core)
        self.flight[stream] = (second, across)

    def result(self, stream):
        second, across = self.flight[stream]
        mine = pl.ds(pl.multiple_of(self.place.c * TOK, TOK), TOK)
        second.wait_recv()
        total = self.own[stream, mine, :] + self.take[stream, 1].astype(F32)
        across.wait_recv()
        return total + self.got[stream].astype(F32)


def scatter_scratch(name, width):
    give, take, send, got = (name + part for part in PASSED)
    return {
        "terms_away": pltpu.VMEM((2 * TOK, width), F32),
        "terms_own": pltpu.VMEM((2, 2 * TOK, width), F32),
        give: pltpu.VMEM((2, 2, TOK, width), BF),
        take: pltpu.VMEM((2, 2, TOK, width), BF),
        send: pltpu.VMEM((2, TOK, width), BF),
        got: pltpu.VMEM((2, TOK, width), BF),
    }


def gelu_both(x):
    cubic = x * x * 0.044715
    bent = jnp.tanh(0.7978845608028654 * (x + cubic * x))
    half = 0.5 * (1.0 + bent)
    slope = half + 0.5 * x * (1.0 - bent * bent) * (0.7978845608028654 * (1.0 + 3.0 * cubic))
    return x * half, slope


def norm_back_in(values, gain, grad):
    rstd = lax.rsqrt(jnp.mean(values * values, axis=-1, keepdims=True) + EPS)
    hat = values * rstd
    scaled = grad * gain
    back = rstd * (scaled - hat * jnp.mean(scaled * hat, axis=-1, keepdims=True))
    return back, jnp.sum(grad * hat, axis=0, keepdims=True)


def next_qkv(ns, place, blocks, tick, wait_weights, order=(0, 1), late=None):
    gather = Gather(ns.copies, place, ns.normed_v, order)
    for stream in range(2):
        if late and stream == 1:
            late()
        gather.start(stream, blocks[stream]())
        tick()
    if late:
        for stream in range(2):
            gather.forward(stream)
            tick()
    wait_weights()
    for stream in range(2):

        def project(side):
            at = gather.pair(stream, side)

            def sink(cols, value):
                ns.qkv_v[at, cols] = value.astype(BF)

            times(lambda: ns.normed_v[at, :], ns.wq_v, 384, sink)

        gather.wait_chip(stream)
        project(place.side)
        if not late:
            gather.forward(stream)
        gather.wait_rest(stream)
        project(1 - place.side)
        tick()
        here = pl.ds(pl.multiple_of(order[stream] * 4 * TOK, 4 * TOK), 4 * TOK)
        ns.copies.store(ns.normed_v.at[here, :], ns.normed.at[here, :])
        ns.copies.store(ns.qkv_v.at[here, :], ns.qkv.at[here, :])


def fwd_mid(ns, place, gain, tick, wait_out, wait_up, wait_down):
    copies = ns.copies
    attn = Scatter(copies, place, ns, ATTN)
    down = Scatter(copies, place, ns, DOWN)
    gather = Gather(copies, place, ns.mlp_v)
    wo, wu, wd = ns.wo_v, ns.wu_v, ns.wd_v
    for stream in range(2):

        def product(side, sink):
            at = gather.pair(stream, side)
            times(lambda: ns.mixed_v[at, :], wo, 512, sink)

        attend(ns, stream)
        tick()
        if stream == 0:
            wait_out()
        attn.push(stream, product)
        tick()
    ns.load.hidden.wait()
    for stream in range(2):
        value = attn.result(stream)
        ns.attn_out_v[stream] = value
        resid = ns.hidden_v[stream].astype(F32) + norm(value, gain(1))
        ns.resid_v[stream] = resid
        gather.start(stream, norm(resid, gain(2)).astype(BF))
        tick()
    wait_up()
    for stream in range(2):

        def expand(side):
            at = gather.pair(stream, side)

            def sink(cols, value):
                active, slope = gelu_both(value)
                ns.active_v[at, cols] = active.astype(BF)
                ns.slope_v[at, cols] = slope.astype(BF)

            times(lambda: ns.mlp_v[at, :], wu, 256, sink)

        gather.wait_chip(stream)
        expand(place.side)
        gather.forward(stream)
        gather.wait_rest(stream)
        expand(1 - place.side)
        if stream == 0:
            wait_down()

        def product(side, sink):
            at = gather.pair(stream, side)
            times(lambda: ns.active_v[at, :], wd, 512, sink)

        down.push(stream, product)
        tick()
    return down


def bwd_mid(ns, place, layer, grads, tick, on_down, on_up, order=(0, 1)):
    copies, gain, base = ns.copies, rows_of(ns, layer), layer * 4
    up = Scatter(copies, place, ns, UP)
    first = Gather(copies, place, ns.down_grad_v)
    second = Gather(copies, place, ns.attn_grad_v)
    wo, wu, wd = ns.wo_v, ns.wu_v, ns.wd_v
    for stream in order:
        grad = grads[stream]()
        ns.grad_v[stream] = grad
        back, four = norm_back_in(ns.down_out_v[stream], gain(3), grad)
        ns.dg_v[base + 3 : base + 4, :] += four
        first.start(stream, back.astype(BF))
        tick()
    for stream in order:

        def shrink(side):
            at = first.pair(stream, side)

            def sink(cols, value):
                slope = ns.slope_v[at, cols].astype(F32)
                ns.up_grad_v[at, cols] = (value * slope).astype(BF)

            times_rows(lambda: ns.down_grad_v[at, :], wd, 512, sink)

        first.wait_chip(stream)
        shrink(place.side)
        first.forward(stream)
        first.wait_rest(stream)
        shrink(1 - place.side)

        def product(side, sink):
            at = first.pair(stream, side)
            times_rows(lambda: ns.up_grad_v[at, :], wu, 512, sink)

        up.push(stream, product)
        tick()
    for stream in order:
        back, three = norm_back_in(ns.resid_v[stream], gain(2), up.result(stream))
        grad = ns.grad_v[stream] + back
        ns.grad_v[stream] = grad
        ns.dg_v[base + 2 : base + 3, :] += three
        back, two = norm_back_in(ns.attn_out_v[stream], gain(1), grad)
        ns.dg_v[base + 1 : base + 2, :] += two
        second.start(stream, back.astype(BF))
        tick()
        if stream == order[0]:
            gram(ns.active_v, ns.down_grad_v, ns.gd_v)
            on_down()
        else:
            gram(ns.mlp_v, ns.up_grad_v, ns.gu_v)
            on_up()
            tick()
    copies.store(ns.grad_v, ns.resid_grad)
    for stream in order:

        def project(side):
            at = second.pair(stream, side)
            ns.mixed_grad_v[at, :] = dot_nt(ns.attn_grad_v[at, :], matrix(wo[...])).astype(BF)

        second.wait_chip(stream)
        project(place.side)
        second.forward(stream)
        second.wait_rest(stream)
        project(1 - place.side)
        tick()
        here = pl.ds(stream * 4 * TOK, 4 * TOK)
        copies.store(ns.mixed_grad_v.at[here, :], ns.mixed_grad.at[here, :])
    gram(ns.mixed_v, ns.attn_grad_v, ns.go_v)


def bwd_head(ns, place, layer, tick, on_qkv, weight_first):
    copies, gain = ns.copies, rows_of(ns, layer)
    qkv = Scatter(copies, place, ns, QKV)
    walk = Gather(copies, place, None)

    def weight():
        ns.load.normed.wait()
        gram(ns.normed_v, ns.qkv_grad_v, ns.gq_v)
        on_qkv()
        tick()

    ns.dk_v[...] = jnp.zeros_like(ns.dk_v)
    ns.dv_v[...] = jnp.zeros_like(ns.dv_v)
    for stream in (1, 0):

        def product(side, sink):
            at = walk.pair(stream, side)
            times_rows(lambda: ns.qkv_grad_v[at, :], ns.wq_v, 512, sink)

        attend_back(ns, stream)
        tick()
        if stream == 1:
            ns.load.wq.wait()
        elif weight_first:
            weight()
        qkv.push(stream, product)
        tick()
    if not weight_first:
        weight()
    ns.load.hidden.wait()
    ns.load.grad.wait()

    def result(stream):
        back, one = norm_back_in(ns.hidden_v[stream].astype(F32), gain(0), qkv.result(stream))
        ns.dg_v[layer * 4 : layer * 4 + 1, :] += one
        return ns.grad_v[stream] + back

    return [functools.partial(result, stream) for stream in range(2)]


def kernel_of(body, reach, inputs, outputs, scratch, slot, remotes, locals_, vmem, flops):
    names = [*inputs, *outputs, *scratch]

    def kernel(*refs):
        ns = types.SimpleNamespace(**dict(zip(names, refs)))
        ns.copies = Copies(*refs[len(names) :])
        announce(reach(Place()))
        ns.load = types.SimpleNamespace()
        for name in inputs:
            if name + HELD in scratch:
                copy = ns.copies.local(getattr(ns, name), getattr(ns, name + HELD))
                setattr(ns.load, name, copy)
        body(ns)
        ns.copies.finish()

    moved = sum(v.size * v.dtype.itemsize for v in [*inputs.values(), *outputs.values()])
    return kernel, dict(
        name=body.__name__,
        out_shape=list(outputs.values()),
        in_specs=[pl.BlockSpec(memory_space=pl.ANY)] * len(inputs),
        out_specs=[pl.BlockSpec(memory_space=pl.ANY)] * len(outputs),
        scratch_shapes=[
            *scratch.values(),
            pltpu.SemaphoreType.DMA((remotes,)),
            pltpu.SemaphoreType.DMA((remotes,)),
            pltpu.SemaphoreType.DMA((locals_,)),
        ],
        compiler_params=pltpu.CompilerParams(
            collective_id=slot, has_side_effects=True, vmem_limit_bytes=vmem << 20
        ),
        cost_estimate=pl.CostEstimate(flops=flops, bytes_accessed=moved, transcendentals=0),
    )


def named(outputs, results):
    return types.SimpleNamespace(**dict(zip(outputs, results)))


def held(*groups):
    merged = {name: value for group in groups for name, value in group.items()}
    return {name + HELD: pltpu.VMEM(value.shape, value.dtype) for name, value in merged.items()}


def struct(shape, dtype):
    return jax.ShapeDtypeStruct(shape, dtype)


def rows_of(ns, layer):
    return lambda index, level=layer: ns.gains_v[level * 4 + index : level * 4 + index + 1, :]


def quarter_of(ns, place, weight, layer, target):
    rows = weight.shape[1] // 4
    at = pl.ds(pl.multiple_of(place.rep * rows, rows), rows)
    return ns.copies.local(weight.at[layer, at, :], target)


def arrange(quarter, dealt, groups):
    unit = quarter.shape[1] // (groups * 4)
    for t in range(4):
        for k in range(groups):
            start = (k * 4 + t) * unit
            dealt[t, :, k * unit : (k + 1) * unit] = quarter[:, start : start + unit]


def by_rows(ref, place):
    return lambda half, a, b: ref.at[1 - place.upper, a, b, half]


def by_columns(ref):
    return lambda half, a, b: ref.at[half, :, a, b]


def first_kernel(block, gain_part, w_qkv, w_up, w_down, w_out):
    width, part = block.shape[2], w_qkv.shape[2] // 4
    length, mixed_width = 8 * TOK, part // 3
    units, rows = w_up.shape[2] // 4, width // 32
    inputs = dict(
        block=block, gain_part=gain_part, w_qkv=w_qkv, w_up=w_up, w_down=w_down, w_out=w_out
    )
    blocks = struct((2, TOK, width), F32)
    wide = struct((length, width), BF)
    next_u, next_o = struct((2, 4, rows, units), BF), struct((2, *w_out.shape[1:]), BF)
    early = dict(
        hidden=struct(block.shape, BF),
        gains=struct((gain_part.shape[0], width), F32),
        normed_0=wide,
        qkv_0=struct((length, part), BF),
        wq_0=struct((2, 4, 2, 2, rows, part), BF),
    )
    outputs = dict(
        early,
        mixed=struct((length, mixed_width), BF),
        lse=struct((length, 128), F32),
        attn_out=blocks,
        resid=blocks,
        mlp=wide,
        active=struct((length, units), BF),
        slope=struct((length, units), BF),
        down_out=blocks,
        hidden_out=blocks,
        normed=wide,
        qkv=struct((length, part), BF),
        wu=struct((2, 4, 2, 2, rows, units), BF),
        wd=struct((2, *w_down.shape[1:]), BF),
        wo=next_o,
        wq=struct((2, 4, 2, 2, rows, part), BF),
    )
    kept = dict(
        quarter_q=struct((rows, 4 * part), BF),
        quarter_u=struct((rows, 4 * units), BF),
        deal_q=struct((4, rows, part), BF),
        deal_u=struct((4, rows, units), BF),
        quarter_q0=struct((rows, 4 * part), BF),
        quarter_u0=struct((rows, 4 * units), BF),
        deal_q0=struct((4, rows, part), BF),
        deal_u0=struct((4, rows, units), BF),
    )
    scratch = held(outputs, kept)
    outputs = dict(outputs, next_u=next_u, next_o=next_o)
    scratch |= scatter_scratch(ATTN, width) | scatter_scratch(DOWN, width)

    def tokens_in(ns, place, ahead):
        copies = ns.copies
        upper, y, x = place.upper, place.y, place.x
        columns = pl.ds(pl.multiple_of(place.grp * TOK, TOK), TOK)
        line = [place.line(offset)[0] for offset in range(1, 8)]
        quarter_q = quarter_of(ns, place, ns.w_qkv, 0, ns.quarter_q_v)
        quarter_u = quarter_of(ns, place, ns.w_up, 0, ns.quarter_u_v)
        kept = copies.local(ns.block.at[upper], ns.hidden_v.at[upper])
        gain_own = copies.local(ns.gain_part, ns.gains_v.at[:, columns])
        quarter_q.wait()
        arrange(ns.quarter_q_v, ns.deal_q_v, 6)
        meet(with_line(place))
        gain_rest = [copies.remote(ns.gain_part, ns.gains_v.at[:, columns], at) for at in line]
        wq_dealt = deal(copies, place, ns.deal_q_v, ns.wq_v.at[upper, place.t, y, x])
        next(wq_dealt)
        next(wq_dealt)
        brought = copies.remote(ns.block.at[1 - upper], ns.hidden_v.at[upper], place.far)
        next(ahead)
        out_in = copies.remote(ns.w_out.at[0, y, x], ns.wo_v.at[upper, y, x], place.far)
        wq_spread = spread(copies, place, by_columns(ns.wq_v))
        out_spread = spread(copies, place, by_rows(ns.wo_v, place))
        up_dealt = deal(copies, place, ns.deal_u_v, ns.wu_v.at[upper, place.t, y, x])
        quarter_u.wait()
        arrange(ns.quarter_u_v, ns.deal_u_v, 2)
        next(up_dealt)
        kept.wait()
        gain_own.wait()
        for copy in gain_rest:
            copy.wait_recv()

        def late():
            next(wq_spread)
            brought.wait_recv()
            copies.store(ns.hidden_v, ns.hidden)

        def out_arrived():
            out_in.wait_recv()
            next(out_spread)

        def wait_weights():
            next(ahead)
            next(wq_spread)
            copies.store(ns.wq_v, ns.wq)

        copies.store(ns.gains_v, ns.gains)
        order = (upper, 1 - upper)
        blocks = [
            functools.partial(
                lambda s: norm(ns.hidden_v[s].astype(F32), ns.gains_v[0:1, :]).astype(BF), stream
            )
            for stream in order
        ]
        plan = Plan(
            [stages(wq_dealt), stages(wq_spread)],
            [stages(up_dealt)],
            [out_arrived],
            [stages(out_spread)],
        )
        next_qkv(ns, place, blocks, plan.tick, wait_weights, order, late)
        next(out_spread)
        return up_dealt

    def rest_of(ns, place, up_dealt, loads, down_in, q_deal):
        copies = ns.copies
        upper, t, y, x = place.upper, place.t, place.y, place.x
        unused, whole_o, whole_d, quarter_u = loads
        next(up_dealt)
        up_spread = spread(copies, place, by_columns(ns.wu_v))
        down_spread = spread(copies, place, by_rows(ns.wd_v, place))
        next(up_spread)
        q_spread = spread(copies, place, by_columns(ns.wq_v))
        u_deal = deal(copies, place, ns.deal_u_v, ns.next_u.at[upper, t])
        o_spread = spread(copies, place, by_rows(ns.next_o, place))
        rest = []

        def out_part():
            rest.append(copies.remote(ns.w_out.at[1, y, x], ns.next_o.at[upper, y, x], place.far))

        def deal_up():
            quarter_u.wait()
            arrange(ns.quarter_u_v, ns.deal_u_v, 2)
            next(u_deal)
            next(u_deal)

        def down_arrived():
            down_in.wait_recv()
            next(down_spread)

        def out_arrived():
            rest[0].wait_recv()
            next(o_spread)

        plan = Plan(
            [],
            [],
            [stages(up_spread)],
            [deal_up],
            [down_arrived],
            [stages(down_spread), out_part],
            [stages(q_deal), stages(q_spread)],
            [stages(q_spread)],
            [out_arrived],
            [],
            [stages(o_spread)],
            [stages(o_spread)],
        )
        gain = rows_of(ns, 0)

        def wait_out():
            whole_o.wait()
            copies.store(ns.wo_v, ns.wo)

        def wait_down():
            next(down_spread)
            whole_d.wait()
            copies.store(ns.wu_v, ns.wu)
            copies.store(ns.wd_v, ns.wd)

        def wait_next():
            next(q_spread)
            copies.store(ns.wq_v, ns.wq)

        down = fwd_mid(ns, place, gain, plan.tick, wait_out, lambda: next(up_spread), wait_down)
        copies.store(ns.mixed_v, ns.mixed)
        copies.store(ns.lse_v, ns.lse)
        copies.store(ns.attn_out_v, ns.attn_out)
        copies.store(ns.resid_v, ns.resid)
        copies.store(ns.mlp_v, ns.mlp)
        copies.store(ns.active_v, ns.active)
        copies.store(ns.slope_v, ns.slope)

        def block(stream):
            value = down.result(stream)
            ns.down_out_v[stream] = value
            hidden_out = ns.resid_v[stream] + norm(value, gain(3))
            ns.hidden_out_v[stream] = hidden_out
            return norm(hidden_out, gain(0, 1)).astype(BF)

        blocks = [functools.partial(block, stream) for stream in range(2)]
        next_qkv(ns, place, blocks, plan.tick, wait_next)
        copies.store(ns.down_out_v, ns.down_out)
        copies.store(ns.hidden_out_v, ns.hidden_out)
        plan.drain()
        next(u_deal)

    def first(ns):
        place = Place()
        initial = types.SimpleNamespace(**vars(ns))
        initial.normed, initial.normed_v = ns.normed_0, ns.normed_0_v
        initial.qkv, initial.qkv_v = ns.qkv_0, ns.qkv_0_v
        initial.wq, initial.wq_v = ns.wq_0, ns.wq_0_v
        initial.quarter_q_v, initial.quarter_u_v = ns.quarter_q0_v, ns.quarter_u0_v
        initial.deal_q_v, initial.deal_u_v = ns.deal_q0_v, ns.deal_u0_v
        upper, y, x = place.upper, place.y, place.x
        copies = ns.copies
        q_deal = deal(copies, place, ns.deal_q_v, ns.wq_v.at[upper, place.t, y, x])
        loads, down_in = [], []

        def ahead():
            loads.append(quarter_of(ns, place, ns.w_qkv, 1, ns.quarter_q_v))
            loads.append(copies.local(ns.w_out.at[0], ns.wo_v.at[upper]))
            loads.append(copies.local(ns.w_down.at[0], ns.wd_v.at[upper]))
            loads.append(quarter_of(ns, place, ns.w_up, 1, ns.quarter_u_v))
            yield
            loads[0].wait()
            arrange(ns.quarter_q_v, ns.deal_q_v, 6)
            target = ns.wd_v.at[upper, y, x]
            down_in.append(copies.remote(ns.w_down.at[0, y, x], target, place.far))
            next(q_deal)
            next(q_deal)
            yield

        up_dealt = tokens_in(initial, place, ahead())
        ns.qkv_in_v = ns.qkv_0_v
        ns.load.hidden = types.SimpleNamespace(wait=lambda: None)
        rest_of(ns, place, up_dealt, loads, down_in[0], q_deal)

    flops = 2 * length * width * (mixed_width + 2 * units + 2 * part)
    kernel, options = kernel_of(first, with_line, inputs, outputs, scratch, 0, 128, 96, 62, flops)
    results = pl.pallas_call(kernel, **options)(*inputs.values())
    return named(outputs, results)


def turn_kernel(lower, gains, w_down, w_out, cotangent):
    hidden = lower.hidden_out
    width = hidden.shape[2]
    length, part = lower.qkv.shape
    mixed_width = part // 3
    inputs = dict(
        qkv_in=lower.qkv, gains=gains, hidden=hidden, cot=cotangent,
        part_u=lower.next_u, part_o=lower.next_o, w_down=w_down, w_out=w_out,
    )
    rows, units = lower.next_u.shape[2:]
    blocks = struct((2, TOK, width), F32)
    outputs = dict(
        out=struct((2, TOK, width), BF),
        lse=struct((length, 128), F32),
        mixed_grad=struct((length, mixed_width), BF),
        gd=by_device((units, width), 1),
        gu=by_device((width, units), 4),
        go=by_device((mixed_width, width), 1),
        dg=struct((8, width), F32),
    )
    kept = dict(
        qkv_in=lower.qkv,
        hidden=hidden,
        gains=gains,
        cot=cotangent,
        wd=struct((2, *w_down.shape[1:]), BF),
        wo=lower.next_o,
        wu=struct((2, 4, 2, 2, rows, units), BF),
        mixed=struct((length, mixed_width), BF),
        attn_out=blocks,
        resid=blocks,
        grad=blocks,
        mlp=struct((length, width), BF),
        active=struct((length, units), BF),
        slope=struct((length, units), BF),
        up_grad=struct((length, units), BF),
        down_out=blocks,
        down_grad=struct((length, width), BF),
        attn_grad=struct((length, width), BF),
    )
    scratch = held(outputs, kept)
    outputs |= dict(resid_grad=blocks)
    for name in (ATTN, DOWN, UP):
        scratch |= scatter_scratch(name, width)
    scratch |= reduce_scratch(D1, 1, units // 8, width, 1)

    def turn(ns):
        place, copies = Place(), ns.copies
        upper, y, x = place.upper, place.y, place.x
        part_u = copies.local(ns.part_u, ns.wu_v.at[:, :, y, x])
        part_o = copies.local(ns.part_o.at[1 - upper], ns.wo_v.at[1 - upper])
        whole_o = copies.local(ns.w_out.at[1], ns.wo_v.at[upper])
        whole_d = copies.local(ns.w_down.at[1], ns.wd_v.at[upper])
        meet(with_few(place))
        down_in = copies.remote(ns.w_down.at[1, y, x], ns.wd_v.at[upper, y, x], place.far)
        part_u.wait()
        up_spread = spread(copies, place, by_columns(ns.wu_v))
        down_spread = spread(copies, place, by_rows(ns.wd_v, place))
        next(up_spread)
        ns.load.qkv_in.wait()
        far_in = []

        def bring():
            ns.load.cot.wait()
            far_in.append(copies.remote(ns.cot.at[1 - upper], ns.cot_far_v, place.far))

        def down_arrived():
            down_in.wait_recv()
            next(down_spread)

        plan = Plan(
            [],
            [],
            [stages(up_spread)],
            [],
            [down_arrived],
            [stages(down_spread), bring],
        )
        ns.load.gains.wait()
        ns.dg_v[...] = jnp.zeros_like(ns.dg_v)
        gain = rows_of(ns, 1)

        def wait_out():
            part_o.wait()
            whole_o.wait()

        def wait_down():
            next(down_spread)
            whole_d.wait()

        down = fwd_mid(
            ns, place, gain, plan.tick, wait_out, lambda: next(up_spread), wait_down
        )
        copies.store(ns.lse_v, ns.lse)
        far_in[0].wait_recv()

        def grad(stream):
            value = down.result(stream)
            ns.down_out_v[stream] = value
            own = jnp.where(upper == stream, ns.cot_v[stream], ns.cot_far_v[...])
            return own.astype(F32)

        def finish():
            for stream in range(2):
                out = ns.resid_v[stream] + norm(ns.down_out_v[stream], gain(3))
                ns.out_v[stream] = out.astype(BF)
            copies.store(ns.out_v, ns.out)

        d_first, unused = reduce_rep(copies, place, ns.gd_v, ns, D1)
        plan = Plan(
            [],
            [finish],
            [],
            [],
            [],
        )
        grads = [functools.partial(grad, stream) for stream in range(2)]
        store_up = functools.partial(copies.store, ns.gu_v, ns.gu)
        bwd_mid(ns, place, 1, grads, plan.tick, stages(d_first), store_up)
        copies.store(ns.go_v, ns.go)
        copies.store(ns.dg_v, ns.dg)
        next(d_first)
        copies.store(ns.gd_v, ns.gd)

    scratch["cot_far_v"] = pltpu.VMEM((TOK, width), BF)
    flops = 6 * length * width * (mixed_width + 2 * units)
    kernel, options = kernel_of(turn, with_few, inputs, outputs, scratch, 2, 64, 64, 63, flops)
    results = pl.pallas_call(kernel, **options)(*inputs.values())
    return named(outputs, results)


def backward_kernel(lower, turned):
    wo, wu, wd, wq = (matrix(value) for value in (lower.wo, lower.wu, lower.wd, lower.wq))
    width, units = wu.shape
    length, part = lower.qkv.shape
    mixed_width = wo.shape[0]
    inputs = dict(
        gu=turned.gu, d1=turned.gd, o1=turned.go, qkv_in=lower.qkv, lse=turned.lse,
        mixed_grad=turned.mixed_grad, dg=turned.dg, gains=lower.gains, wq=wq, normed=lower.normed,
        hidden=lower.hidden_out, grad=turned.resid_grad, down_out=lower.down_out, wd=wd,
        slope=lower.slope, wu=wu, active=lower.active, mlp=lower.mlp, resid=lower.resid,
        attn_out=lower.attn_out, wo=wo, mixed=lower.mixed,
    )
    blocks = struct((2, TOK, width), F32)
    kept = dict(
        gq=by_device(wq.shape, 4),
        gd=by_device(wd.shape, 1),
        gu=by_device(wu.shape, 4),
        go=by_device(wo.shape, 1),
        qkv_grad=struct(lower.qkv.shape, BF),
        dk=struct((length, mixed_width), F32),
        dv=struct((length, mixed_width), F32),
        down_grad=struct((length, width), BF),
        attn_grad=struct((length, width), BF),
    )
    outputs = dict(
        resid_grad=blocks,
        mixed_out=struct((length, mixed_width), BF),
        gd=kept["gd"],
        up_out=kept["gu"],
        go=kept["go"],
        dg_out=turned.dg,
        full_d=struct((2, 2, 2, units // 16, width), BF),
        full_u=struct((2, 2, width // 32, 4 * units), BF),
        full_q=struct((2, 2, width // 32, 4 * part), BF),
        full_o=struct((2, 2, 2, mixed_width // 16, width), BF),
    )
    loaded = dict(inputs)
    del loaded["d1"]
    scratch = held(loaded, kept)
    for name in (QKV, UP):
        scratch |= scatter_scratch(name, width)
    rows = width // 32
    for name, count, high, wide, steps in (
        (D1, 1, units // 8, width, 2),
        (U1, 4, rows, units, 3),
        (Q1, 4, rows, part, 3),
        (O1, 1, mixed_width // 8, width, 3),
    ):
        scratch |= finish_scratch(name, count, high, wide)
        scratch |= reduce_scratch(name, count, high, wide, steps)
    scratch |= reduce_scratch(D0, 1, units // 8, width, 1)

    def backward(ns):
        place, copies = Place(), ns.copies
        ns.up_grad_v = ns.normed_v
        line = [place.line(offset)[0] for offset in range(1, 8)]
        meet(with_line(place))
        unused, d1_second = reduce_rep(copies, place, ns.d1, ns, D1)
        u1_first, u1_second = reduce_rep(copies, place, ns.gu_v, ns, U1)
        o1_first, o1_second = reduce_rep(copies, place, ns.o1_v, ns, O1)
        q1_first, q1_second = reduce_rep(copies, place, ns.gq_v, ns, Q1)
        d0_first, unused = reduce_rep(copies, place, ns.gd_v, ns, D0)
        d1_line = line_rows(copies, place, ns, D1)
        u1_line = line_columns(copies, place, ns, U1)
        o1_line = line_rows(copies, place, ns, O1)
        q1_line = line_columns(copies, place, ns, Q1)
        d1_whole = whole_rows(copies, place, ns, D1, ns.full_d)
        u1_whole = whole_columns(copies, place, ns, U1, ns.full_u, 2)
        q1_whole = whole_columns(copies, place, ns, Q1, ns.full_q, 6)
        o1_whole = whole_rows(copies, place, ns, O1, ns.full_o)
        next(d1_second)
        ns.load.gu.wait()
        next(u1_first)
        ns.load.o1.wait()
        ns.load.qkv_in.wait()
        ns.load.lse.wait()
        ns.load.mixed_grad.wait()
        ns.load.dg.wait()
        plan = Plan(
            [stages(d1_second), stages(d1_line)],
            [],
            [],
            [stages(u1_first), stages(u1_second), stages(o1_first)],
            [],
            [stages(u1_second), stages(u1_line), stages(d1_line), stages(d1_whole)],
            [stages(o1_first), stages(o1_second), stages(q1_first), stages(q1_second)],
            [stages(d1_whole), stages(u1_line), stages(u1_whole)]
            + [stages(q1_second), stages(q1_line)],
            [stages(o1_second), stages(o1_line)],
            [stages(d1_whole), stages(u1_whole), stages(q1_line), stages(q1_whole)],
            [],
            [stages(o1_line), stages(o1_whole), stages(q1_whole)],
            [stages(u1_whole)],
            [stages(d0_first), stages(o1_whole)],
        )
        ns.load.gains.wait()
        grads = bwd_head(ns, place, 1, plan.tick, stages(q1_first), False)
        for copy in (ns.load.down_out, ns.load.wd, ns.load.slope, ns.load.wu, ns.load.active):
            copy.wait()
        for copy in (ns.load.mlp, ns.load.resid, ns.load.attn_out, ns.load.wo, ns.load.mixed):
            copy.wait()
        ns.mixed_grad = ns.mixed_out
        store_up = functools.partial(copies.store, ns.gu_v, ns.up_out)
        bwd_mid(ns, place, 0, grads, plan.tick, stages(d0_first), store_up, (1, 0))
        plan.drain()
        copies.store(ns.go_v, ns.go)
        copies.store(ns.gd_v, ns.gd)
        copies.store(ns.dg_v, ns.dg_out)
        next(q1_whole)
        next(o1_whole)

    flops = 6 * length * width * (mixed_width + 2 * units) + 4 * length * width * part
    kernel, options = kernel_of(backward, with_line, inputs, outputs, scratch, 3, 128, 128, 63, flops)
    results = pl.pallas_call(kernel, **options)(*inputs.values())
    return named(outputs, results)


def last_kernel(lower, turned, back):
    wq = matrix(lower.wq_0)
    width, part = wq.shape
    length, mixed_width = back.mixed_out.shape
    units, rows = back.up_out.shape[-1], width // 32
    inputs = dict(
        u0=back.up_out, d0=back.gd, o0=back.go, qkv_in=lower.qkv_0, lse=lower.lse,
        mixed_grad=back.mixed_out, dg=back.dg_out, gains=lower.gains, normed=lower.normed_0, wq=wq,
        hidden=lower.hidden, grad=back.resid_grad, second=turned.out,
    )
    outputs = dict(
        out=struct((2, TOK, width), BF),
        block_out=struct((2, TOK, width), BF),
        gain_grad=struct((8, TOK), F32),
        full_d=struct(back.full_d.shape, BF),
        full_u=struct(back.full_u.shape, BF),
        full_q=struct(back.full_q.shape, BF),
        full_o=struct(back.full_o.shape, BF),
    )
    kept = dict(
        out=outputs["out"],
        gq=by_device(wq.shape, 4),
        qkv_grad=struct(lower.qkv_0.shape, BF),
        dk=struct((length, mixed_width), F32),
        dv=struct((length, mixed_width), F32),
        dg_line=struct((8, 8, TOK), F32),
        dg_pass=struct((5, 8, TOK), F32),
    )
    loaded = dict(inputs)
    del loaded["d0"]
    scratch = held(loaded, kept)
    scratch |= scatter_scratch(QKV, width)
    for name, count, high, wide, steps in (
        (D0, 1, units // 8, width, 2),
        (U0, 4, rows, units, 3),
        (Q0, 4, rows, part, 3),
        (O0, 1, mixed_width // 8, width, 3),
    ):
        scratch |= reduce_scratch(name, count, high, wide, steps)
        scratch |= finish_scratch(name, count, high, wide)

    def last(ns):
        place, copies = Place(), ns.copies
        line = [place.line(offset)[0] for offset in range(1, 8)]
        meet(with_line(place))
        unused, d0_second = reduce_rep(copies, place, ns.d0, ns, D0)
        u0_first, u0_second = reduce_rep(copies, place, ns.u0_v, ns, U0)
        o0_first, o0_second = reduce_rep(copies, place, ns.o0_v, ns, O0)
        q0_first, q0_second = reduce_rep(copies, place, ns.gq_v, ns, Q0)
        d0_line = line_rows(copies, place, ns, D0)
        o0_line = line_rows(copies, place, ns, O0)
        u0_line = line_columns(copies, place, ns, U0)
        q0_line = line_columns(copies, place, ns, Q0)
        d0_whole = whole_rows(copies, place, ns, D0, ns.full_d)
        o0_whole = whole_rows(copies, place, ns, O0, ns.full_o)
        u0_whole = whole_columns(copies, place, ns, U0, ns.full_u, 2)
        q0_whole = whole_columns(copies, place, ns, Q0, ns.full_q, 6)
        upper = place.upper
        second = copies.remote(ns.second.at[1 - upper], ns.block_out.at[upper], place.far)
        next(d0_second)
        ns.load.u0.wait()
        next(u0_first)
        ns.load.qkv_in.wait()
        ns.load.lse.wait()
        ns.load.mixed_grad.wait()
        ns.load.dg.wait()
        ns.load.o0.wait()
        plan = Plan(
            [stages(d0_second), stages(d0_line)],
            [],
            [],
            [stages(u0_first), stages(u0_second), stages(q0_first)],
            [stages(d0_line), stages(d0_whole)],
        )
        ns.load.gains.wait()
        grads = bwd_head(ns, place, 0, plan.tick, lambda: None, True)
        ns.load.second.wait()
        copies.store(ns.second_v.at[upper], ns.block_out.at[upper])
        ns.out_v[1] = grads[1]().astype(BF)
        for task in (u0_second, u0_line, q0_first, q0_second, o0_first, d0_whole):
            next(task)
        ns.out_v[0] = grads[0]().astype(BF)
        copies.store(ns.out_v.at[upper], ns.out.at[upper])
        gain_grad = gain_sum(ns, copies, place)
        for task in (
            gain_grad, q0_second, q0_line, o0_first, o0_second, u0_line, u0_whole, d0_whole,
            gain_grad, o0_second, o0_line,
        ):
            next(task)
        moved = copies.remote(ns.out_v.at[1 - upper], ns.out.at[upper], place.far)
        for task in (
            u0_whole, q0_line, q0_whole, o0_line, o0_whole, gain_grad, u0_whole, q0_whole,
            o0_whole, gain_grad, q0_whole, o0_whole,
        ):
            next(task)
        moved.wait_recv()
        second.wait_recv()

    flops = 4 * length * width * part
    kernel, options = kernel_of(last, with_line, inputs, outputs, scratch, 4, 128, 128, 60, flops)
    results = pl.pallas_call(kernel, **options)(*inputs.values())
    return named(outputs, results)


def widen(pairs):
    flat = [value for group in pairs for value in group]
    outs = [struct((len(group), *group[0].shape), F32) for group in pairs]

    def finish(*refs):
        sources, targets = refs[: len(flat)], refs[len(flat) : len(flat) + len(outs)]
        low, wide = refs[len(flat) + len(outs) :][: len(flat)], refs[-len(flat) - 2 : -2]
        sem_in, sem_out = refs[-2:]
        slots = [(g, n) for g, group in enumerate(pairs) for n in range(len(group))]
        loads = [pltpu.make_async_copy(sources[i], low[i], sem_in.at[i]) for i in range(len(flat))]
        for copy in loads:
            copy.start()
        stores = []
        for i, (g, n) in enumerate(slots):
            loads[i].wait()

            def step(index):
                at = tile_of(index, 32)
                wide[i][at, :] = low[i][at, :].astype(F32)

            loop(low[i].shape[0] // 32, step)
            stores.append(pltpu.make_async_copy(wide[i], targets[g].at[n], sem_out.at[i]))
            stores[-1].start()
        for copy in stores:
            copy.wait()

    size = sum(value.size for value in flat)
    return pl.pallas_call(
        finish,
        name=finish.__name__,
        out_shape=outs,
        in_specs=[pl.BlockSpec(memory_space=pl.ANY)] * len(flat),
        out_specs=[pl.BlockSpec(memory_space=pl.ANY)] * len(outs),
        scratch_shapes=[
            *(pltpu.VMEM(value.shape, BF) for value in flat),
            *(pltpu.VMEM(value.shape, F32) for value in flat),
            pltpu.SemaphoreType.DMA((len(flat),)),
            pltpu.SemaphoreType.DMA((len(flat),)),
        ],
        compiler_params=pltpu.CompilerParams(vmem_limit_bytes=63 << 20),
        cost_estimate=pl.CostEstimate(flops=size, bytes_accessed=6 * size, transcendentals=0),
    )(*flat)


def gain_sum(ns, copies, place):
    def columns(grp):
        return pl.ds(pl.multiple_of(grp * TOK, TOK), TOK)

    moved = []
    for offset in range(1, 8):
        device, upper, t = place.line(offset)
        source = ns.dg_v.at[:, columns(upper * 4 + t)]
        moved.append(copies.remote(source, ns.dg_line_v.at[place.grp], device))
    ns.dg_line_v[place.grp] = ns.dg_v[:, columns(place.grp)]
    yield
    for copy in moved:
        copy.wait_recv()
    ns.dg_pass_v[0] = jnp.sum(ns.dg_line_v[...], axis=0)
    moved = copies.remote(ns.dg_pass_v.at[0], ns.dg_pass_v.at[1], place.along_x)
    yield
    moved.wait_recv()
    ns.dg_pass_v[2] = ns.dg_pass_v[0] + ns.dg_pass_v[1]
    moved = copies.remote(ns.dg_pass_v.at[2], ns.dg_pass_v.at[3], place.along_y)
    yield
    moved.wait_recv()
    ns.dg_pass_v[4] = ns.dg_pass_v[2] + ns.dg_pass_v[3]
    copies.store(ns.dg_pass_v.at[4], ns.gain_grad)
    yield


def body_pairs(block_in, cotangent, w_qkv, w_out, w_up, w_down, norm_gains):
    layers, rows, width = w_out.shape
    hidden_unit = w_down.shape[1]
    gain_part = jnp.transpose(norm_gains.astype(F32), (0, 2, 1)).reshape(layers * 4, rows)
    down_parts = w_down.reshape(layers, 2, 2, 2, hidden_unit // 8, width)
    out_parts = w_out.reshape(layers, 2, 2, 2, rows // 8, width)

    lower = first_kernel(block_in[:, 0], gain_part, w_qkv, w_up, down_parts, out_parts)
    turned = turn_kernel(lower, lower.gains, down_parts, out_parts, cotangent[:, 0])
    back = backward_kernel(lower, turned)
    last = last_kernel(lower, turned, back)

    pairs = (
        (last.full_d, back.full_d),
        (last.full_u, back.full_u),
        (last.full_q, back.full_q),
        (last.full_o, back.full_o),
        (last.out,),
    )
    wide = widen([[matrix(value) for value in group] for group in pairs])
    return (
        last.block_out[:, None],
        wide[4].reshape(block_in.shape),
        wide[2],
        wide[3],
        wide[1],
        wide[0],
        jnp.transpose(last.gain_grad.reshape(layers, 4, rows), (0, 2, 1)),
    )


def norm_apply(values, gains):
    return values * lax.rsqrt(jnp.mean(values * values, axis=-1, keepdims=True) + EPS) * gains


def inner_rows(left, right):
    return lax.dot_general(
        left, right, (((0,), (0,)), ((), ())), preferred_element_type=jnp.float32
    )


def times_trans(left, right):
    return lax.dot_general(
        left, right, (((1,), (1,)), ((), ())), preferred_element_type=jnp.float32
    )


def split_blocks(whole):
    length = whole.shape[0]
    width = min(512, length)
    count = length // width
    return (whole.reshape(count, width, HEADS, HDIM), width, count)


def block_at(blocks, index):
    return lax.dynamic_index_in_dim(blocks, index, 0, keepdims=False)


def key_scores(query, key_block, key_start, query_pos):
    scale = HDIM ** (-0.5)
    scores = (
        jnp.einsum("qhd,khd->hqk", query, key_block, preferred_element_type=jnp.float32) * scale
    )
    key_pos = key_start + jnp.arange(key_block.shape[0], dtype=jnp.int32)
    allowed = key_pos[None, :] <= query_pos[:, None]
    return (scores, allowed[None])


def attend_split(query, keys_all, values_all, query_pos):
    key_blocks, width, count = split_blocks(keys_all)
    value_blocks = split_blocks(values_all)[0]
    row_count = query.shape[0]
    upper = query_pos[row_count - 1] // width + 1

    def total_step(index, carry):
        running, total = carry
        scores, allowed = key_scores(query, block_at(key_blocks, index), index * width, query_pos)
        newest = jnp.maximum(running, jnp.max(jnp.where(allowed, scores, NEGATIVE), axis=-1))
        terms = jnp.where(allowed, jnp.exp(scores - newest[..., None]), 0.0)
        total = total * jnp.exp(running - newest) + jnp.sum(terms, axis=-1)
        return (newest, total)

    start_run = jnp.full((HEADS, row_count), NEGATIVE, jnp.float32)
    start_total = jnp.zeros((HEADS, row_count), jnp.float32)
    running, total = lax.fori_loop(0, upper, total_step, (start_run, start_total))
    log_total = running + jnp.log(total)

    def mix_step(index, accum):
        scores, allowed = key_scores(query, block_at(key_blocks, index), index * width, query_pos)
        probs = jnp.where(allowed, jnp.exp(scores - log_total[..., None]), 0.0)
        return accum + jnp.einsum(
            "hqk,khd->qhd",
            probs.astype(jnp.bfloat16),
            block_at(value_blocks, index),
            preferred_element_type=jnp.float32,
        )

    start_mix = jnp.zeros((row_count, HEADS, HDIM), jnp.float32)
    mixed = lax.fori_loop(0, upper, mix_step, start_mix)
    return (mixed.reshape(row_count, HEADS * HDIM), log_total)


def attend_back_split(query, keys_all, values_all, log_total, out_grad, delta, query_pos):
    key_blocks, width, count = split_blocks(keys_all)
    value_blocks = split_blocks(values_all)[0]
    row_count = query.shape[0]
    upper = query_pos[row_count - 1] // width + 1
    scale = HDIM ** (-0.5)

    def back_step(index, carry):
        query_acc, pieces = carry
        key_block = block_at(key_blocks, index)
        value_block = block_at(value_blocks, index)
        scores, allowed = key_scores(query, key_block, index * width, query_pos)
        probs = jnp.where(allowed, jnp.exp(scores - log_total[..., None]), 0.0)
        prob_grad = jnp.einsum(
            "qhd,khd->hqk", out_grad, value_block, preferred_element_type=jnp.float32
        )
        score_grad = (probs * (prob_grad - delta[..., None])).astype(jnp.bfloat16)
        query_acc = (
            query_acc
            + jnp.einsum("hqk,khd->qhd", score_grad, key_block, preferred_element_type=jnp.float32)
            * scale
        )
        key_grad = (
            jnp.einsum("hqk,qhd->khd", score_grad, query, preferred_element_type=jnp.float32)
            * scale
        )
        value_grad = jnp.einsum(
            "hqk,qhd->khd", probs.astype(jnp.bfloat16), out_grad, preferred_element_type=jnp.float32
        )
        joined = jnp.concatenate(
            [key_grad.reshape(width, HEADS * HDIM), value_grad.reshape(width, HEADS * HDIM)], axis=1
        )
        pieces = lax.dynamic_update_index_in_dim(pieces, joined, index, 0)
        return (query_acc, pieces)

    start_acc = jnp.zeros((row_count, HEADS, HDIM), jnp.float32)
    start_pieces = jnp.zeros((count, width, 2 * HEADS * HDIM), jnp.float32)
    query_grad, pieces = lax.fori_loop(0, upper, back_step, (start_acc, start_pieces))
    return (query_grad.reshape(row_count, HEADS * HDIM), pieces.reshape(-1, pieces.shape[-1]))


def layer_forward(hidden_in, weights, query_pos):
    w_qkv_full, w_out_full, w_up_full, w_down_full, gain_full = weights
    gains_f = gain_full.astype(jnp.float32)
    row_count = hidden_in.shape[0]
    width = w_out_full.shape[1]
    normed = norm_apply(hidden_in, gains_f[:, 0]).astype(jnp.bfloat16)
    qkv_low = jnp.dot(normed, w_qkv_full, preferred_element_type=jnp.float32).astype(jnp.bfloat16)
    query = qkv_low[:, :width]
    keys_all, values_all = (
        lax.all_gather(qkv_low[:, width : 2 * width], "grp", axis=0, tiled=True),
        lax.all_gather(qkv_low[:, 2 * width :], "grp", axis=0, tiled=True),
    )
    mixed, log_total = attend_split(
        query.reshape(row_count, HEADS, HDIM),
        keys_all.reshape(-1, HEADS, HDIM),
        values_all.reshape(-1, HEADS, HDIM),
        query_pos,
    )
    mixed_low = mixed.astype(jnp.bfloat16)
    attn_out = jnp.dot(mixed_low, w_out_full, preferred_element_type=jnp.float32)
    resid = hidden_in + norm_apply(attn_out, gains_f[:, 1])
    mlp_in = norm_apply(resid, gains_f[:, 2]).astype(jnp.bfloat16)
    up_out = jnp.dot(mlp_in, w_up_full, preferred_element_type=jnp.float32)
    active = jax.nn.gelu(up_out).astype(jnp.bfloat16)
    down_out = jnp.dot(active, w_down_full, preferred_element_type=jnp.float32)
    result = resid + norm_apply(down_out, gains_f[:, 3])
    kept = (
        hidden_in,
        normed,
        qkv_low,
        mixed,
        mixed_low,
        log_total,
        attn_out,
        resid,
        mlp_in,
        up_out,
        active,
        down_out,
    )
    return (result, kept)


def layer_backward(grad_out, weights, kept, query_pos):
    w_qkv_full, w_out_full, w_up_full, w_down_full, gain_full = weights
    (
        hidden_in,
        normed,
        qkv_low,
        mixed,
        mixed_low,
        log_total,
        attn_out,
        resid,
        mlp_in,
        up_out,
        active,
        down_out,
    ) = kept
    gains_f = gain_full.astype(jnp.float32)
    row_count = hidden_in.shape[0]
    width = w_out_full.shape[1]
    unused, puller = jax.vjp(norm_apply, down_out, gains_f[:, 3])
    down_grad, gain_four = puller(grad_out)
    down_low = down_grad.astype(jnp.bfloat16)
    w_down_grad = inner_rows(active, down_low)
    active_grad = times_trans(down_low, w_down_full)
    unused, puller = jax.vjp(jax.nn.gelu, up_out)
    up_low = puller(active_grad)[0].astype(jnp.bfloat16)
    w_up_grad = inner_rows(mlp_in, up_low)
    mlp_grad = times_trans(up_low, w_up_full)
    unused, puller = jax.vjp(norm_apply, resid, gains_f[:, 2])
    resid_part, gain_three = puller(mlp_grad)
    resid_grad = grad_out + resid_part
    unused, puller = jax.vjp(norm_apply, attn_out, gains_f[:, 1])
    attn_grad, gain_two = puller(resid_grad)
    attn_low = attn_grad.astype(jnp.bfloat16)
    w_out_grad = inner_rows(mixed_low, attn_low)
    mixed_grad = times_trans(attn_low, w_out_full).astype(jnp.bfloat16)
    keys_all, values_all = (
        lax.all_gather(qkv_low[:, width : 2 * width], "grp", axis=0, tiled=True),
        lax.all_gather(qkv_low[:, 2 * width :], "grp", axis=0, tiled=True),
    )
    delta = jnp.sum(
        (mixed_grad.astype(jnp.float32) * mixed).reshape(row_count, HEADS, HDIM), axis=-1
    ).T
    query_low = qkv_low[:, :width]
    query_grad, key_value_terms = attend_back_split(
        query_low.reshape(row_count, HEADS, HDIM),
        keys_all.reshape(-1, HEADS, HDIM),
        values_all.reshape(-1, HEADS, HDIM),
        log_total,
        mixed_grad.reshape(row_count, HEADS, HDIM),
        delta,
        query_pos,
    )
    key_value_grad = lax.psum_scatter(
        key_value_terms.astype(jnp.bfloat16), "grp", scatter_dimension=0, tiled=True
    ).astype(jnp.float32)
    qkv_grad = jnp.concatenate([query_grad, key_value_grad], axis=1).astype(jnp.bfloat16)
    w_qkv_grad = inner_rows(normed, qkv_grad)
    normed_grad = times_trans(qkv_grad, w_qkv_full)
    unused, puller = jax.vjp(norm_apply, hidden_in, gains_f[:, 0])
    input_part, gain_one = puller(normed_grad)
    gain_grad = jnp.stack([gain_one, gain_two, gain_three, gain_four], axis=1)
    return (resid_grad + input_part, (w_qkv_grad, w_out_grad, w_up_grad, w_down_grad, gain_grad))


def body_general(block_in, cotangent, w_qkv, w_out, w_up, w_down, norm_gains):
    layer_count = w_qkv.shape[0]
    micro_count = block_in.shape[0]
    row_count = block_in.shape[2]
    query_pos = lax.axis_index("grp") * row_count + jnp.arange(row_count, dtype=jnp.int32)
    totals = [None] * layer_count
    outputs = []
    input_grads = []
    for micro_idx in range(micro_count):
        hidden = block_in[micro_idx, 0].astype(jnp.float32)
        saved = []
        for layer_idx in range(layer_count):
            hidden, kept = layer_forward(
                hidden,
                (
                    lax.all_gather(w_qkv[layer_idx], "grp", axis=0, tiled=True),
                    lax.all_gather(w_out[layer_idx], "grp", axis=0, tiled=True),
                    lax.all_gather(w_up[layer_idx], "grp", axis=0, tiled=True),
                    lax.all_gather(w_down[layer_idx], "grp", axis=0, tiled=True),
                    lax.all_gather(norm_gains[layer_idx], "grp", axis=0, tiled=True),
                ),
                query_pos,
            )
            saved.append(kept)
        outputs.append(hidden.astype(jnp.bfloat16))
        grad_flow = cotangent[micro_idx, 0].astype(jnp.float32)
        for layer_idx in reversed(range(layer_count)):
            grad_flow, parts = layer_backward(
                grad_flow,
                (
                    lax.all_gather(w_qkv[layer_idx], "grp", axis=0, tiled=True),
                    lax.all_gather(w_out[layer_idx], "grp", axis=0, tiled=True),
                    lax.all_gather(w_up[layer_idx], "grp", axis=0, tiled=True),
                    lax.all_gather(w_down[layer_idx], "grp", axis=0, tiled=True),
                    lax.all_gather(norm_gains[layer_idx], "grp", axis=0, tiled=True),
                ),
                saved[layer_idx],
                query_pos,
            )
            if totals[layer_idx] is None:
                totals[layer_idx] = parts
            else:
                totals[layer_idx] = tuple(
                    (left + right for left, right in zip(totals[layer_idx], parts))
                )
        input_grads.append(grad_flow)
    reduced = []
    for layer_idx in range(layer_count):
        accum = totals[layer_idx]
        shards = (
            lax.psum_scatter(
                accum[0].astype(jnp.bfloat16), "grp", scatter_dimension=0, tiled=True
            ).astype(jnp.float32),
            lax.psum_scatter(
                accum[1].astype(jnp.bfloat16), "grp", scatter_dimension=0, tiled=True
            ).astype(jnp.float32),
            lax.psum_scatter(
                accum[2].astype(jnp.bfloat16), "grp", scatter_dimension=0, tiled=True
            ).astype(jnp.float32),
            lax.psum_scatter(
                accum[3].astype(jnp.bfloat16), "grp", scatter_dimension=0, tiled=True
            ).astype(jnp.float32),
            lax.psum_scatter(
                accum[4].astype(jnp.bfloat16), "grp", scatter_dimension=0, tiled=True
            ).astype(jnp.float32),
        )
        reduced.append(
            (
                lax.psum(shards[0].astype(jnp.bfloat16), "rep").astype(jnp.float32),
                lax.psum(shards[1].astype(jnp.bfloat16), "rep").astype(jnp.float32),
                lax.psum(shards[2].astype(jnp.bfloat16), "rep").astype(jnp.float32),
                lax.psum(shards[3].astype(jnp.bfloat16), "rep").astype(jnp.float32),
                lax.psum(shards[4].astype(jnp.bfloat16), "rep").astype(jnp.float32),
            )
        )
    block_out = jnp.stack(outputs)[:, None]
    block_in_grad = jnp.stack(input_grads)[:, None]
    stacked = [
        jnp.stack([reduced[layer_idx][member] for layer_idx in range(layer_count)])
        for member in range(5)
    ]
    return (block_out, block_in_grad, stacked[0], stacked[1], stacked[2], stacked[3], stacked[4])


def solution(mesh):
    rep_size, grp_size = mesh.shape["rep"], mesh.shape["grp"]

    def body(block_in, cotangent, w_qkv, w_out, w_up, w_down, norm_gains):
        sizes = (rep_size, grp_size, block_in.shape[0], w_qkv.shape[0], block_in.shape[2])
        fits = sizes == (4, 8, 2, 2, TOK)
        chosen = body_pairs if fits else body_general
        return chosen(block_in, cotangent, w_qkv, w_out, w_up, w_down, norm_gains)

    tokens = P(None, "rep", "grp", None)
    rows = P(None, "grp", None)
    return jax.shard_map(
        body,
        mesh=mesh,
        in_specs=(tokens, tokens, rows, rows, rows, rows, rows),
        out_specs=(tokens, tokens, rows, rows, rows, rows, rows),
        check_vma=False,
    )
```
